128 devices in a mesh: layer: 4 (over y_lo, core), latent: 16 (over x, z), row: 2 (over y_hi).
Axes of the slice: x: 4, y: 4 (y_hi: 2, y_lo: 2; y = y_hi * 2 + y_lo), z: 4, core: 2. Of those that a mesh axis runs over, the one named last changes fastest.
Arguments:
- inputs: bfloat16 [1024, 4, 3584], P('row', 'layer'), may hold values from -6 to 6
- clean_acts: bfloat16 [1024, 4, 3584], P('row', 'layer'), may hold values from -6 to 6
- enc_weight: bfloat16 [4, 3584, 12288], P('layer', None, 'latent'), may hold values from -0.0625 to 0.0625
- enc_bias: float32 [12288], P('latent'), may hold values from -3 to 3
- dec_weight: bfloat16 [4, 12288, 3584], P('layer', 'latent'), may hold values from -0.109375 to 0.109375
- dec_bias: float32 [4, 3584], P('layer'), may hold values from -3 to 3
- pairing: int32 [1024], replicated, may hold values from 0 to 1023, each once
- targets: int32 [1024], replicated, may hold values from 0 to 12287
Outputs:
- input_grad: bfloat16 [1024, 4, 3584], P('row', 'layer', 'latent')
The draws below stay inside these ranges and needn't reach their ends.
Inputs may be any that keep to these rules, and one draw needn't show every extreme that they name: pairing is a permutation of the rows.
All inputs are finite; a program needn't handle non-finite values.
Results may differ from the reference program's by a relative error of at most 0.018.
Values may be sent and summed in bfloat16 or wider, within the bound.
A program may use at most 128 MiB of HBM per device.

```python
import jax
import jax.numpy as jnp

D = 3584
LATENTS = 12288
LAYERS = 4
ROWS = 1024
N_LATENT = 16


def touch_ends(result, key, low, high):
    longest = result.shape.index(max(result.shape))
    spots = []
    for shift in (0, 1):
        where = [jax.random.randint(jax.random.fold_in(key, axis), (), 0, length) for axis, length in enumerate(result.shape)]
        where[longest] = (where[longest] + shift) % result.shape[longest]
        spots.append(tuple(where))
    return result.at[spots[0]].set(low).at[spots[1]].set(high)


def raised(array, key, source, target, shards_of, factor):
    owner, partner = [(jnp.arange(array.shape[axis_at]) // (array.shape[axis_at] // shards_of)).reshape([-1 if axis == axis_at else 1 for axis in range(array.ndim)]) for axis_at in (source, target)]
    chosen = jax.random.permutation(key, shards_of)[partner]
    strong = (owner == chosen) | (owner == (partner + shards_of // 2) % shards_of)
    return jnp.where(strong, factor * array, array)


def block_levels(key, shape, cuts, least, high):
    level, own = 1.0, jax.random.fold_in(key, 6)
    for position, parts in cuts:
        draws = jnp.exp(jax.random.uniform(jax.random.fold_in(own, position), (parts,), jnp.float32, least / len(cuts), high / len(cuts)))
        level = level * jnp.repeat(draws, shape[position] // parts).reshape([-1 if axis == position else 1 for axis in range(len(shape))])
    return level


def normal_values(stream_key, extent, width, reach, cuts=(), kind=jnp.bfloat16):
    entries = width * jax.random.normal(stream_key, extent, jnp.float32)
    if cuts:
        entries = entries * block_levels(stream_key, extent, cuts, -0.22, 0.18)
    return jnp.clip(entries, -reach, reach).astype(kind)


def noise_with(stream_key, shape, scale, most, cuts, heavy, held_as=jnp.bfloat16):
    array = scale * jax.random.normal(stream_key, shape, jnp.float32)
    if cuts:
        array = array * block_levels(stream_key, shape, cuts, -0.22, 0.18)
    return jnp.clip(raised(array, jax.random.fold_in(stream_key, 3), *heavy), -most, most).astype(held_as)


def setup_inputs(seed: int = 0) -> dict:
    key_of = jax.random.split(jax.random.key(seed), 9)
    inputs = normal_values(key_of[0], (ROWS, LAYERS, D), 1.0, 6.0, ((0, 2), (1, 4)))
    clean_acts = normal_values(key_of[1], (ROWS, LAYERS, D), 1.0, 6.0, ((0, 2), (1, 4)))
    enc_weight = noise_with(key_of[2], (LAYERS, D, LATENTS), (D * LAYERS) ** -0.5, 0.0625, ((0, 4), (2, 16)), (2, 1, 16, 2.0))
    enc_bias = normal_values(key_of[3], (LATENTS,), 0.5, 3.0, ((0, 16),), jnp.float32)
    dec_weight = normal_values(key_of[4], (LAYERS, LATENTS, D), (LATENTS // 4) ** -0.5, 0.109375, ((0, 4), (1, 16)))
    dec_bias = normal_values(key_of[5], (LAYERS, D), 0.5, 3.0, ((0, 4),), jnp.float32)
    pairing = jax.random.permutation(key_of[6], ROWS).astype(jnp.int32)
    targets = touch_ends(jax.random.randint(key_of[7], (ROWS,), 0, LATENTS), jax.random.fold_in(key_of[7], 1), 0, LATENTS - 1).astype(jnp.int32)
    return {"inputs": inputs, "clean_acts": clean_acts, "enc_weight": enc_weight, "enc_bias": enc_bias, "dec_weight": dec_weight, "dec_bias": dec_bias, "pairing": pairing, "targets": targets}


MARGIN = 16.0


def reference(inputs, clean_acts, enc_weight, enc_bias, dec_weight, dec_bias, pairing, targets):
    group = LATENTS // N_LATENT
    preact = jnp.zeros((ROWS, LATENTS), jnp.float32)
    for layer_idx in range(LAYERS):
        preact = preact + jnp.dot(inputs[:, layer_idx], enc_weight[layer_idx], preferred_element_type=jnp.float32)
    preact = preact + enc_bias
    features = jnp.maximum(preact, 0.0).astype(jnp.bfloat16)
    feat_split = features.reshape(ROWS, N_LATENT, group)
    feat_grad = jnp.zeros((ROWS, LATENTS), jnp.float32)
    for layer_idx in range(LAYERS):
        dec_split = dec_weight[layer_idx].reshape(N_LATENT, group, D)
        partials = jnp.einsum("rng,ngd->nrd", feat_split, dec_split, preferred_element_type=jnp.float32)
        recon = jnp.sum(partials.astype(jnp.bfloat16).astype(jnp.float32), axis=0) + dec_bias[layer_idx]
        recon_error = (recon - clean_acts[:, layer_idx].astype(jnp.float32)).astype(jnp.bfloat16)
        layer_term = jnp.dot(recon_error, dec_weight[layer_idx].T, preferred_element_type=jnp.float32)
        feat_grad = feat_grad + layer_term.astype(jnp.bfloat16).astype(jnp.float32)
    latent_ids = jnp.arange(LATENTS, dtype=jnp.int32)
    target_hot = (targets[:, None] == latent_ids[None, :]).astype(jnp.float32)
    moved = jnp.zeros((ROWS, LATENTS), jnp.float32).at[pairing].add(target_hot)
    margin_table = target_hot - moved
    pre_grad = jnp.where(preact > 0, feat_grad - MARGIN * margin_table, 0.0).astype(jnp.bfloat16)
    pre_split = pre_grad.reshape(ROWS, N_LATENT, group)
    outputs = []
    for layer_idx in range(LAYERS):
        enc_split = enc_weight[layer_idx].reshape(D, N_LATENT, group)
        partials = jnp.einsum("rng,dng->nrd", pre_split, enc_split, preferred_element_type=jnp.float32)
        total = jnp.sum(partials.astype(jnp.bfloat16).astype(jnp.float32), axis=0)
        outputs.append(total.astype(jnp.bfloat16))
    return jnp.stack(outputs, axis=1)
```

```python
import jax
import jax.numpy as jnp
from jax import lax
from jax.sharding import PartitionSpec as P

MARGIN = 16.0


def local(inputs, clean_acts, enc_weight, enc_bias, dec_weight, dec_bias, pairing, targets):
    row_count = inputs.shape[0]
    lat_count = enc_weight.shape[2]
    all_rows = pairing.shape[0]
    n_lat = lax.psum(1, "latent")
    d_model = inputs.shape[2]
    chunk = d_model // n_lat
    partial_pre = jnp.einsum("rld,ldf->rf", inputs, enc_weight, preferred_element_type=jnp.float32)
    preact = lax.psum(partial_pre, "layer") + enc_bias
    features = jnp.maximum(preact, 0.0).astype(jnp.bfloat16)
    partial_recon = jnp.einsum(
        "rf,lfd->rld", features, dec_weight, preferred_element_type=jnp.float32
    )
    recon = (
        lax.psum(partial_recon.astype(jnp.bfloat16), "latent").astype(jnp.float32) + dec_bias[None]
    )
    recon_error = (recon - clean_acts.astype(jnp.float32)).astype(jnp.bfloat16)
    partial_grad = jnp.einsum(
        "rld,lfd->rf", recon_error, dec_weight, preferred_element_type=jnp.float32
    )
    feat_grad = lax.psum(partial_grad.astype(jnp.bfloat16), "layer").astype(jnp.float32)
    row_ids = lax.axis_index("row") * row_count + jnp.arange(row_count, dtype=jnp.int32)
    latent_ids = lax.axis_index("latent") * lat_count + jnp.arange(lat_count, dtype=jnp.int32)
    every_row = jnp.arange(all_rows, dtype=jnp.int32)
    pair_table = (
        (every_row[None, :] == row_ids[:, None]).astype(jnp.float32)
        - (pairing[None, :] == row_ids[:, None]).astype(jnp.float32)
    ).astype(jnp.bfloat16)
    target_hot = (targets[:, None] == latent_ids[None, :]).astype(jnp.bfloat16)
    margin_table = jnp.dot(pair_table, target_hot, preferred_element_type=jnp.float32)
    pre_grad = jnp.where(preact > 0, feat_grad - MARGIN * margin_table, 0.0).astype(jnp.bfloat16)
    enc_split = enc_weight[0].reshape(n_lat, chunk, lat_count)
    partial_input = jnp.einsum(
        "rf,gdf->grd", pre_grad, enc_split, preferred_element_type=jnp.float32
    ).astype(jnp.bfloat16)
    gathered = lax.all_to_all(partial_input, "latent", 0, 0, tiled=True)
    total = jnp.sum(gathered.astype(jnp.float32), axis=0).astype(jnp.bfloat16)
    return total[:, None, :]


def solution(mesh):
    placed = (
        P("row", "layer", None),
        P("row", "layer", None),
        P("layer", None, "latent"),
        P("latent"),
        P("layer", "latent", None),
        P("layer", None),
        P(),
        P(),
    )
    return jax.shard_map(
        local, mesh=mesh, in_specs=placed, out_specs=P("row", "layer", "latent"), check_vma=False
    )
```

```python
import jax
import jax.numpy as jnp
from jax import lax
from jax.experimental import pallas as pl
from jax.experimental.pallas import tpu as pltpu
from jax.sharding import PartitionSpec as P

MARGIN = 16.0
MESH = pl.DeviceIdType.MESH


def _layer_sum_kernel(x_ref, o_ref, recv_a, recv_b, recv_c, send_sems, recv_sems):
    me = lax.axis_index("layer")
    core = me % 2
    chip = me // 2
    mate = me + 1 - 2 * core
    far = me + 2 - 4 * chip
    half = x_ref.shape[0] // 2
    mine = pl.ds(pl.multiple_of(core * half, half), half)
    other = pl.ds(pl.multiple_of((1 - core) * half, half), half)

    barrier = pltpu.get_barrier_semaphore()
    for peer in (mate, far):
        pl.semaphore_signal(barrier, inc=1, device_id={"layer": peer}, device_id_type=MESH)
    pl.semaphore_wait(barrier, 2)

    def send(src, dst, slot, peer):
        return pltpu.make_async_remote_copy(
            src_ref=src, dst_ref=dst, send_sem=send_sems.at[slot], recv_sem=recv_sems.at[slot],
            device_id={"layer": peer}, device_id_type=MESH,
        )

    step_a = send(x_ref.at[other], recv_a, 0, mate)
    step_a.start()
    step_a.wait()
    o_ref[mine] = x_ref[mine].astype(jnp.float32) + recv_a[...].astype(jnp.float32)
    step_b = send(o_ref.at[mine], recv_b, 1, far)
    step_b.start()
    step_b.wait()
    o_ref[mine] = o_ref[mine] + recv_b[...]
    step_c = send(o_ref.at[mine], recv_c, 2, mate)
    step_c.start()
    step_c.wait()
    o_ref[other] = recv_c[...]


def layer_sum(x, collective_id):
    rows, cols = x.shape
    half = rows // 2
    return pl.pallas_call(
        _layer_sum_kernel,
        out_shape=jax.ShapeDtypeStruct((rows, cols), jnp.float32),
        in_specs=[pl.BlockSpec(memory_space=pltpu.VMEM)],
        out_specs=pl.BlockSpec(memory_space=pltpu.VMEM),
        scratch_shapes=[
            pltpu.VMEM((half, cols), x.dtype),
            pltpu.VMEM((half, cols), jnp.float32),
            pltpu.VMEM((half, cols), jnp.float32),
            pltpu.SemaphoreType.DMA((3,)),
            pltpu.SemaphoreType.DMA((3,)),
        ],
        compiler_params=pltpu.CompilerParams(collective_id=collective_id, has_side_effects=True),
    )(x)


def local(inputs, clean_acts, enc_weight, enc_bias, dec_weight, dec_bias, pairing, targets):
    row_count = inputs.shape[0]
    lat_count = enc_weight.shape[2]
    all_rows = pairing.shape[0]
    n_lat = lax.psum(1, "latent")
    d_model = inputs.shape[2]
    chunk = d_model // n_lat
    partial_pre = jnp.einsum("rld,ldf->rf", inputs, enc_weight, preferred_element_type=jnp.float32)
    preact = layer_sum(partial_pre, 1) + enc_bias
    features = jnp.maximum(preact, 0.0).astype(jnp.bfloat16)
    partial_recon = jnp.einsum(
        "rf,lfd->rld", features, dec_weight, preferred_element_type=jnp.float32
    )
    recon = (
        lax.psum(partial_recon.astype(jnp.bfloat16), "latent").astype(jnp.float32) + dec_bias[None]
    )
    recon_error = (recon - clean_acts.astype(jnp.float32)).astype(jnp.bfloat16)
    partial_grad = jnp.einsum(
        "rld,lfd->rf", recon_error, dec_weight, preferred_element_type=jnp.float32
    )
    feat_grad = layer_sum(partial_grad.astype(jnp.bfloat16), 2)
    row_ids = lax.axis_index("row") * row_count + jnp.arange(row_count, dtype=jnp.int32)
    latent_ids = lax.axis_index("latent") * lat_count + jnp.arange(lat_count, dtype=jnp.int32)
    every_row = jnp.arange(all_rows, dtype=jnp.int32)
    pair_table = (
        (every_row[None, :] == row_ids[:, None]).astype(jnp.float32)
        - (pairing[None, :] == row_ids[:, None]).astype(jnp.float32)
    ).astype(jnp.bfloat16)
    target_hot = (targets[:, None] == latent_ids[None, :]).astype(jnp.bfloat16)
    margin_table = jnp.dot(pair_table, target_hot, preferred_element_type=jnp.float32)
    pre_grad = jnp.where(preact > 0, feat_grad - MARGIN * margin_table, 0.0).astype(jnp.bfloat16)
    enc_split = enc_weight[0].reshape(n_lat, chunk, lat_count)
    partial_input = jnp.einsum(
        "rf,gdf->grd", pre_grad, enc_split, preferred_element_type=jnp.float32
    ).astype(jnp.bfloat16)
    gathered = lax.all_to_all(partial_input, "latent", 0, 0, tiled=True)
    total = jnp.sum(gathered.astype(jnp.float32), axis=0).astype(jnp.bfloat16)
    return total[:, None, :]


def solution(mesh):
    placed = (
        P("row", "layer", None),
        P("row", "layer", None),
        P("layer", None, "latent"),
        P("latent"),
        P("layer", "latent", None),
        P("layer", None),
        P(),
        P(),
    )
    return jax.shard_map(
        local, mesh=mesh, in_specs=placed, out_specs=P("row", "layer", "latent"), check_vma=False
    )
```

```python
import jax
import jax.numpy as jnp
from jax import lax
from jax.experimental import pallas as pl
from jax.experimental.pallas import tpu as pltpu
from jax.sharding import PartitionSpec as P

MARGIN = 16.0
MESH = pl.DeviceIdType.MESH
RING = 4


def _latent_coords():
    me = lax.axis_index("latent")
    return me // RING, me % RING


def _greet(a, b):
    barrier = pltpu.get_barrier_semaphore()
    for k in range(1, RING):
        pl.semaphore_signal(barrier, inc=1, device_id={"latent": a * RING + (b + k) % RING}, device_id_type=MESH)
        pl.semaphore_signal(barrier, inc=1, device_id={"latent": ((a + k) % RING) * RING + b}, device_id_type=MESH)
    pl.semaphore_wait(barrier, 2 * (RING - 1))


def _copy(src, dst, send_sem, recv_sem, peer):
    return pltpu.make_async_remote_copy(
        src_ref=src, dst_ref=dst, send_sem=send_sem, recv_sem=recv_sem,
        device_id={"latent": peer}, device_id_type=MESH,
    )


def _reduce_kernel(xa, xb, out, r1a, r1b, s1a, s1b, r2a, r2b, send_sems, recv_sems):
    a, b = _latent_coords()
    _greet(a, b)
    peers_z = [(b + k) % RING for k in range(1, RING)]
    peers_x = [(a + k) % RING for k in range(1, RING)]
    first = []
    for t in peers_z:
        c = _copy(xa.at[t], r1a.at[b], send_sems.at[0, t], recv_sems.at[0, b], a * RING + t)
        c.start()
        first.append(c)
    for t in peers_x:
        c = _copy(xb.at[t], r1b.at[a], send_sems.at[1, t], recv_sems.at[1, a], t * RING + b)
        c.start()
        first.append(c)
    for t in peers_z:
        _copy(xa.at[t], r1a.at[t], send_sems.at[0, t], recv_sems.at[0, t], 0).wait_recv()
    for t in peers_x:
        _copy(xb.at[t], r1b.at[t], send_sems.at[1, t], recv_sems.at[1, t], 0).wait_recv()
    sum_a = xa[b].astype(jnp.float32)
    for t in peers_z:
        sum_a = sum_a + r1a[t].astype(jnp.float32)
    sum_b = xb[a].astype(jnp.float32)
    for t in peers_x:
        sum_b = sum_b + r1b[t].astype(jnp.float32)
    s1a[...] = sum_a.astype(s1a.dtype)
    s1b[...] = sum_b.astype(s1b.dtype)
    second = []
    for t in peers_x:
        c = _copy(s1a.at[t], r2a.at[a], send_sems.at[2, t], recv_sems.at[2, a], t * RING + b)
        c.start()
        second.append(c)
    for t in peers_z:
        c = _copy(s1b.at[t], r2b.at[b], send_sems.at[3, t], recv_sems.at[3, b], a * RING + t)
        c.start()
        second.append(c)
    for t in peers_x:
        _copy(s1a.at[t], r2a.at[t], send_sems.at[2, t], recv_sems.at[2, t], 0).wait_recv()
    for t in peers_z:
        _copy(s1b.at[t], r2b.at[t], send_sems.at[3, t], recv_sems.at[3, t], 0).wait_recv()
    own_a = xa[b, a].astype(jnp.float32)
    for t in peers_z:
        own_a = own_a + r1a[t, a].astype(jnp.float32)
    own_b = xb[a, b].astype(jnp.float32)
    for t in peers_x:
        own_b = own_b + r1b[t, b].astype(jnp.float32)
    for t in peers_x:
        own_a = own_a + r2a[t].astype(jnp.float32)
    for t in peers_z:
        own_b = own_b + r2b[t].astype(jnp.float32)
    out[0] = own_a
    out[1] = own_b
    for c in first + second:
        c.wait_send()


def latent_reduce(xa, xb, collective_id):
    n, _, h, c = xa.shape
    dt = xa.dtype
    return pl.pallas_call(
        _reduce_kernel,
        out_shape=jax.ShapeDtypeStruct((2, h, c), jnp.float32),
        in_specs=[pl.BlockSpec(memory_space=pltpu.VMEM)] * 2,
        out_specs=pl.BlockSpec(memory_space=pltpu.VMEM),
        scratch_shapes=[
            pltpu.VMEM((n, n, h, c), dt),
            pltpu.VMEM((n, n, h, c), dt),
            pltpu.VMEM((n, h, c), dt),
            pltpu.VMEM((n, h, c), dt),
            pltpu.VMEM((n, h, c), dt),
            pltpu.VMEM((n, h, c), dt),
            pltpu.SemaphoreType.DMA((4, n)),
            pltpu.SemaphoreType.DMA((4, n)),
        ],
        compiler_params=pltpu.CompilerParams(collective_id=collective_id, has_side_effects=True),
    )(xa, xb)


def _gather_kernel(e, oa, ob, g1a, g1b, ga, gb, send_sems, recv_sems):
    a, b = _latent_coords()
    _greet(a, b)
    peers_z = [(b + k) % RING for k in range(1, RING)]
    peers_x = [(a + k) % RING for k in range(1, RING)]
    first = []
    for t in peers_z:
        c = _copy(e.at[0], g1a.at[b], send_sems.at[0, t], recv_sems.at[0, b], a * RING + t)
        c.start()
        first.append(c)
    for t in peers_x:
        c = _copy(e.at[1], g1b.at[a], send_sems.at[1, t], recv_sems.at[1, a], t * RING + b)
        c.start()
        first.append(c)
    g1a[b] = e[0]
    g1b[a] = e[1]
    for t in peers_z:
        _copy(e.at[0], g1a.at[t], send_sems.at[0, t], recv_sems.at[0, t], 0).wait_recv()
    for t in peers_x:
        _copy(e.at[1], g1b.at[t], send_sems.at[1, t], recv_sems.at[1, t], 0).wait_recv()
    second = []
    for t in peers_x:
        c = _copy(g1a, ga.at[a], send_sems.at[2, t], recv_sems.at[2, a], t * RING + b)
        c.start()
        second.append(c)
    for t in peers_z:
        c = _copy(g1b, gb.at[b], send_sems.at[3, t], recv_sems.at[3, b], a * RING + t)
        c.start()
        second.append(c)
    oa[a] = g1a[...]
    ob[b] = g1b[...]
    for t in peers_x:
        _copy(g1a, ga.at[t], send_sems.at[2, t], recv_sems.at[2, t], 0).wait_recv()
        oa[t] = ga[t]
    for t in peers_z:
        _copy(g1b, gb.at[t], send_sems.at[3, t], recv_sems.at[3, t], 0).wait_recv()
        ob[t] = gb[t]
    for c in first + second:
        c.wait_send()


def latent_gather(e, collective_id):
    _, h, c = e.shape
    n = RING
    dt = e.dtype
    full = jax.ShapeDtypeStruct((n, n, h, c), dt)
    return pl.pallas_call(
        _gather_kernel,
        out_shape=(full, full),
        in_specs=[pl.BlockSpec(memory_space=pltpu.VMEM)],
        out_specs=(pl.BlockSpec(memory_space=pltpu.VMEM), pl.BlockSpec(memory_space=pltpu.VMEM)),
        scratch_shapes=[
            pltpu.VMEM((n, h, c), dt),
            pltpu.VMEM((n, h, c), dt),
            pltpu.VMEM((n, n, h, c), dt),
            pltpu.VMEM((n, n, h, c), dt),
            pltpu.SemaphoreType.DMA((4, n)),
            pltpu.SemaphoreType.DMA((4, n)),
        ],
        compiler_params=pltpu.CompilerParams(collective_id=collective_id, has_side_effects=True),
    )(e)


def _layer_sum_kernel(x_ref, o_ref, recv_a, recv_b, recv_c, send_sems, recv_sems):
    me = lax.axis_index("layer")
    core = me % 2
    chip = me // 2
    mate = me + 1 - 2 * core
    far = me + 2 - 4 * chip
    half = x_ref.shape[0] // 2
    mine = pl.ds(pl.multiple_of(core * half, half), half)
    other = pl.ds(pl.multiple_of((1 - core) * half, half), half)

    barrier = pltpu.get_barrier_semaphore()
    for peer in (mate, far):
        pl.semaphore_signal(barrier, inc=1, device_id={"layer": peer}, device_id_type=MESH)
    pl.semaphore_wait(barrier, 2)

    def send(src, dst, slot, peer):
        return pltpu.make_async_remote_copy(
            src_ref=src, dst_ref=dst, send_sem=send_sems.at[slot], recv_sem=recv_sems.at[slot],
            device_id={"layer": peer}, device_id_type=MESH,
        )

    step_a = send(x_ref.at[other], recv_a, 0, mate)
    step_a.start()
    step_a.wait()
    o_ref[mine] = x_ref[mine].astype(jnp.float32) + recv_a[...].astype(jnp.float32)
    step_b = send(o_ref.at[mine], recv_b, 1, far)
    step_b.start()
    step_b.wait()
    o_ref[mine] = o_ref[mine] + recv_b[...]
    step_c = send(o_ref.at[mine], recv_c, 2, mate)
    step_c.start()
    step_c.wait()
    o_ref[other] = recv_c[...]


def layer_sum(x, collective_id):
    rows, cols = x.shape
    half = rows // 2
    return pl.pallas_call(
        _layer_sum_kernel,
        out_shape=jax.ShapeDtypeStruct((rows, cols), jnp.float32),
        in_specs=[pl.BlockSpec(memory_space=pltpu.VMEM)],
        out_specs=pl.BlockSpec(memory_space=pltpu.VMEM),
        scratch_shapes=[
            pltpu.VMEM((half, cols), x.dtype),
            pltpu.VMEM((half, cols), jnp.float32),
            pltpu.VMEM((half, cols), jnp.float32),
            pltpu.SemaphoreType.DMA((3,)),
            pltpu.SemaphoreType.DMA((3,)),
        ],
        compiler_params=pltpu.CompilerParams(collective_id=collective_id, has_side_effects=True),
    )(x)


def local(inputs, clean_acts, enc_weight, enc_bias, dec_weight, dec_bias, pairing, targets):
    row_count = inputs.shape[0]
    lat_count = enc_weight.shape[2]
    all_rows = pairing.shape[0]
    d_model = inputs.shape[2]
    chunk = d_model // (RING * RING)
    half = row_count // 2
    me = lax.axis_index("latent")
    partial_pre = jnp.einsum("rld,ldf->rf", inputs, enc_weight, preferred_element_type=jnp.float32)
    preact = layer_sum(partial_pre, 1) + enc_bias
    features = jnp.maximum(preact, 0.0).astype(jnp.bfloat16)
    dec4 = dec_weight[0].reshape(lat_count, RING, RING, chunk)
    recon_a = jnp.einsum("rf,fabd->bard", features[:half], dec4, preferred_element_type=jnp.float32)
    recon_b = jnp.einsum("rf,fabd->abrd", features[half:], dec4, preferred_element_type=jnp.float32)
    recon_sum = latent_reduce(recon_a.astype(jnp.bfloat16), recon_b.astype(jnp.bfloat16), 3)
    bias_part = lax.dynamic_slice_in_dim(dec_bias[0], me * chunk, chunk)
    clean_part = lax.dynamic_slice_in_dim(clean_acts[:, 0, :], me * chunk, chunk, axis=1)
    recon_error = (
        recon_sum + bias_part - clean_part.reshape(2, half, chunk).astype(jnp.float32)
    ).astype(jnp.bfloat16)
    error_a, error_b = latent_gather(recon_error, 4)
    grad_a = jnp.einsum("abrd,fabd->rf", error_a, dec4, preferred_element_type=jnp.float32)
    grad_b = jnp.einsum("bard,fabd->rf", error_b, dec4, preferred_element_type=jnp.float32)
    partial_grad = jnp.concatenate([grad_a, grad_b], axis=0)
    feat_grad = layer_sum(partial_grad.astype(jnp.bfloat16), 2)
    row_ids = lax.axis_index("row") * row_count + jnp.arange(row_count, dtype=jnp.int32)
    latent_ids = me * lat_count + jnp.arange(lat_count, dtype=jnp.int32)
    every_row = jnp.arange(all_rows, dtype=jnp.int32)
    pair_table = (
        (every_row[None, :] == row_ids[:, None]).astype(jnp.float32)
        - (pairing[None, :] == row_ids[:, None]).astype(jnp.float32)
    ).astype(jnp.bfloat16)
    target_hot = (targets[:, None] == latent_ids[None, :]).astype(jnp.bfloat16)
    margin_table = jnp.dot(pair_table, target_hot, preferred_element_type=jnp.float32)
    pre_grad = jnp.where(preact > 0, feat_grad - MARGIN * margin_table, 0.0).astype(jnp.bfloat16)
    enc4 = enc_weight[0].reshape(RING, RING, chunk, lat_count)
    input_a = jnp.einsum("rf,abdf->bard", pre_grad[:half], enc4, preferred_element_type=jnp.float32)
    input_b = jnp.einsum("rf,abdf->abrd", pre_grad[half:], enc4, preferred_element_type=jnp.float32)
    total = latent_reduce(input_a.astype(jnp.bfloat16), input_b.astype(jnp.bfloat16), 5)
    return total.reshape(row_count, 1, chunk).astype(jnp.bfloat16)


def solution(mesh):
    placed = (
        P("row", "layer", None),
        P("row", "layer", None),
        P("layer", None, "latent"),
        P("latent"),
        P("layer", "latent", None),
        P("layer", None),
        P(),
        P(),
    )
    return jax.shard_map(
        local, mesh=mesh, in_specs=placed, out_specs=P("row", "layer", "latent"), check_vma=False
    )
```

```python
import jax
import jax.numpy as jnp
from jax import lax
from jax.experimental import pallas as pl
from jax.experimental.pallas import tpu as pltpu
from jax.sharding import PartitionSpec as P

MARGIN = 16.0
MESH = pl.DeviceIdType.MESH
RING = 4


def _latent_coords():
    me = lax.axis_index("latent")
    return me // RING, me % RING


def _greet(a, b):
    barrier = pltpu.get_barrier_semaphore()
    for peer in (a * RING + (b + 1) % RING, a * RING + (b + RING - 1) % RING,
                 ((a + 1) % RING) * RING + b, ((a + RING - 1) % RING) * RING + b):
        pl.semaphore_signal(barrier, inc=1, device_id={"latent": peer}, device_id_type=MESH)
    pl.semaphore_wait(barrier, 4)


def _rows(ref, lo, n):
    return ref.at[(slice(None),) * (len(ref.shape) - 2) + (pl.ds(lo, n), slice(None))]


class _RingStage:
    def __init__(self, src, dst, relay_l, relay_r, send_sems, recv_sems, a, b, on_z):
        self.src, self.dst = src, dst
        self.relay_l, self.relay_r = relay_l, relay_r
        self.ss, self.rs = send_sems, recv_sems
        self.a, self.b, self.on_z = a, b, on_z
        self.m = b if on_z else a
        self.p1 = (self.m + 1) % RING
        self.m1 = (self.m + RING - 1) % RING
        self.p2 = (self.m + 2) % RING
        self.sent = []

    def _peer(self, c):
        return self.a * RING + c if self.on_z else c * RING + self.b

    def _copy(self, src, dst, k, c):
        return pltpu.make_async_remote_copy(
            src_ref=src, dst_ref=dst, send_sem=self.ss.at[k], recv_sem=self.rs.at[k],
            device_id={"latent": self._peer(c)}, device_id_type=MESH,
        )

    def _half(self):
        return self.relay_l.shape[-2]

    def start(self):
        h = self._half()
        far = self.src(self.p2)
        for c in (
            self._copy(self.src(self.p1), self.dst(self.m), 0, self.p1),
            self._copy(self.src(self.m1), self.dst(self.m), 1, self.m1),
            self._copy(_rows(far, 0, h), self.relay_l, 2, self.p1),
            self._copy(_rows(far, h, h), self.relay_r, 3, self.m1),
        ):
            c.start()
            self.sent.append(c)

    def forward(self):
        h = self._half()
        self._copy(self.relay_l, self.relay_l, 2, 0).wait_recv()
        fl = self._copy(self.relay_l, _rows(self.dst(self.m1), 0, h), 4, self.p1)
        fl.start()
        self._copy(self.relay_r, self.relay_r, 3, 0).wait_recv()
        fr = self._copy(self.relay_r, _rows(self.dst(self.p1), h, h), 5, self.m1)
        fr.start()
        self.sent += [fl, fr]

    def finish(self):
        h = self._half()
        self._copy(self.src(0), self.dst(self.m1), 0, 0).wait_recv()
        self._copy(self.src(0), self.dst(self.p1), 1, 0).wait_recv()
        self._copy(self.relay_l, _rows(self.dst(self.p2), 0, h), 4, 0).wait_recv()
        self._copy(self.relay_r, _rows(self.dst(self.p2), h, h), 5, 0).wait_recv()

    def drain(self):
        for c in self.sent:
            c.wait_send()


def _reduce_kernel(xa, xb, out, r1a, r1b, s1a, s1b, r2a, r2b, l1, r1, l2, r2, send_sems, recv_sems):
    a, b = _latent_coords()
    _greet(a, b)
    st_a = _RingStage(lambda c: xa.at[c], lambda s: r1a.at[s], l1.at[0], r1.at[0],
                      send_sems.at[0], recv_sems.at[0], a, b, True)
    st_b = _RingStage(lambda c: xb.at[c], lambda s: r1b.at[s], l1.at[1], r1.at[1],
                      send_sems.at[1], recv_sems.at[1], a, b, False)
    for st in (st_a, st_b):
        st.start()
    for st in (st_a, st_b):
        st.forward()
    for st in (st_a, st_b):
        st.finish()
    sum_a = xa[b].astype(jnp.float32)
    sum_b = xb[a].astype(jnp.float32)
    for k in range(1, RING):
        sum_a = sum_a + r1a[(b + k) % RING].astype(jnp.float32)
        sum_b = sum_b + r1b[(a + k) % RING].astype(jnp.float32)
    s1a[...] = sum_a.astype(s1a.dtype)
    s1b[...] = sum_b.astype(s1b.dtype)
    nd_a = _RingStage(lambda c: s1a.at[c], lambda s: r2a.at[s], l2.at[0], r2.at[0],
                      send_sems.at[2], recv_sems.at[2], a, b, False)
    nd_b = _RingStage(lambda c: s1b.at[c], lambda s: r2b.at[s], l2.at[1], r2.at[1],
                      send_sems.at[3], recv_sems.at[3], a, b, True)
    for st in (nd_a, nd_b):
        st.start()
    for st in (nd_a, nd_b):
        st.forward()
    for st in (nd_a, nd_b):
        st.finish()
    own_a = xa[b, a].astype(jnp.float32)
    own_b = xb[a, b].astype(jnp.float32)
    for k in range(1, RING):
        own_a = own_a + r1a[(b + k) % RING, a].astype(jnp.float32)
        own_b = own_b + r1b[(a + k) % RING, b].astype(jnp.float32)
    for k in range(1, RING):
        own_a = own_a + r2a[(a + k) % RING].astype(jnp.float32)
        own_b = own_b + r2b[(b + k) % RING].astype(jnp.float32)
    out[0] = own_a
    out[1] = own_b
    for st in (st_a, st_b, nd_a, nd_b):
        st.drain()


def latent_reduce(xa, xb, collective_id):
    n, _, h, c = xa.shape
    dt = xa.dtype
    return pl.pallas_call(
        _reduce_kernel,
        out_shape=jax.ShapeDtypeStruct((2, h, c), jnp.float32),
        in_specs=[pl.BlockSpec(memory_space=pltpu.VMEM)] * 2,
        out_specs=pl.BlockSpec(memory_space=pltpu.VMEM),
        scratch_shapes=[
            pltpu.VMEM((n, n, h, c), dt),
            pltpu.VMEM((n, n, h, c), dt),
            pltpu.VMEM((n, h, c), dt),
            pltpu.VMEM((n, h, c), dt),
            pltpu.VMEM((n, h, c), dt),
            pltpu.VMEM((n, h, c), dt),
            pltpu.VMEM((2, n, h // 2, c), dt),
            pltpu.VMEM((2, n, h // 2, c), dt),
            pltpu.VMEM((2, h // 2, c), dt),
            pltpu.VMEM((2, h // 2, c), dt),
            pltpu.SemaphoreType.DMA((4, 6)),
            pltpu.SemaphoreType.DMA((4, 6)),
        ],
        compiler_params=pltpu.CompilerParams(collective_id=collective_id, has_side_effects=True),
    )(xa, xb)


def _gather_kernel(e, oa, ob, g1a, g1b, ga, gb, l1, r1, l2, r2, send_sems, recv_sems):
    a, b = _latent_coords()
    _greet(a, b)
    st_a = _RingStage(lambda c: e.at[0], lambda s: g1a.at[s], l1.at[0], r1.at[0],
                      send_sems.at[0], recv_sems.at[0], a, b, True)
    st_b = _RingStage(lambda c: e.at[1], lambda s: g1b.at[s], l1.at[1], r1.at[1],
                      send_sems.at[1], recv_sems.at[1], a, b, False)
    for st in (st_a, st_b):
        st.start()
    g1a[b] = e[0]
    g1b[a] = e[1]
    for st in (st_a, st_b):
        st.forward()
    for st in (st_a, st_b):
        st.finish()
    nd_a = _RingStage(lambda c: g1a, lambda s: ga.at[s], l2.at[0], r2.at[0],
                      send_sems.at[2], recv_sems.at[2], a, b, False)
    nd_b = _RingStage(lambda c: g1b, lambda s: gb.at[s], l2.at[1], r2.at[1],
                      send_sems.at[3], recv_sems.at[3], a, b, True)
    for st in (nd_a, nd_b):
        st.start()
    oa[a] = g1a[...]
    ob[b] = g1b[...]
    for st in (nd_a, nd_b):
        st.forward()
    for st in (nd_a, nd_b):
        st.finish()
    for k in range(1, RING):
        oa[(a + k) % RING] = ga[(a + k) % RING]
        ob[(b + k) % RING] = gb[(b + k) % RING]
    for st in (st_a, st_b, nd_a, nd_b):
        st.drain()


def latent_gather(e, collective_id):
    _, h, c = e.shape
    n = RING
    dt = e.dtype
    full = jax.ShapeDtypeStruct((n, n, h, c), dt)
    return pl.pallas_call(
        _gather_kernel,
        out_shape=(full, full),
        in_specs=[pl.BlockSpec(memory_space=pltpu.VMEM)],
        out_specs=(pl.BlockSpec(memory_space=pltpu.VMEM), pl.BlockSpec(memory_space=pltpu.VMEM)),
        scratch_shapes=[
            pltpu.VMEM((n, h, c), dt),
            pltpu.VMEM((n, h, c), dt),
            pltpu.VMEM((n, n, h, c), dt),
            pltpu.VMEM((n, n, h, c), dt),
            pltpu.VMEM((2, h // 2, c), dt),
            pltpu.VMEM((2, h // 2, c), dt),
            pltpu.VMEM((2, n, h // 2, c), dt),
            pltpu.VMEM((2, n, h // 2, c), dt),
            pltpu.SemaphoreType.DMA((4, 6)),
            pltpu.SemaphoreType.DMA((4, 6)),
        ],
        compiler_params=pltpu.CompilerParams(collective_id=collective_id, has_side_effects=True),
    )(e)


def _layer_sum_kernel(x_ref, o_ref, recv_a, recv_b, recv_c, send_sems, recv_sems):
    me = lax.axis_index("layer")
    core = me % 2
    chip = me // 2
    mate = me + 1 - 2 * core
    far = me + 2 - 4 * chip
    half = x_ref.shape[0] // 2
    mine = pl.ds(pl.multiple_of(core * half, half), half)
    other = pl.ds(pl.multiple_of((1 - core) * half, half), half)

    barrier = pltpu.get_barrier_semaphore()
    for peer in (mate, far):
        pl.semaphore_signal(barrier, inc=1, device_id={"layer": peer}, device_id_type=MESH)
    pl.semaphore_wait(barrier, 2)

    def send(src, dst, slot, peer):
        return pltpu.make_async_remote_copy(
            src_ref=src, dst_ref=dst, send_sem=send_sems.at[slot], recv_sem=recv_sems.at[slot],
            device_id={"layer": peer}, device_id_type=MESH,
        )

    step_a = send(x_ref.at[other], recv_a, 0, mate)
    step_a.start()
    step_a.wait()
    o_ref[mine] = x_ref[mine].astype(jnp.float32) + recv_a[...].astype(jnp.float32)
    step_b = send(o_ref.at[mine], recv_b, 1, far)
    step_b.start()
    step_b.wait()
    o_ref[mine] = o_ref[mine] + recv_b[...]
    step_c = send(o_ref.at[mine], recv_c, 2, mate)
    step_c.start()
    step_c.wait()
    o_ref[other] = recv_c[...]


def layer_sum(x, collective_id):
    rows, cols = x.shape
    half = rows // 2
    return pl.pallas_call(
        _layer_sum_kernel,
        out_shape=jax.ShapeDtypeStruct((rows, cols), jnp.float32),
        in_specs=[pl.BlockSpec(memory_space=pltpu.VMEM)],
        out_specs=pl.BlockSpec(memory_space=pltpu.VMEM),
        scratch_shapes=[
            pltpu.VMEM((half, cols), x.dtype),
            pltpu.VMEM((half, cols), jnp.float32),
            pltpu.VMEM((half, cols), jnp.float32),
            pltpu.SemaphoreType.DMA((3,)),
            pltpu.SemaphoreType.DMA((3,)),
        ],
        compiler_params=pltpu.CompilerParams(collective_id=collective_id, has_side_effects=True),
    )(x)


def local(inputs, clean_acts, enc_weight, enc_bias, dec_weight, dec_bias, pairing, targets):
    row_count = inputs.shape[0]
    lat_count = enc_weight.shape[2]
    all_rows = pairing.shape[0]
    d_model = inputs.shape[2]
    chunk = d_model // (RING * RING)
    half = row_count // 2
    me = lax.axis_index("latent")
    partial_pre = jnp.einsum("rld,ldf->rf", inputs, enc_weight, preferred_element_type=jnp.float32)
    preact = layer_sum(partial_pre, 1) + enc_bias
    features = jnp.maximum(preact, 0.0).astype(jnp.bfloat16)
    dec4 = dec_weight[0].reshape(lat_count, RING, RING, chunk)
    recon_a = jnp.einsum("rf,fabd->bard", features[:half], dec4, preferred_element_type=jnp.float32)
    recon_b = jnp.einsum("rf,fabd->abrd", features[half:], dec4, preferred_element_type=jnp.float32)
    recon_sum = latent_reduce(recon_a.astype(jnp.bfloat16), recon_b.astype(jnp.bfloat16), 3)
    bias_part = lax.dynamic_slice_in_dim(dec_bias[0], me * chunk, chunk)
    clean_part = lax.dynamic_slice_in_dim(clean_acts[:, 0, :], me * chunk, chunk, axis=1)
    recon_error = (
        recon_sum + bias_part - clean_part.reshape(2, half, chunk).astype(jnp.float32)
    ).astype(jnp.bfloat16)
    error_a, error_b = latent_gather(recon_error, 4)
    grad_a = jnp.einsum("abrd,fabd->rf", error_a, dec4, preferred_element_type=jnp.float32)
    grad_b = jnp.einsum("bard,fabd->rf", error_b, dec4, preferred_element_type=jnp.float32)
    partial_grad = jnp.concatenate([grad_a, grad_b], axis=0)
    feat_grad = layer_sum(partial_grad.astype(jnp.bfloat16), 2)
    row_ids = lax.axis_index("row") * row_count + jnp.arange(row_count, dtype=jnp.int32)
    latent_ids = me * lat_count + jnp.arange(lat_count, dtype=jnp.int32)
    every_row = jnp.arange(all_rows, dtype=jnp.int32)
    pair_table = (
        (every_row[None, :] == row_ids[:, None]).astype(jnp.float32)
        - (pairing[None, :] == row_ids[:, None]).astype(jnp.float32)
    ).astype(jnp.bfloat16)
    target_hot = (targets[:, None] == latent_ids[None, :]).astype(jnp.bfloat16)
    margin_table = jnp.dot(pair_table, target_hot, preferred_element_type=jnp.float32)
    pre_grad = jnp.where(preact > 0, feat_grad - MARGIN * margin_table, 0.0).astype(jnp.bfloat16)
    enc4 = enc_weight[0].reshape(RING, RING, chunk, lat_count)
    input_a = jnp.einsum("rf,abdf->bard", pre_grad[:half], enc4, preferred_element_type=jnp.float32)
    input_b = jnp.einsum("rf,abdf->abrd", pre_grad[half:], enc4, preferred_element_type=jnp.float32)
    total = latent_reduce(input_a.astype(jnp.bfloat16), input_b.astype(jnp.bfloat16), 5)
    return total.reshape(row_count, 1, chunk).astype(jnp.bfloat16)


def solution(mesh):
    placed = (
        P("row", "layer", None),
        P("row", "layer", None),
        P("layer", None, "latent"),
        P("latent"),
        P("layer", "latent", None),
        P("layer", None),
        P(),
        P(),
    )
    return jax.shard_map(
        local, mesh=mesh, in_specs=placed, out_specs=P("row", "layer", "latent"), check_vma=False
    )
```

```python
import jax
import jax.numpy as jnp
from jax import lax
from jax.experimental import pallas as pl
from jax.experimental.pallas import tpu as pltpu
from jax.sharding import PartitionSpec as P

MARGIN = 16.0
MESH = pl.DeviceIdType.MESH
RING = 4


def _latent_coords():
    me = lax.axis_index("latent")
    return me // RING, me % RING


def _greet(a, b):
    barrier = pltpu.get_barrier_semaphore()
    for k in range(1, RING):
        pl.semaphore_signal(barrier, inc=1, device_id={"latent": a * RING + (b + k) % RING}, device_id_type=MESH)
        pl.semaphore_signal(barrier, inc=1, device_id={"latent": ((a + k) % RING) * RING + b}, device_id_type=MESH)
    pl.semaphore_wait(barrier, 2 * (RING - 1))


def _copy(src, dst, send_sem, recv_sem, peer):
    return pltpu.make_async_remote_copy(
        src_ref=src, dst_ref=dst, send_sem=send_sem, recv_sem=recv_sem,
        device_id={"latent": peer}, device_id_type=MESH,
    )


def _reduce_kernel(xa, xb, out, r1a, r1b, s1a, s1b, r2a, r2b, send_sems, recv_sems):
    a, b = _latent_coords()
    _greet(a, b)
    peers_z = [(b + k) % RING for k in range(1, RING)]
    peers_x = [(a + k) % RING for k in range(1, RING)]
    first = []
    for t in peers_z:
        c = _copy(xa.at[t], r1a.at[b], send_sems.at[0, t], recv_sems.at[0, b], a * RING + t)
        c.start()
        first.append(c)
    for t in peers_x:
        c = _copy(xb.at[t], r1b.at[a], send_sems.at[1, t], recv_sems.at[1, a], t * RING + b)
        c.start()
        first.append(c)
    for t in peers_z:
        _copy(xa.at[t], r1a.at[t], send_sems.at[0, t], recv_sems.at[0, t], 0).wait_recv()
    for t in peers_x:
        _copy(xb.at[t], r1b.at[t], send_sems.at[1, t], recv_sems.at[1, t], 0).wait_recv()
    sum_a = xa[b].astype(jnp.float32)
    for t in peers_z:
        sum_a = sum_a + r1a[t].astype(jnp.float32)
    sum_b = xb[a].astype(jnp.float32)
    for t in peers_x:
        sum_b = sum_b + r1b[t].astype(jnp.float32)
    s1a[...] = sum_a.astype(s1a.dtype)
    s1b[...] = sum_b.astype(s1b.dtype)
    second = []
    for t in peers_x:
        c = _copy(s1a.at[t], r2a.at[a], send_sems.at[2, t], recv_sems.at[2, a], t * RING + b)
        c.start()
        second.append(c)
    for t in peers_z:
        c = _copy(s1b.at[t], r2b.at[b], send_sems.at[3, t], recv_sems.at[3, b], a * RING + t)
        c.start()
        second.append(c)
    for t in peers_x:
        _copy(s1a.at[t], r2a.at[t], send_sems.at[2, t], recv_sems.at[2, t], 0).wait_recv()
    for t in peers_z:
        _copy(s1b.at[t], r2b.at[t], send_sems.at[3, t], recv_sems.at[3, t], 0).wait_recv()
    own_a = xa[b, a].astype(jnp.float32)
    for t in peers_z:
        own_a = own_a + r1a[t, a].astype(jnp.float32)
    own_b = xb[a, b].astype(jnp.float32)
    for t in peers_x:
        own_b = own_b + r1b[t, b].astype(jnp.float32)
    for t in peers_x:
        own_a = own_a + r2a[t].astype(jnp.float32)
    for t in peers_z:
        own_b = own_b + r2b[t].astype(jnp.float32)
    out[0] = own_a
    out[1] = own_b
    for c in first + second:
        c.wait_send()


def latent_reduce(xa, xb, collective_id):
    n, _, h, c = xa.shape
    dt = xa.dtype
    return pl.pallas_call(
        _reduce_kernel,
        out_shape=jax.ShapeDtypeStruct((2, h, c), jnp.float32),
        in_specs=[pl.BlockSpec(memory_space=pltpu.VMEM)] * 2,
        out_specs=pl.BlockSpec(memory_space=pltpu.VMEM),
        scratch_shapes=[
            pltpu.VMEM((n, n, h, c), dt),
            pltpu.VMEM((n, n, h, c), dt),
            pltpu.VMEM((n, h, c), dt),
            pltpu.VMEM((n, h, c), dt),
            pltpu.VMEM((n, h, c), dt),
            pltpu.VMEM((n, h, c), dt),
            pltpu.SemaphoreType.DMA((4, n)),
            pltpu.SemaphoreType.DMA((4, n)),
        ],
        compiler_params=pltpu.CompilerParams(collective_id=collective_id, has_side_effects=True),
    )(xa, xb)


def _gather_kernel(e, oa, ob, g1a, g1b, ga, gb, send_sems, recv_sems):
    a, b = _latent_coords()
    _greet(a, b)
    peers_z = [(b + k) % RING for k in range(1, RING)]
    peers_x = [(a + k) % RING for k in range(1, RING)]
    first = []
    for t in peers_z:
        c = _copy(e.at[0], g1a.at[b], send_sems.at[0, t], recv_sems.at[0, b], a * RING + t)
        c.start()
        first.append(c)
    for t in peers_x:
        c = _copy(e.at[1], g1b.at[a], send_sems.at[1, t], recv_sems.at[1, a], t * RING + b)
        c.start()
        first.append(c)
    g1a[b] = e[0]
    g1b[a] = e[1]
    for t in peers_z:
        _copy(e.at[0], g1a.at[t], send_sems.at[0, t], recv_sems.at[0, t], 0).wait_recv()
    for t in peers_x:
        _copy(e.at[1], g1b.at[t], send_sems.at[1, t], recv_sems.at[1, t], 0).wait_recv()
    second = []
    for t in peers_x:
        c = _copy(g1a, ga.at[a], send_sems.at[2, t], recv_sems.at[2, a], t * RING + b)
        c.start()
        second.append(c)
    for t in peers_z:
        c = _copy(g1b, gb.at[b], send_sems.at[3, t], recv_sems.at[3, b], a * RING + t)
        c.start()
        second.append(c)
    oa[a] = g1a[...]
    ob[b] = g1b[...]
    for t in peers_x:
        _copy(g1a, ga.at[t], send_sems.at[2, t], recv_sems.at[2, t], 0).wait_recv()
        oa[t] = ga[t]
    for t in peers_z:
        _copy(g1b, gb.at[t], send_sems.at[3, t], recv_sems.at[3, t], 0).wait_recv()
        ob[t] = gb[t]
    for c in first + second:
        c.wait_send()


def latent_gather(e, collective_id):
    _, h, c = e.shape
    n = RING
    dt = e.dtype
    full = jax.ShapeDtypeStruct((n, n, h, c), dt)
    return pl.pallas_call(
        _gather_kernel,
        out_shape=(full, full),
        in_specs=[pl.BlockSpec(memory_space=pltpu.VMEM)],
        out_specs=(pl.BlockSpec(memory_space=pltpu.VMEM), pl.BlockSpec(memory_space=pltpu.VMEM)),
        scratch_shapes=[
            pltpu.VMEM((n, h, c), dt),
            pltpu.VMEM((n, h, c), dt),
            pltpu.VMEM((n, n, h, c), dt),
            pltpu.VMEM((n, n, h, c), dt),
            pltpu.SemaphoreType.DMA((4, n)),
            pltpu.SemaphoreType.DMA((4, n)),
        ],
        compiler_params=pltpu.CompilerParams(collective_id=collective_id, has_side_effects=True),
    )(e)


def _layer_sum_kernel(x_ref, o_ref, recv_a, recv_b, recv_c, send_sems, recv_sems):
    me = lax.axis_index("layer")
    core = me % 2
    chip = me // 2
    mate = me + 1 - 2 * core
    far = me + 2 - 4 * chip
    half = x_ref.shape[0] // 2
    mine = pl.ds(pl.multiple_of(core * half, half), half)
    other = pl.ds(pl.multiple_of((1 - core) * half, half), half)

    barrier = pltpu.get_barrier_semaphore()
    for peer in (mate, far):
        pl.semaphore_signal(barrier, inc=1, device_id={"layer": peer}, device_id_type=MESH)
    pl.semaphore_wait(barrier, 2)

    def send(src, dst, slot, peer):
        return pltpu.make_async_remote_copy(
            src_ref=src, dst_ref=dst, send_sem=send_sems.at[slot], recv_sem=recv_sems.at[slot],
            device_id={"layer": peer}, device_id_type=MESH,
        )

    step_a = send(x_ref.at[other], recv_a, 0, mate)
    step_a.start()
    step_a.wait()
    o_ref[mine] = x_ref[mine].astype(jnp.float32) + recv_a[...].astype(jnp.float32)
    step_b = send(o_ref.at[mine], recv_b, 1, far)
    step_b.start()
    step_b.wait()
    o_ref[mine] = o_ref[mine] + recv_b[...]
    step_c = send(o_ref.at[mine], recv_c, 2, mate)
    step_c.start()
    step_c.wait()
    o_ref[other] = recv_c[...]


def layer_sum(x, collective_id):
    rows, cols = x.shape
    half = rows // 2
    return pl.pallas_call(
        _layer_sum_kernel,
        out_shape=jax.ShapeDtypeStruct((rows, cols), jnp.float32),
        in_specs=[pl.BlockSpec(memory_space=pltpu.VMEM)],
        out_specs=pl.BlockSpec(memory_space=pltpu.VMEM),
        scratch_shapes=[
            pltpu.VMEM((half, cols), x.dtype),
            pltpu.VMEM((half, cols), jnp.float32),
            pltpu.VMEM((half, cols), jnp.float32),
            pltpu.SemaphoreType.DMA((3,)),
            pltpu.SemaphoreType.DMA((3,)),
        ],
        compiler_params=pltpu.CompilerParams(collective_id=collective_id, has_side_effects=True),
    )(x)


def local(inputs, clean_acts, enc_weight, enc_bias, dec_weight, dec_bias, pairing, targets):
    row_count = inputs.shape[0]
    lat_count = enc_weight.shape[2]
    all_rows = pairing.shape[0]
    d_model = inputs.shape[2]
    chunk = d_model // (RING * RING)
    half = row_count // 2
    me = lax.axis_index("latent")
    partial_pre = jnp.einsum("rld,ldf->rf", inputs, enc_weight, preferred_element_type=jnp.float32)
    preact = layer_sum(partial_pre, 1) + enc_bias
    features = jnp.maximum(preact, 0.0).astype(jnp.bfloat16)
    dec4 = dec_weight[0].reshape(lat_count, RING, RING, chunk)
    recon_a = jnp.einsum("rf,fabd->badr", features[:half], dec4, preferred_element_type=jnp.float32)
    recon_b = jnp.einsum("rf,fabd->abdr", features[half:], dec4, preferred_element_type=jnp.float32)
    recon_sum = latent_reduce(recon_a.astype(jnp.bfloat16), recon_b.astype(jnp.bfloat16), 3)
    bias_part = lax.dynamic_slice_in_dim(dec_bias[0], me * chunk, chunk)
    clean_part = lax.dynamic_slice_in_dim(clean_acts[:, 0, :], me * chunk, chunk, axis=1)
    clean_t = jnp.swapaxes(clean_part.reshape(2, half, chunk), 1, 2).astype(jnp.float32)
    recon_error = (recon_sum + bias_part[:, None] - clean_t).astype(jnp.bfloat16)
    error_a, error_b = latent_gather(recon_error, 4)
    grad_a = jnp.einsum("abdr,fabd->rf", error_a, dec4, preferred_element_type=jnp.float32)
    grad_b = jnp.einsum("badr,fabd->rf", error_b, dec4, preferred_element_type=jnp.float32)
    partial_grad = jnp.concatenate([grad_a, grad_b], axis=0)
    feat_grad = layer_sum(partial_grad.astype(jnp.bfloat16), 2)
    row_ids = lax.axis_index("row") * row_count + jnp.arange(row_count, dtype=jnp.int32)
    latent_ids = me * lat_count + jnp.arange(lat_count, dtype=jnp.int32)
    every_row = jnp.arange(all_rows, dtype=jnp.int32)
    pair_table = (
        (every_row[None, :] == row_ids[:, None]).astype(jnp.float32)
        - (pairing[None, :] == row_ids[:, None]).astype(jnp.float32)
    ).astype(jnp.bfloat16)
    target_hot = (targets[:, None] == latent_ids[None, :]).astype(jnp.bfloat16)
    margin_table = jnp.dot(pair_table, target_hot, preferred_element_type=jnp.float32)
    pre_grad = jnp.where(preact > 0, feat_grad - MARGIN * margin_table, 0.0).astype(jnp.bfloat16)
    enc4 = enc_weight[0].reshape(RING, RING, chunk, lat_count)
    input_a = jnp.einsum("rf,abdf->badr", pre_grad[:half], enc4, preferred_element_type=jnp.float32)
    input_b = jnp.einsum("rf,abdf->abdr", pre_grad[half:], enc4, preferred_element_type=jnp.float32)
    total = latent_reduce(input_a.astype(jnp.bfloat16), input_b.astype(jnp.bfloat16), 5)
    return jnp.swapaxes(total.astype(jnp.bfloat16), 1, 2).reshape(row_count, 1, chunk)


def solution(mesh):
    placed = (
        P("row", "layer", None),
        P("row", "layer", None),
        P("layer", None, "latent"),
        P("latent"),
        P("layer", "latent", None),
        P("layer", None),
        P(),
        P(),
    )
    return jax.shard_map(
        local, mesh=mesh, in_specs=placed, out_specs=P("row", "layer", "latent"), check_vma=False
    )
```

```python
import jax
import jax.numpy as jnp
from jax import lax
from jax.experimental import pallas as pl
from jax.experimental.pallas import tpu as pltpu
from jax.sharding import PartitionSpec as P

MARGIN = 16.0
MESH = pl.DeviceIdType.MESH
RING = 4


def _latent_coords():
    me = lax.axis_index("latent")
    return me // RING, me % RING


def _greet(a, b):
    barrier = pltpu.get_barrier_semaphore()
    for k in range(1, RING):
        pl.semaphore_signal(barrier, inc=1, device_id={"latent": a * RING + (b + k) % RING}, device_id_type=MESH)
        pl.semaphore_signal(barrier, inc=1, device_id={"latent": ((a + k) % RING) * RING + b}, device_id_type=MESH)
    pl.semaphore_wait(barrier, 2 * (RING - 1))


def _copy(src, dst, send_sem, recv_sem, peer):
    return pltpu.make_async_remote_copy(
        src_ref=src, dst_ref=dst, send_sem=send_sem, recv_sem=recv_sem,
        device_id={"latent": peer}, device_id_type=MESH,
    )


def _reduce_kernel(xa, xb, out, r1a, r1b, s1a, s1b, r2a, r2b, send_sems, recv_sems):
    a, b = _latent_coords()
    _greet(a, b)
    peers_z = [(b + k) % RING for k in range(1, RING)]
    peers_x = [(a + k) % RING for k in range(1, RING)]
    first = []
    for t in peers_z:
        c = _copy(xa.at[t], r1a.at[b], send_sems.at[0, t], recv_sems.at[0, b], a * RING + t)
        c.start()
        first.append(c)
    for t in peers_x:
        c = _copy(xb.at[t], r1b.at[a], send_sems.at[1, t], recv_sems.at[1, a], t * RING + b)
        c.start()
        first.append(c)
    for t in peers_z:
        _copy(xa.at[t], r1a.at[t], send_sems.at[0, t], recv_sems.at[0, t], 0).wait_recv()
    for t in peers_x:
        _copy(xb.at[t], r1b.at[t], send_sems.at[1, t], recv_sems.at[1, t], 0).wait_recv()
    sum_a = xa[b].astype(jnp.float32)
    for t in peers_z:
        sum_a = sum_a + r1a[t].astype(jnp.float32)
    sum_b = xb[a].astype(jnp.float32)
    for t in peers_x:
        sum_b = sum_b + r1b[t].astype(jnp.float32)
    s1a[...] = sum_a.astype(s1a.dtype)
    s1b[...] = sum_b.astype(s1b.dtype)
    second = []
    for t in peers_x:
        c = _copy(s1a.at[t], r2a.at[a], send_sems.at[2, t], recv_sems.at[2, a], t * RING + b)
        c.start()
        second.append(c)
    for t in peers_z:
        c = _copy(s1b.at[t], r2b.at[b], send_sems.at[3, t], recv_sems.at[3, b], a * RING + t)
        c.start()
        second.append(c)
    for t in peers_x:
        _copy(s1a.at[t], r2a.at[t], send_sems.at[2, t], recv_sems.at[2, t], 0).wait_recv()
    for t in peers_z:
        _copy(s1b.at[t], r2b.at[t], send_sems.at[3, t], recv_sems.at[3, t], 0).wait_recv()
    own_a = xa[b, a].astype(jnp.float32)
    for t in peers_z:
        own_a = own_a + r1a[t, a].astype(jnp.float32)
    own_b = xb[a, b].astype(jnp.float32)
    for t in peers_x:
        own_b = own_b + r1b[t, b].astype(jnp.float32)
    for t in peers_x:
        own_a = own_a + r2a[t].astype(jnp.float32)
    for t in peers_z:
        own_b = own_b + r2b[t].astype(jnp.float32)
    out[0] = own_a
    out[1] = own_b
    for c in first + second:
        c.wait_send()


def latent_reduce(xa, xb, collective_id):
    n, _, h, c = xa.shape
    dt = xa.dtype
    return pl.pallas_call(
        _reduce_kernel,
        out_shape=jax.ShapeDtypeStruct((2, h, c), jnp.float32),
        in_specs=[pl.BlockSpec(memory_space=pltpu.VMEM)] * 2,
        out_specs=pl.BlockSpec(memory_space=pltpu.VMEM),
        scratch_shapes=[
            pltpu.VMEM((n, n, h, c), dt),
            pltpu.VMEM((n, n, h, c), dt),
            pltpu.VMEM((n, h, c), dt),
            pltpu.VMEM((n, h, c), dt),
            pltpu.VMEM((n, h, c), dt),
            pltpu.VMEM((n, h, c), dt),
            pltpu.SemaphoreType.DMA((4, n)),
            pltpu.SemaphoreType.DMA((4, n)),
        ],
        compiler_params=pltpu.CompilerParams(collective_id=collective_id, has_side_effects=True),
    )(xa, xb)


def _gather_kernel(e, oa, ob, g1a, g1b, ga, gb, send_sems, recv_sems):
    a, b = _latent_coords()
    _greet(a, b)
    peers_z = [(b + k) % RING for k in range(1, RING)]
    peers_x = [(a + k) % RING for k in range(1, RING)]
    first = []
    for t in peers_z:
        c = _copy(e.at[0], g1a.at[b], send_sems.at[0, t], recv_sems.at[0, b], a * RING + t)
        c.start()
        first.append(c)
    for t in peers_x:
        c = _copy(e.at[1], g1b.at[a], send_sems.at[1, t], recv_sems.at[1, a], t * RING + b)
        c.start()
        first.append(c)
    g1a[b] = e[0]
    g1b[a] = e[1]
    for t in peers_z:
        _copy(e.at[0], g1a.at[t], send_sems.at[0, t], recv_sems.at[0, t], 0).wait_recv()
    for t in peers_x:
        _copy(e.at[1], g1b.at[t], send_sems.at[1, t], recv_sems.at[1, t], 0).wait_recv()
    second = []
    for t in peers_x:
        c = _copy(g1a, ga.at[a], send_sems.at[2, t], recv_sems.at[2, a], t * RING + b)
        c.start()
        second.append(c)
    for t in peers_z:
        c = _copy(g1b, gb.at[b], send_sems.at[3, t], recv_sems.at[3, b], a * RING + t)
        c.start()
        second.append(c)
    oa[a] = g1a[...]
    for j in range(RING):
        ob[j, b] = g1b[j]
    for t in peers_x:
        _copy(g1a, ga.at[t], send_sems.at[2, t], recv_sems.at[2, t], 0).wait_recv()
        oa[t] = ga[t]
    for t in peers_z:
        _copy(g1b, gb.at[t], send_sems.at[3, t], recv_sems.at[3, t], 0).wait_recv()
        for j in range(RING):
            ob[j, t] = gb[t, j]
    for c in first + second:
        c.wait_send()


def latent_gather(e, collective_id):
    _, h, c = e.shape
    n = RING
    dt = e.dtype
    full = jax.ShapeDtypeStruct((n, n, h, c), dt)
    return pl.pallas_call(
        _gather_kernel,
        out_shape=(full, full),
        in_specs=[pl.BlockSpec(memory_space=pltpu.VMEM)],
        out_specs=(pl.BlockSpec(memory_space=pltpu.VMEM), pl.BlockSpec(memory_space=pltpu.VMEM)),
        scratch_shapes=[
            pltpu.VMEM((n, h, c), dt),
            pltpu.VMEM((n, h, c), dt),
            pltpu.VMEM((n, n, h, c), dt),
            pltpu.VMEM((n, n, h, c), dt),
            pltpu.SemaphoreType.DMA((4, n)),
            pltpu.SemaphoreType.DMA((4, n)),
        ],
        compiler_params=pltpu.CompilerParams(collective_id=collective_id, has_side_effects=True),
    )(e)


def _layer_sum_kernel(x_ref, o_ref, recv_a, recv_b, recv_c, send_sems, recv_sems):
    me = lax.axis_index("layer")
    core = me % 2
    chip = me // 2
    mate = me + 1 - 2 * core
    far = me + 2 - 4 * chip
    half = x_ref.shape[0] // 2
    mine = pl.ds(pl.multiple_of(core * half, half), half)
    other = pl.ds(pl.multiple_of((1 - core) * half, half), half)

    barrier = pltpu.get_barrier_semaphore()
    for peer in (mate, far):
        pl.semaphore_signal(barrier, inc=1, device_id={"layer": peer}, device_id_type=MESH)
    pl.semaphore_wait(barrier, 2)

    def send(src, dst, slot, peer):
        return pltpu.make_async_remote_copy(
            src_ref=src, dst_ref=dst, send_sem=send_sems.at[slot], recv_sem=recv_sems.at[slot],
            device_id={"layer": peer}, device_id_type=MESH,
        )

    step_a = send(x_ref.at[other], recv_a, 0, mate)
    step_a.start()
    step_a.wait()
    o_ref[mine] = x_ref[mine].astype(jnp.float32) + recv_a[...].astype(jnp.float32)
    step_b = send(o_ref.at[mine], recv_b, 1, far)
    step_b.start()
    step_b.wait()
    o_ref[mine] = o_ref[mine] + recv_b[...]
    step_c = send(o_ref.at[mine], recv_c, 2, mate)
    step_c.start()
    step_c.wait()
    o_ref[other] = recv_c[...]


def layer_sum(x, collective_id):
    rows, cols = x.shape
    half = rows // 2
    return pl.pallas_call(
        _layer_sum_kernel,
        out_shape=jax.ShapeDtypeStruct((rows, cols), jnp.float32),
        in_specs=[pl.BlockSpec(memory_space=pltpu.VMEM)],
        out_specs=pl.BlockSpec(memory_space=pltpu.VMEM),
        scratch_shapes=[
            pltpu.VMEM((half, cols), x.dtype),
            pltpu.VMEM((half, cols), jnp.float32),
            pltpu.VMEM((half, cols), jnp.float32),
            pltpu.SemaphoreType.DMA((3,)),
            pltpu.SemaphoreType.DMA((3,)),
        ],
        compiler_params=pltpu.CompilerParams(collective_id=collective_id, has_side_effects=True),
    )(x)


def local(inputs, clean_acts, enc_weight, enc_bias, dec_weight, dec_bias, pairing, targets):
    row_count = inputs.shape[0]
    lat_count = enc_weight.shape[2]
    all_rows = pairing.shape[0]
    d_model = inputs.shape[2]
    chunk = d_model // (RING * RING)
    half = row_count // 2
    me = lax.axis_index("latent")
    partial_pre = jnp.einsum("rld,ldf->rf", inputs, enc_weight, preferred_element_type=jnp.float32)
    preact = layer_sum(partial_pre, 1) + enc_bias
    features = jnp.maximum(preact, 0.0).astype(jnp.bfloat16)
    dec4 = dec_weight[0].reshape(lat_count, RING, RING, chunk)
    recon_a = jnp.einsum("rf,fabd->badr", features[:half], dec4, preferred_element_type=jnp.float32)
    recon_b = jnp.einsum("rf,fabd->abdr", features[half:], dec4, preferred_element_type=jnp.float32)
    recon_sum = latent_reduce(recon_a.astype(jnp.bfloat16), recon_b.astype(jnp.bfloat16), 3)
    bias_part = lax.dynamic_slice_in_dim(dec_bias[0], me * chunk, chunk)
    clean_part = lax.dynamic_slice_in_dim(clean_acts[:, 0, :], me * chunk, chunk, axis=1)
    clean_t = jnp.swapaxes(clean_part.reshape(2, half, chunk), 1, 2).astype(jnp.float32)
    recon_error = (recon_sum + bias_part[:, None] - clean_t).astype(jnp.bfloat16)
    error_a, error_b = latent_gather(recon_error, 4)
    error_all = jnp.concatenate(
        [error_a.reshape(d_model, half), error_b.reshape(d_model, half)], axis=1
    )
    partial_grad_t = jnp.dot(dec_weight[0], error_all, preferred_element_type=jnp.float32)
    feat_grad_t = layer_sum(partial_grad_t.astype(jnp.bfloat16), 2)
    row_ids = lax.axis_index("row") * row_count + jnp.arange(row_count, dtype=jnp.int32)
    latent_ids = me * lat_count + jnp.arange(lat_count, dtype=jnp.int32)
    every_row = jnp.arange(all_rows, dtype=jnp.int32)
    pair_table_t = (
        (every_row[:, None] == row_ids[None, :]).astype(jnp.float32)
        - (pairing[:, None] == row_ids[None, :]).astype(jnp.float32)
    ).astype(jnp.bfloat16)
    target_hot_t = (latent_ids[:, None] == targets[None, :]).astype(jnp.bfloat16)
    margin_t = jnp.dot(target_hot_t, pair_table_t, preferred_element_type=jnp.float32)
    pre_grad_t = jnp.where(preact.T > 0, feat_grad_t - MARGIN * margin_t, 0.0).astype(jnp.bfloat16)
    enc4 = enc_weight[0].reshape(RING, RING, chunk, lat_count)
    input_a = jnp.einsum("abdf,fr->badr", enc4, pre_grad_t[:, :half], preferred_element_type=jnp.float32)
    input_b = jnp.einsum("abdf,fr->abdr", enc4, pre_grad_t[:, half:], preferred_element_type=jnp.float32)
    total = latent_reduce(input_a.astype(jnp.bfloat16), input_b.astype(jnp.bfloat16), 5)
    return jnp.swapaxes(total.astype(jnp.bfloat16), 1, 2).reshape(row_count, 1, chunk)


def solution(mesh):
    placed = (
        P("row", "layer", None),
        P("row", "layer", None),
        P("layer", None, "latent"),
        P("latent"),
        P("layer", "latent", None),
        P("layer", None),
        P(),
        P(),
    )
    return jax.shard_map(
        local, mesh=mesh, in_specs=placed, out_specs=P("row", "layer", "latent"), check_vma=False
    )
```

```python
import jax
import jax.numpy as jnp
from jax import lax
from jax.experimental import pallas as pl
from jax.experimental.pallas import tpu as pltpu
from jax.sharding import PartitionSpec as P

MARGIN = 16.0
MESH = pl.DeviceIdType.MESH
RING = 4
LAYERS = 4


def _latent_coords():
    me = lax.axis_index("latent")
    return me // RING, me % RING


def _greet(a, b):
    barrier = pltpu.get_barrier_semaphore()
    for k in range(1, RING):
        pl.semaphore_signal(barrier, inc=1, device_id={"latent": a * RING + (b + k) % RING}, device_id_type=MESH)
        pl.semaphore_signal(barrier, inc=1, device_id={"latent": ((a + k) % RING) * RING + b}, device_id_type=MESH)
    pl.semaphore_wait(barrier, 2 * (RING - 1))


def _copy(src, dst, send_sem, recv_sem, peer):
    return pltpu.make_async_remote_copy(
        src_ref=src, dst_ref=dst, send_sem=send_sem, recv_sem=recv_sem,
        device_id={"latent": peer}, device_id_type=MESH,
    )


def _reduce_kernel(xa, xb, out, r1a, r1b, s1a, s1b, r2a, r2b, send_sems, recv_sems):
    a, b = _latent_coords()
    _greet(a, b)
    peers_z = [(b + k) % RING for k in range(1, RING)]
    peers_x = [(a + k) % RING for k in range(1, RING)]
    first = []
    for t in peers_z:
        c = _copy(xa.at[t], r1a.at[b], send_sems.at[0, t], recv_sems.at[0, b], a * RING + t)
        c.start()
        first.append(c)
    for t in peers_x:
        c = _copy(xb.at[t], r1b.at[a], send_sems.at[1, t], recv_sems.at[1, a], t * RING + b)
        c.start()
        first.append(c)
    for t in peers_z:
        _copy(xa.at[t], r1a.at[t], send_sems.at[0, t], recv_sems.at[0, t], 0).wait_recv()
    for t in peers_x:
        _copy(xb.at[t], r1b.at[t], send_sems.at[1, t], recv_sems.at[1, t], 0).wait_recv()
    sum_a = xa[b].astype(jnp.float32)
    for t in peers_z:
        sum_a = sum_a + r1a[t].astype(jnp.float32)
    sum_b = xb[a].astype(jnp.float32)
    for t in peers_x:
        sum_b = sum_b + r1b[t].astype(jnp.float32)
    s1a[...] = sum_a.astype(s1a.dtype)
    s1b[...] = sum_b.astype(s1b.dtype)
    second = []
    for t in peers_x:
        c = _copy(s1a.at[t], r2a.at[a], send_sems.at[2, t], recv_sems.at[2, a], t * RING + b)
        c.start()
        second.append(c)
    for t in peers_z:
        c = _copy(s1b.at[t], r2b.at[b], send_sems.at[3, t], recv_sems.at[3, b], a * RING + t)
        c.start()
        second.append(c)
    for t in peers_x:
        _copy(s1a.at[t], r2a.at[t], send_sems.at[2, t], recv_sems.at[2, t], 0).wait_recv()
    for t in peers_z:
        _copy(s1b.at[t], r2b.at[t], send_sems.at[3, t], recv_sems.at[3, t], 0).wait_recv()
    own_a = xa[b, a].astype(jnp.float32)
    for t in peers_z:
        own_a = own_a + r1a[t, a].astype(jnp.float32)
    own_b = xb[a, b].astype(jnp.float32)
    for t in peers_x:
        own_b = own_b + r1b[t, b].astype(jnp.float32)
    for t in peers_x:
        own_a = own_a + r2a[t].astype(jnp.float32)
    for t in peers_z:
        own_b = own_b + r2b[t].astype(jnp.float32)
    out[0] = own_a
    out[1] = own_b
    for c in first + second:
        c.wait_send()


def latent_reduce(xa, xb, collective_id):
    n, _, h, c = xa.shape
    dt = xa.dtype
    return pl.pallas_call(
        _reduce_kernel,
        out_shape=jax.ShapeDtypeStruct((2, h, c), jnp.float32),
        in_specs=[pl.BlockSpec(memory_space=pltpu.VMEM)] * 2,
        out_specs=pl.BlockSpec(memory_space=pltpu.VMEM),
        scratch_shapes=[
            pltpu.VMEM((n, n, h, c), dt),
            pltpu.VMEM((n, n, h, c), dt),
            pltpu.VMEM((n, h, c), dt),
            pltpu.VMEM((n, h, c), dt),
            pltpu.VMEM((n, h, c), dt),
            pltpu.VMEM((n, h, c), dt),
            pltpu.SemaphoreType.DMA((4, n)),
            pltpu.SemaphoreType.DMA((4, n)),
        ],
        compiler_params=pltpu.CompilerParams(collective_id=collective_id, has_side_effects=True),
    )(xa, xb)


def _gather_kernel(e, oa, ob, g1a, g1b, ga, gb, send_sems, recv_sems):
    a, b = _latent_coords()
    _greet(a, b)
    peers_z = [(b + k) % RING for k in range(1, RING)]
    peers_x = [(a + k) % RING for k in range(1, RING)]
    first = []
    for t in peers_z:
        c = _copy(e.at[0], g1a.at[b], send_sems.at[0, t], recv_sems.at[0, b], a * RING + t)
        c.start()
        first.append(c)
    for t in peers_x:
        c = _copy(e.at[1], g1b.at[a], send_sems.at[1, t], recv_sems.at[1, a], t * RING + b)
        c.start()
        first.append(c)
    g1a[b] = e[0]
    g1b[a] = e[1]
    for t in peers_z:
        _copy(e.at[0], g1a.at[t], send_sems.at[0, t], recv_sems.at[0, t], 0).wait_recv()
    for t in peers_x:
        _copy(e.at[1], g1b.at[t], send_sems.at[1, t], recv_sems.at[1, t], 0).wait_recv()
    second = []
    for t in peers_x:
        c = _copy(g1a, ga.at[a], send_sems.at[2, t], recv_sems.at[2, a], t * RING + b)
        c.start()
        second.append(c)
    for t in peers_z:
        c = _copy(g1b, gb.at[b], send_sems.at[3, t], recv_sems.at[3, b], a * RING + t)
        c.start()
        second.append(c)
    oa[a] = g1a[...]
    for j in range(RING):
        ob[j, b] = g1b[j]
    for t in peers_x:
        _copy(g1a, ga.at[t], send_sems.at[2, t], recv_sems.at[2, t], 0).wait_recv()
        oa[t] = ga[t]
    for t in peers_z:
        _copy(g1b, gb.at[t], send_sems.at[3, t], recv_sems.at[3, t], 0).wait_recv()
        for j in range(RING):
            ob[j, t] = gb[t, j]
    for c in first + second:
        c.wait_send()


def latent_gather(e, collective_id):
    _, h, c = e.shape
    n = RING
    dt = e.dtype
    full = jax.ShapeDtypeStruct((n, n, h, c), dt)
    return pl.pallas_call(
        _gather_kernel,
        out_shape=(full, full),
        in_specs=[pl.BlockSpec(memory_space=pltpu.VMEM)],
        out_specs=(pl.BlockSpec(memory_space=pltpu.VMEM), pl.BlockSpec(memory_space=pltpu.VMEM)),
        scratch_shapes=[
            pltpu.VMEM((n, h, c), dt),
            pltpu.VMEM((n, h, c), dt),
            pltpu.VMEM((n, n, h, c), dt),
            pltpu.VMEM((n, n, h, c), dt),
            pltpu.SemaphoreType.DMA((4, n)),
            pltpu.SemaphoreType.DMA((4, n)),
        ],
        compiler_params=pltpu.CompilerParams(collective_id=collective_id, has_side_effects=True),
    )(e)


def _layer_peers():
    me = lax.axis_index("layer")
    return me, [(me + k) % LAYERS for k in range(1, LAYERS)]


def _layer_greet(peers):
    barrier = pltpu.get_barrier_semaphore()
    for p in peers:
        pl.semaphore_signal(barrier, inc=1, device_id={"layer": p}, device_id_type=MESH)
    pl.semaphore_wait(barrier, LAYERS - 1)


def _layer_copy(src, dst, send_sems, recv_sems, k, p, slot):
    return pltpu.make_async_remote_copy(
        src_ref=src, dst_ref=dst, send_sem=send_sems.at[k, p], recv_sem=recv_sems.at[k, slot],
        device_id={"layer": p}, device_id_type=MESH,
    )


def _layer_pre_kernel(x, bias, feats, pre_q, r1, r2, send_sems, recv_sems):
    me, peers = _layer_peers()
    q = x.shape[0] // LAYERS
    rows = lambda i: pl.ds(pl.multiple_of(i * q, q), q)
    _layer_greet(peers)
    sent = []
    for p in peers:
        c = _layer_copy(x.at[rows(p)], r1.at[me], send_sems, recv_sems, 0, p, me)
        c.start()
        sent.append(c)
    total = x[rows(me)]
    for p in peers:
        _layer_copy(x.at[rows(p)], r1.at[p], send_sems, recv_sems, 0, p, p).wait_recv()
        total = total + r1[p]
    total = total + bias[...]
    pre_q[...] = total
    feats[rows(me)] = jnp.maximum(total, 0.0).astype(feats.dtype)
    for p in peers:
        c = _layer_copy(feats.at[rows(me)], r2.at[me], send_sems, recv_sems, 1, p, me)
        c.start()
        sent.append(c)
    for p in peers:
        _layer_copy(feats.at[rows(p)], r2.at[p], send_sems, recv_sems, 1, p, p).wait_recv()
        feats[rows(p)] = r2[p]
    for c in sent:
        c.wait_send()


def layer_pre(x, bias):
    rows, cols = x.shape
    q = rows // LAYERS
    return pl.pallas_call(
        _layer_pre_kernel,
        out_shape=(jax.ShapeDtypeStruct((rows, cols), jnp.bfloat16),
                   jax.ShapeDtypeStruct((q, cols), jnp.float32)),
        in_specs=[pl.BlockSpec(memory_space=pltpu.VMEM)] * 2,
        out_specs=(pl.BlockSpec(memory_space=pltpu.VMEM), pl.BlockSpec(memory_space=pltpu.VMEM)),
        scratch_shapes=[
            pltpu.VMEM((LAYERS, q, cols), jnp.float32),
            pltpu.VMEM((LAYERS, q, cols), jnp.bfloat16),
            pltpu.SemaphoreType.DMA((2, LAYERS)),
            pltpu.SemaphoreType.DMA((2, LAYERS)),
        ],
        compiler_params=pltpu.CompilerParams(collective_id=1, has_side_effects=True),
    )(x, bias)


def _layer_grad_kernel(g, pre_q, margin_q, out, r1, r2, send_sems, recv_sems):
    me, peers = _layer_peers()
    q = g.shape[1] // LAYERS
    lanes = lambda i: pl.ds(pl.multiple_of(i * q, q), q)
    _layer_greet(peers)
    sent = []
    for p in peers:
        c = _layer_copy(g.at[:, lanes(p)], r1.at[me], send_sems, recv_sems, 0, p, me)
        c.start()
        sent.append(c)
    total = g[:, lanes(me)].astype(jnp.float32)
    for p in peers:
        _layer_copy(g.at[:, lanes(p)], r1.at[p], send_sems, recv_sems, 0, p, p).wait_recv()
        total = total + r1[p].astype(jnp.float32)
    grad = jnp.where(pre_q[...] > 0, total - MARGIN * margin_q[...], 0.0)
    out[:, lanes(me)] = grad.astype(out.dtype)
    for p in peers:
        c = _layer_copy(out.at[:, lanes(me)], r2.at[me], send_sems, recv_sems, 1, p, me)
        c.start()
        sent.append(c)
    for p in peers:
        _layer_copy(out.at[:, lanes(p)], r2.at[p], send_sems, recv_sems, 1, p, p).wait_recv()
        out[:, lanes(p)] = r2[p]
    for c in sent:
        c.wait_send()


def layer_grad(g, pre_q, margin_q):
    cols, rows = g.shape
    q = rows // LAYERS
    return pl.pallas_call(
        _layer_grad_kernel,
        out_shape=jax.ShapeDtypeStruct((cols, rows), jnp.bfloat16),
        in_specs=[pl.BlockSpec(memory_space=pltpu.VMEM)] * 3,
        out_specs=pl.BlockSpec(memory_space=pltpu.VMEM),
        scratch_shapes=[
            pltpu.VMEM((LAYERS, cols, q), jnp.bfloat16),
            pltpu.VMEM((LAYERS, cols, q), jnp.bfloat16),
            pltpu.SemaphoreType.DMA((2, LAYERS)),
            pltpu.SemaphoreType.DMA((2, LAYERS)),
        ],
        compiler_params=pltpu.CompilerParams(collective_id=2, has_side_effects=True),
    )(g, pre_q, margin_q)


def local(inputs, clean_acts, enc_weight, enc_bias, dec_weight, dec_bias, pairing, targets):
    row_count = inputs.shape[0]
    lat_count = enc_weight.shape[2]
    all_rows = pairing.shape[0]
    d_model = inputs.shape[2]
    chunk = d_model // (RING * RING)
    half = row_count // 2
    me = lax.axis_index("latent")
    partial_pre = jnp.einsum("rld,ldf->rf", inputs, enc_weight, preferred_element_type=jnp.float32)
    features, pre_q = layer_pre(partial_pre, enc_bias[None, :])
    dec4 = dec_weight[0].reshape(lat_count, RING, RING, chunk)
    recon_a = jnp.einsum("rf,fabd->badr", features[:half], dec4, preferred_element_type=jnp.float32)
    recon_b = jnp.einsum("rf,fabd->abdr", features[half:], dec4, preferred_element_type=jnp.float32)
    recon_sum = latent_reduce(recon_a.astype(jnp.bfloat16), recon_b.astype(jnp.bfloat16), 3)
    bias_part = lax.dynamic_slice_in_dim(dec_bias[0], me * chunk, chunk)
    clean_part = lax.dynamic_slice_in_dim(clean_acts[:, 0, :], me * chunk, chunk, axis=1)
    clean_t = jnp.swapaxes(clean_part.reshape(2, half, chunk), 1, 2).astype(jnp.float32)
    recon_error = (recon_sum + bias_part[:, None] - clean_t).astype(jnp.bfloat16)
    error_a, error_b = latent_gather(recon_error, 4)
    error_all = jnp.concatenate(
        [error_a.reshape(d_model, half), error_b.reshape(d_model, half)], axis=1
    )
    partial_grad_t = jnp.dot(dec_weight[0], error_all, preferred_element_type=jnp.float32)
    quarter = row_count // LAYERS
    row_ids = (
        lax.axis_index("row") * row_count
        + lax.axis_index("layer") * quarter
        + jnp.arange(quarter, dtype=jnp.int32)
    )
    latent_ids = me * lat_count + jnp.arange(lat_count, dtype=jnp.int32)
    every_row = jnp.arange(all_rows, dtype=jnp.int32)
    pair_table_t = (
        (every_row[:, None] == row_ids[None, :]).astype(jnp.float32)
        - (pairing[:, None] == row_ids[None, :]).astype(jnp.float32)
    ).astype(jnp.bfloat16)
    target_hot_t = (latent_ids[:, None] == targets[None, :]).astype(jnp.bfloat16)
    margin_q = jnp.dot(target_hot_t, pair_table_t, preferred_element_type=jnp.float32)
    pre_grad_t = layer_grad(partial_grad_t.astype(jnp.bfloat16), pre_q.T, margin_q)
    enc4 = enc_weight[0].reshape(RING, RING, chunk, lat_count)
    input_a = jnp.einsum("abdf,fr->badr", enc4, pre_grad_t[:, :half], preferred_element_type=jnp.float32)
    input_b = jnp.einsum("abdf,fr->abdr", enc4, pre_grad_t[:, half:], preferred_element_type=jnp.float32)
    total = latent_reduce(input_a.astype(jnp.bfloat16), input_b.astype(jnp.bfloat16), 5)
    return jnp.swapaxes(total.astype(jnp.bfloat16), 1, 2).reshape(row_count, 1, chunk)


def solution(mesh):
    placed = (
        P("row", "layer", None),
        P("row", "layer", None),
        P("layer", None, "latent"),
        P("latent"),
        P("layer", "latent", None),
        P("layer", None),
        P(),
        P(),
    )
    return jax.shard_map(
        local, mesh=mesh, in_specs=placed, out_specs=P("row", "layer", "latent"), check_vma=False
    )
```

```python
import jax
import jax.numpy as jnp
from jax import lax
from jax.experimental import pallas as pl
from jax.experimental.pallas import tpu as pltpu
from jax.sharding import PartitionSpec as P

MARGIN = 16.0
MESH = pl.DeviceIdType.MESH
RING = 4
LAYERS = 4


def _latent_coords():
    me = lax.axis_index("latent")
    return me // RING, me % RING


def _greet(a, b):
    barrier = pltpu.get_barrier_semaphore()
    for k in range(1, RING):
        pl.semaphore_signal(barrier, inc=1, device_id={"latent": a * RING + (b + k) % RING}, device_id_type=MESH)
        pl.semaphore_signal(barrier, inc=1, device_id={"latent": ((a + k) % RING) * RING + b}, device_id_type=MESH)
    pl.semaphore_wait(barrier, 2 * (RING - 1))


def _copy(src, dst, send_sem, recv_sem, peer):
    return pltpu.make_async_remote_copy(
        src_ref=src, dst_ref=dst, send_sem=send_sem, recv_sem=recv_sem,
        device_id={"latent": peer}, device_id_type=MESH,
    )


def _reduce_kernel(xa, xb, out, r1a, r1b, s1a, s1b, r2a, r2b, send_sems, recv_sems):
    a, b = _latent_coords()
    _greet(a, b)
    peers_z = [(b + k) % RING for k in range(1, RING)]
    peers_x = [(a + k) % RING for k in range(1, RING)]
    first = []
    for t in peers_z:
        c = _copy(xa.at[t], r1a.at[b], send_sems.at[0, t], recv_sems.at[0, b], a * RING + t)
        c.start()
        first.append(c)
    for t in peers_x:
        c = _copy(xb.at[t], r1b.at[a], send_sems.at[1, t], recv_sems.at[1, a], t * RING + b)
        c.start()
        first.append(c)
    for t in peers_z:
        _copy(xa.at[t], r1a.at[t], send_sems.at[0, t], recv_sems.at[0, t], 0).wait_recv()
    for t in peers_x:
        _copy(xb.at[t], r1b.at[t], send_sems.at[1, t], recv_sems.at[1, t], 0).wait_recv()
    sum_a = xa[b].astype(jnp.float32)
    for t in peers_z:
        sum_a = sum_a + r1a[t].astype(jnp.float32)
    sum_b = xb[a].astype(jnp.float32)
    for t in peers_x:
        sum_b = sum_b + r1b[t].astype(jnp.float32)
    s1a[...] = sum_a.astype(s1a.dtype)
    s1b[...] = sum_b.astype(s1b.dtype)
    second = []
    for t in peers_x:
        c = _copy(s1a.at[t], r2a.at[a], send_sems.at[2, t], recv_sems.at[2, a], t * RING + b)
        c.start()
        second.append(c)
    for t in peers_z:
        c = _copy(s1b.at[t], r2b.at[b], send_sems.at[3, t], recv_sems.at[3, b], a * RING + t)
        c.start()
        second.append(c)
    for t in peers_x:
        _copy(s1a.at[t], r2a.at[t], send_sems.at[2, t], recv_sems.at[2, t], 0).wait_recv()
    for t in peers_z:
        _copy(s1b.at[t], r2b.at[t], send_sems.at[3, t], recv_sems.at[3, t], 0).wait_recv()
    own_a = xa[b, a].astype(jnp.float32)
    for t in peers_z:
        own_a = own_a + r1a[t, a].astype(jnp.float32)
    own_b = xb[a, b].astype(jnp.float32)
    for t in peers_x:
        own_b = own_b + r1b[t, b].astype(jnp.float32)
    for t in peers_x:
        own_a = own_a + r2a[t].astype(jnp.float32)
    for t in peers_z:
        own_b = own_b + r2b[t].astype(jnp.float32)
    out[0] = own_a
    out[1] = own_b
    for c in first + second:
        c.wait_send()


def latent_reduce(xa, xb, collective_id):
    n, _, h, c = xa.shape
    dt = xa.dtype
    return pl.pallas_call(
        _reduce_kernel,
        out_shape=jax.ShapeDtypeStruct((2, h, c), jnp.float32),
        in_specs=[pl.BlockSpec(memory_space=pltpu.VMEM)] * 2,
        out_specs=pl.BlockSpec(memory_space=pltpu.VMEM),
        scratch_shapes=[
            pltpu.VMEM((n, n, h, c), dt),
            pltpu.VMEM((n, n, h, c), dt),
            pltpu.VMEM((n, h, c), dt),
            pltpu.VMEM((n, h, c), dt),
            pltpu.VMEM((n, h, c), dt),
            pltpu.VMEM((n, h, c), dt),
            pltpu.SemaphoreType.DMA((4, n)),
            pltpu.SemaphoreType.DMA((4, n)),
        ],
        compiler_params=pltpu.CompilerParams(collective_id=collective_id, has_side_effects=True),
    )(xa, xb)


def _gather_kernel(e, oa, ob, g1a, g1b, ga, gb, send_sems, recv_sems):
    a, b = _latent_coords()
    _greet(a, b)
    peers_z = [(b + k) % RING for k in range(1, RING)]
    peers_x = [(a + k) % RING for k in range(1, RING)]
    first = []
    for t in peers_z:
        c = _copy(e.at[0], g1a.at[b], send_sems.at[0, t], recv_sems.at[0, b], a * RING + t)
        c.start()
        first.append(c)
    for t in peers_x:
        c = _copy(e.at[1], g1b.at[a], send_sems.at[1, t], recv_sems.at[1, a], t * RING + b)
        c.start()
        first.append(c)
    g1a[b] = e[0]
    g1b[a] = e[1]
    for t in peers_z:
        _copy(e.at[0], g1a.at[t], send_sems.at[0, t], recv_sems.at[0, t], 0).wait_recv()
    for t in peers_x:
        _copy(e.at[1], g1b.at[t], send_sems.at[1, t], recv_sems.at[1, t], 0).wait_recv()
    second = []
    for t in peers_x:
        c = _copy(g1a, ga.at[a], send_sems.at[2, t], recv_sems.at[2, a], t * RING + b)
        c.start()
        second.append(c)
    for t in peers_z:
        c = _copy(g1b, gb.at[b], send_sems.at[3, t], recv_sems.at[3, b], a * RING + t)
        c.start()
        second.append(c)
    oa[a] = g1a[...]
    for j in range(RING):
        ob[j, b] = g1b[j]
    for t in peers_x:
        _copy(g1a, ga.at[t], send_sems.at[2, t], recv_sems.at[2, t], 0).wait_recv()
        oa[t] = ga[t]
    for t in peers_z:
        _copy(g1b, gb.at[t], send_sems.at[3, t], recv_sems.at[3, t], 0).wait_recv()
        for j in range(RING):
            ob[j, t] = gb[t, j]
    for c in first + second:
        c.wait_send()


def latent_gather(e, collective_id):
    _, h, c = e.shape
    n = RING
    dt = e.dtype
    full = jax.ShapeDtypeStruct((n, n, h, c), dt)
    return pl.pallas_call(
        _gather_kernel,
        out_shape=(full, full),
        in_specs=[pl.BlockSpec(memory_space=pltpu.VMEM)],
        out_specs=(pl.BlockSpec(memory_space=pltpu.VMEM), pl.BlockSpec(memory_space=pltpu.VMEM)),
        scratch_shapes=[
            pltpu.VMEM((n, h, c), dt),
            pltpu.VMEM((n, h, c), dt),
            pltpu.VMEM((n, n, h, c), dt),
            pltpu.VMEM((n, n, h, c), dt),
            pltpu.SemaphoreType.DMA((4, n)),
            pltpu.SemaphoreType.DMA((4, n)),
        ],
        compiler_params=pltpu.CompilerParams(collective_id=collective_id, has_side_effects=True),
    )(e)


def _layer_roles():
    me = lax.axis_index("layer")
    mate = me + 1 - 2 * (me % 2)
    far = (me + 2) % LAYERS
    return me, mate, far, (mate + 2) % LAYERS


def _layer_exchange(quarter, x, out, finish, ra, sb, rb, rc, rd, send_sems, recv_sems):
    me, mate, far, mate_far = _layer_roles()
    barrier = pltpu.get_barrier_semaphore()
    for p in (mate, far):
        pl.semaphore_signal(barrier, inc=1, device_id={"layer": p}, device_id_type=MESH)
    pl.semaphore_wait(barrier, 2)

    def copy(src, dst, k, p):
        return pltpu.make_async_remote_copy(
            src_ref=src, dst_ref=dst, send_sem=send_sems.at[k], recv_sem=recv_sems.at[k],
            device_id={"layer": p}, device_id_type=MESH,
        )

    sent = [copy(quarter(x, mate), ra.at[0], 0, mate), copy(quarter(x, mate_far), ra.at[1], 1, mate)]
    for c in sent:
        c.start()
    sent[0].wait_recv()
    sent[1].wait_recv()
    sb[...] = quarter(x, far)[...].astype(jnp.float32) + ra[1].astype(jnp.float32)
    step_b = copy(sb, rb, 2, far)
    step_b.start()
    own = quarter(x, me)[...].astype(jnp.float32) + ra[0].astype(jnp.float32)
    step_b.wait_recv()
    quarter(out, me)[...] = finish(own + rb[...])
    step_c = copy(quarter(out, me), rc, 3, far)
    step_c.start()
    step_c.wait_recv()
    quarter(out, far)[...] = rc[...]
    step_d = [copy(quarter(out, me), rd.at[0], 4, mate), copy(rc, rd.at[1], 5, mate)]
    for c in step_d:
        c.start()
    for c in step_d:
        c.wait_recv()
    quarter(out, mate)[...] = rd[0]
    quarter(out, mate_far)[...] = rd[1]
    for c in sent + [step_b, step_c] + step_d:
        c.wait_send()


def _row_quarter(ref, i):
    q = ref.shape[0] // LAYERS
    return ref.at[pl.ds(pl.multiple_of(i * q, q), q)]


def _lane_quarter(ref, i):
    q = ref.shape[1] // LAYERS
    return ref.at[:, pl.ds(pl.multiple_of(i * q, q), q)]


def _layer_pre_kernel(x, bias, feats, pre_q, *scratch):
    def finish(total):
        pre = total + bias[...]
        pre_q[...] = pre
        return jnp.maximum(pre, 0.0).astype(feats.dtype)

    _layer_exchange(_row_quarter, x, feats, finish, *scratch)


def _layer_scratch(in_q, out_q, in_dtype):
    return [
        pltpu.VMEM((2,) + in_q, in_dtype),
        pltpu.VMEM(in_q, jnp.float32),
        pltpu.VMEM(in_q, jnp.float32),
        pltpu.VMEM(out_q, jnp.bfloat16),
        pltpu.VMEM((2,) + out_q, jnp.bfloat16),
        pltpu.SemaphoreType.DMA((6,)),
        pltpu.SemaphoreType.DMA((6,)),
    ]


def layer_pre(x, bias):
    rows, cols = x.shape
    q = rows // LAYERS
    return pl.pallas_call(
        _layer_pre_kernel,
        out_shape=(jax.ShapeDtypeStruct((rows, cols), jnp.bfloat16),
                   jax.ShapeDtypeStruct((q, cols), jnp.float32)),
        in_specs=[pl.BlockSpec(memory_space=pltpu.VMEM)] * 2,
        out_specs=(pl.BlockSpec(memory_space=pltpu.VMEM), pl.BlockSpec(memory_space=pltpu.VMEM)),
        scratch_shapes=_layer_scratch((q, cols), (q, cols), x.dtype),
        compiler_params=pltpu.CompilerParams(collective_id=1, has_side_effects=True),
    )(x, bias)


def _layer_grad_kernel(g, pre_q, margin_q, out, *scratch):
    def finish(total):
        grad = jnp.where(pre_q[...] > 0, total - MARGIN * margin_q[...], 0.0)
        return grad.astype(out.dtype)

    _layer_exchange(_lane_quarter, g, out, finish, *scratch)


def layer_grad(g, pre_q, margin_q):
    cols, rows = g.shape
    q = rows // LAYERS
    return pl.pallas_call(
        _layer_grad_kernel,
        out_shape=jax.ShapeDtypeStruct((cols, rows), jnp.bfloat16),
        in_specs=[pl.BlockSpec(memory_space=pltpu.VMEM)] * 3,
        out_specs=pl.BlockSpec(memory_space=pltpu.VMEM),
        scratch_shapes=_layer_scratch((cols, q), (cols, q), g.dtype),
        compiler_params=pltpu.CompilerParams(collective_id=2, has_side_effects=True),
    )(g, pre_q, margin_q)


def local(inputs, clean_acts, enc_weight, enc_bias, dec_weight, dec_bias, pairing, targets):
    row_count = inputs.shape[0]
    lat_count = enc_weight.shape[2]
    all_rows = pairing.shape[0]
    d_model = inputs.shape[2]
    chunk = d_model // (RING * RING)
    half = row_count // 2
    me = lax.axis_index("latent")
    partial_pre = jnp.einsum("rld,ldf->rf", inputs, enc_weight, preferred_element_type=jnp.float32)
    features, pre_q = layer_pre(partial_pre, enc_bias[None, :])
    dec4 = dec_weight[0].reshape(lat_count, RING, RING, chunk)
    recon_a = jnp.einsum("rf,fabd->badr", features[:half], dec4, preferred_element_type=jnp.float32)
    recon_b = jnp.einsum("rf,fabd->abdr", features[half:], dec4, preferred_element_type=jnp.float32)
    recon_sum = latent_reduce(recon_a.astype(jnp.bfloat16), recon_b.astype(jnp.bfloat16), 3)
    bias_part = lax.dynamic_slice_in_dim(dec_bias[0], me * chunk, chunk)
    clean_part = lax.dynamic_slice_in_dim(clean_acts[:, 0, :], me * chunk, chunk, axis=1)
    clean_t = jnp.swapaxes(clean_part.reshape(2, half, chunk), 1, 2).astype(jnp.float32)
    recon_error = (recon_sum + bias_part[:, None] - clean_t).astype(jnp.bfloat16)
    error_a, error_b = latent_gather(recon_error, 4)
    error_all = jnp.concatenate(
        [error_a.reshape(d_model, half), error_b.reshape(d_model, half)], axis=1
    )
    partial_grad_t = jnp.dot(dec_weight[0], error_all, preferred_element_type=jnp.float32)
    quarter = row_count // LAYERS
    row_ids = (
        lax.axis_index("row") * row_count
        + lax.axis_index("layer") * quarter
        + jnp.arange(quarter, dtype=jnp.int32)
    )
    latent_ids = me * lat_count + jnp.arange(lat_count, dtype=jnp.int32)
    every_row = jnp.arange(all_rows, dtype=jnp.int32)
    pair_table_t = (
        (every_row[:, None] == row_ids[None, :]).astype(jnp.float32)
        - (pairing[:, None] == row_ids[None, :]).astype(jnp.float32)
    ).astype(jnp.bfloat16)
    target_hot_t = (latent_ids[:, None] == targets[None, :]).astype(jnp.bfloat16)
    margin_q = jnp.dot(target_hot_t, pair_table_t, preferred_element_type=jnp.float32)
    pre_grad_t = layer_grad(partial_grad_t.astype(jnp.bfloat16), pre_q.T, margin_q)
    enc4 = enc_weight[0].reshape(RING, RING, chunk, lat_count)
    input_a = jnp.einsum("abdf,fr->badr", enc4, pre_grad_t[:, :half], preferred_element_type=jnp.float32)
    input_b = jnp.einsum("abdf,fr->abdr", enc4, pre_grad_t[:, half:], preferred_element_type=jnp.float32)
    total = latent_reduce(input_a.astype(jnp.bfloat16), input_b.astype(jnp.bfloat16), 5)
    return jnp.swapaxes(total.astype(jnp.bfloat16), 1, 2).reshape(row_count, 1, chunk)


def solution(mesh):
    placed = (
        P("row", "layer", None),
        P("row", "layer", None),
        P("layer", None, "latent"),
        P("latent"),
        P("layer", "latent", None),
        P("layer", None),
        P(),
        P(),
    )
    return jax.shard_map(
        local, mesh=mesh, in_specs=placed, out_specs=P("row", "layer", "latent"), check_vma=False
    )
```

```python
import jax
import jax.numpy as jnp
from jax import lax
from jax.experimental import pallas as pl
from jax.experimental.pallas import tpu as pltpu
from jax.sharding import PartitionSpec as P

MARGIN = 16.0
MESH = pl.DeviceIdType.MESH
RING = 4
LAYERS = 4


def _latent_coords():
    me = lax.axis_index("latent")
    return me // RING, me % RING


def _greet(a, b):
    barrier = pltpu.get_barrier_semaphore()
    for k in range(1, RING):
        pl.semaphore_signal(barrier, inc=1, device_id={"latent": a * RING + (b + k) % RING}, device_id_type=MESH)
        pl.semaphore_signal(barrier, inc=1, device_id={"latent": ((a + k) % RING) * RING + b}, device_id_type=MESH)
    pl.semaphore_wait(barrier, 2 * (RING - 1))


def _copy(src, dst, send_sem, recv_sem, peer):
    return pltpu.make_async_remote_copy(
        src_ref=src, dst_ref=dst, send_sem=send_sem, recv_sem=recv_sem,
        device_id={"latent": peer}, device_id_type=MESH,
    )


def _reduce_kernel(xa, xb, out, r1a, r1b, s1a, s1b, r2a, r2b, send_sems, recv_sems):
    a, b = _latent_coords()
    _greet(a, b)
    peers_z = [(b + k) % RING for k in range(1, RING)]
    peers_x = [(a + k) % RING for k in range(1, RING)]
    first = []
    for t in peers_z:
        c = _copy(xa.at[:, t], r1a.at[b], send_sems.at[0, t], recv_sems.at[0, b], a * RING + t)
        c.start()
        first.append(c)
    for t in peers_x:
        c = _copy(xb.at[t], r1b.at[a], send_sems.at[1, t], recv_sems.at[1, a], t * RING + b)
        c.start()
        first.append(c)
    for t in peers_z:
        _copy(xa.at[:, t], r1a.at[t], send_sems.at[0, t], recv_sems.at[0, t], 0).wait_recv()
    for t in peers_x:
        _copy(xb.at[t], r1b.at[t], send_sems.at[1, t], recv_sems.at[1, t], 0).wait_recv()
    sum_a = xa[:, b].astype(jnp.float32)
    for t in peers_z:
        sum_a = sum_a + r1a[t].astype(jnp.float32)
    sum_b = xb[a].astype(jnp.float32)
    for t in peers_x:
        sum_b = sum_b + r1b[t].astype(jnp.float32)
    s1a[...] = sum_a.astype(s1a.dtype)
    s1b[...] = sum_b.astype(s1b.dtype)
    second = []
    for t in peers_x:
        c = _copy(s1a.at[t], r2a.at[a], send_sems.at[2, t], recv_sems.at[2, a], t * RING + b)
        c.start()
        second.append(c)
    for t in peers_z:
        c = _copy(s1b.at[t], r2b.at[b], send_sems.at[3, t], recv_sems.at[3, b], a * RING + t)
        c.start()
        second.append(c)
    for t in peers_x:
        _copy(s1a.at[t], r2a.at[t], send_sems.at[2, t], recv_sems.at[2, t], 0).wait_recv()
    for t in peers_z:
        _copy(s1b.at[t], r2b.at[t], send_sems.at[3, t], recv_sems.at[3, t], 0).wait_recv()
    own_a = xa[a, b].astype(jnp.float32)
    for t in peers_z:
        own_a = own_a + r1a[t, a].astype(jnp.float32)
    own_b = xb[a, b].astype(jnp.float32)
    for t in peers_x:
        own_b = own_b + r1b[t, b].astype(jnp.float32)
    for t in peers_x:
        own_a = own_a + r2a[t].astype(jnp.float32)
    for t in peers_z:
        own_b = own_b + r2b[t].astype(jnp.float32)
    out[0] = own_a
    out[1] = own_b
    for c in first + second:
        c.wait_send()


def latent_reduce(xa, xb, collective_id):
    n, _, h, c = xa.shape
    dt = xa.dtype
    return pl.pallas_call(
        _reduce_kernel,
        out_shape=jax.ShapeDtypeStruct((2, h, c), jnp.float32),
        in_specs=[pl.BlockSpec(memory_space=pltpu.VMEM)] * 2,
        out_specs=pl.BlockSpec(memory_space=pltpu.VMEM),
        scratch_shapes=[
            pltpu.VMEM((n, n, h, c), dt),
            pltpu.VMEM((n, n, h, c), dt),
            pltpu.VMEM((n, h, c), dt),
            pltpu.VMEM((n, h, c), dt),
            pltpu.VMEM((n, h, c), dt),
            pltpu.VMEM((n, h, c), dt),
            pltpu.SemaphoreType.DMA((4, n)),
            pltpu.SemaphoreType.DMA((4, n)),
        ],
        compiler_params=pltpu.CompilerParams(collective_id=collective_id, has_side_effects=True),
    )(xa, xb)


def _gather_kernel(e, oa, ob, g1a, g1b, ga, gb, send_sems, recv_sems):
    a, b = _latent_coords()
    _greet(a, b)
    peers_z = [(b + k) % RING for k in range(1, RING)]
    peers_x = [(a + k) % RING for k in range(1, RING)]
    first = []
    for t in peers_z:
        c = _copy(e.at[0], g1a.at[b], send_sems.at[0, t], recv_sems.at[0, b], a * RING + t)
        c.start()
        first.append(c)
    for t in peers_x:
        c = _copy(e.at[1], g1b.at[a], send_sems.at[1, t], recv_sems.at[1, a], t * RING + b)
        c.start()
        first.append(c)
    g1a[b] = e[0]
    g1b[a] = e[1]
    for t in peers_z:
        _copy(e.at[0], g1a.at[t], send_sems.at[0, t], recv_sems.at[0, t], 0).wait_recv()
    for t in peers_x:
        _copy(e.at[1], g1b.at[t], send_sems.at[1, t], recv_sems.at[1, t], 0).wait_recv()
    second = []
    for t in peers_x:
        c = _copy(g1a, ga.at[a], send_sems.at[2, t], recv_sems.at[2, a], t * RING + b)
        c.start()
        second.append(c)
    for t in peers_z:
        c = _copy(g1b, gb.at[b], send_sems.at[3, t], recv_sems.at[3, b], a * RING + t)
        c.start()
        second.append(c)
    oa[a] = g1a[...]
    for j in range(RING):
        ob[j, b] = g1b[j]
    for t in peers_x:
        _copy(g1a, ga.at[t], send_sems.at[2, t], recv_sems.at[2, t], 0).wait_recv()
        oa[t] = ga[t]
    for t in peers_z:
        _copy(g1b, gb.at[t], send_sems.at[3, t], recv_sems.at[3, t], 0).wait_recv()
        for j in range(RING):
            ob[j, t] = gb[t, j]
    for c in first + second:
        c.wait_send()


def latent_gather(e, collective_id):
    _, h, c = e.shape
    n = RING
    dt = e.dtype
    full = jax.ShapeDtypeStruct((n, n, h, c), dt)
    return pl.pallas_call(
        _gather_kernel,
        out_shape=(full, full),
        in_specs=[pl.BlockSpec(memory_space=pltpu.VMEM)],
        out_specs=(pl.BlockSpec(memory_space=pltpu.VMEM), pl.BlockSpec(memory_space=pltpu.VMEM)),
        scratch_shapes=[
            pltpu.VMEM((n, h, c), dt),
            pltpu.VMEM((n, h, c), dt),
            pltpu.VMEM((n, n, h, c), dt),
            pltpu.VMEM((n, n, h, c), dt),
            pltpu.SemaphoreType.DMA((4, n)),
            pltpu.SemaphoreType.DMA((4, n)),
        ],
        compiler_params=pltpu.CompilerParams(collective_id=collective_id, has_side_effects=True),
    )(e)


def _layer_roles():
    me = lax.axis_index("layer")
    mate = me + 1 - 2 * (me % 2)
    far = (me + 2) % LAYERS
    return me, mate, far, (mate + 2) % LAYERS


def _layer_exchange(quarter, x, out, finish, ra, sb, rb, rc, rd, send_sems, recv_sems):
    me, mate, far, mate_far = _layer_roles()
    barrier = pltpu.get_barrier_semaphore()
    for p in (mate, far):
        pl.semaphore_signal(barrier, inc=1, device_id={"layer": p}, device_id_type=MESH)
    pl.semaphore_wait(barrier, 2)

    def copy(src, dst, k, p):
        return pltpu.make_async_remote_copy(
            src_ref=src, dst_ref=dst, send_sem=send_sems.at[k], recv_sem=recv_sems.at[k],
            device_id={"layer": p}, device_id_type=MESH,
        )

    sent = [copy(quarter(x, mate), ra.at[0], 0, mate), copy(quarter(x, mate_far), ra.at[1], 1, mate)]
    for c in sent:
        c.start()
    sent[0].wait_recv()
    sent[1].wait_recv()
    sb[...] = quarter(x, far)[...].astype(jnp.float32) + ra[1].astype(jnp.float32)
    step_b = copy(sb, rb, 2, far)
    step_b.start()
    own = quarter(x, me)[...].astype(jnp.float32) + ra[0].astype(jnp.float32)
    step_b.wait_recv()
    quarter(out, me)[...] = finish(own + rb[...])
    step_c = copy(quarter(out, me), rc, 3, far)
    step_c.start()
    step_c.wait_recv()
    quarter(out, far)[...] = rc[...]
    step_d = [copy(quarter(out, me), rd.at[0], 4, mate), copy(rc, rd.at[1], 5, mate)]
    for c in step_d:
        c.start()
    for c in step_d:
        c.wait_recv()
    quarter(out, mate)[...] = rd[0]
    quarter(out, mate_far)[...] = rd[1]
    for c in sent + [step_b, step_c] + step_d:
        c.wait_send()


def _row_quarter(ref, i):
    q = ref.shape[0] // LAYERS
    return ref.at[pl.ds(pl.multiple_of(i * q, q), q)]


def _lane_quarter(ref, i):
    q = ref.shape[1] // LAYERS
    return ref.at[:, pl.ds(pl.multiple_of(i * q, q), q)]


def _layer_pre_kernel(x, bias, feats, pre_q, *scratch):
    def finish(total):
        pre = total + bias[...]
        pre_q[...] = pre
        return jnp.maximum(pre, 0.0).astype(feats.dtype)

    _layer_exchange(_row_quarter, x, feats, finish, *scratch)


def _layer_scratch(in_q, out_q, in_dtype):
    return [
        pltpu.VMEM((2,) + in_q, in_dtype),
        pltpu.VMEM(in_q, jnp.float32),
        pltpu.VMEM(in_q, jnp.float32),
        pltpu.VMEM(out_q, jnp.bfloat16),
        pltpu.VMEM((2,) + out_q, jnp.bfloat16),
        pltpu.SemaphoreType.DMA((6,)),
        pltpu.SemaphoreType.DMA((6,)),
    ]


def layer_pre(x, bias):
    rows, cols = x.shape
    q = rows // LAYERS
    return pl.pallas_call(
        _layer_pre_kernel,
        out_shape=(jax.ShapeDtypeStruct((rows, cols), jnp.bfloat16),
                   jax.ShapeDtypeStruct((q, cols), jnp.float32)),
        in_specs=[pl.BlockSpec(memory_space=pltpu.VMEM)] * 2,
        out_specs=(pl.BlockSpec(memory_space=pltpu.VMEM), pl.BlockSpec(memory_space=pltpu.VMEM)),
        scratch_shapes=_layer_scratch((q, cols), (q, cols), x.dtype),
        compiler_params=pltpu.CompilerParams(collective_id=1, has_side_effects=True),
    )(x, bias)


def _layer_peers():
    me = lax.axis_index("layer")
    return me, [(me + k) % LAYERS for k in range(1, LAYERS)]


def _layer_greet(peers):
    barrier = pltpu.get_barrier_semaphore()
    for p in peers:
        pl.semaphore_signal(barrier, inc=1, device_id={"layer": p}, device_id_type=MESH)
    pl.semaphore_wait(barrier, LAYERS - 1)


def _layer_copy(src, dst, send_sems, recv_sems, k, p, slot):
    return pltpu.make_async_remote_copy(
        src_ref=src, dst_ref=dst, send_sem=send_sems.at[k, p], recv_sem=recv_sems.at[k, slot],
        device_id={"layer": p}, device_id_type=MESH,
    )


def _layer_grad_kernel(g, pre_q, margin_q, out, r1, r2, send_sems, recv_sems):
    me, peers = _layer_peers()
    q = g.shape[1] // LAYERS
    lanes = lambda i: pl.ds(pl.multiple_of(i * q, q), q)
    _layer_greet(peers)
    sent = []
    for p in peers:
        c = _layer_copy(g.at[:, lanes(p)], r1.at[me], send_sems, recv_sems, 0, p, me)
        c.start()
        sent.append(c)
    total = g[:, lanes(me)].astype(jnp.float32)
    for p in peers:
        _layer_copy(g.at[:, lanes(p)], r1.at[p], send_sems, recv_sems, 0, p, p).wait_recv()
        total = total + r1[p].astype(jnp.float32)
    grad = jnp.where(pre_q[...] > 0, total - MARGIN * margin_q[...], 0.0)
    out[:, lanes(me)] = grad.astype(out.dtype)
    for p in peers:
        c = _layer_copy(out.at[:, lanes(me)], r2.at[me], send_sems, recv_sems, 1, p, me)
        c.start()
        sent.append(c)
    for p in peers:
        _layer_copy(out.at[:, lanes(p)], r2.at[p], send_sems, recv_sems, 1, p, p).wait_recv()
        out[:, lanes(p)] = r2[p]
    for c in sent:
        c.wait_send()


def layer_grad(g, pre_q, margin_q):
    cols, rows = g.shape
    q = rows // LAYERS
    return pl.pallas_call(
        _layer_grad_kernel,
        out_shape=jax.ShapeDtypeStruct((cols, rows), jnp.bfloat16),
        in_specs=[pl.BlockSpec(memory_space=pltpu.VMEM)] * 3,
        out_specs=pl.BlockSpec(memory_space=pltpu.VMEM),
        scratch_shapes=[
            pltpu.VMEM((LAYERS, cols, q), jnp.bfloat16),
            pltpu.VMEM((LAYERS, cols, q), jnp.bfloat16),
            pltpu.SemaphoreType.DMA((2, LAYERS)),
            pltpu.SemaphoreType.DMA((2, LAYERS)),
        ],
        compiler_params=pltpu.CompilerParams(collective_id=2, has_side_effects=True),
    )(g, pre_q, margin_q)


def local(inputs, clean_acts, enc_weight, enc_bias, dec_weight, dec_bias, pairing, targets):
    row_count = inputs.shape[0]
    lat_count = enc_weight.shape[2]
    all_rows = pairing.shape[0]
    d_model = inputs.shape[2]
    chunk = d_model // (RING * RING)
    half = row_count // 2
    me = lax.axis_index("latent")
    partial_pre = jnp.einsum("rld,ldf->rf", inputs, enc_weight, preferred_element_type=jnp.float32)
    features, pre_q = layer_pre(partial_pre, enc_bias[None, :])
    dec4 = dec_weight[0].reshape(lat_count, RING, RING, chunk)
    recon_a = jnp.einsum("rf,fabd->abdr", features[:half], dec4, preferred_element_type=jnp.float32)
    recon_b = jnp.einsum("rf,fabd->abdr", features[half:], dec4, preferred_element_type=jnp.float32)
    recon_sum = latent_reduce(recon_a.astype(jnp.bfloat16), recon_b.astype(jnp.bfloat16), 3)
    bias_part = lax.dynamic_slice_in_dim(dec_bias[0], me * chunk, chunk)
    clean_part = lax.dynamic_slice_in_dim(clean_acts[:, 0, :], me * chunk, chunk, axis=1)
    clean_t = jnp.swapaxes(clean_part.reshape(2, half, chunk), 1, 2).astype(jnp.float32)
    recon_error = (recon_sum + bias_part[:, None] - clean_t).astype(jnp.bfloat16)
    error_a, error_b = latent_gather(recon_error, 4)
    error_all = jnp.concatenate(
        [error_a.reshape(d_model, half), error_b.reshape(d_model, half)], axis=1
    )
    partial_grad_t = jnp.dot(dec_weight[0], error_all, preferred_element_type=jnp.float32)
    quarter = row_count // LAYERS
    row_ids = (
        lax.axis_index("row") * row_count
        + lax.axis_index("layer") * quarter
        + jnp.arange(quarter, dtype=jnp.int32)
    )
    latent_ids = me * lat_count + jnp.arange(lat_count, dtype=jnp.int32)
    every_row = jnp.arange(all_rows, dtype=jnp.int32)
    pair_table_t = (
        (every_row[:, None] == row_ids[None, :]).astype(jnp.float32)
        - (pairing[:, None] == row_ids[None, :]).astype(jnp.float32)
    ).astype(jnp.bfloat16)
    target_hot_t = (latent_ids[:, None] == targets[None, :]).astype(jnp.bfloat16)
    margin_q = jnp.dot(target_hot_t, pair_table_t, preferred_element_type=jnp.float32)
    pre_grad_t = layer_grad(partial_grad_t.astype(jnp.bfloat16), pre_q.T, margin_q)
    enc4 = enc_weight[0].reshape(RING, RING, chunk, lat_count)
    input_a = jnp.einsum("abdf,fr->abdr", enc4, pre_grad_t[:, :half], preferred_element_type=jnp.float32)
    input_b = jnp.einsum("abdf,fr->abdr", enc4, pre_grad_t[:, half:], preferred_element_type=jnp.float32)
    total = latent_reduce(input_a.astype(jnp.bfloat16), input_b.astype(jnp.bfloat16), 5)
    return jnp.swapaxes(total.astype(jnp.bfloat16), 1, 2).reshape(row_count, 1, chunk)


def solution(mesh):
    placed = (
        P("row", "layer", None),
        P("row", "layer", None),
        P("layer", None, "latent"),
        P("latent"),
        P("layer", "latent", None),
        P("layer", None),
        P(),
        P(),
    )
    return jax.shard_map(
        local, mesh=mesh, in_specs=placed, out_specs=P("row", "layer", "latent"), check_vma=False
    )
```

```python
import jax
import jax.numpy as jnp
from jax import lax
from jax.experimental import pallas as pl
from jax.experimental.pallas import tpu as pltpu
from jax.sharding import PartitionSpec as P

MARGIN = 16.0
MESH = pl.DeviceIdType.MESH
RING = 4
LAYERS = 4


def _latent_coords():
    me = lax.axis_index("latent")
    return me // RING, me % RING


def _greet(a, b):
    barrier = pltpu.get_barrier_semaphore()
    for k in range(1, RING):
        pl.semaphore_signal(barrier, inc=1, device_id={"latent": a * RING + (b + k) % RING}, device_id_type=MESH)
        pl.semaphore_signal(barrier, inc=1, device_id={"latent": ((a + k) % RING) * RING + b}, device_id_type=MESH)
    pl.semaphore_wait(barrier, 2 * (RING - 1))


def _copy(src, dst, send_sem, recv_sem, peer):
    return pltpu.make_async_remote_copy(
        src_ref=src, dst_ref=dst, send_sem=send_sem, recv_sem=recv_sem,
        device_id={"latent": peer}, device_id_type=MESH,
    )


def _reduce_kernel(xa, xb, out, r1a, r1b, s1a, s1b, r2a, r2b, send_sems, recv_sems):
    a, b = _latent_coords()
    _greet(a, b)
    peers_z = [(b + k) % RING for k in range(1, RING)]
    peers_x = [(a + k) % RING for k in range(1, RING)]
    first = []
    for t in peers_z:
        c = _copy(xa.at[:, t], r1a.at[b], send_sems.at[0, t], recv_sems.at[0, b], a * RING + t)
        c.start()
        first.append(c)
    for t in peers_x:
        c = _copy(xb.at[t], r1b.at[a], send_sems.at[1, t], recv_sems.at[1, a], t * RING + b)
        c.start()
        first.append(c)
    for t in peers_z:
        _copy(xa.at[:, t], r1a.at[t], send_sems.at[0, t], recv_sems.at[0, t], 0).wait_recv()
    for t in peers_x:
        _copy(xb.at[t], r1b.at[t], send_sems.at[1, t], recv_sems.at[1, t], 0).wait_recv()
    sum_a = xa[:, b].astype(jnp.float32)
    for t in peers_z:
        sum_a = sum_a + r1a[t].astype(jnp.float32)
    sum_b = xb[a].astype(jnp.float32)
    for t in peers_x:
        sum_b = sum_b + r1b[t].astype(jnp.float32)
    s1a[...] = sum_a.astype(s1a.dtype)
    s1b[...] = sum_b.astype(s1b.dtype)
    second = []
    for t in peers_x:
        c = _copy(s1a.at[t], r2a.at[a], send_sems.at[2, t], recv_sems.at[2, a], t * RING + b)
        c.start()
        second.append(c)
    for t in peers_z:
        c = _copy(s1b.at[t], r2b.at[b], send_sems.at[3, t], recv_sems.at[3, b], a * RING + t)
        c.start()
        second.append(c)
    for t in peers_x:
        _copy(s1a.at[t], r2a.at[t], send_sems.at[2, t], recv_sems.at[2, t], 0).wait_recv()
    for t in peers_z:
        _copy(s1b.at[t], r2b.at[t], send_sems.at[3, t], recv_sems.at[3, t], 0).wait_recv()
    own_a = xa[a, b].astype(jnp.float32)
    for t in peers_z:
        own_a = own_a + r1a[t, a].astype(jnp.float32)
    own_b = xb[a, b].astype(jnp.float32)
    for t in peers_x:
        own_b = own_b + r1b[t, b].astype(jnp.float32)
    for t in peers_x:
        own_a = own_a + r2a[t].astype(jnp.float32)
    for t in peers_z:
        own_b = own_b + r2b[t].astype(jnp.float32)
    out[0] = own_a
    out[1] = own_b
    for c in first + second:
        c.wait_send()


def latent_reduce(xa, xb, collective_id):
    n, _, h, c = xa.shape
    dt = xa.dtype
    return pl.pallas_call(
        _reduce_kernel,
        out_shape=jax.ShapeDtypeStruct((2, h, c), jnp.float32),
        in_specs=[pl.BlockSpec(memory_space=pltpu.VMEM)] * 2,
        out_specs=pl.BlockSpec(memory_space=pltpu.VMEM),
        scratch_shapes=[
            pltpu.VMEM((n, n, h, c), dt),
            pltpu.VMEM((n, n, h, c), dt),
            pltpu.VMEM((n, h, c), dt),
            pltpu.VMEM((n, h, c), dt),
            pltpu.VMEM((n, h, c), dt),
            pltpu.VMEM((n, h, c), dt),
            pltpu.SemaphoreType.DMA((4, n)),
            pltpu.SemaphoreType.DMA((4, n)),
        ],
        compiler_params=pltpu.CompilerParams(collective_id=collective_id, has_side_effects=True),
    )(xa, xb)


def _reduce_mm_kernel(w, v, out, xa, xb, r1a, r1b, s1a, s1b, r2a, r2b, send_sems, recv_sems):
    a, b = _latent_coords()
    _greet(a, b)
    h = v.shape[1] // 2
    peers_z = [(b + k) % RING for k in range(1, RING)]
    peers_x = [(a + k) % RING for k in range(1, RING)]

    def fill(dst, i, j, half):
        prod = jnp.dot(w[i, j], v[:, half * h:(half + 1) * h], preferred_element_type=jnp.float32)
        dst[i, j] = prod.astype(dst.dtype)

    first = []
    for kz, kx in zip(peers_z, peers_x):
        for i in range(RING):
            fill(xa, i, kz, 0)
        c = _copy(xa.at[:, kz], r1a.at[b], send_sems.at[0, kz], recv_sems.at[0, b], a * RING + kz)
        c.start()
        first.append(c)
        for j in range(RING):
            fill(xb, kx, j, 1)
        c = _copy(xb.at[kx], r1b.at[a], send_sems.at[1, kx], recv_sems.at[1, a], kx * RING + b)
        c.start()
        first.append(c)
    for i in range(RING):
        fill(xa, i, b, 0)
    for j in range(RING):
        fill(xb, a, j, 1)
    for t in peers_z:
        _copy(xa.at[:, t], r1a.at[t], send_sems.at[0, t], recv_sems.at[0, t], 0).wait_recv()
    for t in peers_x:
        _copy(xb.at[t], r1b.at[t], send_sems.at[1, t], recv_sems.at[1, t], 0).wait_recv()
    sum_a = xa[:, b].astype(jnp.float32)
    for t in peers_z:
        sum_a = sum_a + r1a[t].astype(jnp.float32)
    sum_b = xb[a].astype(jnp.float32)
    for t in peers_x:
        sum_b = sum_b + r1b[t].astype(jnp.float32)
    s1a[...] = sum_a.astype(s1a.dtype)
    s1b[...] = sum_b.astype(s1b.dtype)
    second = []
    for t in peers_x:
        c = _copy(s1a.at[t], r2a.at[a], send_sems.at[2, t], recv_sems.at[2, a], t * RING + b)
        c.start()
        second.append(c)
    for t in peers_z:
        c = _copy(s1b.at[t], r2b.at[b], send_sems.at[3, t], recv_sems.at[3, b], a * RING + t)
        c.start()
        second.append(c)
    for t in peers_x:
        _copy(s1a.at[t], r2a.at[t], send_sems.at[2, t], recv_sems.at[2, t], 0).wait_recv()
    for t in peers_z:
        _copy(s1b.at[t], r2b.at[t], send_sems.at[3, t], recv_sems.at[3, t], 0).wait_recv()
    own_a = xa[a, b].astype(jnp.float32)
    own_b = xb[a, b].astype(jnp.float32)
    for k in range(1, RING):
        own_a = own_a + r1a[(b + k) % RING, a].astype(jnp.float32)
        own_b = own_b + r1b[(a + k) % RING, b].astype(jnp.float32)
    for k in range(1, RING):
        own_a = own_a + r2a[(a + k) % RING].astype(jnp.float32)
        own_b = own_b + r2b[(b + k) % RING].astype(jnp.float32)
    out[0] = own_a
    out[1] = own_b
    for c in first + second:
        c.wait_send()


def latent_reduce_mm(w, v, collective_id):
    n, _, d, _ = w.shape
    h = v.shape[1] // 2
    dt = w.dtype
    return pl.pallas_call(
        _reduce_mm_kernel,
        out_shape=jax.ShapeDtypeStruct((2, d, h), jnp.float32),
        in_specs=[pl.BlockSpec(memory_space=pltpu.VMEM)] * 2,
        out_specs=pl.BlockSpec(memory_space=pltpu.VMEM),
        scratch_shapes=[
            pltpu.VMEM((n, n, d, h), dt),
            pltpu.VMEM((n, n, d, h), dt),
            pltpu.VMEM((n, n, d, h), dt),
            pltpu.VMEM((n, n, d, h), dt),
            pltpu.VMEM((n, d, h), dt),
            pltpu.VMEM((n, d, h), dt),
            pltpu.VMEM((n, d, h), dt),
            pltpu.VMEM((n, d, h), dt),
            pltpu.SemaphoreType.DMA((4, n)),
            pltpu.SemaphoreType.DMA((4, n)),
        ],
        compiler_params=pltpu.CompilerParams(collective_id=collective_id, has_side_effects=True),
    )(w, v)


def _gather_kernel(e, oa, ob, g1a, g1b, ga, gb, send_sems, recv_sems):
    a, b = _latent_coords()
    _greet(a, b)
    peers_z = [(b + k) % RING for k in range(1, RING)]
    peers_x = [(a + k) % RING for k in range(1, RING)]
    first = []
    for t in peers_z:
        c = _copy(e.at[0], g1a.at[b], send_sems.at[0, t], recv_sems.at[0, b], a * RING + t)
        c.start()
        first.append(c)
    for t in peers_x:
        c = _copy(e.at[1], g1b.at[a], send_sems.at[1, t], recv_sems.at[1, a], t * RING + b)
        c.start()
        first.append(c)
    g1a[b] = e[0]
    g1b[a] = e[1]
    for t in peers_z:
        _copy(e.at[0], g1a.at[t], send_sems.at[0, t], recv_sems.at[0, t], 0).wait_recv()
    for t in peers_x:
        _copy(e.at[1], g1b.at[t], send_sems.at[1, t], recv_sems.at[1, t], 0).wait_recv()
    second = []
    for t in peers_x:
        c = _copy(g1a, ga.at[a], send_sems.at[2, t], recv_sems.at[2, a], t * RING + b)
        c.start()
        second.append(c)
    for t in peers_z:
        c = _copy(g1b, gb.at[b], send_sems.at[3, t], recv_sems.at[3, b], a * RING + t)
        c.start()
        second.append(c)
    oa[a] = g1a[...]
    for j in range(RING):
        ob[j, b] = g1b[j]
    for t in peers_x:
        _copy(g1a, ga.at[t], send_sems.at[2, t], recv_sems.at[2, t], 0).wait_recv()
        oa[t] = ga[t]
    for t in peers_z:
        _copy(g1b, gb.at[t], send_sems.at[3, t], recv_sems.at[3, t], 0).wait_recv()
        for j in range(RING):
            ob[j, t] = gb[t, j]
    for c in first + second:
        c.wait_send()


def latent_gather(e, collective_id):
    _, h, c = e.shape
    n = RING
    dt = e.dtype
    full = jax.ShapeDtypeStruct((n, n, h, c), dt)
    return pl.pallas_call(
        _gather_kernel,
        out_shape=(full, full),
        in_specs=[pl.BlockSpec(memory_space=pltpu.VMEM)],
        out_specs=(pl.BlockSpec(memory_space=pltpu.VMEM), pl.BlockSpec(memory_space=pltpu.VMEM)),
        scratch_shapes=[
            pltpu.VMEM((n, h, c), dt),
            pltpu.VMEM((n, h, c), dt),
            pltpu.VMEM((n, n, h, c), dt),
            pltpu.VMEM((n, n, h, c), dt),
            pltpu.SemaphoreType.DMA((4, n)),
            pltpu.SemaphoreType.DMA((4, n)),
        ],
        compiler_params=pltpu.CompilerParams(collective_id=collective_id, has_side_effects=True),
    )(e)


def _layer_roles():
    me = lax.axis_index("layer")
    mate = me + 1 - 2 * (me % 2)
    far = (me + 2) % LAYERS
    return me, mate, far, (mate + 2) % LAYERS


def _layer_exchange(quarter, x, out, finish, ra, sb, rb, rc, rd, send_sems, recv_sems):
    me, mate, far, mate_far = _layer_roles()
    barrier = pltpu.get_barrier_semaphore()
    for p in (mate, far):
        pl.semaphore_signal(barrier, inc=1, device_id={"layer": p}, device_id_type=MESH)
    pl.semaphore_wait(barrier, 2)

    def copy(src, dst, k, p):
        return pltpu.make_async_remote_copy(
            src_ref=src, dst_ref=dst, send_sem=send_sems.at[k], recv_sem=recv_sems.at[k],
            device_id={"layer": p}, device_id_type=MESH,
        )

    sent = [copy(quarter(x, mate), ra.at[0], 0, mate), copy(quarter(x, mate_far), ra.at[1], 1, mate)]
    for c in sent:
        c.start()
    sent[0].wait_recv()
    sent[1].wait_recv()
    sb[...] = quarter(x, far)[...].astype(jnp.float32) + ra[1].astype(jnp.float32)
    step_b = copy(sb, rb, 2, far)
    step_b.start()
    own = quarter(x, me)[...].astype(jnp.float32) + ra[0].astype(jnp.float32)
    step_b.wait_recv()
    quarter(out, me)[...] = finish(own + rb[...])
    step_c = copy(quarter(out, me), rc, 3, far)
    step_c.start()
    step_c.wait_recv()
    quarter(out, far)[...] = rc[...]
    step_d = [copy(quarter(out, me), rd.at[0], 4, mate), copy(rc, rd.at[1], 5, mate)]
    for c in step_d:
        c.start()
    for c in step_d:
        c.wait_recv()
    quarter(out, mate)[...] = rd[0]
    quarter(out, mate_far)[...] = rd[1]
    for c in sent + [step_b, step_c] + step_d:
        c.wait_send()


def _row_quarter(ref, i):
    q = ref.shape[0] // LAYERS
    return ref.at[pl.ds(pl.multiple_of(i * q, q), q)]


def _lane_quarter(ref, i):
    q = ref.shape[1] // LAYERS
    return ref.at[:, pl.ds(pl.multiple_of(i * q, q), q)]


def _layer_pre_kernel(x, bias, feats, pre_q, *scratch):
    def finish(total):
        pre = total + bias[...]
        pre_q[...] = pre
        return jnp.maximum(pre, 0.0).astype(feats.dtype)

    _layer_exchange(_row_quarter, x, feats, finish, *scratch)


def _layer_scratch(in_q, out_q, in_dtype):
    return [
        pltpu.VMEM((2,) + in_q, in_dtype),
        pltpu.VMEM(in_q, jnp.float32),
        pltpu.VMEM(in_q, jnp.float32),
        pltpu.VMEM(out_q, jnp.bfloat16),
        pltpu.VMEM((2,) + out_q, jnp.bfloat16),
        pltpu.SemaphoreType.DMA((6,)),
        pltpu.SemaphoreType.DMA((6,)),
    ]


def layer_pre(x, bias):
    rows, cols = x.shape
    q = rows // LAYERS
    return pl.pallas_call(
        _layer_pre_kernel,
        out_shape=(jax.ShapeDtypeStruct((rows, cols), jnp.bfloat16),
                   jax.ShapeDtypeStruct((q, cols), jnp.float32)),
        in_specs=[pl.BlockSpec(memory_space=pltpu.VMEM)] * 2,
        out_specs=(pl.BlockSpec(memory_space=pltpu.VMEM), pl.BlockSpec(memory_space=pltpu.VMEM)),
        scratch_shapes=_layer_scratch((q, cols), (q, cols), x.dtype),
        compiler_params=pltpu.CompilerParams(collective_id=1, has_side_effects=True),
    )(x, bias)


def _layer_peers():
    me = lax.axis_index("layer")
    return me, [(me + k) % LAYERS for k in range(1, LAYERS)]


def _layer_greet(peers):
    barrier = pltpu.get_barrier_semaphore()
    for p in peers:
        pl.semaphore_signal(barrier, inc=1, device_id={"layer": p}, device_id_type=MESH)
    pl.semaphore_wait(barrier, LAYERS - 1)


def _layer_copy(src, dst, send_sems, recv_sems, k, p, slot):
    return pltpu.make_async_remote_copy(
        src_ref=src, dst_ref=dst, send_sem=send_sems.at[k, p], recv_sem=recv_sems.at[k, slot],
        device_id={"layer": p}, device_id_type=MESH,
    )


def _layer_grad_kernel(g, pre_q, margin_q, out, r1, r2, send_sems, recv_sems):
    me, peers = _layer_peers()
    q = g.shape[1] // LAYERS
    lanes = lambda i: pl.ds(pl.multiple_of(i * q, q), q)
    _layer_greet(peers)
    sent = []
    for p in peers:
        c = _layer_copy(g.at[:, lanes(p)], r1.at[me], send_sems, recv_sems, 0, p, me)
        c.start()
        sent.append(c)
    total = g[:, lanes(me)].astype(jnp.float32)
    for p in peers:
        _layer_copy(g.at[:, lanes(p)], r1.at[p], send_sems, recv_sems, 0, p, p).wait_recv()
        total = total + r1[p].astype(jnp.float32)
    grad = jnp.where(pre_q[...] > 0, total - MARGIN * margin_q[...], 0.0)
    out[:, lanes(me)] = grad.astype(out.dtype)
    for p in peers:
        c = _layer_copy(out.at[:, lanes(me)], r2.at[me], send_sems, recv_sems, 1, p, me)
        c.start()
        sent.append(c)
    for p in peers:
        _layer_copy(out.at[:, lanes(p)], r2.at[p], send_sems, recv_sems, 1, p, p).wait_recv()
        out[:, lanes(p)] = r2[p]
    for c in sent:
        c.wait_send()


def layer_grad(g, pre_q, margin_q):
    cols, rows = g.shape
    q = rows // LAYERS
    return pl.pallas_call(
        _layer_grad_kernel,
        out_shape=jax.ShapeDtypeStruct((cols, rows), jnp.bfloat16),
        in_specs=[pl.BlockSpec(memory_space=pltpu.VMEM)] * 3,
        out_specs=pl.BlockSpec(memory_space=pltpu.VMEM),
        scratch_shapes=[
            pltpu.VMEM((LAYERS, cols, q), jnp.bfloat16),
            pltpu.VMEM((LAYERS, cols, q), jnp.bfloat16),
            pltpu.SemaphoreType.DMA((2, LAYERS)),
            pltpu.SemaphoreType.DMA((2, LAYERS)),
        ],
        compiler_params=pltpu.CompilerParams(collective_id=2, has_side_effects=True),
    )(g, pre_q, margin_q)


def local(inputs, clean_acts, enc_weight, enc_bias, dec_weight, dec_bias, pairing, targets):
    row_count = inputs.shape[0]
    lat_count = enc_weight.shape[2]
    all_rows = pairing.shape[0]
    d_model = inputs.shape[2]
    chunk = d_model // (RING * RING)
    half = row_count // 2
    me = lax.axis_index("latent")
    partial_pre = jnp.einsum("rld,ldf->rf", inputs, enc_weight, preferred_element_type=jnp.float32)
    features, pre_q = layer_pre(partial_pre, enc_bias[None, :])
    dec4 = dec_weight[0].reshape(lat_count, RING, RING, chunk)
    recon_a = jnp.einsum("rf,fabd->abdr", features[:half], dec4, preferred_element_type=jnp.float32)
    recon_b = jnp.einsum("rf,fabd->abdr", features[half:], dec4, preferred_element_type=jnp.float32)
    recon_sum = latent_reduce(recon_a.astype(jnp.bfloat16), recon_b.astype(jnp.bfloat16), 3)
    bias_part = lax.dynamic_slice_in_dim(dec_bias[0], me * chunk, chunk)
    clean_part = lax.dynamic_slice_in_dim(clean_acts[:, 0, :], me * chunk, chunk, axis=1)
    clean_t = jnp.swapaxes(clean_part.reshape(2, half, chunk), 1, 2).astype(jnp.float32)
    recon_error = (recon_sum + bias_part[:, None] - clean_t).astype(jnp.bfloat16)
    error_a, error_b = latent_gather(recon_error, 4)
    error_all = jnp.concatenate(
        [error_a.reshape(d_model, half), error_b.reshape(d_model, half)], axis=1
    )
    partial_grad_t = jnp.dot(dec_weight[0], error_all, preferred_element_type=jnp.float32)
    quarter = row_count // LAYERS
    row_ids = (
        lax.axis_index("row") * row_count
        + lax.axis_index("layer") * quarter
        + jnp.arange(quarter, dtype=jnp.int32)
    )
    latent_ids = me * lat_count + jnp.arange(lat_count, dtype=jnp.int32)
    every_row = jnp.arange(all_rows, dtype=jnp.int32)
    pair_table_t = (
        (every_row[:, None] == row_ids[None, :]).astype(jnp.float32)
        - (pairing[:, None] == row_ids[None, :]).astype(jnp.float32)
    ).astype(jnp.bfloat16)
    target_hot_t = (latent_ids[:, None] == targets[None, :]).astype(jnp.bfloat16)
    margin_q = jnp.dot(target_hot_t, pair_table_t, preferred_element_type=jnp.float32)
    pre_grad_t = layer_grad(partial_grad_t.astype(jnp.bfloat16), pre_q.T, margin_q)
    enc4 = enc_weight[0].reshape(RING, RING, chunk, lat_count)
    total = latent_reduce_mm(enc4, pre_grad_t, 5)
    return jnp.swapaxes(total.astype(jnp.bfloat16), 1, 2).reshape(row_count, 1, chunk)


def solution(mesh):
    placed = (
        P("row", "layer", None),
        P("row", "layer", None),
        P("layer", None, "latent"),
        P("latent"),
        P("layer", "latent", None),
        P("layer", None),
        P(),
        P(),
    )
    return jax.shard_map(
        local, mesh=mesh, in_specs=placed, out_specs=P("row", "layer", "latent"), check_vma=False
    )
```

```python
import jax
import jax.numpy as jnp
from jax import lax
from jax.experimental import pallas as pl
from jax.experimental.pallas import tpu as pltpu
from jax.sharding import PartitionSpec as P

MARGIN = 16.0
MESH = pl.DeviceIdType.MESH
RING = 4
LAYERS = 4


def _latent_coords():
    me = lax.axis_index("latent")
    return me // RING, me % RING


def _greet(a, b):
    barrier = pltpu.get_barrier_semaphore()
    for k in range(1, RING):
        pl.semaphore_signal(barrier, inc=1, device_id={"latent": a * RING + (b + k) % RING}, device_id_type=MESH)
        pl.semaphore_signal(barrier, inc=1, device_id={"latent": ((a + k) % RING) * RING + b}, device_id_type=MESH)
    pl.semaphore_wait(barrier, 2 * (RING - 1))


def _copy(src, dst, send_sem, recv_sem, peer):
    return pltpu.make_async_remote_copy(
        src_ref=src, dst_ref=dst, send_sem=send_sem, recv_sem=recv_sem,
        device_id={"latent": peer}, device_id_type=MESH,
    )


def _reduce_kernel(xa, xb, out, r1a, r1b, s1a, s1b, r2a, r2b, send_sems, recv_sems):
    a, b = _latent_coords()
    _greet(a, b)
    peers_z = [(b + k) % RING for k in range(1, RING)]
    peers_x = [(a + k) % RING for k in range(1, RING)]
    first = []
    for t in peers_z:
        c = _copy(xa.at[:, t], r1a.at[b], send_sems.at[0, t], recv_sems.at[0, b], a * RING + t)
        c.start()
        first.append(c)
    for t in peers_x:
        c = _copy(xb.at[t], r1b.at[a], send_sems.at[1, t], recv_sems.at[1, a], t * RING + b)
        c.start()
        first.append(c)
    for t in peers_z:
        _copy(xa.at[:, t], r1a.at[t], send_sems.at[0, t], recv_sems.at[0, t], 0).wait_recv()
    for t in peers_x:
        _copy(xb.at[t], r1b.at[t], send_sems.at[1, t], recv_sems.at[1, t], 0).wait_recv()
    sum_a = xa[:, b].astype(jnp.float32)
    for t in peers_z:
        sum_a = sum_a + r1a[t].astype(jnp.float32)
    sum_b = xb[a].astype(jnp.float32)
    for t in peers_x:
        sum_b = sum_b + r1b[t].astype(jnp.float32)
    s1a[...] = sum_a.astype(s1a.dtype)
    s1b[...] = sum_b.astype(s1b.dtype)
    second = []
    for t in peers_x:
        c = _copy(s1a.at[t], r2a.at[a], send_sems.at[2, t], recv_sems.at[2, a], t * RING + b)
        c.start()
        second.append(c)
    for t in peers_z:
        c = _copy(s1b.at[t], r2b.at[b], send_sems.at[3, t], recv_sems.at[3, b], a * RING + t)
        c.start()
        second.append(c)
    for t in peers_x:
        _copy(s1a.at[t], r2a.at[t], send_sems.at[2, t], recv_sems.at[2, t], 0).wait_recv()
    for t in peers_z:
        _copy(s1b.at[t], r2b.at[t], send_sems.at[3, t], recv_sems.at[3, t], 0).wait_recv()
    own_a = xa[a, b].astype(jnp.float32)
    for t in peers_z:
        own_a = own_a + r1a[t, a].astype(jnp.float32)
    own_b = xb[a, b].astype(jnp.float32)
    for t in peers_x:
        own_b = own_b + r1b[t, b].astype(jnp.float32)
    for t in peers_x:
        own_a = own_a + r2a[t].astype(jnp.float32)
    for t in peers_z:
        own_b = own_b + r2b[t].astype(jnp.float32)
    out[0] = own_a
    out[1] = own_b
    for c in first + second:
        c.wait_send()


def latent_reduce(xa, xb, collective_id):
    n, _, h, c = xa.shape
    dt = xa.dtype
    return pl.pallas_call(
        _reduce_kernel,
        out_shape=jax.ShapeDtypeStruct((2, h, c), jnp.float32),
        in_specs=[pl.BlockSpec(memory_space=pltpu.VMEM)] * 2,
        out_specs=pl.BlockSpec(memory_space=pltpu.VMEM),
        scratch_shapes=[
            pltpu.VMEM((n, n, h, c), dt),
            pltpu.VMEM((n, n, h, c), dt),
            pltpu.VMEM((n, h, c), dt),
            pltpu.VMEM((n, h, c), dt),
            pltpu.VMEM((n, h, c), dt),
            pltpu.VMEM((n, h, c), dt),
            pltpu.SemaphoreType.DMA((4, n)),
            pltpu.SemaphoreType.DMA((4, n)),
        ],
        compiler_params=pltpu.CompilerParams(collective_id=collective_id, has_side_effects=True),
    )(xa, xb)


def _reduce_mm_kernel(w, v, out, xa, xb, r1a, r1b, s1a, s1b, r2a, r2b, send_sems, recv_sems):
    a, b = _latent_coords()
    _greet(a, b)
    h = v.shape[1] // 2
    peers_z = [(b + k) % RING for k in range(1, RING)]
    peers_x = [(a + k) % RING for k in range(1, RING)]

    def fill(dst, i, j, half):
        prod = jnp.dot(w[i, j], v[:, half * h:(half + 1) * h], preferred_element_type=jnp.float32)
        dst[i, j] = prod.astype(dst.dtype)

    first = []
    for kz, kx in zip(peers_z, peers_x):
        for i in range(RING):
            fill(xa, i, kz, 0)
        c = _copy(xa.at[:, kz], r1a.at[b], send_sems.at[0, kz], recv_sems.at[0, b], a * RING + kz)
        c.start()
        first.append(c)
        for j in range(RING):
            fill(xb, kx, j, 1)
        c = _copy(xb.at[kx], r1b.at[a], send_sems.at[1, kx], recv_sems.at[1, a], kx * RING + b)
        c.start()
        first.append(c)
    for i in range(RING):
        fill(xa, i, b, 0)
    for j in range(RING):
        fill(xb, a, j, 1)
    for t in peers_z:
        _copy(xa.at[:, t], r1a.at[t], send_sems.at[0, t], recv_sems.at[0, t], 0).wait_recv()
    for t in peers_x:
        _copy(xb.at[t], r1b.at[t], send_sems.at[1, t], recv_sems.at[1, t], 0).wait_recv()
    sum_a = xa[:, b].astype(jnp.float32)
    for t in peers_z:
        sum_a = sum_a + r1a[t].astype(jnp.float32)
    sum_b = xb[a].astype(jnp.float32)
    for t in peers_x:
        sum_b = sum_b + r1b[t].astype(jnp.float32)
    s1a[...] = sum_a.astype(s1a.dtype)
    s1b[...] = sum_b.astype(s1b.dtype)
    second = []
    for t in peers_x:
        c = _copy(s1a.at[t], r2a.at[a], send_sems.at[2, t], recv_sems.at[2, a], t * RING + b)
        c.start()
        second.append(c)
    for t in peers_z:
        c = _copy(s1b.at[t], r2b.at[b], send_sems.at[3, t], recv_sems.at[3, b], a * RING + t)
        c.start()
        second.append(c)
    for t in peers_x:
        _copy(s1a.at[t], r2a.at[t], send_sems.at[2, t], recv_sems.at[2, t], 0).wait_recv()
    for t in peers_z:
        _copy(s1b.at[t], r2b.at[t], send_sems.at[3, t], recv_sems.at[3, t], 0).wait_recv()
    own_a = xa[a, b].astype(jnp.float32)
    own_b = xb[a, b].astype(jnp.float32)
    for k in range(1, RING):
        own_a = own_a + r1a[(b + k) % RING, a].astype(jnp.float32)
        own_b = own_b + r1b[(a + k) % RING, b].astype(jnp.float32)
    for k in range(1, RING):
        own_a = own_a + r2a[(a + k) % RING].astype(jnp.float32)
        own_b = own_b + r2b[(b + k) % RING].astype(jnp.float32)
    out[0] = own_a
    out[1] = own_b
    for c in first + second:
        c.wait_send()


def latent_reduce_mm(w, v, collective_id):
    n, _, d, _ = w.shape
    h = v.shape[1] // 2
    dt = w.dtype
    return pl.pallas_call(
        _reduce_mm_kernel,
        out_shape=jax.ShapeDtypeStruct((2, d, h), jnp.float32),
        in_specs=[pl.BlockSpec(memory_space=pltpu.VMEM)] * 2,
        out_specs=pl.BlockSpec(memory_space=pltpu.VMEM),
        scratch_shapes=[
            pltpu.VMEM((n, n, d, h), dt),
            pltpu.VMEM((n, n, d, h), dt),
            pltpu.VMEM((n, n, d, h), dt),
            pltpu.VMEM((n, n, d, h), dt),
            pltpu.VMEM((n, d, h), dt),
            pltpu.VMEM((n, d, h), dt),
            pltpu.VMEM((n, d, h), dt),
            pltpu.VMEM((n, d, h), dt),
            pltpu.SemaphoreType.DMA((4, n)),
            pltpu.SemaphoreType.DMA((4, n)),
        ],
        compiler_params=pltpu.CompilerParams(collective_id=collective_id, has_side_effects=True),
    )(w, v)


def _gather_kernel(e, oa, ob, g1a, g1b, ga, gb, send_sems, recv_sems):
    a, b = _latent_coords()
    _greet(a, b)
    peers_z = [(b + k) % RING for k in range(1, RING)]
    peers_x = [(a + k) % RING for k in range(1, RING)]
    first = []
    for t in peers_z:
        c = _copy(e.at[0], g1a.at[b], send_sems.at[0, t], recv_sems.at[0, b], a * RING + t)
        c.start()
        first.append(c)
    for t in peers_x:
        c = _copy(e.at[1], g1b.at[a], send_sems.at[1, t], recv_sems.at[1, a], t * RING + b)
        c.start()
        first.append(c)
    g1a[b] = e[0]
    g1b[a] = e[1]
    for t in peers_z:
        _copy(e.at[0], g1a.at[t], send_sems.at[0, t], recv_sems.at[0, t], 0).wait_recv()
    for t in peers_x:
        _copy(e.at[1], g1b.at[t], send_sems.at[1, t], recv_sems.at[1, t], 0).wait_recv()
    second = []
    for t in peers_x:
        c = _copy(g1a, ga.at[a], send_sems.at[2, t], recv_sems.at[2, a], t * RING + b)
        c.start()
        second.append(c)
    for t in peers_z:
        c = _copy(g1b, gb.at[b], send_sems.at[3, t], recv_sems.at[3, b], a * RING + t)
        c.start()
        second.append(c)
    oa[a] = g1a[...]
    for j in range(RING):
        ob[j, b] = g1b[j]
    for t in peers_x:
        _copy(g1a, ga.at[t], send_sems.at[2, t], recv_sems.at[2, t], 0).wait_recv()
        oa[t] = ga[t]
    for t in peers_z:
        _copy(g1b, gb.at[t], send_sems.at[3, t], recv_sems.at[3, t], 0).wait_recv()
        for j in range(RING):
            ob[j, t] = gb[t, j]
    for c in first + second:
        c.wait_send()


def latent_gather(e, collective_id):
    _, h, c = e.shape
    n = RING
    dt = e.dtype
    full = jax.ShapeDtypeStruct((n, n, h, c), dt)
    return pl.pallas_call(
        _gather_kernel,
        out_shape=(full, full),
        in_specs=[pl.BlockSpec(memory_space=pltpu.VMEM)],
        out_specs=(pl.BlockSpec(memory_space=pltpu.VMEM), pl.BlockSpec(memory_space=pltpu.VMEM)),
        scratch_shapes=[
            pltpu.VMEM((n, h, c), dt),
            pltpu.VMEM((n, h, c), dt),
            pltpu.VMEM((n, n, h, c), dt),
            pltpu.VMEM((n, n, h, c), dt),
            pltpu.SemaphoreType.DMA((4, n)),
            pltpu.SemaphoreType.DMA((4, n)),
        ],
        compiler_params=pltpu.CompilerParams(collective_id=collective_id, has_side_effects=True),
    )(e)


def _gather_mm_kernel(e, w, out, g1, gx, acc, send_sems, recv_sems):
    a, b = _latent_coords()
    _greet(a, b)
    peers_z = [(b + k) % RING for k in range(1, RING)]
    peers_x = [(a + k) % RING for k in range(1, RING)]
    halves, n, d, r = g1.shape
    group = n * d

    def add_group(block, i):
        cols = w[:, pl.ds(pl.multiple_of(i * group, 128), group)]
        for h in range(halves):
            part = jnp.dot(cols, block[h].reshape(group, r), preferred_element_type=jnp.float32)
            acc[:, h * r:(h + 1) * r] += part

    sent = []
    for t in peers_z:
        c = _copy(e, g1.at[:, b], send_sems.at[0, t], recv_sems.at[0, b], a * RING + t)
        c.start()
        sent.append(c)
    g1[:, b] = e[...]
    for t in peers_z:
        _copy(e, g1.at[:, t], send_sems.at[0, t], recv_sems.at[0, t], 0).wait_recv()
    for t in peers_x:
        c = _copy(g1, gx.at[a], send_sems.at[1, t], recv_sems.at[1, a], t * RING + b)
        c.start()
        sent.append(c)
    acc[...] = jnp.zeros_like(acc)
    add_group(g1, a)
    for t in peers_x:
        _copy(g1, gx.at[t], send_sems.at[1, t], recv_sems.at[1, t], 0).wait_recv()
        add_group(gx.at[t], t)
    out[...] = acc[...].astype(out.dtype)
    for c in sent:
        c.wait_send()


def latent_gather_mm(e, w, collective_id):
    halves, d, r = e.shape
    n = RING
    f = w.shape[0]
    dt = e.dtype
    return pl.pallas_call(
        _gather_mm_kernel,
        out_shape=jax.ShapeDtypeStruct((f, halves * r), jnp.bfloat16),
        in_specs=[pl.BlockSpec(memory_space=pltpu.VMEM)] * 2,
        out_specs=pl.BlockSpec(memory_space=pltpu.VMEM),
        scratch_shapes=[
            pltpu.VMEM((halves, n, d, r), dt),
            pltpu.VMEM((n, halves, n, d, r), dt),
            pltpu.VMEM((f, halves * r), jnp.float32),
            pltpu.SemaphoreType.DMA((2, n)),
            pltpu.SemaphoreType.DMA((2, n)),
        ],
        compiler_params=pltpu.CompilerParams(collective_id=collective_id, has_side_effects=True),
    )(e, w)


def _layer_roles():
    me = lax.axis_index("layer")
    mate = me + 1 - 2 * (me % 2)
    far = (me + 2) % LAYERS
    return me, mate, far, (mate + 2) % LAYERS


def _layer_exchange(quarter, x, out, finish, ra, sb, rb, rc, rd, send_sems, recv_sems):
    me, mate, far, mate_far = _layer_roles()
    barrier = pltpu.get_barrier_semaphore()
    for p in (mate, far):
        pl.semaphore_signal(barrier, inc=1, device_id={"layer": p}, device_id_type=MESH)
    pl.semaphore_wait(barrier, 2)

    def copy(src, dst, k, p):
        return pltpu.make_async_remote_copy(
            src_ref=src, dst_ref=dst, send_sem=send_sems.at[k], recv_sem=recv_sems.at[k],
            device_id={"layer": p}, device_id_type=MESH,
        )

    sent = [copy(quarter(x, mate), ra.at[0], 0, mate), copy(quarter(x, mate_far), ra.at[1], 1, mate)]
    for c in sent:
        c.start()
    sent[0].wait_recv()
    sent[1].wait_recv()
    sb[...] = quarter(x, far)[...].astype(jnp.float32) + ra[1].astype(jnp.float32)
    step_b = copy(sb, rb, 2, far)
    step_b.start()
    own = quarter(x, me)[...].astype(jnp.float32) + ra[0].astype(jnp.float32)
    step_b.wait_recv()
    quarter(out, me)[...] = finish(own + rb[...])
    step_c = copy(quarter(out, me), rc, 3, far)
    step_c.start()
    step_c.wait_recv()
    quarter(out, far)[...] = rc[...]
    step_d = [copy(quarter(out, me), rd.at[0], 4, mate), copy(rc, rd.at[1], 5, mate)]
    for c in step_d:
        c.start()
    for c in step_d:
        c.wait_recv()
    quarter(out, mate)[...] = rd[0]
    quarter(out, mate_far)[...] = rd[1]
    for c in sent + [step_b, step_c] + step_d:
        c.wait_send()


def _row_quarter(ref, i):
    q = ref.shape[0] // LAYERS
    return ref.at[pl.ds(pl.multiple_of(i * q, q), q)]


def _lane_quarter(ref, i):
    q = ref.shape[1] // LAYERS
    return ref.at[:, pl.ds(pl.multiple_of(i * q, q), q)]


def _layer_pre_kernel(x, bias, feats, pre_q, *scratch):
    def finish(total):
        pre = total + bias[...]
        pre_q[...] = pre
        return jnp.maximum(pre, 0.0).astype(feats.dtype)

    _layer_exchange(_row_quarter, x, feats, finish, *scratch)


def _layer_scratch(in_q, out_q, in_dtype):
    return [
        pltpu.VMEM((2,) + in_q, in_dtype),
        pltpu.VMEM(in_q, jnp.float32),
        pltpu.VMEM(in_q, jnp.float32),
        pltpu.VMEM(out_q, jnp.bfloat16),
        pltpu.VMEM((2,) + out_q, jnp.bfloat16),
        pltpu.SemaphoreType.DMA((6,)),
        pltpu.SemaphoreType.DMA((6,)),
    ]


def layer_pre(x, bias):
    rows, cols = x.shape
    q = rows // LAYERS
    return pl.pallas_call(
        _layer_pre_kernel,
        out_shape=(jax.ShapeDtypeStruct((rows, cols), jnp.bfloat16),
                   jax.ShapeDtypeStruct((q, cols), jnp.float32)),
        in_specs=[pl.BlockSpec(memory_space=pltpu.VMEM)] * 2,
        out_specs=(pl.BlockSpec(memory_space=pltpu.VMEM), pl.BlockSpec(memory_space=pltpu.VMEM)),
        scratch_shapes=_layer_scratch((q, cols), (q, cols), x.dtype),
        compiler_params=pltpu.CompilerParams(collective_id=1, has_side_effects=True),
    )(x, bias)


def _layer_peers():
    me = lax.axis_index("layer")
    return me, [(me + k) % LAYERS for k in range(1, LAYERS)]


def _layer_greet(peers):
    barrier = pltpu.get_barrier_semaphore()
    for p in peers:
        pl.semaphore_signal(barrier, inc=1, device_id={"layer": p}, device_id_type=MESH)
    pl.semaphore_wait(barrier, LAYERS - 1)


def _layer_copy(src, dst, send_sems, recv_sems, k, p, slot):
    return pltpu.make_async_remote_copy(
        src_ref=src, dst_ref=dst, send_sem=send_sems.at[k, p], recv_sem=recv_sems.at[k, slot],
        device_id={"layer": p}, device_id_type=MESH,
    )


def _layer_grad_kernel(g, pre_q, margin_q, out, r1, r2, send_sems, recv_sems):
    me, peers = _layer_peers()
    q = g.shape[1] // LAYERS
    lanes = lambda i: pl.ds(pl.multiple_of(i * q, q), q)
    _layer_greet(peers)
    sent = []
    for p in peers:
        c = _layer_copy(g.at[:, lanes(p)], r1.at[me], send_sems, recv_sems, 0, p, me)
        c.start()
        sent.append(c)
    total = g[:, lanes(me)].astype(jnp.float32)
    for p in peers:
        _layer_copy(g.at[:, lanes(p)], r1.at[p], send_sems, recv_sems, 0, p, p).wait_recv()
        total = total + r1[p].astype(jnp.float32)
    grad = jnp.where(pre_q[...] > 0, total - MARGIN * margin_q[...], 0.0)
    out[:, lanes(me)] = grad.astype(out.dtype)
    for p in peers:
        c = _layer_copy(out.at[:, lanes(me)], r2.at[me], send_sems, recv_sems, 1, p, me)
        c.start()
        sent.append(c)
    for p in peers:
        _layer_copy(out.at[:, lanes(p)], r2.at[p], send_sems, recv_sems, 1, p, p).wait_recv()
        out[:, lanes(p)] = r2[p]
    for c in sent:
        c.wait_send()


def layer_grad(g, pre_q, margin_q):
    cols, rows = g.shape
    q = rows // LAYERS
    return pl.pallas_call(
        _layer_grad_kernel,
        out_shape=jax.ShapeDtypeStruct((cols, rows), jnp.bfloat16),
        in_specs=[pl.BlockSpec(memory_space=pltpu.VMEM)] * 3,
        out_specs=pl.BlockSpec(memory_space=pltpu.VMEM),
        scratch_shapes=[
            pltpu.VMEM((LAYERS, cols, q), jnp.bfloat16),
            pltpu.VMEM((LAYERS, cols, q), jnp.bfloat16),
            pltpu.SemaphoreType.DMA((2, LAYERS)),
            pltpu.SemaphoreType.DMA((2, LAYERS)),
        ],
        compiler_params=pltpu.CompilerParams(collective_id=2, has_side_effects=True),
    )(g, pre_q, margin_q)


def local(inputs, clean_acts, enc_weight, enc_bias, dec_weight, dec_bias, pairing, targets):
    row_count = inputs.shape[0]
    lat_count = enc_weight.shape[2]
    all_rows = pairing.shape[0]
    d_model = inputs.shape[2]
    chunk = d_model // (RING * RING)
    half = row_count // 2
    me = lax.axis_index("latent")
    partial_pre = jnp.einsum("rld,ldf->rf", inputs, enc_weight, preferred_element_type=jnp.float32)
    features, pre_q = layer_pre(partial_pre, enc_bias[None, :])
    dec4 = dec_weight[0].reshape(lat_count, RING, RING, chunk)
    recon_a = jnp.einsum("rf,fabd->abdr", features[:half], dec4, preferred_element_type=jnp.float32)
    recon_b = jnp.einsum("rf,fabd->abdr", features[half:], dec4, preferred_element_type=jnp.float32)
    recon_sum = latent_reduce(recon_a.astype(jnp.bfloat16), recon_b.astype(jnp.bfloat16), 3)
    bias_part = lax.dynamic_slice_in_dim(dec_bias[0], me * chunk, chunk)
    clean_part = lax.dynamic_slice_in_dim(clean_acts[:, 0, :], me * chunk, chunk, axis=1)
    clean_t = jnp.swapaxes(clean_part.reshape(2, half, chunk), 1, 2).astype(jnp.float32)
    recon_error = (recon_sum + bias_part[:, None] - clean_t).astype(jnp.bfloat16)
    partial_grad_t = latent_gather_mm(recon_error, dec_weight[0], 4)
    quarter = row_count // LAYERS
    row_ids = (
        lax.axis_index("row") * row_count
        + lax.axis_index("layer") * quarter
        + jnp.arange(quarter, dtype=jnp.int32)
    )
    latent_ids = me * lat_count + jnp.arange(lat_count, dtype=jnp.int32)
    every_row = jnp.arange(all_rows, dtype=jnp.int32)
    pair_table_t = (
        (every_row[:, None] == row_ids[None, :]).astype(jnp.float32)
        - (pairing[:, None] == row_ids[None, :]).astype(jnp.float32)
    ).astype(jnp.bfloat16)
    target_hot_t = (latent_ids[:, None] == targets[None, :]).astype(jnp.bfloat16)
    margin_q = jnp.dot(target_hot_t, pair_table_t, preferred_element_type=jnp.float32)
    pre_grad_t = layer_grad(partial_grad_t, pre_q.T, margin_q)
    enc4 = enc_weight[0].reshape(RING, RING, chunk, lat_count)
    total = latent_reduce_mm(enc4, pre_grad_t, 5)
    return jnp.swapaxes(total.astype(jnp.bfloat16), 1, 2).reshape(row_count, 1, chunk)


def solution(mesh):
    placed = (
        P("row", "layer", None),
        P("row", "layer", None),
        P("layer", None, "latent"),
        P("latent"),
        P("layer", "latent", None),
        P("layer", None),
        P(),
        P(),
    )
    return jax.shard_map(
        local, mesh=mesh, in_specs=placed, out_specs=P("row", "layer", "latent"), check_vma=False
    )
```

```python
import jax
import jax.numpy as jnp
from jax import lax
from jax.experimental import pallas as pl
from jax.experimental.pallas import tpu as pltpu
from jax.sharding import PartitionSpec as P

MARGIN = 16.0
MESH = pl.DeviceIdType.MESH
RING = 4
LAYERS = 4


def _latent_coords():
    me = lax.axis_index("latent")
    return me // RING, me % RING


def _greet(a, b):
    barrier = pltpu.get_barrier_semaphore()
    for k in range(1, RING):
        pl.semaphore_signal(barrier, inc=1, device_id={"latent": a * RING + (b + k) % RING}, device_id_type=MESH)
        pl.semaphore_signal(barrier, inc=1, device_id={"latent": ((a + k) % RING) * RING + b}, device_id_type=MESH)
    pl.semaphore_wait(barrier, 2 * (RING - 1))


def _copy(src, dst, send_sem, recv_sem, peer):
    return pltpu.make_async_remote_copy(
        src_ref=src, dst_ref=dst, send_sem=send_sem, recv_sem=recv_sem,
        device_id={"latent": peer}, device_id_type=MESH,
    )


def _reduce_kernel(xa, xb, out, r1a, r1b, s1a, s1b, r2a, r2b, send_sems, recv_sems):
    a, b = _latent_coords()
    _greet(a, b)
    peers_z = [(b + k) % RING for k in range(1, RING)]
    peers_x = [(a + k) % RING for k in range(1, RING)]
    first = []
    for t in peers_z:
        c = _copy(xa.at[:, t], r1a.at[b], send_sems.at[0, t], recv_sems.at[0, b], a * RING + t)
        c.start()
        first.append(c)
    for t in peers_x:
        c = _copy(xb.at[t], r1b.at[a], send_sems.at[1, t], recv_sems.at[1, a], t * RING + b)
        c.start()
        first.append(c)
    for t in peers_z:
        _copy(xa.at[:, t], r1a.at[t], send_sems.at[0, t], recv_sems.at[0, t], 0).wait_recv()
    for t in peers_x:
        _copy(xb.at[t], r1b.at[t], send_sems.at[1, t], recv_sems.at[1, t], 0).wait_recv()
    sum_a = xa[:, b].astype(jnp.float32)
    for t in peers_z:
        sum_a = sum_a + r1a[t].astype(jnp.float32)
    sum_b = xb[a].astype(jnp.float32)
    for t in peers_x:
        sum_b = sum_b + r1b[t].astype(jnp.float32)
    s1a[...] = sum_a.astype(s1a.dtype)
    s1b[...] = sum_b.astype(s1b.dtype)
    second = []
    for t in peers_x:
        c = _copy(s1a.at[t], r2a.at[a], send_sems.at[2, t], recv_sems.at[2, a], t * RING + b)
        c.start()
        second.append(c)
    for t in peers_z:
        c = _copy(s1b.at[t], r2b.at[b], send_sems.at[3, t], recv_sems.at[3, b], a * RING + t)
        c.start()
        second.append(c)
    for t in peers_x:
        _copy(s1a.at[t], r2a.at[t], send_sems.at[2, t], recv_sems.at[2, t], 0).wait_recv()
    for t in peers_z:
        _copy(s1b.at[t], r2b.at[t], send_sems.at[3, t], recv_sems.at[3, t], 0).wait_recv()
    own_a = xa[a, b].astype(jnp.float32)
    for t in peers_z:
        own_a = own_a + r1a[t, a].astype(jnp.float32)
    own_b = xb[a, b].astype(jnp.float32)
    for t in peers_x:
        own_b = own_b + r1b[t, b].astype(jnp.float32)
    for t in peers_x:
        own_a = own_a + r2a[t].astype(jnp.float32)
    for t in peers_z:
        own_b = own_b + r2b[t].astype(jnp.float32)
    out[0] = own_a
    out[1] = own_b
    for c in first + second:
        c.wait_send()


def latent_reduce(xa, xb, collective_id):
    n, _, h, c = xa.shape
    dt = xa.dtype
    return pl.pallas_call(
        _reduce_kernel,
        out_shape=jax.ShapeDtypeStruct((2, h, c), jnp.float32),
        in_specs=[pl.BlockSpec(memory_space=pltpu.VMEM)] * 2,
        out_specs=pl.BlockSpec(memory_space=pltpu.VMEM),
        scratch_shapes=[
            pltpu.VMEM((n, n, h, c), dt),
            pltpu.VMEM((n, n, h, c), dt),
            pltpu.VMEM((n, h, c), dt),
            pltpu.VMEM((n, h, c), dt),
            pltpu.VMEM((n, h, c), dt),
            pltpu.VMEM((n, h, c), dt),
            pltpu.SemaphoreType.DMA((4, n)),
            pltpu.SemaphoreType.DMA((4, n)),
        ],
        compiler_params=pltpu.CompilerParams(collective_id=collective_id, has_side_effects=True),
    )(xa, xb)


def _reduce_mm_kernel(w, v, out, xa, xb, r1a, r1b, s1a, s1b, r2a, r2b, send_sems, recv_sems):
    a, b = _latent_coords()
    _greet(a, b)
    h = v.shape[1] // 2
    peers_z = [(b + k) % RING for k in range(1, RING)]
    peers_x = [(a + k) % RING for k in range(1, RING)]

    def fill(dst, i, j, half):
        prod = jnp.dot(w[i, j], v[:, half * h:(half + 1) * h], preferred_element_type=jnp.float32)
        dst[i, j] = prod.astype(dst.dtype)

    first = []
    for kz, kx in zip(peers_z, peers_x):
        for i in range(RING):
            fill(xa, i, kz, 0)
        c = _copy(xa.at[:, kz], r1a.at[b], send_sems.at[0, kz], recv_sems.at[0, b], a * RING + kz)
        c.start()
        first.append(c)
        for j in range(RING):
            fill(xb, kx, j, 1)
        c = _copy(xb.at[kx], r1b.at[a], send_sems.at[1, kx], recv_sems.at[1, a], kx * RING + b)
        c.start()
        first.append(c)
    for i in range(RING):
        fill(xa, i, b, 0)
    for j in range(RING):
        fill(xb, a, j, 1)
    for t in peers_z:
        _copy(xa.at[:, t], r1a.at[t], send_sems.at[0, t], recv_sems.at[0, t], 0).wait_recv()
    for t in peers_x:
        _copy(xb.at[t], r1b.at[t], send_sems.at[1, t], recv_sems.at[1, t], 0).wait_recv()
    sum_a = xa[:, b].astype(jnp.float32)
    for t in peers_z:
        sum_a = sum_a + r1a[t].astype(jnp.float32)
    sum_b = xb[a].astype(jnp.float32)
    for t in peers_x:
        sum_b = sum_b + r1b[t].astype(jnp.float32)
    s1a[...] = sum_a.astype(s1a.dtype)
    s1b[...] = sum_b.astype(s1b.dtype)
    second = []
    for t in peers_x:
        c = _copy(s1a.at[t], r2a.at[a], send_sems.at[2, t], recv_sems.at[2, a], t * RING + b)
        c.start()
        second.append(c)
    for t in peers_z:
        c = _copy(s1b.at[t], r2b.at[b], send_sems.at[3, t], recv_sems.at[3, b], a * RING + t)
        c.start()
        second.append(c)
    for t in peers_x:
        _copy(s1a.at[t], r2a.at[t], send_sems.at[2, t], recv_sems.at[2, t], 0).wait_recv()
    for t in peers_z:
        _copy(s1b.at[t], r2b.at[t], send_sems.at[3, t], recv_sems.at[3, t], 0).wait_recv()
    own_a = xa[a, b].astype(jnp.float32)
    own_b = xb[a, b].astype(jnp.float32)
    for k in range(1, RING):
        own_a = own_a + r1a[(b + k) % RING, a].astype(jnp.float32)
        own_b = own_b + r1b[(a + k) % RING, b].astype(jnp.float32)
    for k in range(1, RING):
        own_a = own_a + r2a[(a + k) % RING].astype(jnp.float32)
        own_b = own_b + r2b[(b + k) % RING].astype(jnp.float32)
    out[0] = own_a
    out[1] = own_b
    for c in first + second:
        c.wait_send()


def latent_reduce_mm(w, v, collective_id):
    n, _, d, _ = w.shape
    h = v.shape[1] // 2
    dt = w.dtype
    return pl.pallas_call(
        _reduce_mm_kernel,
        out_shape=jax.ShapeDtypeStruct((2, d, h), jnp.float32),
        in_specs=[pl.BlockSpec(memory_space=pltpu.VMEM)] * 2,
        out_specs=pl.BlockSpec(memory_space=pltpu.VMEM),
        scratch_shapes=[
            pltpu.VMEM((n, n, d, h), dt),
            pltpu.VMEM((n, n, d, h), dt),
            pltpu.VMEM((n, n, d, h), dt),
            pltpu.VMEM((n, n, d, h), dt),
            pltpu.VMEM((n, d, h), dt),
            pltpu.VMEM((n, d, h), dt),
            pltpu.VMEM((n, d, h), dt),
            pltpu.VMEM((n, d, h), dt),
            pltpu.SemaphoreType.DMA((4, n)),
            pltpu.SemaphoreType.DMA((4, n)),
        ],
        compiler_params=pltpu.CompilerParams(collective_id=collective_id, has_side_effects=True),
    )(w, v)


def _gather_kernel(e, oa, ob, g1a, g1b, ga, gb, send_sems, recv_sems):
    a, b = _latent_coords()
    _greet(a, b)
    peers_z = [(b + k) % RING for k in range(1, RING)]
    peers_x = [(a + k) % RING for k in range(1, RING)]
    first = []
    for t in peers_z:
        c = _copy(e.at[0], g1a.at[b], send_sems.at[0, t], recv_sems.at[0, b], a * RING + t)
        c.start()
        first.append(c)
    for t in peers_x:
        c = _copy(e.at[1], g1b.at[a], send_sems.at[1, t], recv_sems.at[1, a], t * RING + b)
        c.start()
        first.append(c)
    g1a[b] = e[0]
    g1b[a] = e[1]
    for t in peers_z:
        _copy(e.at[0], g1a.at[t], send_sems.at[0, t], recv_sems.at[0, t], 0).wait_recv()
    for t in peers_x:
        _copy(e.at[1], g1b.at[t], send_sems.at[1, t], recv_sems.at[1, t], 0).wait_recv()
    second = []
    for t in peers_x:
        c = _copy(g1a, ga.at[a], send_sems.at[2, t], recv_sems.at[2, a], t * RING + b)
        c.start()
        second.append(c)
    for t in peers_z:
        c = _copy(g1b, gb.at[b], send_sems.at[3, t], recv_sems.at[3, b], a * RING + t)
        c.start()
        second.append(c)
    oa[a] = g1a[...]
    for j in range(RING):
        ob[j, b] = g1b[j]
    for t in peers_x:
        _copy(g1a, ga.at[t], send_sems.at[2, t], recv_sems.at[2, t], 0).wait_recv()
        oa[t] = ga[t]
    for t in peers_z:
        _copy(g1b, gb.at[t], send_sems.at[3, t], recv_sems.at[3, t], 0).wait_recv()
        for j in range(RING):
            ob[j, t] = gb[t, j]
    for c in first + second:
        c.wait_send()


def latent_gather(e, collective_id):
    _, h, c = e.shape
    n = RING
    dt = e.dtype
    full = jax.ShapeDtypeStruct((n, n, h, c), dt)
    return pl.pallas_call(
        _gather_kernel,
        out_shape=(full, full),
        in_specs=[pl.BlockSpec(memory_space=pltpu.VMEM)],
        out_specs=(pl.BlockSpec(memory_space=pltpu.VMEM), pl.BlockSpec(memory_space=pltpu.VMEM)),
        scratch_shapes=[
            pltpu.VMEM((n, h, c), dt),
            pltpu.VMEM((n, h, c), dt),
            pltpu.VMEM((n, n, h, c), dt),
            pltpu.VMEM((n, n, h, c), dt),
            pltpu.SemaphoreType.DMA((4, n)),
            pltpu.SemaphoreType.DMA((4, n)),
        ],
        compiler_params=pltpu.CompilerParams(collective_id=collective_id, has_side_effects=True),
    )(e)


def _layer_roles():
    me = lax.axis_index("layer")
    mate = me + 1 - 2 * (me % 2)
    far = (me + 2) % LAYERS
    return me, mate, far, (mate + 2) % LAYERS


def _layer_exchange(quarter, x, out, finish, produce, ra, sb, rb, rc, rd, send_sems, recv_sems):
    me, mate, far, mate_far = _layer_roles()
    barrier = pltpu.get_barrier_semaphore()
    for p in (mate, far):
        pl.semaphore_signal(barrier, inc=1, device_id={"layer": p}, device_id_type=MESH)
    pl.semaphore_wait(barrier, 2)

    def copy(src, dst, k, p):
        return pltpu.make_async_remote_copy(
            src_ref=src, dst_ref=dst, send_sem=send_sems.at[k], recv_sem=recv_sems.at[k],
            device_id={"layer": p}, device_id_type=MESH,
        )

    produce(mate)
    produce(mate_far)
    sent = [copy(quarter(x, mate), ra.at[0], 0, mate), copy(quarter(x, mate_far), ra.at[1], 1, mate)]
    for c in sent:
        c.start()
    produce(far)
    produce(me)
    sent[0].wait_recv()
    sent[1].wait_recv()
    sb[...] = quarter(x, far)[...].astype(jnp.float32) + ra[1].astype(jnp.float32)
    step_b = copy(sb, rb, 2, far)
    step_b.start()
    own = quarter(x, me)[...].astype(jnp.float32) + ra[0].astype(jnp.float32)
    step_b.wait_recv()
    quarter(out, me)[...] = finish(own + rb[...])
    step_c = copy(quarter(out, me), rc, 3, far)
    step_c.start()
    step_c.wait_recv()
    quarter(out, far)[...] = rc[...]
    step_d = [copy(quarter(out, me), rd.at[0], 4, mate), copy(rc, rd.at[1], 5, mate)]
    for c in step_d:
        c.start()
    for c in step_d:
        c.wait_recv()
    quarter(out, mate)[...] = rd[0]
    quarter(out, mate_far)[...] = rd[1]
    for c in sent + [step_b, step_c] + step_d:
        c.wait_send()


def _row_quarter(ref, i):
    q = ref.shape[0] // LAYERS
    return ref.at[pl.ds(pl.multiple_of(i * q, q), q)]


def _lane_quarter(ref, i):
    q = ref.shape[1] // LAYERS
    return ref.at[:, pl.ds(pl.multiple_of(i * q, q), q)]


def _layer_pre_kernel(inp, w, bias, feats, pre_q, x, *scratch):
    def finish(total):
        pre = total + bias[...]
        pre_q[...] = pre
        return jnp.maximum(pre, 0.0).astype(feats.dtype)

    def produce(i):
        _row_quarter(x, i)[...] = jnp.dot(
            _row_quarter(inp, i)[...], w[...], preferred_element_type=jnp.float32
        )

    _layer_exchange(_row_quarter, x, feats, finish, produce, *scratch)


def _layer_scratch(in_q, out_q, in_dtype):
    return [
        pltpu.VMEM((2,) + in_q, in_dtype),
        pltpu.VMEM(in_q, jnp.float32),
        pltpu.VMEM(in_q, jnp.float32),
        pltpu.VMEM(out_q, jnp.bfloat16),
        pltpu.VMEM((2,) + out_q, jnp.bfloat16),
        pltpu.SemaphoreType.DMA((6,)),
        pltpu.SemaphoreType.DMA((6,)),
    ]


def layer_pre(inp, w, bias):
    rows, cols = inp.shape[0], w.shape[1]
    q = rows // LAYERS
    return pl.pallas_call(
        _layer_pre_kernel,
        out_shape=(jax.ShapeDtypeStruct((rows, cols), jnp.bfloat16),
                   jax.ShapeDtypeStruct((q, cols), jnp.float32)),
        in_specs=[pl.BlockSpec(memory_space=pltpu.VMEM)] * 3,
        out_specs=(pl.BlockSpec(memory_space=pltpu.VMEM), pl.BlockSpec(memory_space=pltpu.VMEM)),
        scratch_shapes=[pltpu.VMEM((rows, cols), jnp.float32)]
        + _layer_scratch((q, cols), (q, cols), jnp.float32),
        compiler_params=pltpu.CompilerParams(collective_id=1, has_side_effects=True),
    )(inp, w, bias)


def _layer_peers():
    me = lax.axis_index("layer")
    return me, [(me + k) % LAYERS for k in range(1, LAYERS)]


def _layer_greet(peers):
    barrier = pltpu.get_barrier_semaphore()
    for p in peers:
        pl.semaphore_signal(barrier, inc=1, device_id={"layer": p}, device_id_type=MESH)
    pl.semaphore_wait(barrier, LAYERS - 1)


def _layer_copy(src, dst, send_sems, recv_sems, k, p, slot):
    return pltpu.make_async_remote_copy(
        src_ref=src, dst_ref=dst, send_sem=send_sems.at[k, p], recv_sem=recv_sems.at[k, slot],
        device_id={"layer": p}, device_id_type=MESH,
    )


def _layer_grad_kernel(g, pre_q, margin_q, out, r1, r2, send_sems, recv_sems):
    me, peers = _layer_peers()
    q = g.shape[1] // LAYERS
    lanes = lambda i: pl.ds(pl.multiple_of(i * q, q), q)
    _layer_greet(peers)
    sent = []
    for p in peers:
        c = _layer_copy(g.at[:, lanes(p)], r1.at[me], send_sems, recv_sems, 0, p, me)
        c.start()
        sent.append(c)
    total = g[:, lanes(me)].astype(jnp.float32)
    for p in peers:
        _layer_copy(g.at[:, lanes(p)], r1.at[p], send_sems, recv_sems, 0, p, p).wait_recv()
        total = total + r1[p].astype(jnp.float32)
    grad = jnp.where(pre_q[...] > 0, total - MARGIN * margin_q[...], 0.0)
    out[:, lanes(me)] = grad.astype(out.dtype)
    for p in peers:
        c = _layer_copy(out.at[:, lanes(me)], r2.at[me], send_sems, recv_sems, 1, p, me)
        c.start()
        sent.append(c)
    for p in peers:
        _layer_copy(out.at[:, lanes(p)], r2.at[p], send_sems, recv_sems, 1, p, p).wait_recv()
        out[:, lanes(p)] = r2[p]
    for c in sent:
        c.wait_send()


def layer_grad(g, pre_q, margin_q):
    cols, rows = g.shape
    q = rows // LAYERS
    return pl.pallas_call(
        _layer_grad_kernel,
        out_shape=jax.ShapeDtypeStruct((cols, rows), jnp.bfloat16),
        in_specs=[pl.BlockSpec(memory_space=pltpu.VMEM)] * 3,
        out_specs=pl.BlockSpec(memory_space=pltpu.VMEM),
        scratch_shapes=[
            pltpu.VMEM((LAYERS, cols, q), jnp.bfloat16),
            pltpu.VMEM((LAYERS, cols, q), jnp.bfloat16),
            pltpu.SemaphoreType.DMA((2, LAYERS)),
            pltpu.SemaphoreType.DMA((2, LAYERS)),
        ],
        compiler_params=pltpu.CompilerParams(collective_id=2, has_side_effects=True),
    )(g, pre_q, margin_q)


def local(inputs, clean_acts, enc_weight, enc_bias, dec_weight, dec_bias, pairing, targets):
    row_count = inputs.shape[0]
    lat_count = enc_weight.shape[2]
    all_rows = pairing.shape[0]
    d_model = inputs.shape[2]
    chunk = d_model // (RING * RING)
    half = row_count // 2
    me = lax.axis_index("latent")
    features, pre_q = layer_pre(inputs[:, 0, :], enc_weight[0], enc_bias[None, :])
    dec4 = dec_weight[0].reshape(lat_count, RING, RING, chunk)
    recon_a = jnp.einsum("rf,fabd->abdr", features[:half], dec4, preferred_element_type=jnp.float32)
    recon_b = jnp.einsum("rf,fabd->abdr", features[half:], dec4, preferred_element_type=jnp.float32)
    recon_sum = latent_reduce(recon_a.astype(jnp.bfloat16), recon_b.astype(jnp.bfloat16), 3)
    bias_part = lax.dynamic_slice_in_dim(dec_bias[0], me * chunk, chunk)
    clean_part = lax.dynamic_slice_in_dim(clean_acts[:, 0, :], me * chunk, chunk, axis=1)
    clean_t = jnp.swapaxes(clean_part.reshape(2, half, chunk), 1, 2).astype(jnp.float32)
    recon_error = (recon_sum + bias_part[:, None] - clean_t).astype(jnp.bfloat16)
    error_a, error_b = latent_gather(recon_error, 4)
    error_all = jnp.concatenate(
        [error_a.reshape(d_model, half), error_b.reshape(d_model, half)], axis=1
    )
    partial_grad_t = jnp.dot(dec_weight[0], error_all, preferred_element_type=jnp.float32)
    quarter = row_count // LAYERS
    row_ids = (
        lax.axis_index("row") * row_count
        + lax.axis_index("layer") * quarter
        + jnp.arange(quarter, dtype=jnp.int32)
    )
    latent_ids = me * lat_count + jnp.arange(lat_count, dtype=jnp.int32)
    every_row = jnp.arange(all_rows, dtype=jnp.int32)
    pair_table_t = (
        (every_row[:, None] == row_ids[None, :]).astype(jnp.float32)
        - (pairing[:, None] == row_ids[None, :]).astype(jnp.float32)
    ).astype(jnp.bfloat16)
    target_hot_t = (latent_ids[:, None] == targets[None, :]).astype(jnp.bfloat16)
    margin_q = jnp.dot(target_hot_t, pair_table_t, preferred_element_type=jnp.float32)
    pre_grad_t = layer_grad(partial_grad_t.astype(jnp.bfloat16), pre_q.T, margin_q)
    enc4 = enc_weight[0].reshape(RING, RING, chunk, lat_count)
    total = latent_reduce_mm(enc4, pre_grad_t, 5)
    return jnp.swapaxes(total.astype(jnp.bfloat16), 1, 2).reshape(row_count, 1, chunk)


def solution(mesh):
    placed = (
        P("row", "layer", None),
        P("row", "layer", None),
        P("layer", None, "latent"),
        P("latent"),
        P("layer", "latent", None),
        P("layer", None),
        P(),
        P(),
    )
    return jax.shard_map(
        local, mesh=mesh, in_specs=placed, out_specs=P("row", "layer", "latent"), check_vma=False
    )
```

```python
import jax
import jax.numpy as jnp
from jax import lax
from jax.experimental import pallas as pl
from jax.experimental.pallas import tpu as pltpu
from jax.sharding import PartitionSpec as P

MARGIN = 16.0
MESH = pl.DeviceIdType.MESH
RING = 4
LAYERS = 4


def _latent_coords():
    me = lax.axis_index("latent")
    return me // RING, me % RING


def _greet(a, b):
    barrier = pltpu.get_barrier_semaphore()
    for k in range(1, RING):
        pl.semaphore_signal(barrier, inc=1, device_id={"latent": a * RING + (b + k) % RING}, device_id_type=MESH)
        pl.semaphore_signal(barrier, inc=1, device_id={"latent": ((a + k) % RING) * RING + b}, device_id_type=MESH)
    pl.semaphore_wait(barrier, 2 * (RING - 1))


def _copy(src, dst, send_sem, recv_sem, peer):
    return pltpu.make_async_remote_copy(
        src_ref=src, dst_ref=dst, send_sem=send_sem, recv_sem=recv_sem,
        device_id={"latent": peer}, device_id_type=MESH,
    )


def _reduce_kernel(xa, xb, out, r1a, r1b, s1a, s1b, r2a, r2b, send_sems, recv_sems):
    a, b = _latent_coords()
    _greet(a, b)
    peers_z = [(b + k) % RING for k in range(1, RING)]
    peers_x = [(a + k) % RING for k in range(1, RING)]
    first = []
    for t in peers_z:
        c = _copy(xa.at[:, t], r1a.at[b], send_sems.at[0, t], recv_sems.at[0, b], a * RING + t)
        c.start()
        first.append(c)
    for t in peers_x:
        c = _copy(xb.at[t], r1b.at[a], send_sems.at[1, t], recv_sems.at[1, a], t * RING + b)
        c.start()
        first.append(c)
    for t in peers_z:
        _copy(xa.at[:, t], r1a.at[t], send_sems.at[0, t], recv_sems.at[0, t], 0).wait_recv()
    for t in peers_x:
        _copy(xb.at[t], r1b.at[t], send_sems.at[1, t], recv_sems.at[1, t], 0).wait_recv()
    sum_a = xa[:, b].astype(jnp.float32)
    for t in peers_z:
        sum_a = sum_a + r1a[t].astype(jnp.float32)
    sum_b = xb[a].astype(jnp.float32)
    for t in peers_x:
        sum_b = sum_b + r1b[t].astype(jnp.float32)
    s1a[...] = sum_a.astype(s1a.dtype)
    s1b[...] = sum_b.astype(s1b.dtype)
    second = []
    for t in peers_x:
        c = _copy(s1a.at[t], r2a.at[a], send_sems.at[2, t], recv_sems.at[2, a], t * RING + b)
        c.start()
        second.append(c)
    for t in peers_z:
        c = _copy(s1b.at[t], r2b.at[b], send_sems.at[3, t], recv_sems.at[3, b], a * RING + t)
        c.start()
        second.append(c)
    for t in peers_x:
        _copy(s1a.at[t], r2a.at[t], send_sems.at[2, t], recv_sems.at[2, t], 0).wait_recv()
    for t in peers_z:
        _copy(s1b.at[t], r2b.at[t], send_sems.at[3, t], recv_sems.at[3, t], 0).wait_recv()
    own_a = xa[a, b].astype(jnp.float32)
    for t in peers_z:
        own_a = own_a + r1a[t, a].astype(jnp.float32)
    own_b = xb[a, b].astype(jnp.float32)
    for t in peers_x:
        own_b = own_b + r1b[t, b].astype(jnp.float32)
    for t in peers_x:
        own_a = own_a + r2a[t].astype(jnp.float32)
    for t in peers_z:
        own_b = own_b + r2b[t].astype(jnp.float32)
    out[0] = own_a
    out[1] = own_b
    for c in first + second:
        c.wait_send()


def latent_reduce(xa, xb, collective_id):
    n, _, h, c = xa.shape
    dt = xa.dtype
    return pl.pallas_call(
        _reduce_kernel,
        out_shape=jax.ShapeDtypeStruct((2, h, c), jnp.float32),
        in_specs=[pl.BlockSpec(memory_space=pltpu.VMEM)] * 2,
        out_specs=pl.BlockSpec(memory_space=pltpu.VMEM),
        scratch_shapes=[
            pltpu.VMEM((n, n, h, c), dt),
            pltpu.VMEM((n, n, h, c), dt),
            pltpu.VMEM((n, h, c), dt),
            pltpu.VMEM((n, h, c), dt),
            pltpu.VMEM((n, h, c), dt),
            pltpu.VMEM((n, h, c), dt),
            pltpu.SemaphoreType.DMA((4, n)),
            pltpu.SemaphoreType.DMA((4, n)),
        ],
        compiler_params=pltpu.CompilerParams(collective_id=collective_id, has_side_effects=True),
    )(xa, xb)


def _reduce_mm_kernel(w, v, out, xa, xb, r1a, r1b, s1a, s1b, r2a, r2b, send_sems, recv_sems):
    a, b = _latent_coords()
    _greet(a, b)
    h = v.shape[1] // 2
    peers_z = [(b + k) % RING for k in range(1, RING)]
    peers_x = [(a + k) % RING for k in range(1, RING)]

    def fill(dst, i, j, half):
        prod = jnp.dot(w[i, j], v[:, half * h:(half + 1) * h], preferred_element_type=jnp.float32)
        dst[i, j] = prod.astype(dst.dtype)

    first = []
    for kz, kx in zip(peers_z, peers_x):
        for i in range(RING):
            fill(xa, i, kz, 0)
        c = _copy(xa.at[:, kz], r1a.at[b], send_sems.at[0, kz], recv_sems.at[0, b], a * RING + kz)
        c.start()
        first.append(c)
        for j in range(RING):
            fill(xb, kx, j, 1)
        c = _copy(xb.at[kx], r1b.at[a], send_sems.at[1, kx], recv_sems.at[1, a], kx * RING + b)
        c.start()
        first.append(c)
    for i in range(RING):
        fill(xa, i, b, 0)
    for j in range(RING):
        fill(xb, a, j, 1)
    for t in peers_z:
        _copy(xa.at[:, t], r1a.at[t], send_sems.at[0, t], recv_sems.at[0, t], 0).wait_recv()
    for t in peers_x:
        _copy(xb.at[t], r1b.at[t], send_sems.at[1, t], recv_sems.at[1, t], 0).wait_recv()
    sum_a = xa[:, b].astype(jnp.float32)
    for t in peers_z:
        sum_a = sum_a + r1a[t].astype(jnp.float32)
    sum_b = xb[a].astype(jnp.float32)
    for t in peers_x:
        sum_b = sum_b + r1b[t].astype(jnp.float32)
    s1a[...] = sum_a.astype(s1a.dtype)
    s1b[...] = sum_b.astype(s1b.dtype)
    second = []
    for t in peers_x:
        c = _copy(s1a.at[t], r2a.at[a], send_sems.at[2, t], recv_sems.at[2, a], t * RING + b)
        c.start()
        second.append(c)
    for t in peers_z:
        c = _copy(s1b.at[t], r2b.at[b], send_sems.at[3, t], recv_sems.at[3, b], a * RING + t)
        c.start()
        second.append(c)
    for t in peers_x:
        _copy(s1a.at[t], r2a.at[t], send_sems.at[2, t], recv_sems.at[2, t], 0).wait_recv()
    for t in peers_z:
        _copy(s1b.at[t], r2b.at[t], send_sems.at[3, t], recv_sems.at[3, t], 0).wait_recv()
    own_a = xa[a, b].astype(jnp.float32)
    own_b = xb[a, b].astype(jnp.float32)
    for k in range(1, RING):
        own_a = own_a + r1a[(b + k) % RING, a].astype(jnp.float32)
        own_b = own_b + r1b[(a + k) % RING, b].astype(jnp.float32)
    for k in range(1, RING):
        own_a = own_a + r2a[(a + k) % RING].astype(jnp.float32)
        own_b = own_b + r2b[(b + k) % RING].astype(jnp.float32)
    out[0] = own_a
    out[1] = own_b
    for c in first + second:
        c.wait_send()


def latent_reduce_mm(w, v, collective_id):
    n, _, d, _ = w.shape
    h = v.shape[1] // 2
    dt = w.dtype
    return pl.pallas_call(
        _reduce_mm_kernel,
        out_shape=jax.ShapeDtypeStruct((2, d, h), jnp.float32),
        in_specs=[pl.BlockSpec(memory_space=pltpu.VMEM)] * 2,
        out_specs=pl.BlockSpec(memory_space=pltpu.VMEM),
        scratch_shapes=[
            pltpu.VMEM((n, n, d, h), dt),
            pltpu.VMEM((n, n, d, h), dt),
            pltpu.VMEM((n, n, d, h), dt),
            pltpu.VMEM((n, n, d, h), dt),
            pltpu.VMEM((n, d, h), dt),
            pltpu.VMEM((n, d, h), dt),
            pltpu.VMEM((n, d, h), dt),
            pltpu.VMEM((n, d, h), dt),
            pltpu.SemaphoreType.DMA((4, n)),
            pltpu.SemaphoreType.DMA((4, n)),
        ],
        compiler_params=pltpu.CompilerParams(collective_id=collective_id, has_side_effects=True),
    )(w, v)


def _gather_kernel(e, oa, ob, g1a, g1b, ga, gb, send_sems, recv_sems):
    a, b = _latent_coords()
    _greet(a, b)
    peers_z = [(b + k) % RING for k in range(1, RING)]
    peers_x = [(a + k) % RING for k in range(1, RING)]
    first = []
    for t in peers_z:
        c = _copy(e.at[0], g1a.at[b], send_sems.at[0, t], recv_sems.at[0, b], a * RING + t)
        c.start()
        first.append(c)
    for t in peers_x:
        c = _copy(e.at[1], g1b.at[a], send_sems.at[1, t], recv_sems.at[1, a], t * RING + b)
        c.start()
        first.append(c)
    g1a[b] = e[0]
    g1b[a] = e[1]
    for t in peers_z:
        _copy(e.at[0], g1a.at[t], send_sems.at[0, t], recv_sems.at[0, t], 0).wait_recv()
    for t in peers_x:
        _copy(e.at[1], g1b.at[t], send_sems.at[1, t], recv_sems.at[1, t], 0).wait_recv()
    second = []
    for t in peers_x:
        c = _copy(g1a, ga.at[a], send_sems.at[2, t], recv_sems.at[2, a], t * RING + b)
        c.start()
        second.append(c)
    for t in peers_z:
        c = _copy(g1b, gb.at[b], send_sems.at[3, t], recv_sems.at[3, b], a * RING + t)
        c.start()
        second.append(c)
    oa[a] = g1a[...]
    for j in range(RING):
        ob[j, b] = g1b[j]
    for t in peers_x:
        _copy(g1a, ga.at[t], send_sems.at[2, t], recv_sems.at[2, t], 0).wait_recv()
        oa[t] = ga[t]
    for t in peers_z:
        _copy(g1b, gb.at[t], send_sems.at[3, t], recv_sems.at[3, t], 0).wait_recv()
        for j in range(RING):
            ob[j, t] = gb[t, j]
    for c in first + second:
        c.wait_send()


def latent_gather(e, collective_id):
    _, h, c = e.shape
    n = RING
    dt = e.dtype
    full = jax.ShapeDtypeStruct((n, n, h, c), dt)
    return pl.pallas_call(
        _gather_kernel,
        out_shape=(full, full),
        in_specs=[pl.BlockSpec(memory_space=pltpu.VMEM)],
        out_specs=(pl.BlockSpec(memory_space=pltpu.VMEM), pl.BlockSpec(memory_space=pltpu.VMEM)),
        scratch_shapes=[
            pltpu.VMEM((n, h, c), dt),
            pltpu.VMEM((n, h, c), dt),
            pltpu.VMEM((n, n, h, c), dt),
            pltpu.VMEM((n, n, h, c), dt),
            pltpu.SemaphoreType.DMA((4, n)),
            pltpu.SemaphoreType.DMA((4, n)),
        ],
        compiler_params=pltpu.CompilerParams(collective_id=collective_id, has_side_effects=True),
    )(e)


def _layer_roles():
    me = lax.axis_index("layer")
    mate = me + 1 - 2 * (me % 2)
    far = (me + 2) % LAYERS
    return me, mate, far, (mate + 2) % LAYERS


def _layer_exchange(quarter, x, out, finish, produce, ra, sb, rb, rc, rd, send_sems, recv_sems):
    me, mate, far, mate_far = _layer_roles()
    barrier = pltpu.get_barrier_semaphore()
    for p in (mate, far):
        pl.semaphore_signal(barrier, inc=1, device_id={"layer": p}, device_id_type=MESH)
    pl.semaphore_wait(barrier, 2)

    def copy(src, dst, k, p):
        return pltpu.make_async_remote_copy(
            src_ref=src, dst_ref=dst, send_sem=send_sems.at[k], recv_sem=recv_sems.at[k],
            device_id={"layer": p}, device_id_type=MESH,
        )

    produce(mate)
    produce(mate_far)
    sent = [copy(quarter(x, mate), ra.at[0], 0, mate), copy(quarter(x, mate_far), ra.at[1], 1, mate)]
    for c in sent:
        c.start()
    produce(far)
    produce(me)
    sent[0].wait_recv()
    sent[1].wait_recv()
    sb[...] = quarter(x, far)[...].astype(jnp.float32) + ra[1].astype(jnp.float32)
    step_b = copy(sb, rb, 2, far)
    step_b.start()
    own = quarter(x, me)[...].astype(jnp.float32) + ra[0].astype(jnp.float32)
    step_b.wait_recv()
    quarter(out, me)[...] = finish(own + rb[...])
    step_c = copy(quarter(out, me), rc, 3, far)
    step_c.start()
    step_c.wait_recv()
    quarter(out, far)[...] = rc[...]
    step_d = [copy(quarter(out, me), rd.at[0], 4, mate), copy(rc, rd.at[1], 5, mate)]
    for c in step_d:
        c.start()
    for c in step_d:
        c.wait_recv()
    quarter(out, mate)[...] = rd[0]
    quarter(out, mate_far)[...] = rd[1]
    for c in sent + [step_b, step_c] + step_d:
        c.wait_send()


def _row_quarter(ref, i):
    q = ref.shape[0] // LAYERS
    return ref.at[pl.ds(pl.multiple_of(i * q, q), q)]


def _lane_quarter(ref, i):
    q = ref.shape[1] // LAYERS
    return ref.at[:, pl.ds(pl.multiple_of(i * q, q), q)]


def _layer_pre_kernel(inp, w, bias, feats, pre_q, x, *scratch):
    def finish(total):
        pre = total + bias[...]
        pre_q[...] = pre
        return jnp.maximum(pre, 0.0).astype(feats.dtype)

    def produce(i):
        _row_quarter(x, i)[...] = jnp.dot(
            _row_quarter(inp, i)[...], w[...], preferred_element_type=jnp.float32
        )

    _layer_exchange(_row_quarter, x, feats, finish, produce, *scratch)


def _layer_scratch(in_q, out_q, in_dtype):
    return [
        pltpu.VMEM((2,) + in_q, in_dtype),
        pltpu.VMEM(in_q, jnp.float32),
        pltpu.VMEM(in_q, jnp.float32),
        pltpu.VMEM(out_q, jnp.bfloat16),
        pltpu.VMEM((2,) + out_q, jnp.bfloat16),
        pltpu.SemaphoreType.DMA((6,)),
        pltpu.SemaphoreType.DMA((6,)),
    ]


def layer_pre(inp, w, bias):
    rows, cols = inp.shape[0], w.shape[1]
    q = rows // LAYERS
    return pl.pallas_call(
        _layer_pre_kernel,
        out_shape=(jax.ShapeDtypeStruct((rows, cols), jnp.bfloat16),
                   jax.ShapeDtypeStruct((q, cols), jnp.float32)),
        in_specs=[pl.BlockSpec(memory_space=pltpu.VMEM)] * 3,
        out_specs=(pl.BlockSpec(memory_space=pltpu.VMEM), pl.BlockSpec(memory_space=pltpu.VMEM)),
        scratch_shapes=[pltpu.VMEM((rows, cols), jnp.float32)]
        + _layer_scratch((q, cols), (q, cols), jnp.float32),
        compiler_params=pltpu.CompilerParams(collective_id=1, has_side_effects=True),
    )(inp, w, bias)


def _layer_peers():
    me = lax.axis_index("layer")
    return me, [(me + k) % LAYERS for k in range(1, LAYERS)]


def _layer_greet(peers):
    barrier = pltpu.get_barrier_semaphore()
    for p in peers:
        pl.semaphore_signal(barrier, inc=1, device_id={"layer": p}, device_id_type=MESH)
    pl.semaphore_wait(barrier, LAYERS - 1)


def _layer_copy(src, dst, send_sems, recv_sems, k, p, slot):
    return pltpu.make_async_remote_copy(
        src_ref=src, dst_ref=dst, send_sem=send_sems.at[k, p], recv_sem=recv_sems.at[k, slot],
        device_id={"layer": p}, device_id_type=MESH,
    )


def _layer_grad_mm_kernel(ea, eb, w, pre_q, margin_q, out, gq, r1, r2, send_sems, recv_sems):
    me, peers = _layer_peers()
    q = out.shape[1] // LAYERS
    lanes = lambda i: pl.ds(pl.multiple_of(i * q, q), q)
    _layer_greet(peers)
    per_half = ea.shape[1] // q

    def first(i):
        return _layer_copy(gq.at[i], r1.at[me], send_sems, recv_sems, 0, i, me)

    for i in range(LAYERS):
        src = ea if i < per_half else eb
        lo = (i % per_half) * q
        part = jnp.dot(w[...], src[:, lo:lo + q], preferred_element_type=jnp.float32)
        gq[i] = part.astype(gq.dtype)

        @pl.when(i != me)
        def _():
            first(i).start()

    total = gq[me].astype(jnp.float32)
    for p in peers:
        _layer_copy(gq.at[p], r1.at[p], send_sems, recv_sems, 0, p, p).wait_recv()
        total = total + r1[p].astype(jnp.float32)
    grad = jnp.where(pre_q[...] > 0, total - MARGIN * margin_q[...], 0.0)
    out[:, lanes(me)] = grad.astype(out.dtype)
    sent = []
    for p in peers:
        c = _layer_copy(out.at[:, lanes(me)], r2.at[me], send_sems, recv_sems, 1, p, me)
        c.start()
        sent.append(c)
    for p in peers:
        _layer_copy(out.at[:, lanes(p)], r2.at[p], send_sems, recv_sems, 1, p, p).wait_recv()
        out[:, lanes(p)] = r2[p]
    for c in sent:
        c.wait_send()
    for i in range(LAYERS):
        @pl.when(i != me)
        def _():
            first(i).wait_send()


def layer_grad_mm(ea, eb, w, pre_q, margin_q):
    cols, rows = w.shape[0], ea.shape[1] + eb.shape[1]
    q = rows // LAYERS
    return pl.pallas_call(
        _layer_grad_mm_kernel,
        out_shape=jax.ShapeDtypeStruct((cols, rows), jnp.bfloat16),
        in_specs=[pl.BlockSpec(memory_space=pltpu.VMEM)] * 5,
        out_specs=pl.BlockSpec(memory_space=pltpu.VMEM),
        scratch_shapes=[
            pltpu.VMEM((LAYERS, cols, q), jnp.bfloat16),
            pltpu.VMEM((LAYERS, cols, q), jnp.bfloat16),
            pltpu.VMEM((LAYERS, cols, q), jnp.bfloat16),
            pltpu.SemaphoreType.DMA((2, LAYERS)),
            pltpu.SemaphoreType.DMA((2, LAYERS)),
        ],
        compiler_params=pltpu.CompilerParams(collective_id=2, has_side_effects=True),
    )(ea, eb, w, pre_q, margin_q)


def local(inputs, clean_acts, enc_weight, enc_bias, dec_weight, dec_bias, pairing, targets):
    row_count = inputs.shape[0]
    lat_count = enc_weight.shape[2]
    all_rows = pairing.shape[0]
    d_model = inputs.shape[2]
    chunk = d_model // (RING * RING)
    half = row_count // 2
    me = lax.axis_index("latent")
    features, pre_q = layer_pre(inputs[:, 0, :], enc_weight[0], enc_bias[None, :])
    dec4 = dec_weight[0].reshape(lat_count, RING, RING, chunk)
    recon_a = jnp.einsum("rf,fabd->abdr", features[:half], dec4, preferred_element_type=jnp.float32)
    recon_b = jnp.einsum("rf,fabd->abdr", features[half:], dec4, preferred_element_type=jnp.float32)
    recon_sum = latent_reduce(recon_a.astype(jnp.bfloat16), recon_b.astype(jnp.bfloat16), 3)
    bias_part = lax.dynamic_slice_in_dim(dec_bias[0], me * chunk, chunk)
    clean_part = lax.dynamic_slice_in_dim(clean_acts[:, 0, :], me * chunk, chunk, axis=1)
    clean_t = jnp.swapaxes(clean_part.reshape(2, half, chunk), 1, 2).astype(jnp.float32)
    recon_error = (recon_sum + bias_part[:, None] - clean_t).astype(jnp.bfloat16)
    error_a, error_b = latent_gather(recon_error, 4)
    quarter = row_count // LAYERS
    row_ids = (
        lax.axis_index("row") * row_count
        + lax.axis_index("layer") * quarter
        + jnp.arange(quarter, dtype=jnp.int32)
    )
    latent_ids = me * lat_count + jnp.arange(lat_count, dtype=jnp.int32)
    every_row = jnp.arange(all_rows, dtype=jnp.int32)
    pair_table_t = (
        (every_row[:, None] == row_ids[None, :]).astype(jnp.float32)
        - (pairing[:, None] == row_ids[None, :]).astype(jnp.float32)
    ).astype(jnp.bfloat16)
    target_hot_t = (latent_ids[:, None] == targets[None, :]).astype(jnp.bfloat16)
    margin_q = jnp.dot(target_hot_t, pair_table_t, preferred_element_type=jnp.float32)
    pre_grad_t = layer_grad_mm(
        error_a.reshape(d_model, half), error_b.reshape(d_model, half), dec_weight[0], pre_q.T, margin_q
    )
    enc4 = enc_weight[0].reshape(RING, RING, chunk, lat_count)
    total = latent_reduce_mm(enc4, pre_grad_t, 5)
    return jnp.swapaxes(total.astype(jnp.bfloat16), 1, 2).reshape(row_count, 1, chunk)


def solution(mesh):
    placed = (
        P("row", "layer", None),
        P("row", "layer", None),
        P("layer", None, "latent"),
        P("latent"),
        P("layer", "latent", None),
        P("layer", None),
        P(),
        P(),
    )
    return jax.shard_map(
        local, mesh=mesh, in_specs=placed, out_specs=P("row", "layer", "latent"), check_vma=False
    )
```

```python
import jax
import jax.numpy as jnp
from jax import lax
from jax.experimental import pallas as pl
from jax.experimental.pallas import tpu as pltpu
from jax.sharding import PartitionSpec as P

MARGIN = 16.0
MESH = pl.DeviceIdType.MESH
RING = 4
LAYERS = 4


def _latent_coords():
    me = lax.axis_index("latent")
    return me // RING, me % RING


def _greet(a, b):
    barrier = pltpu.get_barrier_semaphore()
    for k in range(1, RING):
        pl.semaphore_signal(barrier, inc=1, device_id={"latent": a * RING + (b + k) % RING}, device_id_type=MESH)
        pl.semaphore_signal(barrier, inc=1, device_id={"latent": ((a + k) % RING) * RING + b}, device_id_type=MESH)
    pl.semaphore_wait(barrier, 2 * (RING - 1))


def _copy(src, dst, send_sem, recv_sem, peer):
    return pltpu.make_async_remote_copy(
        src_ref=src, dst_ref=dst, send_sem=send_sem, recv_sem=recv_sem,
        device_id={"latent": peer}, device_id_type=MESH,
    )


def _reduce_kernel(x, out, r1a, r1b, s1a, s1b, r2a, r2b, send_sems, recv_sems):
    h = x.shape[-1] // 2
    xa = x.at[:, :, :, pl.ds(0, h)]
    xb = x.at[:, :, :, pl.ds(h, h)]
    a, b = _latent_coords()
    _greet(a, b)
    peers_z = [(b + k) % RING for k in range(1, RING)]
    peers_x = [(a + k) % RING for k in range(1, RING)]
    first = []
    for t in peers_z:
        c = _copy(xa.at[:, t], r1a.at[b], send_sems.at[0, t], recv_sems.at[0, b], a * RING + t)
        c.start()
        first.append(c)
    for t in peers_x:
        c = _copy(xb.at[t], r1b.at[a], send_sems.at[1, t], recv_sems.at[1, a], t * RING + b)
        c.start()
        first.append(c)
    for t in peers_z:
        _copy(xa.at[:, t], r1a.at[t], send_sems.at[0, t], recv_sems.at[0, t], 0).wait_recv()
    for t in peers_x:
        _copy(xb.at[t], r1b.at[t], send_sems.at[1, t], recv_sems.at[1, t], 0).wait_recv()
    sum_a = xa[:, b].astype(jnp.float32)
    for t in peers_z:
        sum_a = sum_a + r1a[t].astype(jnp.float32)
    sum_b = xb[a].astype(jnp.float32)
    for t in peers_x:
        sum_b = sum_b + r1b[t].astype(jnp.float32)
    s1a[...] = sum_a.astype(s1a.dtype)
    s1b[...] = sum_b.astype(s1b.dtype)
    second = []
    for t in peers_x:
        c = _copy(s1a.at[t], r2a.at[a], send_sems.at[2, t], recv_sems.at[2, a], t * RING + b)
        c.start()
        second.append(c)
    for t in peers_z:
        c = _copy(s1b.at[t], r2b.at[b], send_sems.at[3, t], recv_sems.at[3, b], a * RING + t)
        c.start()
        second.append(c)
    for t in peers_x:
        _copy(s1a.at[t], r2a.at[t], send_sems.at[2, t], recv_sems.at[2, t], 0).wait_recv()
    for t in peers_z:
        _copy(s1b.at[t], r2b.at[t], send_sems.at[3, t], recv_sems.at[3, t], 0).wait_recv()
    own_a = xa[a, b].astype(jnp.float32)
    for t in peers_z:
        own_a = own_a + r1a[t, a].astype(jnp.float32)
    own_b = xb[a, b].astype(jnp.float32)
    for t in peers_x:
        own_b = own_b + r1b[t, b].astype(jnp.float32)
    for t in peers_x:
        own_a = own_a + r2a[t].astype(jnp.float32)
    for t in peers_z:
        own_b = own_b + r2b[t].astype(jnp.float32)
    out[0] = own_a
    out[1] = own_b
    for c in first + second:
        c.wait_send()


def latent_reduce(x, collective_id):
    n, _, h, c = x.shape
    c = c // 2
    dt = x.dtype
    return pl.pallas_call(
        _reduce_kernel,
        out_shape=jax.ShapeDtypeStruct((2, h, c), jnp.float32),
        in_specs=[pl.BlockSpec(memory_space=pltpu.VMEM)],
        out_specs=pl.BlockSpec(memory_space=pltpu.VMEM),
        scratch_shapes=[
            pltpu.VMEM((n, n, h, c), dt),
            pltpu.VMEM((n, n, h, c), dt),
            pltpu.VMEM((n, h, c), dt),
            pltpu.VMEM((n, h, c), dt),
            pltpu.VMEM((n, h, c), dt),
            pltpu.VMEM((n, h, c), dt),
            pltpu.SemaphoreType.DMA((4, n)),
            pltpu.SemaphoreType.DMA((4, n)),
        ],
        compiler_params=pltpu.CompilerParams(collective_id=collective_id, has_side_effects=True),
    )(x)


def _reduce_mm_kernel(w, v, out, xa, xb, r1a, r1b, s1a, s1b, r2a, r2b, send_sems, recv_sems):
    a, b = _latent_coords()
    _greet(a, b)
    h = v.shape[1] // 2
    peers_z = [(b + k) % RING for k in range(1, RING)]
    peers_x = [(a + k) % RING for k in range(1, RING)]

    def fill(dst, i, j, half):
        prod = jnp.dot(w[i, j], v[:, half * h:(half + 1) * h], preferred_element_type=jnp.float32)
        dst[i, j] = prod.astype(dst.dtype)

    first = []
    for kz, kx in zip(peers_z, peers_x):
        for i in range(RING):
            fill(xa, i, kz, 0)
        c = _copy(xa.at[:, kz], r1a.at[b], send_sems.at[0, kz], recv_sems.at[0, b], a * RING + kz)
        c.start()
        first.append(c)
        for j in range(RING):
            fill(xb, kx, j, 1)
        c = _copy(xb.at[kx], r1b.at[a], send_sems.at[1, kx], recv_sems.at[1, a], kx * RING + b)
        c.start()
        first.append(c)
    for i in range(RING):
        fill(xa, i, b, 0)
    for j in range(RING):
        fill(xb, a, j, 1)
    for t in peers_z:
        _copy(xa.at[:, t], r1a.at[t], send_sems.at[0, t], recv_sems.at[0, t], 0).wait_recv()
    for t in peers_x:
        _copy(xb.at[t], r1b.at[t], send_sems.at[1, t], recv_sems.at[1, t], 0).wait_recv()
    sum_a = xa[:, b].astype(jnp.float32)
    for t in peers_z:
        sum_a = sum_a + r1a[t].astype(jnp.float32)
    sum_b = xb[a].astype(jnp.float32)
    for t in peers_x:
        sum_b = sum_b + r1b[t].astype(jnp.float32)
    s1a[...] = sum_a.astype(s1a.dtype)
    s1b[...] = sum_b.astype(s1b.dtype)
    second = []
    for t in peers_x:
        c = _copy(s1a.at[t], r2a.at[a], send_sems.at[2, t], recv_sems.at[2, a], t * RING + b)
        c.start()
        second.append(c)
    for t in peers_z:
        c = _copy(s1b.at[t], r2b.at[b], send_sems.at[3, t], recv_sems.at[3, b], a * RING + t)
        c.start()
        second.append(c)
    for t in peers_x:
        _copy(s1a.at[t], r2a.at[t], send_sems.at[2, t], recv_sems.at[2, t], 0).wait_recv()
    for t in peers_z:
        _copy(s1b.at[t], r2b.at[t], send_sems.at[3, t], recv_sems.at[3, t], 0).wait_recv()
    own_a = xa[a, b].astype(jnp.float32)
    own_b = xb[a, b].astype(jnp.float32)
    for k in range(1, RING):
        own_a = own_a + r1a[(b + k) % RING, a].astype(jnp.float32)
        own_b = own_b + r1b[(a + k) % RING, b].astype(jnp.float32)
    for k in range(1, RING):
        own_a = own_a + r2a[(a + k) % RING].astype(jnp.float32)
        own_b = own_b + r2b[(b + k) % RING].astype(jnp.float32)
    out[0] = own_a
    out[1] = own_b
    for c in first + second:
        c.wait_send()


def latent_reduce_mm(w, v, collective_id):
    n, _, d, _ = w.shape
    h = v.shape[1] // 2
    dt = w.dtype
    return pl.pallas_call(
        _reduce_mm_kernel,
        out_shape=jax.ShapeDtypeStruct((2, d, h), jnp.float32),
        in_specs=[pl.BlockSpec(memory_space=pltpu.VMEM)] * 2,
        out_specs=pl.BlockSpec(memory_space=pltpu.VMEM),
        scratch_shapes=[
            pltpu.VMEM((n, n, d, h), dt),
            pltpu.VMEM((n, n, d, h), dt),
            pltpu.VMEM((n, n, d, h), dt),
            pltpu.VMEM((n, n, d, h), dt),
            pltpu.VMEM((n, d, h), dt),
            pltpu.VMEM((n, d, h), dt),
            pltpu.VMEM((n, d, h), dt),
            pltpu.VMEM((n, d, h), dt),
            pltpu.SemaphoreType.DMA((4, n)),
            pltpu.SemaphoreType.DMA((4, n)),
        ],
        compiler_params=pltpu.CompilerParams(collective_id=collective_id, has_side_effects=True),
    )(w, v)


def _gather_kernel(e, oa, ob, g1a, g1b, ga, gb, send_sems, recv_sems):
    a, b = _latent_coords()
    _greet(a, b)
    peers_z = [(b + k) % RING for k in range(1, RING)]
    peers_x = [(a + k) % RING for k in range(1, RING)]
    first = []
    for t in peers_z:
        c = _copy(e.at[0], g1a.at[b], send_sems.at[0, t], recv_sems.at[0, b], a * RING + t)
        c.start()
        first.append(c)
    for t in peers_x:
        c = _copy(e.at[1], g1b.at[a], send_sems.at[1, t], recv_sems.at[1, a], t * RING + b)
        c.start()
        first.append(c)
    g1a[b] = e[0]
    g1b[a] = e[1]
    for t in peers_z:
        _copy(e.at[0], g1a.at[t], send_sems.at[0, t], recv_sems.at[0, t], 0).wait_recv()
    for t in peers_x:
        _copy(e.at[1], g1b.at[t], send_sems.at[1, t], recv_sems.at[1, t], 0).wait_recv()
    second = []
    for t in peers_x:
        c = _copy(g1a, ga.at[a], send_sems.at[2, t], recv_sems.at[2, a], t * RING + b)
        c.start()
        second.append(c)
    for t in peers_z:
        c = _copy(g1b, gb.at[b], send_sems.at[3, t], recv_sems.at[3, b], a * RING + t)
        c.start()
        second.append(c)
    oa[a] = g1a[...]
    for j in range(RING):
        ob[j, b] = g1b[j]
    for t in peers_x:
        _copy(g1a, ga.at[t], send_sems.at[2, t], recv_sems.at[2, t], 0).wait_recv()
        oa[t] = ga[t]
    for t in peers_z:
        _copy(g1b, gb.at[t], send_sems.at[3, t], recv_sems.at[3, t], 0).wait_recv()
        for j in range(RING):
            ob[j, t] = gb[t, j]
    for c in first + second:
        c.wait_send()


def latent_gather(e, collective_id):
    _, h, c = e.shape
    n = RING
    dt = e.dtype
    full = jax.ShapeDtypeStruct((n, n, h, c), dt)
    return pl.pallas_call(
        _gather_kernel,
        out_shape=(full, full),
        in_specs=[pl.BlockSpec(memory_space=pltpu.VMEM)],
        out_specs=(pl.BlockSpec(memory_space=pltpu.VMEM), pl.BlockSpec(memory_space=pltpu.VMEM)),
        scratch_shapes=[
            pltpu.VMEM((n, h, c), dt),
            pltpu.VMEM((n, h, c), dt),
            pltpu.VMEM((n, n, h, c), dt),
            pltpu.VMEM((n, n, h, c), dt),
            pltpu.SemaphoreType.DMA((4, n)),
            pltpu.SemaphoreType.DMA((4, n)),
        ],
        compiler_params=pltpu.CompilerParams(collective_id=collective_id, has_side_effects=True),
    )(e)


def _layer_roles():
    me = lax.axis_index("layer")
    mate = me + 1 - 2 * (me % 2)
    far = (me + 2) % LAYERS
    return me, mate, far, (mate + 2) % LAYERS


def _layer_exchange(quarter, x, out, finish, produce, ra, sb, rb, rc, rd, send_sems, recv_sems):
    me, mate, far, mate_far = _layer_roles()
    barrier = pltpu.get_barrier_semaphore()
    for p in (mate, far):
        pl.semaphore_signal(barrier, inc=1, device_id={"layer": p}, device_id_type=MESH)
    pl.semaphore_wait(barrier, 2)

    def copy(src, dst, k, p):
        return pltpu.make_async_remote_copy(
            src_ref=src, dst_ref=dst, send_sem=send_sems.at[k], recv_sem=recv_sems.at[k],
            device_id={"layer": p}, device_id_type=MESH,
        )

    produce(mate)
    produce(mate_far)
    sent = [copy(quarter(x, mate), ra.at[0], 0, mate), copy(quarter(x, mate_far), ra.at[1], 1, mate)]
    for c in sent:
        c.start()
    produce(far)
    produce(me)
    sent[0].wait_recv()
    sent[1].wait_recv()
    sb[...] = quarter(x, far)[...].astype(jnp.float32) + ra[1].astype(jnp.float32)
    step_b = copy(sb, rb, 2, far)
    step_b.start()
    own = quarter(x, me)[...].astype(jnp.float32) + ra[0].astype(jnp.float32)
    step_b.wait_recv()
    quarter(out, me)[...] = finish(own + rb[...])
    step_c = copy(quarter(out, me), rc, 3, far)
    step_c.start()
    step_c.wait_recv()
    quarter(out, far)[...] = rc[...]
    step_d = [copy(quarter(out, me), rd.at[0], 4, mate), copy(rc, rd.at[1], 5, mate)]
    for c in step_d:
        c.start()
    for c in step_d:
        c.wait_recv()
    quarter(out, mate)[...] = rd[0]
    quarter(out, mate_far)[...] = rd[1]
    for c in sent + [step_b, step_c] + step_d:
        c.wait_send()


def _row_quarter(ref, i):
    q = ref.shape[0] // LAYERS
    return ref.at[pl.ds(pl.multiple_of(i * q, q), q)]


def _lane_quarter(ref, i):
    q = ref.shape[1] // LAYERS
    return ref.at[:, pl.ds(pl.multiple_of(i * q, q), q)]


def _layer_pre_kernel(inp, w, bias, feats, pre_q, x, *scratch):
    def finish(total):
        pre = total + bias[...]
        pre_q[...] = pre
        return jnp.maximum(pre, 0.0).astype(feats.dtype)

    def produce(i):
        _row_quarter(x, i)[...] = jnp.dot(
            _row_quarter(inp, i)[...], w[...], preferred_element_type=jnp.float32
        )

    _layer_exchange(_row_quarter, x, feats, finish, produce, *scratch)


def _layer_scratch(in_q, out_q, in_dtype):
    return [
        pltpu.VMEM((2,) + in_q, in_dtype),
        pltpu.VMEM(in_q, jnp.float32),
        pltpu.VMEM(in_q, jnp.float32),
        pltpu.VMEM(out_q, jnp.bfloat16),
        pltpu.VMEM((2,) + out_q, jnp.bfloat16),
        pltpu.SemaphoreType.DMA((6,)),
        pltpu.SemaphoreType.DMA((6,)),
    ]


def layer_pre(inp, w, bias):
    rows, cols = inp.shape[0], w.shape[1]
    q = rows // LAYERS
    return pl.pallas_call(
        _layer_pre_kernel,
        out_shape=(jax.ShapeDtypeStruct((rows, cols), jnp.bfloat16),
                   jax.ShapeDtypeStruct((q, cols), jnp.float32)),
        in_specs=[pl.BlockSpec(memory_space=pltpu.VMEM)] * 3,
        out_specs=(pl.BlockSpec(memory_space=pltpu.VMEM), pl.BlockSpec(memory_space=pltpu.VMEM)),
        scratch_shapes=[pltpu.VMEM((rows, cols), jnp.float32)]
        + _layer_scratch((q, cols), (q, cols), jnp.float32),
        compiler_params=pltpu.CompilerParams(collective_id=1, has_side_effects=True),
    )(inp, w, bias)


def _layer_peers():
    me = lax.axis_index("layer")
    return me, [(me + k) % LAYERS for k in range(1, LAYERS)]


def _layer_greet(peers):
    barrier = pltpu.get_barrier_semaphore()
    for p in peers:
        pl.semaphore_signal(barrier, inc=1, device_id={"layer": p}, device_id_type=MESH)
    pl.semaphore_wait(barrier, LAYERS - 1)


def _layer_copy(src, dst, send_sems, recv_sems, k, p, slot):
    return pltpu.make_async_remote_copy(
        src_ref=src, dst_ref=dst, send_sem=send_sems.at[k, p], recv_sem=recv_sems.at[k, slot],
        device_id={"layer": p}, device_id_type=MESH,
    )


def _layer_grad_kernel(g, pre_q, margin_q, out, r1, r2, send_sems, recv_sems):
    me, peers = _layer_peers()
    q = g.shape[1] // LAYERS
    lanes = lambda i: pl.ds(pl.multiple_of(i * q, q), q)
    _layer_greet(peers)
    sent = []
    for p in peers:
        c = _layer_copy(g.at[:, lanes(p)], r1.at[me], send_sems, recv_sems, 0, p, me)
        c.start()
        sent.append(c)
    total = g[:, lanes(me)].astype(jnp.float32)
    for p in peers:
        _layer_copy(g.at[:, lanes(p)], r1.at[p], send_sems, recv_sems, 0, p, p).wait_recv()
        total = total + r1[p].astype(jnp.float32)
    grad = jnp.where(pre_q[...] > 0, total - MARGIN * margin_q[...], 0.0)
    out[:, lanes(me)] = grad.astype(out.dtype)
    for p in peers:
        c = _layer_copy(out.at[:, lanes(me)], r2.at[me], send_sems, recv_sems, 1, p, me)
        c.start()
        sent.append(c)
    for p in peers:
        _layer_copy(out.at[:, lanes(p)], r2.at[p], send_sems, recv_sems, 1, p, p).wait_recv()
        out[:, lanes(p)] = r2[p]
    for c in sent:
        c.wait_send()


def layer_grad(g, pre_q, margin_q):
    cols, rows = g.shape
    q = rows // LAYERS
    return pl.pallas_call(
        _layer_grad_kernel,
        out_shape=jax.ShapeDtypeStruct((cols, rows), jnp.bfloat16),
        in_specs=[pl.BlockSpec(memory_space=pltpu.VMEM)] * 3,
        out_specs=pl.BlockSpec(memory_space=pltpu.VMEM),
        scratch_shapes=[
            pltpu.VMEM((LAYERS, cols, q), jnp.bfloat16),
            pltpu.VMEM((LAYERS, cols, q), jnp.bfloat16),
            pltpu.SemaphoreType.DMA((2, LAYERS)),
            pltpu.SemaphoreType.DMA((2, LAYERS)),
        ],
        compiler_params=pltpu.CompilerParams(collective_id=2, has_side_effects=True),
    )(g, pre_q, margin_q)


def local(inputs, clean_acts, enc_weight, enc_bias, dec_weight, dec_bias, pairing, targets):
    row_count = inputs.shape[0]
    lat_count = enc_weight.shape[2]
    all_rows = pairing.shape[0]
    d_model = inputs.shape[2]
    chunk = d_model // (RING * RING)
    half = row_count // 2
    me = lax.axis_index("latent")
    features, pre_q = layer_pre(inputs[:, 0, :], enc_weight[0], enc_bias.reshape(1, lat_count))
    dec4 = dec_weight[0].reshape(lat_count, RING, RING, chunk)
    recon_part = jnp.einsum("rf,fabd->abdr", features, dec4, preferred_element_type=jnp.float32)
    recon_sum = latent_reduce(recon_part.astype(jnp.bfloat16), 3)
    bias_part = lax.dynamic_slice_in_dim(dec_bias[0], me * chunk, chunk)
    clean_part = lax.dynamic_slice_in_dim(clean_acts[:, 0, :], me * chunk, chunk, axis=1)
    clean_t = jnp.swapaxes(clean_part.reshape(2, half, chunk), 1, 2).astype(jnp.float32)
    recon_error = (recon_sum + bias_part[:, None] - clean_t).astype(jnp.bfloat16)
    error_a, error_b = latent_gather(recon_error, 4)
    error_all = jnp.concatenate(
        [error_a.reshape(d_model, half), error_b.reshape(d_model, half)], axis=1
    )
    partial_grad_t = jnp.dot(dec_weight[0], error_all, preferred_element_type=jnp.float32)
    quarter = row_count // LAYERS
    row_ids = (
        lax.axis_index("row") * row_count
        + lax.axis_index("layer") * quarter
        + jnp.arange(quarter, dtype=jnp.int32)
    )
    latent_ids = me * lat_count + jnp.arange(lat_count, dtype=jnp.int32)
    every_row = jnp.arange(all_rows, dtype=jnp.int32)
    pair_table_t = (
        (every_row[:, None] == row_ids[None, :]).astype(jnp.float32)
        - (pairing[:, None] == row_ids[None, :]).astype(jnp.float32)
    ).astype(jnp.bfloat16)
    target_hot_t = (latent_ids[:, None] == targets[None, :]).astype(jnp.bfloat16)
    margin_q = jnp.dot(target_hot_t, pair_table_t, preferred_element_type=jnp.float32)
    pre_grad_t = layer_grad(partial_grad_t.astype(jnp.bfloat16), pre_q.T, margin_q)
    enc4 = enc_weight[0].reshape(RING, RING, chunk, lat_count)
    total = latent_reduce_mm(enc4, pre_grad_t, 5)
    return jnp.swapaxes(total.astype(jnp.bfloat16), 1, 2).reshape(row_count, 1, chunk)


def solution(mesh):
    placed = (
        P("row", "layer", None),
        P("row", "layer", None),
        P("layer", None, "latent"),
        P("latent"),
        P("layer", "latent", None),
        P("layer", None),
        P(),
        P(),
    )
    return jax.shard_map(
        local, mesh=mesh, in_specs=placed, out_specs=P("row", "layer", "latent"), check_vma=False
    )
```

```python
import jax
import jax.numpy as jnp
from jax import lax
from jax.experimental import pallas as pl
from jax.experimental.pallas import tpu as pltpu
from jax.sharding import PartitionSpec as P

MARGIN = 16.0
MESH = pl.DeviceIdType.MESH
RING = 4
LAYERS = 4


def _latent_coords():
    me = lax.axis_index("latent")
    return me // RING, me % RING


def _greet(a, b):
    barrier = pltpu.get_barrier_semaphore()
    for k in range(1, RING):
        pl.semaphore_signal(barrier, inc=1, device_id={"latent": a * RING + (b + k) % RING}, device_id_type=MESH)
        pl.semaphore_signal(barrier, inc=1, device_id={"latent": ((a + k) % RING) * RING + b}, device_id_type=MESH)
    pl.semaphore_wait(barrier, 2 * (RING - 1))


def _copy(src, dst, send_sem, recv_sem, peer):
    return pltpu.make_async_remote_copy(
        src_ref=src, dst_ref=dst, send_sem=send_sem, recv_sem=recv_sem,
        device_id={"latent": peer}, device_id_type=MESH,
    )


def _reduce_kernel(x, out, r1a, r1b, s1a, s1b, r2a, r2b, send_sems, recv_sems):
    h = x.shape[-1] // 2
    xa = x.at[:, :, :, pl.ds(0, h)]
    xb = x.at[:, :, :, pl.ds(h, h)]
    a, b = _latent_coords()
    _greet(a, b)
    peers_z = [(b + k) % RING for k in range(1, RING)]
    peers_x = [(a + k) % RING for k in range(1, RING)]
    first = []
    for t in peers_z:
        c = _copy(xa.at[:, t], r1a.at[b], send_sems.at[0, t], recv_sems.at[0, b], a * RING + t)
        c.start()
        first.append(c)
    for t in peers_x:
        c = _copy(xb.at[t], r1b.at[a], send_sems.at[1, t], recv_sems.at[1, a], t * RING + b)
        c.start()
        first.append(c)
    for t in peers_z:
        _copy(xa.at[:, t], r1a.at[t], send_sems.at[0, t], recv_sems.at[0, t], 0).wait_recv()
    for t in peers_x:
        _copy(xb.at[t], r1b.at[t], send_sems.at[1, t], recv_sems.at[1, t], 0).wait_recv()
    sum_a = xa[:, b].astype(jnp.float32)
    for t in peers_z:
        sum_a = sum_a + r1a[t].astype(jnp.float32)
    sum_b = xb[a].astype(jnp.float32)
    for t in peers_x:
        sum_b = sum_b + r1b[t].astype(jnp.float32)
    s1a[...] = sum_a.astype(s1a.dtype)
    s1b[...] = sum_b.astype(s1b.dtype)
    second = []
    for t in peers_x:
        c = _copy(s1a.at[t], r2a.at[a], send_sems.at[2, t], recv_sems.at[2, a], t * RING + b)
        c.start()
        second.append(c)
    for t in peers_z:
        c = _copy(s1b.at[t], r2b.at[b], send_sems.at[3, t], recv_sems.at[3, b], a * RING + t)
        c.start()
        second.append(c)
    for t in peers_x:
        _copy(s1a.at[t], r2a.at[t], send_sems.at[2, t], recv_sems.at[2, t], 0).wait_recv()
    for t in peers_z:
        _copy(s1b.at[t], r2b.at[t], send_sems.at[3, t], recv_sems.at[3, t], 0).wait_recv()
    own_a = xa[a, b].astype(jnp.float32)
    for t in peers_z:
        own_a = own_a + r1a[t, a].astype(jnp.float32)
    own_b = xb[a, b].astype(jnp.float32)
    for t in peers_x:
        own_b = own_b + r1b[t, b].astype(jnp.float32)
    for t in peers_x:
        own_a = own_a + r2a[t].astype(jnp.float32)
    for t in peers_z:
        own_b = own_b + r2b[t].astype(jnp.float32)
    out[0] = own_a
    out[1] = own_b
    for c in first + second:
        c.wait_send()


def latent_reduce(x, collective_id):
    n, _, h, c = x.shape
    c = c // 2
    dt = x.dtype
    return pl.pallas_call(
        _reduce_kernel,
        out_shape=jax.ShapeDtypeStruct((2, h, c), jnp.float32),
        in_specs=[pl.BlockSpec(memory_space=pltpu.VMEM)],
        out_specs=pl.BlockSpec(memory_space=pltpu.VMEM),
        scratch_shapes=[
            pltpu.VMEM((n, n, h, c), dt),
            pltpu.VMEM((n, n, h, c), dt),
            pltpu.VMEM((n, h, c), dt),
            pltpu.VMEM((n, h, c), dt),
            pltpu.VMEM((n, h, c), dt),
            pltpu.VMEM((n, h, c), dt),
            pltpu.SemaphoreType.DMA((4, n)),
            pltpu.SemaphoreType.DMA((4, n)),
        ],
        compiler_params=pltpu.CompilerParams(collective_id=collective_id, has_side_effects=True),
    )(x)


def _reduce_mm_kernel(w, v, out, xa, xb, r1a, r1b, s1a, s1b, r2a, r2b, send_sems, recv_sems):
    a, b = _latent_coords()
    _greet(a, b)
    h = v.shape[1] // 2
    peers_z = [(b + k) % RING for k in range(1, RING)]
    peers_x = [(a + k) % RING for k in range(1, RING)]

    def fill(dst, i, j, half):
        prod = jnp.dot(w[i, j], v[:, half * h:(half + 1) * h], preferred_element_type=jnp.float32)
        dst[i, j] = prod.astype(dst.dtype)

    first = []
    for kz, kx in zip(peers_z, peers_x):
        for i in range(RING):
            fill(xa, i, kz, 0)
        c = _copy(xa.at[:, kz], r1a.at[b], send_sems.at[0, kz], recv_sems.at[0, b], a * RING + kz)
        c.start()
        first.append(c)
        for j in range(RING):
            fill(xb, kx, j, 1)
        c = _copy(xb.at[kx], r1b.at[a], send_sems.at[1, kx], recv_sems.at[1, a], kx * RING + b)
        c.start()
        first.append(c)
    for i in range(RING):
        fill(xa, i, b, 0)
    for j in range(RING):
        fill(xb, a, j, 1)
    for t in peers_z:
        _copy(xa.at[:, t], r1a.at[t], send_sems.at[0, t], recv_sems.at[0, t], 0).wait_recv()
    for t in peers_x:
        _copy(xb.at[t], r1b.at[t], send_sems.at[1, t], recv_sems.at[1, t], 0).wait_recv()
    sum_a = xa[:, b].astype(jnp.float32)
    for t in peers_z:
        sum_a = sum_a + r1a[t].astype(jnp.float32)
    sum_b = xb[a].astype(jnp.float32)
    for t in peers_x:
        sum_b = sum_b + r1b[t].astype(jnp.float32)
    s1a[...] = sum_a.astype(s1a.dtype)
    s1b[...] = sum_b.astype(s1b.dtype)
    second = []
    for t in peers_x:
        c = _copy(s1a.at[t], r2a.at[a], send_sems.at[2, t], recv_sems.at[2, a], t * RING + b)
        c.start()
        second.append(c)
    for t in peers_z:
        c = _copy(s1b.at[t], r2b.at[b], send_sems.at[3, t], recv_sems.at[3, b], a * RING + t)
        c.start()
        second.append(c)
    for t in peers_x:
        _copy(s1a.at[t], r2a.at[t], send_sems.at[2, t], recv_sems.at[2, t], 0).wait_recv()
    for t in peers_z:
        _copy(s1b.at[t], r2b.at[t], send_sems.at[3, t], recv_sems.at[3, t], 0).wait_recv()
    own_a = xa[a, b].astype(jnp.float32)
    own_b = xb[a, b].astype(jnp.float32)
    for k in range(1, RING):
        own_a = own_a + r1a[(b + k) % RING, a].astype(jnp.float32)
        own_b = own_b + r1b[(a + k) % RING, b].astype(jnp.float32)
    for k in range(1, RING):
        own_a = own_a + r2a[(a + k) % RING].astype(jnp.float32)
        own_b = own_b + r2b[(b + k) % RING].astype(jnp.float32)
    out[0] = own_a
    out[1] = own_b
    for c in first + second:
        c.wait_send()


def latent_reduce_mm(w, v, collective_id):
    n, _, d, _ = w.shape
    h = v.shape[1] // 2
    dt = w.dtype
    return pl.pallas_call(
        _reduce_mm_kernel,
        out_shape=jax.ShapeDtypeStruct((2, d, h), jnp.float32),
        in_specs=[pl.BlockSpec(memory_space=pltpu.VMEM)] * 2,
        out_specs=pl.BlockSpec(memory_space=pltpu.VMEM),
        scratch_shapes=[
            pltpu.VMEM((n, n, d, h), dt),
            pltpu.VMEM((n, n, d, h), dt),
            pltpu.VMEM((n, n, d, h), dt),
            pltpu.VMEM((n, n, d, h), dt),
            pltpu.VMEM((n, d, h), dt),
            pltpu.VMEM((n, d, h), dt),
            pltpu.VMEM((n, d, h), dt),
            pltpu.VMEM((n, d, h), dt),
            pltpu.SemaphoreType.DMA((4, n)),
            pltpu.SemaphoreType.DMA((4, n)),
        ],
        compiler_params=pltpu.CompilerParams(collective_id=collective_id, has_side_effects=True),
    )(w, v)


def _gather_kernel(e, oa, ob, g1a, g1b, ga, gb, send_sems, recv_sems):
    a, b = _latent_coords()
    _greet(a, b)
    peers_z = [(b + k) % RING for k in range(1, RING)]
    peers_x = [(a + k) % RING for k in range(1, RING)]
    first = []
    for t in peers_z:
        c = _copy(e.at[0], g1a.at[b], send_sems.at[0, t], recv_sems.at[0, b], a * RING + t)
        c.start()
        first.append(c)
    for t in peers_x:
        c = _copy(e.at[1], g1b.at[a], send_sems.at[1, t], recv_sems.at[1, a], t * RING + b)
        c.start()
        first.append(c)
    g1a[b] = e[0]
    g1b[a] = e[1]
    for t in peers_z:
        _copy(e.at[0], g1a.at[t], send_sems.at[0, t], recv_sems.at[0, t], 0).wait_recv()
    for t in peers_x:
        _copy(e.at[1], g1b.at[t], send_sems.at[1, t], recv_sems.at[1, t], 0).wait_recv()
    second = []
    for t in peers_x:
        c = _copy(g1a, ga.at[a], send_sems.at[2, t], recv_sems.at[2, a], t * RING + b)
        c.start()
        second.append(c)
    for t in peers_z:
        c = _copy(g1b, gb.at[b], send_sems.at[3, t], recv_sems.at[3, b], a * RING + t)
        c.start()
        second.append(c)
    oa[a] = g1a[...]
    for j in range(RING):
        ob[j, b] = g1b[j]
    for t in peers_x:
        _copy(g1a, ga.at[t], send_sems.at[2, t], recv_sems.at[2, t], 0).wait_recv()
        oa[t] = ga[t]
    for t in peers_z:
        _copy(g1b, gb.at[t], send_sems.at[3, t], recv_sems.at[3, t], 0).wait_recv()
        for j in range(RING):
            ob[j, t] = gb[t, j]
    for c in first + second:
        c.wait_send()


def latent_gather(e, collective_id):
    _, h, c = e.shape
    n = RING
    dt = e.dtype
    full = jax.ShapeDtypeStruct((n, n, h, c), dt)
    return pl.pallas_call(
        _gather_kernel,
        out_shape=(full, full),
        in_specs=[pl.BlockSpec(memory_space=pltpu.VMEM)],
        out_specs=(pl.BlockSpec(memory_space=pltpu.VMEM), pl.BlockSpec(memory_space=pltpu.VMEM)),
        scratch_shapes=[
            pltpu.VMEM((n, h, c), dt),
            pltpu.VMEM((n, h, c), dt),
            pltpu.VMEM((n, n, h, c), dt),
            pltpu.VMEM((n, n, h, c), dt),
            pltpu.SemaphoreType.DMA((4, n)),
            pltpu.SemaphoreType.DMA((4, n)),
        ],
        compiler_params=pltpu.CompilerParams(collective_id=collective_id, has_side_effects=True),
    )(e)


def _layer_roles():
    me = lax.axis_index("layer")
    mate = me + 1 - 2 * (me % 2)
    far = (me + 2) % LAYERS
    return me, mate, far, (mate + 2) % LAYERS


def _layer_exchange(quarter, x, out, finish, produce, ra, sb, rb, rc, rd, send_sems, recv_sems):
    me, mate, far, mate_far = _layer_roles()
    barrier = pltpu.get_barrier_semaphore()
    for p in (mate, far):
        pl.semaphore_signal(barrier, inc=1, device_id={"layer": p}, device_id_type=MESH)
    pl.semaphore_wait(barrier, 2)

    def copy(src, dst, k, p):
        return pltpu.make_async_remote_copy(
            src_ref=src, dst_ref=dst, send_sem=send_sems.at[k], recv_sem=recv_sems.at[k],
            device_id={"layer": p}, device_id_type=MESH,
        )

    produce(mate)
    produce(mate_far)
    sent = [copy(quarter(x, mate), ra.at[0], 0, mate), copy(quarter(x, mate_far), ra.at[1], 1, mate)]
    for c in sent:
        c.start()
    produce(far)
    produce(me)
    sent[0].wait_recv()
    sent[1].wait_recv()
    sb[...] = quarter(x, far)[...].astype(jnp.float32) + ra[1].astype(jnp.float32)
    step_b = copy(sb, rb, 2, far)
    step_b.start()
    own = quarter(x, me)[...].astype(jnp.float32) + ra[0].astype(jnp.float32)
    step_b.wait_recv()
    quarter(out, me)[...] = finish(own + rb[...])
    step_c = copy(quarter(out, me), rc, 3, far)
    step_c.start()
    step_c.wait_recv()
    quarter(out, far)[...] = rc[...]
    step_d = [copy(quarter(out, me), rd.at[0], 4, mate), copy(rc, rd.at[1], 5, mate)]
    for c in step_d:
        c.start()
    for c in step_d:
        c.wait_recv()
    quarter(out, mate)[...] = rd[0]
    quarter(out, mate_far)[...] = rd[1]
    for c in sent + [step_b, step_c] + step_d:
        c.wait_send()


def _row_quarter(ref, i):
    q = ref.shape[0] // LAYERS
    return ref.at[pl.ds(pl.multiple_of(i * q, q), q)]


def _lane_quarter(ref, i):
    q = ref.shape[1] // LAYERS
    return ref.at[:, pl.ds(pl.multiple_of(i * q, q), q)]


def _layer_pre_kernel(inp, w, bias, feats, pre_q, x, *scratch):
    def finish(total):
        pre = total + bias[...]
        pre_q[...] = pre
        return jnp.maximum(pre, 0.0).astype(feats.dtype)

    def produce(i):
        _row_quarter(x, i)[...] = jnp.dot(
            _row_quarter(inp, i)[...], w[...], preferred_element_type=jnp.float32
        )

    _layer_exchange(_row_quarter, x, feats, finish, produce, *scratch)


def _layer_scratch(in_q, out_q, in_dtype):
    return [
        pltpu.VMEM((2,) + in_q, in_dtype),
        pltpu.VMEM(in_q, jnp.float32),
        pltpu.VMEM(in_q, jnp.float32),
        pltpu.VMEM(out_q, jnp.bfloat16),
        pltpu.VMEM((2,) + out_q, jnp.bfloat16),
        pltpu.SemaphoreType.DMA((6,)),
        pltpu.SemaphoreType.DMA((6,)),
    ]


def layer_pre(inp, w, bias):
    rows, cols = inp.shape[0], w.shape[1]
    q = rows // LAYERS
    return pl.pallas_call(
        _layer_pre_kernel,
        out_shape=(jax.ShapeDtypeStruct((rows, cols), jnp.bfloat16),
                   jax.ShapeDtypeStruct((q, cols), jnp.float32)),
        in_specs=[pl.BlockSpec(memory_space=pltpu.VMEM)] * 3,
        out_specs=(pl.BlockSpec(memory_space=pltpu.VMEM), pl.BlockSpec(memory_space=pltpu.VMEM)),
        scratch_shapes=[pltpu.VMEM((rows, cols), jnp.float32)]
        + _layer_scratch((q, cols), (q, cols), jnp.float32),
        compiler_params=pltpu.CompilerParams(collective_id=1, has_side_effects=True),
    )(inp, w, bias)


def _layer_peers():
    me = lax.axis_index("layer")
    return me, [(me + k) % LAYERS for k in range(1, LAYERS)]


def _layer_greet(peers):
    barrier = pltpu.get_barrier_semaphore()
    for p in peers:
        pl.semaphore_signal(barrier, inc=1, device_id={"layer": p}, device_id_type=MESH)
    pl.semaphore_wait(barrier, LAYERS - 1)


def _layer_copy(src, dst, send_sems, recv_sems, k, p, slot):
    return pltpu.make_async_remote_copy(
        src_ref=src, dst_ref=dst, send_sem=send_sems.at[k, p], recv_sem=recv_sems.at[k, slot],
        device_id={"layer": p}, device_id_type=MESH,
    )


def _layer_grad_kernel(g, pre_q, margin_q, out, r1, r2, send_sems, recv_sems):
    me, peers = _layer_peers()
    q = g.shape[1] // LAYERS
    lanes = lambda i: pl.ds(pl.multiple_of(i * q, q), q)
    _layer_greet(peers)
    sent = []
    for p in peers:
        c = _layer_copy(g.at[:, lanes(p)], r1.at[me], send_sems, recv_sems, 0, p, me)
        c.start()
        sent.append(c)
    total = g[:, lanes(me)].astype(jnp.float32)
    for p in peers:
        _layer_copy(g.at[:, lanes(p)], r1.at[p], send_sems, recv_sems, 0, p, p).wait_recv()
        total = total + r1[p].astype(jnp.float32)
    grad = jnp.where(pre_q[...] > 0, total - MARGIN * margin_q[...], 0.0)
    out[:, lanes(me)] = grad.astype(out.dtype)
    for p in peers:
        c = _layer_copy(out.at[:, lanes(me)], r2.at[me], send_sems, recv_sems, 1, p, me)
        c.start()
        sent.append(c)
    for p in peers:
        _layer_copy(out.at[:, lanes(p)], r2.at[p], send_sems, recv_sems, 1, p, p).wait_recv()
        out[:, lanes(p)] = r2[p]
    for c in sent:
        c.wait_send()


def layer_grad(g, pre_q, margin_q):
    cols, rows = g.shape
    q = rows // LAYERS
    return pl.pallas_call(
        _layer_grad_kernel,
        out_shape=jax.ShapeDtypeStruct((cols, rows), jnp.bfloat16),
        in_specs=[pl.BlockSpec(memory_space=pltpu.VMEM)] * 3,
        out_specs=pl.BlockSpec(memory_space=pltpu.VMEM),
        scratch_shapes=[
            pltpu.VMEM((LAYERS, cols, q), jnp.bfloat16),
            pltpu.VMEM((LAYERS, cols, q), jnp.bfloat16),
            pltpu.SemaphoreType.DMA((2, LAYERS)),
            pltpu.SemaphoreType.DMA((2, LAYERS)),
        ],
        compiler_params=pltpu.CompilerParams(collective_id=2, has_side_effects=True),
    )(g, pre_q, margin_q)


def local(inputs, clean_acts, enc_weight, enc_bias, dec_weight, dec_bias, pairing, targets):
    row_count = inputs.shape[0]
    lat_count = enc_weight.shape[2]
    all_rows = pairing.shape[0]
    d_model = inputs.shape[2]
    chunk = d_model // (RING * RING)
    half = row_count // 2
    me = lax.axis_index("latent")
    features, pre_q = layer_pre(inputs[:, 0, :], enc_weight[0], enc_bias.reshape(1, lat_count))
    dec4 = dec_weight[0].reshape(lat_count, RING, RING, chunk)
    recon_part = jnp.einsum("rf,fabd->abdr", features, dec4, preferred_element_type=jnp.bfloat16)
    recon_sum = latent_reduce(recon_part, 3)
    bias_part = lax.dynamic_slice_in_dim(dec_bias[0], me * chunk, chunk)
    clean_part = lax.dynamic_slice_in_dim(clean_acts[:, 0, :], me * chunk, chunk, axis=1)
    clean_t = jnp.swapaxes(clean_part.reshape(2, half, chunk), 1, 2).astype(jnp.float32)
    recon_error = (recon_sum + bias_part[:, None] - clean_t).astype(jnp.bfloat16)
    error_a, error_b = latent_gather(recon_error, 4)
    error_all = jnp.concatenate(
        [error_a.reshape(d_model, half), error_b.reshape(d_model, half)], axis=1
    )
    partial_grad_t = jnp.dot(dec_weight[0], error_all, preferred_element_type=jnp.float32)
    quarter = row_count // LAYERS
    row_ids = (
        lax.axis_index("row") * row_count
        + lax.axis_index("layer") * quarter
        + jnp.arange(quarter, dtype=jnp.int32)
    )
    latent_ids = me * lat_count + jnp.arange(lat_count, dtype=jnp.int32)
    every_row = jnp.arange(all_rows, dtype=jnp.int32)
    pair_table_t = (
        (every_row[:, None] == row_ids[None, :]).astype(jnp.float32)
        - (pairing[:, None] == row_ids[None, :]).astype(jnp.float32)
    ).astype(jnp.bfloat16)
    target_hot_t = (latent_ids[:, None] == targets[None, :]).astype(jnp.bfloat16)
    margin_q = jnp.dot(target_hot_t, pair_table_t, preferred_element_type=jnp.float32)
    pre_grad_t = layer_grad(partial_grad_t.astype(jnp.bfloat16), pre_q.T, margin_q)
    enc4 = enc_weight[0].reshape(RING, RING, chunk, lat_count)
    total = latent_reduce_mm(enc4, pre_grad_t, 5)
    return jnp.swapaxes(total.astype(jnp.bfloat16), 1, 2).reshape(row_count, 1, chunk)


def solution(mesh):
    placed = (
        P("row", "layer", None),
        P("row", "layer", None),
        P("layer", None, "latent"),
        P("latent"),
        P("layer", "latent", None),
        P("layer", None),
        P(),
        P(),
    )
    return jax.shard_map(
        local, mesh=mesh, in_specs=placed, out_specs=P("row", "layer", "latent"), check_vma=False
    )
```

```python
import jax
import jax.numpy as jnp
from jax import lax
from jax.experimental import pallas as pl
from jax.experimental.pallas import tpu as pltpu
from jax.sharding import PartitionSpec as P

MARGIN = 16.0
MESH = pl.DeviceIdType.MESH
RING = 4
LAYERS = 4


def _latent_coords():
    me = lax.axis_index("latent")
    return me // RING, me % RING


def _greet(a, b):
    barrier = pltpu.get_barrier_semaphore()
    for k in range(1, RING):
        pl.semaphore_signal(barrier, inc=1, device_id={"latent": a * RING + (b + k) % RING}, device_id_type=MESH)
        pl.semaphore_signal(barrier, inc=1, device_id={"latent": ((a + k) % RING) * RING + b}, device_id_type=MESH)
    pl.semaphore_wait(barrier, 2 * (RING - 1))


def _copy(src, dst, send_sem, recv_sem, peer):
    return pltpu.make_async_remote_copy(
        src_ref=src, dst_ref=dst, send_sem=send_sem, recv_sem=recv_sem,
        device_id={"latent": peer}, device_id_type=MESH,
    )


def _reduce_kernel(x, out, r1a, r1b, s1a, s1b, r2a, r2b, send_sems, recv_sems):
    h = x.shape[-1] // 2
    xa = x.at[:, :, :, pl.ds(0, h)]
    xb = x.at[:, :, :, pl.ds(h, h)]
    a, b = _latent_coords()
    _greet(a, b)
    peers_z = [(b + k) % RING for k in range(1, RING)]
    peers_x = [(a + k) % RING for k in range(1, RING)]
    first = []
    for t in peers_z:
        c = _copy(xa.at[:, t], r1a.at[b], send_sems.at[0, t], recv_sems.at[0, b], a * RING + t)
        c.start()
        first.append(c)
    for t in peers_x:
        c = _copy(xb.at[t], r1b.at[a], send_sems.at[1, t], recv_sems.at[1, a], t * RING + b)
        c.start()
        first.append(c)
    for t in peers_z:
        _copy(xa.at[:, t], r1a.at[t], send_sems.at[0, t], recv_sems.at[0, t], 0).wait_recv()
    for t in peers_x:
        _copy(xb.at[t], r1b.at[t], send_sems.at[1, t], recv_sems.at[1, t], 0).wait_recv()
    sum_a = xa[:, b].astype(jnp.float32)
    for t in peers_z:
        sum_a = sum_a + r1a[t].astype(jnp.float32)
    sum_b = xb[a].astype(jnp.float32)
    for t in peers_x:
        sum_b = sum_b + r1b[t].astype(jnp.float32)
    s1a[...] = sum_a.astype(s1a.dtype)
    s1b[...] = sum_b.astype(s1b.dtype)
    second = []
    for t in peers_x:
        c = _copy(s1a.at[t], r2a.at[a], send_sems.at[2, t], recv_sems.at[2, a], t * RING + b)
        c.start()
        second.append(c)
    for t in peers_z:
        c = _copy(s1b.at[t], r2b.at[b], send_sems.at[3, t], recv_sems.at[3, b], a * RING + t)
        c.start()
        second.append(c)
    for t in peers_x:
        _copy(s1a.at[t], r2a.at[t], send_sems.at[2, t], recv_sems.at[2, t], 0).wait_recv()
    for t in peers_z:
        _copy(s1b.at[t], r2b.at[t], send_sems.at[3, t], recv_sems.at[3, t], 0).wait_recv()
    own_a = xa[a, b].astype(jnp.float32)
    for t in peers_z:
        own_a = own_a + r1a[t, a].astype(jnp.float32)
    own_b = xb[a, b].astype(jnp.float32)
    for t in peers_x:
        own_b = own_b + r1b[t, b].astype(jnp.float32)
    for t in peers_x:
        own_a = own_a + r2a[t].astype(jnp.float32)
    for t in peers_z:
        own_b = own_b + r2b[t].astype(jnp.float32)
    out[0] = own_a
    out[1] = own_b
    for c in first + second:
        c.wait_send()


def latent_reduce(x, collective_id):
    n, _, h, c = x.shape
    c = c // 2
    dt = x.dtype
    return pl.pallas_call(
        _reduce_kernel,
        out_shape=jax.ShapeDtypeStruct((2, h, c), jnp.float32),
        in_specs=[pl.BlockSpec(memory_space=pltpu.VMEM)],
        out_specs=pl.BlockSpec(memory_space=pltpu.VMEM),
        scratch_shapes=[
            pltpu.VMEM((n, n, h, c), dt),
            pltpu.VMEM((n, n, h, c), dt),
            pltpu.VMEM((n, h, c), dt),
            pltpu.VMEM((n, h, c), dt),
            pltpu.VMEM((n, h, c), dt),
            pltpu.VMEM((n, h, c), dt),
            pltpu.SemaphoreType.DMA((4, n)),
            pltpu.SemaphoreType.DMA((4, n)),
        ],
        compiler_params=pltpu.CompilerParams(collective_id=collective_id, has_side_effects=True),
    )(x)


def _reduce_mm_kernel(w, v, out, xa, xb, r1a, r1b, s1a, s1b, r2a, r2b, send_sems, recv_sems):
    a, b = _latent_coords()
    _greet(a, b)
    h = v.shape[1] // 2
    peers_z = [(b + k) % RING for k in range(1, RING)]
    peers_x = [(a + k) % RING for k in range(1, RING)]

    def fill(dst, i, j, half):
        prod = jnp.dot(w[i, j], v[:, half * h:(half + 1) * h], preferred_element_type=jnp.float32)
        dst[i, j] = prod.astype(dst.dtype)

    first = []
    for kz, kx in zip(peers_z, peers_x):
        for i in range(RING):
            fill(xa, i, kz, 0)
        c = _copy(xa.at[:, kz], r1a.at[b], send_sems.at[0, kz], recv_sems.at[0, b], a * RING + kz)
        c.start()
        first.append(c)
        for j in range(RING):
            fill(xb, kx, j, 1)
        c = _copy(xb.at[kx], r1b.at[a], send_sems.at[1, kx], recv_sems.at[1, a], kx * RING + b)
        c.start()
        first.append(c)
    for i in range(RING):
        fill(xa, i, b, 0)
    for j in range(RING):
        fill(xb, a, j, 1)
    for t in peers_z:
        _copy(xa.at[:, t], r1a.at[t], send_sems.at[0, t], recv_sems.at[0, t], 0).wait_recv()
    for t in peers_x:
        _copy(xb.at[t], r1b.at[t], send_sems.at[1, t], recv_sems.at[1, t], 0).wait_recv()
    sum_a = xa[:, b].astype(jnp.float32)
    for t in peers_z:
        sum_a = sum_a + r1a[t].astype(jnp.float32)
    sum_b = xb[a].astype(jnp.float32)
    for t in peers_x:
        sum_b = sum_b + r1b[t].astype(jnp.float32)
    s1a[...] = sum_a.astype(s1a.dtype)
    s1b[...] = sum_b.astype(s1b.dtype)
    second = []
    for t in peers_x:
        c = _copy(s1a.at[t], r2a.at[a], send_sems.at[2, t], recv_sems.at[2, a], t * RING + b)
        c.start()
        second.append(c)
    for t in peers_z:
        c = _copy(s1b.at[t], r2b.at[b], send_sems.at[3, t], recv_sems.at[3, b], a * RING + t)
        c.start()
        second.append(c)
    for t in peers_x:
        _copy(s1a.at[t], r2a.at[t], send_sems.at[2, t], recv_sems.at[2, t], 0).wait_recv()
    for t in peers_z:
        _copy(s1b.at[t], r2b.at[t], send_sems.at[3, t], recv_sems.at[3, t], 0).wait_recv()
    own_a = xa[a, b].astype(jnp.float32)
    own_b = xb[a, b].astype(jnp.float32)
    for k in range(1, RING):
        own_a = own_a + r1a[(b + k) % RING, a].astype(jnp.float32)
        own_b = own_b + r1b[(a + k) % RING, b].astype(jnp.float32)
    for k in range(1, RING):
        own_a = own_a + r2a[(a + k) % RING].astype(jnp.float32)
        own_b = own_b + r2b[(b + k) % RING].astype(jnp.float32)
    out[0] = own_a
    out[1] = own_b
    for c in first + second:
        c.wait_send()


def latent_reduce_mm(w, v, collective_id):
    n, _, d, _ = w.shape
    h = v.shape[1] // 2
    dt = w.dtype
    return pl.pallas_call(
        _reduce_mm_kernel,
        out_shape=jax.ShapeDtypeStruct((2, d, h), jnp.float32),
        in_specs=[pl.BlockSpec(memory_space=pltpu.VMEM)] * 2,
        out_specs=pl.BlockSpec(memory_space=pltpu.VMEM),
        scratch_shapes=[
            pltpu.VMEM((n, n, d, h), dt),
            pltpu.VMEM((n, n, d, h), dt),
            pltpu.VMEM((n, n, d, h), dt),
            pltpu.VMEM((n, n, d, h), dt),
            pltpu.VMEM((n, d, h), dt),
            pltpu.VMEM((n, d, h), dt),
            pltpu.VMEM((n, d, h), dt),
            pltpu.VMEM((n, d, h), dt),
            pltpu.SemaphoreType.DMA((4, n)),
            pltpu.SemaphoreType.DMA((4, n)),
        ],
        compiler_params=pltpu.CompilerParams(collective_id=collective_id, has_side_effects=True),
    )(w, v)


def _gather_kernel(e, oa, ob, g1a, g1b, ga, gb, send_sems, recv_sems):
    a, b = _latent_coords()
    _greet(a, b)
    peers_z = [(b + k) % RING for k in range(1, RING)]
    peers_x = [(a + k) % RING for k in range(1, RING)]
    first = []
    for t in peers_z:
        c = _copy(e.at[0], g1a.at[b], send_sems.at[0, t], recv_sems.at[0, b], a * RING + t)
        c.start()
        first.append(c)
    for t in peers_x:
        c = _copy(e.at[1], g1b.at[a], send_sems.at[1, t], recv_sems.at[1, a], t * RING + b)
        c.start()
        first.append(c)
    g1a[b] = e[0]
    g1b[a] = e[1]
    for t in peers_z:
        _copy(e.at[0], g1a.at[t], send_sems.at[0, t], recv_sems.at[0, t], 0).wait_recv()
    for t in peers_x:
        _copy(e.at[1], g1b.at[t], send_sems.at[1, t], recv_sems.at[1, t], 0).wait_recv()
    second = []
    for t in peers_x:
        c = _copy(g1a, ga.at[a], send_sems.at[2, t], recv_sems.at[2, a], t * RING + b)
        c.start()
        second.append(c)
    for t in peers_z:
        c = _copy(g1b, gb.at[b], send_sems.at[3, t], recv_sems.at[3, b], a * RING + t)
        c.start()
        second.append(c)
    oa[a] = g1a[...]
    for j in range(RING):
        ob[j, b] = g1b[j]
    for t in peers_x:
        _copy(g1a, ga.at[t], send_sems.at[2, t], recv_sems.at[2, t], 0).wait_recv()
        oa[t] = ga[t]
    for t in peers_z:
        _copy(g1b, gb.at[t], send_sems.at[3, t], recv_sems.at[3, t], 0).wait_recv()
        for j in range(RING):
            ob[j, t] = gb[t, j]
    for c in first + second:
        c.wait_send()


def latent_gather(e, collective_id):
    _, h, c = e.shape
    n = RING
    dt = e.dtype
    full = jax.ShapeDtypeStruct((n, n, h, c), dt)
    return pl.pallas_call(
        _gather_kernel,
        out_shape=(full, full),
        in_specs=[pl.BlockSpec(memory_space=pltpu.VMEM)],
        out_specs=(pl.BlockSpec(memory_space=pltpu.VMEM), pl.BlockSpec(memory_space=pltpu.VMEM)),
        scratch_shapes=[
            pltpu.VMEM((n, h, c), dt),
            pltpu.VMEM((n, h, c), dt),
            pltpu.VMEM((n, n, h, c), dt),
            pltpu.VMEM((n, n, h, c), dt),
            pltpu.SemaphoreType.DMA((4, n)),
            pltpu.SemaphoreType.DMA((4, n)),
        ],
        compiler_params=pltpu.CompilerParams(collective_id=collective_id, has_side_effects=True),
    )(e)


def _layer_roles():
    me = lax.axis_index("layer")
    mate = me + 1 - 2 * (me % 2)
    far = (me + 2) % LAYERS
    return me, mate, far, (mate + 2) % LAYERS


def _layer_exchange(quarter, x, out, finish, produce, ra, sb, rb, rc, rd, send_sems, recv_sems):
    me, mate, far, mate_far = _layer_roles()
    barrier = pltpu.get_barrier_semaphore()
    for p in (mate, far):
        pl.semaphore_signal(barrier, inc=1, device_id={"layer": p}, device_id_type=MESH)
    pl.semaphore_wait(barrier, 2)

    def copy(src, dst, k, p):
        return pltpu.make_async_remote_copy(
            src_ref=src, dst_ref=dst, send_sem=send_sems.at[k], recv_sem=recv_sems.at[k],
            device_id={"layer": p}, device_id_type=MESH,
        )

    produce(mate)
    produce(mate_far)
    sent = [copy(quarter(x, mate), ra.at[0], 0, mate), copy(quarter(x, mate_far), ra.at[1], 1, mate)]
    for c in sent:
        c.start()
    produce(far)
    produce(me)
    sent[0].wait_recv()
    sent[1].wait_recv()
    sb[...] = quarter(x, far)[...].astype(jnp.float32) + ra[1].astype(jnp.float32)
    step_b = copy(sb, rb, 2, far)
    step_b.start()
    own = quarter(x, me)[...].astype(jnp.float32) + ra[0].astype(jnp.float32)
    step_b.wait_recv()
    quarter(out, me)[...] = finish(own + rb[...])
    step_c = copy(quarter(out, me), rc, 3, far)
    step_c.start()
    step_c.wait_recv()
    quarter(out, far)[...] = rc[...]
    step_d = [copy(quarter(out, me), rd.at[0], 4, mate), copy(rc, rd.at[1], 5, mate)]
    for c in step_d:
        c.start()
    for c in step_d:
        c.wait_recv()
    quarter(out, mate)[...] = rd[0]
    quarter(out, mate_far)[...] = rd[1]
    for c in sent + [step_b, step_c] + step_d:
        c.wait_send()


def _row_quarter(ref, i):
    q = ref.shape[0] // LAYERS
    return ref.at[pl.ds(pl.multiple_of(i * q, q), q)]


def _lane_quarter(ref, i):
    q = ref.shape[1] // LAYERS
    return ref.at[:, pl.ds(pl.multiple_of(i * q, q), q)]


def _layer_pre_kernel(inp, w, bias, feats, pre_q, x, *scratch):
    def finish(total):
        pre = total + bias[...].reshape(1, -1)
        pre_q[...] = pre
        return jnp.maximum(pre, 0.0).astype(feats.dtype)

    def produce(i):
        _row_quarter(x, i)[...] = jnp.dot(
            _row_quarter(inp, i)[...], w[...], preferred_element_type=jnp.float32
        )

    _layer_exchange(_row_quarter, x, feats, finish, produce, *scratch)


def _layer_scratch(in_q, out_q, in_dtype):
    return [
        pltpu.VMEM((2,) + in_q, in_dtype),
        pltpu.VMEM(in_q, jnp.float32),
        pltpu.VMEM(in_q, jnp.float32),
        pltpu.VMEM(out_q, jnp.bfloat16),
        pltpu.VMEM((2,) + out_q, jnp.bfloat16),
        pltpu.SemaphoreType.DMA((6,)),
        pltpu.SemaphoreType.DMA((6,)),
    ]


def layer_pre(inp, w, bias):
    rows, cols = inp.shape[0], w.shape[1]
    q = rows // LAYERS
    return pl.pallas_call(
        _layer_pre_kernel,
        out_shape=(jax.ShapeDtypeStruct((rows, cols), jnp.bfloat16),
                   jax.ShapeDtypeStruct((q, cols), jnp.float32)),
        in_specs=[pl.BlockSpec(memory_space=pltpu.VMEM)] * 3,
        out_specs=(pl.BlockSpec(memory_space=pltpu.VMEM), pl.BlockSpec(memory_space=pltpu.VMEM)),
        scratch_shapes=[pltpu.VMEM((rows, cols), jnp.float32)]
        + _layer_scratch((q, cols), (q, cols), jnp.float32),
        compiler_params=pltpu.CompilerParams(collective_id=1, has_side_effects=True),
    )(inp, w, bias)


def _layer_peers():
    me = lax.axis_index("layer")
    return me, [(me + k) % LAYERS for k in range(1, LAYERS)]


def _layer_greet(peers):
    barrier = pltpu.get_barrier_semaphore()
    for p in peers:
        pl.semaphore_signal(barrier, inc=1, device_id={"layer": p}, device_id_type=MESH)
    pl.semaphore_wait(barrier, LAYERS - 1)


def _layer_copy(src, dst, send_sems, recv_sems, k, p, slot):
    return pltpu.make_async_remote_copy(
        src_ref=src, dst_ref=dst, send_sem=send_sems.at[k, p], recv_sem=recv_sems.at[k, slot],
        device_id={"layer": p}, device_id_type=MESH,
    )


def _layer_grad_kernel(g, pre_q, margin_q, out, r1, r2, send_sems, recv_sems):
    me, peers = _layer_peers()
    q = g.shape[1] // LAYERS
    lanes = lambda i: pl.ds(pl.multiple_of(i * q, q), q)
    _layer_greet(peers)
    sent = []
    for p in peers:
        c = _layer_copy(g.at[:, lanes(p)], r1.at[me], send_sems, recv_sems, 0, p, me)
        c.start()
        sent.append(c)
    total = g[:, lanes(me)].astype(jnp.float32)
    for p in peers:
        _layer_copy(g.at[:, lanes(p)], r1.at[p], send_sems, recv_sems, 0, p, p).wait_recv()
        total = total + r1[p].astype(jnp.float32)
    grad = jnp.where(pre_q[...] > 0, total - MARGIN * margin_q[...], 0.0)
    out[:, lanes(me)] = grad.astype(out.dtype)
    for p in peers:
        c = _layer_copy(out.at[:, lanes(me)], r2.at[me], send_sems, recv_sems, 1, p, me)
        c.start()
        sent.append(c)
    for p in peers:
        _layer_copy(out.at[:, lanes(p)], r2.at[p], send_sems, recv_sems, 1, p, p).wait_recv()
        out[:, lanes(p)] = r2[p]
    for c in sent:
        c.wait_send()


def layer_grad(g, pre_q, margin_q):
    cols, rows = g.shape
    q = rows // LAYERS
    return pl.pallas_call(
        _layer_grad_kernel,
        out_shape=jax.ShapeDtypeStruct((cols, rows), jnp.bfloat16),
        in_specs=[pl.BlockSpec(memory_space=pltpu.VMEM)] * 3,
        out_specs=pl.BlockSpec(memory_space=pltpu.VMEM),
        scratch_shapes=[
            pltpu.VMEM((LAYERS, cols, q), jnp.bfloat16),
            pltpu.VMEM((LAYERS, cols, q), jnp.bfloat16),
            pltpu.SemaphoreType.DMA((2, LAYERS)),
            pltpu.SemaphoreType.DMA((2, LAYERS)),
        ],
        compiler_params=pltpu.CompilerParams(collective_id=2, has_side_effects=True),
    )(g, pre_q, margin_q)


def local(inputs, clean_acts, enc_weight, enc_bias, dec_weight, dec_bias, pairing, targets):
    row_count = inputs.shape[0]
    lat_count = enc_weight.shape[2]
    all_rows = pairing.shape[0]
    d_model = inputs.shape[2]
    chunk = d_model // (RING * RING)
    half = row_count // 2
    me = lax.axis_index("latent")
    features, pre_q = layer_pre(inputs[:, 0, :], enc_weight[0], enc_bias)
    dec4 = dec_weight[0].reshape(lat_count, RING, RING, chunk)
    recon_part = jnp.einsum("rf,fabd->abdr", features, dec4, preferred_element_type=jnp.float32)
    recon_sum = latent_reduce(recon_part.astype(jnp.bfloat16), 3)
    bias_part = lax.dynamic_slice_in_dim(dec_bias[0], me * chunk, chunk)
    clean_part = lax.dynamic_slice_in_dim(clean_acts[:, 0, :], me * chunk, chunk, axis=1)
    clean_t = jnp.swapaxes(clean_part.reshape(2, half, chunk), 1, 2).astype(jnp.float32)
    recon_error = (recon_sum + bias_part[:, None] - clean_t).astype(jnp.bfloat16)
    error_a, error_b = latent_gather(recon_error, 4)
    error_all = jnp.concatenate(
        [error_a.reshape(d_model, half), error_b.reshape(d_model, half)], axis=1
    )
    partial_grad_t = jnp.dot(dec_weight[0], error_all, preferred_element_type=jnp.float32)
    quarter = row_count // LAYERS
    row_ids = (
        lax.axis_index("row") * row_count
        + lax.axis_index("layer") * quarter
        + jnp.arange(quarter, dtype=jnp.int32)
    )
    latent_ids = me * lat_count + jnp.arange(lat_count, dtype=jnp.int32)
    every_row = jnp.arange(all_rows, dtype=jnp.int32)
    pair_table_t = (
        (every_row[:, None] == row_ids[None, :]).astype(jnp.float32)
        - (pairing[:, None] == row_ids[None, :]).astype(jnp.float32)
    ).astype(jnp.bfloat16)
    target_hot_t = (latent_ids[:, None] == targets[None, :]).astype(jnp.bfloat16)
    margin_q = jnp.dot(target_hot_t, pair_table_t, preferred_element_type=jnp.float32)
    pre_grad_t = layer_grad(partial_grad_t.astype(jnp.bfloat16), pre_q.T, margin_q)
    enc4 = enc_weight[0].reshape(RING, RING, chunk, lat_count)
    total = latent_reduce_mm(enc4, pre_grad_t, 5)
    return jnp.swapaxes(total.astype(jnp.bfloat16), 1, 2).reshape(row_count, 1, chunk)


def solution(mesh):
    placed = (
        P("row", "layer", None),
        P("row", "layer", None),
        P("layer", None, "latent"),
        P("latent"),
        P("layer", "latent", None),
        P("layer", None),
        P(),
        P(),
    )
    return jax.shard_map(
        local, mesh=mesh, in_specs=placed, out_specs=P("row", "layer", "latent"), check_vma=False
    )
```

```python
import jax
import jax.numpy as jnp
from jax import lax
from jax.experimental import pallas as pl
from jax.experimental.pallas import tpu as pltpu
from jax.sharding import PartitionSpec as P

MARGIN = 16.0
MESH = pl.DeviceIdType.MESH
RING = 4
LAYERS = 4


def _latent_coords():
    me = lax.axis_index("latent")
    return me // RING, me % RING


def _greet(a, b):
    barrier = pltpu.get_barrier_semaphore()
    for k in range(1, RING):
        pl.semaphore_signal(barrier, inc=1, device_id={"latent": a * RING + (b + k) % RING}, device_id_type=MESH)
        pl.semaphore_signal(barrier, inc=1, device_id={"latent": ((a + k) % RING) * RING + b}, device_id_type=MESH)
    pl.semaphore_wait(barrier, 2 * (RING - 1))


def _copy(src, dst, send_sem, recv_sem, peer):
    return pltpu.make_async_remote_copy(
        src_ref=src, dst_ref=dst, send_sem=send_sem, recv_sem=recv_sem,
        device_id={"latent": peer}, device_id_type=MESH,
    )


def _reduce_kernel(x, out, r1a, r1b, s1a, s1b, r2a, r2b, send_sems, recv_sems):
    h = x.shape[-1] // 2
    xa = x.at[:, :, :, pl.ds(0, h)]
    xb = x.at[:, :, :, pl.ds(h, h)]
    a, b = _latent_coords()
    _greet(a, b)
    peers_z = [(b + k) % RING for k in range(1, RING)]
    peers_x = [(a + k) % RING for k in range(1, RING)]
    first = []
    for t in peers_z:
        c = _copy(xa.at[:, t], r1a.at[b], send_sems.at[0, t], recv_sems.at[0, b], a * RING + t)
        c.start()
        first.append(c)
    for t in peers_x:
        c = _copy(xb.at[t], r1b.at[a], send_sems.at[1, t], recv_sems.at[1, a], t * RING + b)
        c.start()
        first.append(c)
    for t in peers_z:
        _copy(xa.at[:, t], r1a.at[t], send_sems.at[0, t], recv_sems.at[0, t], 0).wait_recv()
    for t in peers_x:
        _copy(xb.at[t], r1b.at[t], send_sems.at[1, t], recv_sems.at[1, t], 0).wait_recv()
    sum_a = xa[:, b].astype(jnp.float32)
    for t in peers_z:
        sum_a = sum_a + r1a[t].astype(jnp.float32)
    sum_b = xb[a].astype(jnp.float32)
    for t in peers_x:
        sum_b = sum_b + r1b[t].astype(jnp.float32)
    s1a[...] = sum_a.astype(s1a.dtype)
    s1b[...] = sum_b.astype(s1b.dtype)
    second = []
    for t in peers_x:
        c = _copy(s1a.at[t], r2a.at[a], send_sems.at[2, t], recv_sems.at[2, a], t * RING + b)
        c.start()
        second.append(c)
    for t in peers_z:
        c = _copy(s1b.at[t], r2b.at[b], send_sems.at[3, t], recv_sems.at[3, b], a * RING + t)
        c.start()
        second.append(c)
    for t in peers_x:
        _copy(s1a.at[t], r2a.at[t], send_sems.at[2, t], recv_sems.at[2, t], 0).wait_recv()
    for t in peers_z:
        _copy(s1b.at[t], r2b.at[t], send_sems.at[3, t], recv_sems.at[3, t], 0).wait_recv()
    own_a = xa[a, b].astype(jnp.float32)
    for t in peers_z:
        own_a = own_a + r1a[t, a].astype(jnp.float32)
    own_b = xb[a, b].astype(jnp.float32)
    for t in peers_x:
        own_b = own_b + r1b[t, b].astype(jnp.float32)
    for t in peers_x:
        own_a = own_a + r2a[t].astype(jnp.float32)
    for t in peers_z:
        own_b = own_b + r2b[t].astype(jnp.float32)
    out[0] = own_a
    out[1] = own_b
    for c in first + second:
        c.wait_send()


def latent_reduce(x, collective_id):
    n, _, h, c = x.shape
    c = c // 2
    dt = x.dtype
    return pl.pallas_call(
        _reduce_kernel,
        out_shape=jax.ShapeDtypeStruct((2, h, c), jnp.float32),
        in_specs=[pl.BlockSpec(memory_space=pltpu.VMEM)],
        out_specs=pl.BlockSpec(memory_space=pltpu.VMEM),
        scratch_shapes=[
            pltpu.VMEM((n, n, h, c), dt),
            pltpu.VMEM((n, n, h, c), dt),
            pltpu.VMEM((n, h, c), dt),
            pltpu.VMEM((n, h, c), dt),
            pltpu.VMEM((n, h, c), dt),
            pltpu.VMEM((n, h, c), dt),
            pltpu.SemaphoreType.DMA((4, n)),
            pltpu.SemaphoreType.DMA((4, n)),
        ],
        compiler_params=pltpu.CompilerParams(collective_id=collective_id, has_side_effects=True),
    )(x)


def _reduce_mm_kernel(w, v, out, xa, xb, r1a, r1b, s1a, s1b, r2a, r2b, send_sems, recv_sems):
    a, b = _latent_coords()
    _greet(a, b)
    h = v.shape[1] // 2
    peers_z = [(b + k) % RING for k in range(1, RING)]
    peers_x = [(a + k) % RING for k in range(1, RING)]

    def fill(dst, i, j, half):
        prod = jnp.dot(w[i, j], v[:, half * h:(half + 1) * h], preferred_element_type=jnp.float32)
        dst[i, j] = prod.astype(dst.dtype)

    first = []
    for kz, kx in zip(peers_z, peers_x):
        for i in range(RING):
            fill(xa, i, kz, 0)
        c = _copy(xa.at[:, kz], r1a.at[b], send_sems.at[0, kz], recv_sems.at[0, b], a * RING + kz)
        c.start()
        first.append(c)
        for j in range(RING):
            fill(xb, kx, j, 1)
        c = _copy(xb.at[kx], r1b.at[a], send_sems.at[1, kx], recv_sems.at[1, a], kx * RING + b)
        c.start()
        first.append(c)
    for i in range(RING):
        fill(xa, i, b, 0)
    for j in range(RING):
        fill(xb, a, j, 1)
    for t in peers_z:
        _copy(xa.at[:, t], r1a.at[t], send_sems.at[0, t], recv_sems.at[0, t], 0).wait_recv()
    for t in peers_x:
        _copy(xb.at[t], r1b.at[t], send_sems.at[1, t], recv_sems.at[1, t], 0).wait_recv()
    sum_a = xa[:, b].astype(jnp.float32)
    for t in peers_z:
        sum_a = sum_a + r1a[t].astype(jnp.float32)
    sum_b = xb[a].astype(jnp.float32)
    for t in peers_x:
        sum_b = sum_b + r1b[t].astype(jnp.float32)
    s1a[...] = sum_a.astype(s1a.dtype)
    s1b[...] = sum_b.astype(s1b.dtype)
    second = []
    for t in peers_x:
        c = _copy(s1a.at[t], r2a.at[a], send_sems.at[2, t], recv_sems.at[2, a], t * RING + b)
        c.start()
        second.append(c)
    for t in peers_z:
        c = _copy(s1b.at[t], r2b.at[b], send_sems.at[3, t], recv_sems.at[3, b], a * RING + t)
        c.start()
        second.append(c)
    for t in peers_x:
        _copy(s1a.at[t], r2a.at[t], send_sems.at[2, t], recv_sems.at[2, t], 0).wait_recv()
    for t in peers_z:
        _copy(s1b.at[t], r2b.at[t], send_sems.at[3, t], recv_sems.at[3, t], 0).wait_recv()
    own_a = xa[a, b].astype(jnp.float32)
    own_b = xb[a, b].astype(jnp.float32)
    for k in range(1, RING):
        own_a = own_a + r1a[(b + k) % RING, a].astype(jnp.float32)
        own_b = own_b + r1b[(a + k) % RING, b].astype(jnp.float32)
    for k in range(1, RING):
        own_a = own_a + r2a[(a + k) % RING].astype(jnp.float32)
        own_b = own_b + r2b[(b + k) % RING].astype(jnp.float32)
    out[0] = own_a
    out[1] = own_b
    for c in first + second:
        c.wait_send()


def latent_reduce_mm(w, v, collective_id):
    n, _, d, _ = w.shape
    h = v.shape[1] // 2
    dt = w.dtype
    return pl.pallas_call(
        _reduce_mm_kernel,
        out_shape=jax.ShapeDtypeStruct((2, d, h), jnp.float32),
        in_specs=[pl.BlockSpec(memory_space=pltpu.VMEM)] * 2,
        out_specs=pl.BlockSpec(memory_space=pltpu.VMEM),
        scratch_shapes=[
            pltpu.VMEM((n, n, d, h), dt),
            pltpu.VMEM((n, n, d, h), dt),
            pltpu.VMEM((n, n, d, h), dt),
            pltpu.VMEM((n, n, d, h), dt),
            pltpu.VMEM((n, d, h), dt),
            pltpu.VMEM((n, d, h), dt),
            pltpu.VMEM((n, d, h), dt),
            pltpu.VMEM((n, d, h), dt),
            pltpu.SemaphoreType.DMA((4, n)),
            pltpu.SemaphoreType.DMA((4, n)),
        ],
        compiler_params=pltpu.CompilerParams(collective_id=collective_id, has_side_effects=True),
    )(w, v)


def _gather_kernel(e, oa, ob, g1a, g1b, send_sems, recv_sems):
    a, b = _latent_coords()
    _greet(a, b)
    peers_z = [(b + k) % RING for k in range(1, RING)]
    peers_x = [(a + k) % RING for k in range(1, RING)]
    first = []
    for t in peers_z:
        c = _copy(e.at[0], g1a.at[b], send_sems.at[0, t], recv_sems.at[0, b], a * RING + t)
        c.start()
        first.append(c)
    for t in peers_x:
        c = _copy(e.at[1], g1b.at[a], send_sems.at[1, t], recv_sems.at[1, a], t * RING + b)
        c.start()
        first.append(c)
    g1a[b] = e[0]
    g1b[a] = e[1]
    for t in peers_z:
        _copy(e.at[0], g1a.at[t], send_sems.at[0, t], recv_sems.at[0, t], 0).wait_recv()
    for t in peers_x:
        _copy(e.at[1], g1b.at[t], send_sems.at[1, t], recv_sems.at[1, t], 0).wait_recv()
    second = []
    for t in peers_x:
        c = _copy(g1a, oa.at[a], send_sems.at[2, t], recv_sems.at[2, a], t * RING + b)
        c.start()
        second.append(c)
    for t in peers_z:
        c = _copy(g1b, ob.at[:, b], send_sems.at[3, t], recv_sems.at[3, b], a * RING + t)
        c.start()
        second.append(c)
    oa[a] = g1a[...]
    for j in range(RING):
        ob[j, b] = g1b[j]
    for t in peers_x:
        _copy(g1a, oa.at[t], send_sems.at[2, t], recv_sems.at[2, t], 0).wait_recv()
    for t in peers_z:
        _copy(g1b, ob.at[:, t], send_sems.at[3, t], recv_sems.at[3, t], 0).wait_recv()
    for c in first + second:
        c.wait_send()


def latent_gather(e, collective_id):
    _, h, c = e.shape
    n = RING
    dt = e.dtype
    full = jax.ShapeDtypeStruct((n, n, h, c), dt)
    return pl.pallas_call(
        _gather_kernel,
        out_shape=(full, full),
        in_specs=[pl.BlockSpec(memory_space=pltpu.VMEM)],
        out_specs=(pl.BlockSpec(memory_space=pltpu.VMEM), pl.BlockSpec(memory_space=pltpu.VMEM)),
        scratch_shapes=[
            pltpu.VMEM((n, h, c), dt),
            pltpu.VMEM((n, h, c), dt),
            pltpu.SemaphoreType.DMA((4, n)),
            pltpu.SemaphoreType.DMA((4, n)),
        ],
        compiler_params=pltpu.CompilerParams(collective_id=collective_id, has_side_effects=True),
    )(e)


def _layer_roles():
    me = lax.axis_index("layer")
    mate = me + 1 - 2 * (me % 2)
    far = (me + 2) % LAYERS
    return me, mate, far, (mate + 2) % LAYERS


def _layer_exchange(quarter, x, out, finish, produce, ra, sb, rb, rc, rd, send_sems, recv_sems):
    me, mate, far, mate_far = _layer_roles()
    barrier = pltpu.get_barrier_semaphore()
    for p in (mate, far):
        pl.semaphore_signal(barrier, inc=1, device_id={"layer": p}, device_id_type=MESH)
    pl.semaphore_wait(barrier, 2)

    def copy(src, dst, k, p):
        return pltpu.make_async_remote_copy(
            src_ref=src, dst_ref=dst, send_sem=send_sems.at[k], recv_sem=recv_sems.at[k],
            device_id={"layer": p}, device_id_type=MESH,
        )

    produce(mate)
    produce(mate_far)
    sent = [copy(quarter(x, mate), ra.at[0], 0, mate), copy(quarter(x, mate_far), ra.at[1], 1, mate)]
    for c in sent:
        c.start()
    produce(far)
    produce(me)
    sent[0].wait_recv()
    sent[1].wait_recv()
    sb[...] = quarter(x, far)[...].astype(jnp.float32) + ra[1].astype(jnp.float32)
    step_b = copy(sb, rb, 2, far)
    step_b.start()
    own = quarter(x, me)[...].astype(jnp.float32) + ra[0].astype(jnp.float32)
    step_b.wait_recv()
    quarter(out, me)[...] = finish(own + rb[...])
    step_c = copy(quarter(out, me), rc, 3, far)
    step_c.start()
    step_c.wait_recv()
    quarter(out, far)[...] = rc[...]
    step_d = [copy(quarter(out, me), rd.at[0], 4, mate), copy(rc, rd.at[1], 5, mate)]
    for c in step_d:
        c.start()
    for c in step_d:
        c.wait_recv()
    quarter(out, mate)[...] = rd[0]
    quarter(out, mate_far)[...] = rd[1]
    for c in sent + [step_b, step_c] + step_d:
        c.wait_send()


def _row_quarter(ref, i):
    q = ref.shape[0] // LAYERS
    return ref.at[pl.ds(pl.multiple_of(i * q, q), q)]


def _lane_quarter(ref, i):
    q = ref.shape[1] // LAYERS
    return ref.at[:, pl.ds(pl.multiple_of(i * q, q), q)]


def _layer_pre_kernel(inp, w, bias, feats, pre_q, x, *scratch):
    def finish(total):
        pre = total + bias[...].reshape(1, -1)
        pre_q[...] = pre
        return jnp.maximum(pre, 0.0).astype(feats.dtype)

    def produce(i):
        _row_quarter(x, i)[...] = jnp.dot(
            _row_quarter(inp, i)[...], w[...], preferred_element_type=jnp.float32
        )

    _layer_exchange(_row_quarter, x, feats, finish, produce, *scratch)


def _layer_scratch(in_q, out_q, in_dtype):
    return [
        pltpu.VMEM((2,) + in_q, in_dtype),
        pltpu.VMEM(in_q, jnp.float32),
        pltpu.VMEM(in_q, jnp.float32),
        pltpu.VMEM(out_q, jnp.bfloat16),
        pltpu.VMEM((2,) + out_q, jnp.bfloat16),
        pltpu.SemaphoreType.DMA((6,)),
        pltpu.SemaphoreType.DMA((6,)),
    ]


def layer_pre(inp, w, bias):
    rows, cols = inp.shape[0], w.shape[1]
    q = rows // LAYERS
    return pl.pallas_call(
        _layer_pre_kernel,
        out_shape=(jax.ShapeDtypeStruct((rows, cols), jnp.bfloat16),
                   jax.ShapeDtypeStruct((q, cols), jnp.float32)),
        in_specs=[pl.BlockSpec(memory_space=pltpu.VMEM)] * 3,
        out_specs=(pl.BlockSpec(memory_space=pltpu.VMEM), pl.BlockSpec(memory_space=pltpu.VMEM)),
        scratch_shapes=[pltpu.VMEM((rows, cols), jnp.float32)]
        + _layer_scratch((q, cols), (q, cols), jnp.float32),
        compiler_params=pltpu.CompilerParams(collective_id=1, has_side_effects=True),
    )(inp, w, bias)


def _layer_peers():
    me = lax.axis_index("layer")
    return me, [(me + k) % LAYERS for k in range(1, LAYERS)]


def _layer_greet(peers):
    barrier = pltpu.get_barrier_semaphore()
    for p in peers:
        pl.semaphore_signal(barrier, inc=1, device_id={"layer": p}, device_id_type=MESH)
    pl.semaphore_wait(barrier, LAYERS - 1)


def _layer_copy(src, dst, send_sems, recv_sems, k, p, slot):
    return pltpu.make_async_remote_copy(
        src_ref=src, dst_ref=dst, send_sem=send_sems.at[k, p], recv_sem=recv_sems.at[k, slot],
        device_id={"layer": p}, device_id_type=MESH,
    )


def _layer_grad_kernel(g, pre_q, margin_q, out, r1, r2, send_sems, recv_sems):
    me, peers = _layer_peers()
    q = g.shape[1] // LAYERS
    lanes = lambda i: pl.ds(pl.multiple_of(i * q, q), q)
    _layer_greet(peers)
    sent = []
    for p in peers:
        c = _layer_copy(g.at[:, lanes(p)], r1.at[me], send_sems, recv_sems, 0, p, me)
        c.start()
        sent.append(c)
    total = g[:, lanes(me)].astype(jnp.float32)
    for p in peers:
        _layer_copy(g.at[:, lanes(p)], r1.at[p], send_sems, recv_sems, 0, p, p).wait_recv()
        total = total + r1[p].astype(jnp.float32)
    grad = jnp.where(pre_q[...] > 0, total - MARGIN * margin_q[...], 0.0)
    out[:, lanes(me)] = grad.astype(out.dtype)
    for p in peers:
        c = _layer_copy(out.at[:, lanes(me)], r2.at[me], send_sems, recv_sems, 1, p, me)
        c.start()
        sent.append(c)
    for p in peers:
        _layer_copy(out.at[:, lanes(p)], r2.at[p], send_sems, recv_sems, 1, p, p).wait_recv()
        out[:, lanes(p)] = r2[p]
    for c in sent:
        c.wait_send()


def layer_grad(g, pre_q, margin_q):
    cols, rows = g.shape
    q = rows // LAYERS
    return pl.pallas_call(
        _layer_grad_kernel,
        out_shape=jax.ShapeDtypeStruct((cols, rows), jnp.bfloat16),
        in_specs=[pl.BlockSpec(memory_space=pltpu.VMEM)] * 3,
        out_specs=pl.BlockSpec(memory_space=pltpu.VMEM),
        scratch_shapes=[
            pltpu.VMEM((LAYERS, cols, q), jnp.bfloat16),
            pltpu.VMEM((LAYERS, cols, q), jnp.bfloat16),
            pltpu.SemaphoreType.DMA((2, LAYERS)),
            pltpu.SemaphoreType.DMA((2, LAYERS)),
        ],
        compiler_params=pltpu.CompilerParams(collective_id=2, has_side_effects=True),
    )(g, pre_q, margin_q)


def local(inputs, clean_acts, enc_weight, enc_bias, dec_weight, dec_bias, pairing, targets):
    row_count = inputs.shape[0]
    lat_count = enc_weight.shape[2]
    all_rows = pairing.shape[0]
    d_model = inputs.shape[2]
    chunk = d_model // (RING * RING)
    half = row_count // 2
    me = lax.axis_index("latent")
    features, pre_q = layer_pre(inputs[:, 0, :], enc_weight[0], enc_bias)
    dec4 = dec_weight[0].reshape(lat_count, RING, RING, chunk)
    recon_part = jnp.einsum("rf,fabd->abdr", features, dec4, preferred_element_type=jnp.float32)
    recon_sum = latent_reduce(recon_part.astype(jnp.bfloat16), 3)
    bias_part = lax.dynamic_slice_in_dim(dec_bias[0], me * chunk, chunk)
    clean_part = lax.dynamic_slice_in_dim(clean_acts[:, 0, :], me * chunk, chunk, axis=1)
    clean_t = jnp.swapaxes(clean_part.reshape(2, half, chunk), 1, 2).astype(jnp.float32)
    recon_error = (recon_sum + bias_part[:, None] - clean_t).astype(jnp.bfloat16)
    error_a, error_b = latent_gather(recon_error, 4)
    error_all = jnp.concatenate(
        [error_a.reshape(d_model, half), error_b.reshape(d_model, half)], axis=1
    )
    partial_grad_t = jnp.dot(dec_weight[0], error_all, preferred_element_type=jnp.float32)
    quarter = row_count // LAYERS
    row_ids = (
        lax.axis_index("row") * row_count
        + lax.axis_index("layer") * quarter
        + jnp.arange(quarter, dtype=jnp.int32)
    )
    latent_ids = me * lat_count + jnp.arange(lat_count, dtype=jnp.int32)
    every_row = jnp.arange(all_rows, dtype=jnp.int32)
    pair_table_t = (
        (every_row[:, None] == row_ids[None, :]).astype(jnp.float32)
        - (pairing[:, None] == row_ids[None, :]).astype(jnp.float32)
    ).astype(jnp.bfloat16)
    target_hot_t = (latent_ids[:, None] == targets[None, :]).astype(jnp.bfloat16)
    margin_q = jnp.dot(target_hot_t, pair_table_t, preferred_element_type=jnp.float32)
    pre_grad_t = layer_grad(partial_grad_t.astype(jnp.bfloat16), pre_q.T, margin_q)
    enc4 = enc_weight[0].reshape(RING, RING, chunk, lat_count)
    total = latent_reduce_mm(enc4, pre_grad_t, 5)
    return jnp.swapaxes(total.astype(jnp.bfloat16), 1, 2).reshape(row_count, 1, chunk)


def solution(mesh):
    placed = (
        P("row", "layer", None),
        P("row", "layer", None),
        P("layer", None, "latent"),
        P("latent"),
        P("layer", "latent", None),
        P("layer", None),
        P(),
        P(),
    )
    return jax.shard_map(
        local, mesh=mesh, in_specs=placed, out_specs=P("row", "layer", "latent"), check_vma=False
    )
```

```python
import jax
import jax.numpy as jnp
from jax import lax
from jax.experimental import pallas as pl
from jax.experimental.pallas import tpu as pltpu
from jax.sharding import PartitionSpec as P

MARGIN = 16.0
MESH = pl.DeviceIdType.MESH
RING = 4
LAYERS = 4


def _latent_coords():
    me = lax.axis_index("latent")
    return me // RING, me % RING


def _greet(a, b):
    barrier = pltpu.get_barrier_semaphore()
    for k in range(1, RING):
        pl.semaphore_signal(barrier, inc=1, device_id={"latent": a * RING + (b + k) % RING}, device_id_type=MESH)
        pl.semaphore_signal(barrier, inc=1, device_id={"latent": ((a + k) % RING) * RING + b}, device_id_type=MESH)
    pl.semaphore_wait(barrier, 2 * (RING - 1))


def _copy(src, dst, send_sem, recv_sem, peer):
    return pltpu.make_async_remote_copy(
        src_ref=src, dst_ref=dst, send_sem=send_sem, recv_sem=recv_sem,
        device_id={"latent": peer}, device_id_type=MESH,
    )


def _reduce_kernel(x, bias, clean, out, r1a, r1b, s1a, s1b, r2a, r2b, send_sems, recv_sems):
    h = x.shape[-1] // 2
    xa = x.at[:, :, :, pl.ds(0, h)]
    xb = x.at[:, :, :, pl.ds(h, h)]
    a, b = _latent_coords()
    _greet(a, b)
    peers_z = [(b + k) % RING for k in range(1, RING)]
    peers_x = [(a + k) % RING for k in range(1, RING)]
    first = []
    for t in peers_z:
        c = _copy(xa.at[:, t], r1a.at[b], send_sems.at[0, t], recv_sems.at[0, b], a * RING + t)
        c.start()
        first.append(c)
    for t in peers_x:
        c = _copy(xb.at[t], r1b.at[a], send_sems.at[1, t], recv_sems.at[1, a], t * RING + b)
        c.start()
        first.append(c)
    for t in peers_z:
        _copy(xa.at[:, t], r1a.at[t], send_sems.at[0, t], recv_sems.at[0, t], 0).wait_recv()
    for t in peers_x:
        _copy(xb.at[t], r1b.at[t], send_sems.at[1, t], recv_sems.at[1, t], 0).wait_recv()
    sum_a = xa[:, b].astype(jnp.float32)
    for t in peers_z:
        sum_a = sum_a + r1a[t].astype(jnp.float32)
    sum_b = xb[a].astype(jnp.float32)
    for t in peers_x:
        sum_b = sum_b + r1b[t].astype(jnp.float32)
    s1a[...] = sum_a.astype(s1a.dtype)
    s1b[...] = sum_b.astype(s1b.dtype)
    second = []
    for t in peers_x:
        c = _copy(s1a.at[t], r2a.at[a], send_sems.at[2, t], recv_sems.at[2, a], t * RING + b)
        c.start()
        second.append(c)
    for t in peers_z:
        c = _copy(s1b.at[t], r2b.at[b], send_sems.at[3, t], recv_sems.at[3, b], a * RING + t)
        c.start()
        second.append(c)
    for t in peers_x:
        _copy(s1a.at[t], r2a.at[t], send_sems.at[2, t], recv_sems.at[2, t], 0).wait_recv()
    for t in peers_z:
        _copy(s1b.at[t], r2b.at[t], send_sems.at[3, t], recv_sems.at[3, t], 0).wait_recv()
    own_a = xa[a, b].astype(jnp.float32)
    for t in peers_z:
        own_a = own_a + r1a[t, a].astype(jnp.float32)
    own_b = xb[a, b].astype(jnp.float32)
    for t in peers_x:
        own_b = own_b + r1b[t, b].astype(jnp.float32)
    for t in peers_x:
        own_a = own_a + r2a[t].astype(jnp.float32)
    for t in peers_z:
        own_b = own_b + r2b[t].astype(jnp.float32)
    out[0] = (own_a + bias[...] - clean[0].astype(jnp.float32)).astype(out.dtype)
    out[1] = (own_b + bias[...] - clean[1].astype(jnp.float32)).astype(out.dtype)
    for c in first + second:
        c.wait_send()


def latent_reduce(x, bias, clean, collective_id):
    n, _, h, c = x.shape
    c = c // 2
    dt = x.dtype
    return pl.pallas_call(
        _reduce_kernel,
        out_shape=jax.ShapeDtypeStruct((2, h, c), jnp.bfloat16),
        in_specs=[pl.BlockSpec(memory_space=pltpu.VMEM)] * 3,
        out_specs=pl.BlockSpec(memory_space=pltpu.VMEM),
        scratch_shapes=[
            pltpu.VMEM((n, n, h, c), dt),
            pltpu.VMEM((n, n, h, c), dt),
            pltpu.VMEM((n, h, c), dt),
            pltpu.VMEM((n, h, c), dt),
            pltpu.VMEM((n, h, c), dt),
            pltpu.VMEM((n, h, c), dt),
            pltpu.SemaphoreType.DMA((4, n)),
            pltpu.SemaphoreType.DMA((4, n)),
        ],
        compiler_params=pltpu.CompilerParams(collective_id=collective_id, has_side_effects=True),
    )(x, bias, clean)


def _reduce_mm_kernel(w, v, out, xa, xb, r1a, r1b, s1a, s1b, r2a, r2b, send_sems, recv_sems):
    a, b = _latent_coords()
    _greet(a, b)
    h = v.shape[1] // 2
    peers_z = [(b + k) % RING for k in range(1, RING)]
    peers_x = [(a + k) % RING for k in range(1, RING)]

    def fill(dst, i, j, half):
        prod = jnp.dot(w[i, j], v[:, half * h:(half + 1) * h], preferred_element_type=jnp.float32)
        dst[i, j] = prod.astype(dst.dtype)

    first = []
    for kz, kx in zip(peers_z, peers_x):
        for i in range(RING):
            fill(xa, i, kz, 0)
        c = _copy(xa.at[:, kz], r1a.at[b], send_sems.at[0, kz], recv_sems.at[0, b], a * RING + kz)
        c.start()
        first.append(c)
        for j in range(RING):
            fill(xb, kx, j, 1)
        c = _copy(xb.at[kx], r1b.at[a], send_sems.at[1, kx], recv_sems.at[1, a], kx * RING + b)
        c.start()
        first.append(c)
    for i in range(RING):
        fill(xa, i, b, 0)
    for j in range(RING):
        fill(xb, a, j, 1)
    for t in peers_z:
        _copy(xa.at[:, t], r1a.at[t], send_sems.at[0, t], recv_sems.at[0, t], 0).wait_recv()
    for t in peers_x:
        _copy(xb.at[t], r1b.at[t], send_sems.at[1, t], recv_sems.at[1, t], 0).wait_recv()
    sum_a = xa[:, b].astype(jnp.float32)
    for t in peers_z:
        sum_a = sum_a + r1a[t].astype(jnp.float32)
    sum_b = xb[a].astype(jnp.float32)
    for t in peers_x:
        sum_b = sum_b + r1b[t].astype(jnp.float32)
    s1a[...] = sum_a.astype(s1a.dtype)
    s1b[...] = sum_b.astype(s1b.dtype)
    second = []
    for t in peers_x:
        c = _copy(s1a.at[t], r2a.at[a], send_sems.at[2, t], recv_sems.at[2, a], t * RING + b)
        c.start()
        second.append(c)
    for t in peers_z:
        c = _copy(s1b.at[t], r2b.at[b], send_sems.at[3, t], recv_sems.at[3, b], a * RING + t)
        c.start()
        second.append(c)
    for t in peers_x:
        _copy(s1a.at[t], r2a.at[t], send_sems.at[2, t], recv_sems.at[2, t], 0).wait_recv()
    for t in peers_z:
        _copy(s1b.at[t], r2b.at[t], send_sems.at[3, t], recv_sems.at[3, t], 0).wait_recv()
    own_a = xa[a, b].astype(jnp.float32)
    own_b = xb[a, b].astype(jnp.float32)
    for k in range(1, RING):
        own_a = own_a + r1a[(b + k) % RING, a].astype(jnp.float32)
        own_b = own_b + r1b[(a + k) % RING, b].astype(jnp.float32)
    for k in range(1, RING):
        own_a = own_a + r2a[(a + k) % RING].astype(jnp.float32)
        own_b = own_b + r2b[(b + k) % RING].astype(jnp.float32)
    out[0] = own_a
    out[1] = own_b
    for c in first + second:
        c.wait_send()


def latent_reduce_mm(w, v, collective_id):
    n, _, d, _ = w.shape
    h = v.shape[1] // 2
    dt = w.dtype
    return pl.pallas_call(
        _reduce_mm_kernel,
        out_shape=jax.ShapeDtypeStruct((2, d, h), jnp.float32),
        in_specs=[pl.BlockSpec(memory_space=pltpu.VMEM)] * 2,
        out_specs=pl.BlockSpec(memory_space=pltpu.VMEM),
        scratch_shapes=[
            pltpu.VMEM((n, n, d, h), dt),
            pltpu.VMEM((n, n, d, h), dt),
            pltpu.VMEM((n, n, d, h), dt),
            pltpu.VMEM((n, n, d, h), dt),
            pltpu.VMEM((n, d, h), dt),
            pltpu.VMEM((n, d, h), dt),
            pltpu.VMEM((n, d, h), dt),
            pltpu.VMEM((n, d, h), dt),
            pltpu.SemaphoreType.DMA((4, n)),
            pltpu.SemaphoreType.DMA((4, n)),
        ],
        compiler_params=pltpu.CompilerParams(collective_id=collective_id, has_side_effects=True),
    )(w, v)


def _gather_kernel(e, oa, ob, g1a, g1b, ga, gb, send_sems, recv_sems):
    a, b = _latent_coords()
    _greet(a, b)
    peers_z = [(b + k) % RING for k in range(1, RING)]
    peers_x = [(a + k) % RING for k in range(1, RING)]
    first = []
    for t in peers_z:
        c = _copy(e.at[0], g1a.at[b], send_sems.at[0, t], recv_sems.at[0, b], a * RING + t)
        c.start()
        first.append(c)
    for t in peers_x:
        c = _copy(e.at[1], g1b.at[a], send_sems.at[1, t], recv_sems.at[1, a], t * RING + b)
        c.start()
        first.append(c)
    g1a[b] = e[0]
    g1b[a] = e[1]
    for t in peers_z:
        _copy(e.at[0], g1a.at[t], send_sems.at[0, t], recv_sems.at[0, t], 0).wait_recv()
    for t in peers_x:
        _copy(e.at[1], g1b.at[t], send_sems.at[1, t], recv_sems.at[1, t], 0).wait_recv()
    second = []
    for t in peers_x:
        c = _copy(g1a, ga.at[a], send_sems.at[2, t], recv_sems.at[2, a], t * RING + b)
        c.start()
        second.append(c)
    for t in peers_z:
        c = _copy(g1b, gb.at[b], send_sems.at[3, t], recv_sems.at[3, b], a * RING + t)
        c.start()
        second.append(c)
    oa[a] = g1a[...]
    for j in range(RING):
        ob[j, b] = g1b[j]
    for t in peers_x:
        _copy(g1a, ga.at[t], send_sems.at[2, t], recv_sems.at[2, t], 0).wait_recv()
        oa[t] = ga[t]
    for t in peers_z:
        _copy(g1b, gb.at[t], send_sems.at[3, t], recv_sems.at[3, t], 0).wait_recv()
        for j in range(RING):
            ob[j, t] = gb[t, j]
    for c in first + second:
        c.wait_send()


def latent_gather(e, collective_id):
    _, h, c = e.shape
    n = RING
    dt = e.dtype
    full = jax.ShapeDtypeStruct((n, n, h, c), dt)
    return pl.pallas_call(
        _gather_kernel,
        out_shape=(full, full),
        in_specs=[pl.BlockSpec(memory_space=pltpu.VMEM)],
        out_specs=(pl.BlockSpec(memory_space=pltpu.VMEM), pl.BlockSpec(memory_space=pltpu.VMEM)),
        scratch_shapes=[
            pltpu.VMEM((n, h, c), dt),
            pltpu.VMEM((n, h, c), dt),
            pltpu.VMEM((n, n, h, c), dt),
            pltpu.VMEM((n, n, h, c), dt),
            pltpu.SemaphoreType.DMA((4, n)),
            pltpu.SemaphoreType.DMA((4, n)),
        ],
        compiler_params=pltpu.CompilerParams(collective_id=collective_id, has_side_effects=True),
    )(e)


def _layer_roles():
    me = lax.axis_index("layer")
    mate = me + 1 - 2 * (me % 2)
    far = (me + 2) % LAYERS
    return me, mate, far, (mate + 2) % LAYERS


def _layer_exchange(quarter, x, out, finish, produce, ra, sb, rb, rc, rd, send_sems, recv_sems):
    me, mate, far, mate_far = _layer_roles()
    barrier = pltpu.get_barrier_semaphore()
    for p in (mate, far):
        pl.semaphore_signal(barrier, inc=1, device_id={"layer": p}, device_id_type=MESH)
    pl.semaphore_wait(barrier, 2)

    def copy(src, dst, k, p):
        return pltpu.make_async_remote_copy(
            src_ref=src, dst_ref=dst, send_sem=send_sems.at[k], recv_sem=recv_sems.at[k],
            device_id={"layer": p}, device_id_type=MESH,
        )

    produce(mate)
    produce(mate_far)
    sent = [copy(quarter(x, mate), ra.at[0], 0, mate), copy(quarter(x, mate_far), ra.at[1], 1, mate)]
    for c in sent:
        c.start()
    produce(far)
    produce(me)
    sent[0].wait_recv()
    sent[1].wait_recv()
    sb[...] = quarter(x, far)[...].astype(jnp.float32) + ra[1].astype(jnp.float32)
    step_b = copy(sb, rb, 2, far)
    step_b.start()
    own = quarter(x, me)[...].astype(jnp.float32) + ra[0].astype(jnp.float32)
    step_b.wait_recv()
    quarter(out, me)[...] = finish(own + rb[...])
    step_c = copy(quarter(out, me), rc, 3, far)
    step_c.start()
    step_c.wait_recv()
    quarter(out, far)[...] = rc[...]
    step_d = [copy(quarter(out, me), rd.at[0], 4, mate), copy(rc, rd.at[1], 5, mate)]
    for c in step_d:
        c.start()
    for c in step_d:
        c.wait_recv()
    quarter(out, mate)[...] = rd[0]
    quarter(out, mate_far)[...] = rd[1]
    for c in sent + [step_b, step_c] + step_d:
        c.wait_send()


def _row_quarter(ref, i):
    q = ref.shape[0] // LAYERS
    return ref.at[pl.ds(pl.multiple_of(i * q, q), q)]


def _lane_quarter(ref, i):
    q = ref.shape[1] // LAYERS
    return ref.at[:, pl.ds(pl.multiple_of(i * q, q), q)]


def _layer_pre_kernel(inp, w, bias, feats, pre_q, x, *scratch):
    def finish(total):
        pre = total + bias[...].reshape(1, -1)
        pre_q[...] = pre
        return jnp.maximum(pre, 0.0).astype(feats.dtype)

    def produce(i):
        _row_quarter(x, i)[...] = jnp.dot(
            _row_quarter(inp, i)[...], w[...], preferred_element_type=jnp.float32
        )

    _layer_exchange(_row_quarter, x, feats, finish, produce, *scratch)


def _layer_scratch(in_q, out_q, in_dtype):
    return [
        pltpu.VMEM((2,) + in_q, in_dtype),
        pltpu.VMEM(in_q, jnp.float32),
        pltpu.VMEM(in_q, jnp.float32),
        pltpu.VMEM(out_q, jnp.bfloat16),
        pltpu.VMEM((2,) + out_q, jnp.bfloat16),
        pltpu.SemaphoreType.DMA((6,)),
        pltpu.SemaphoreType.DMA((6,)),
    ]


def layer_pre(inp, w, bias):
    rows, cols = inp.shape[0], w.shape[1]
    q = rows // LAYERS
    return pl.pallas_call(
        _layer_pre_kernel,
        out_shape=(jax.ShapeDtypeStruct((rows, cols), jnp.bfloat16),
                   jax.ShapeDtypeStruct((q, cols), jnp.float32)),
        in_specs=[pl.BlockSpec(memory_space=pltpu.VMEM)] * 3,
        out_specs=(pl.BlockSpec(memory_space=pltpu.VMEM), pl.BlockSpec(memory_space=pltpu.VMEM)),
        scratch_shapes=[pltpu.VMEM((rows, cols), jnp.float32)]
        + _layer_scratch((q, cols), (q, cols), jnp.float32),
        compiler_params=pltpu.CompilerParams(collective_id=1, has_side_effects=True),
    )(inp, w, bias)


def _layer_peers():
    me = lax.axis_index("layer")
    return me, [(me + k) % LAYERS for k in range(1, LAYERS)]


def _layer_greet(peers):
    barrier = pltpu.get_barrier_semaphore()
    for p in peers:
        pl.semaphore_signal(barrier, inc=1, device_id={"layer": p}, device_id_type=MESH)
    pl.semaphore_wait(barrier, LAYERS - 1)


def _layer_copy(src, dst, send_sems, recv_sems, k, p, slot):
    return pltpu.make_async_remote_copy(
        src_ref=src, dst_ref=dst, send_sem=send_sems.at[k, p], recv_sem=recv_sems.at[k, slot],
        device_id={"layer": p}, device_id_type=MESH,
    )


def _layer_grad_kernel(g, pre_q, margin_q, out, r1, r2, send_sems, recv_sems):
    me, peers = _layer_peers()
    q = g.shape[1] // LAYERS
    lanes = lambda i: pl.ds(pl.multiple_of(i * q, q), q)
    _layer_greet(peers)
    sent = []
    for p in peers:
        c = _layer_copy(g.at[:, lanes(p)], r1.at[me], send_sems, recv_sems, 0, p, me)
        c.start()
        sent.append(c)
    total = g[:, lanes(me)].astype(jnp.float32)
    for p in peers:
        _layer_copy(g.at[:, lanes(p)], r1.at[p], send_sems, recv_sems, 0, p, p).wait_recv()
        total = total + r1[p].astype(jnp.float32)
    grad = jnp.where(pre_q[...] > 0, total - MARGIN * margin_q[...], 0.0)
    out[:, lanes(me)] = grad.astype(out.dtype)
    for p in peers:
        c = _layer_copy(out.at[:, lanes(me)], r2.at[me], send_sems, recv_sems, 1, p, me)
        c.start()
        sent.append(c)
    for p in peers:
        _layer_copy(out.at[:, lanes(p)], r2.at[p], send_sems, recv_sems, 1, p, p).wait_recv()
        out[:, lanes(p)] = r2[p]
    for c in sent:
        c.wait_send()


def layer_grad(g, pre_q, margin_q):
    cols, rows = g.shape
    q = rows // LAYERS
    return pl.pallas_call(
        _layer_grad_kernel,
        out_shape=jax.ShapeDtypeStruct((cols, rows), jnp.bfloat16),
        in_specs=[pl.BlockSpec(memory_space=pltpu.VMEM)] * 3,
        out_specs=pl.BlockSpec(memory_space=pltpu.VMEM),
        scratch_shapes=[
            pltpu.VMEM((LAYERS, cols, q), jnp.bfloat16),
            pltpu.VMEM((LAYERS, cols, q), jnp.bfloat16),
            pltpu.SemaphoreType.DMA((2, LAYERS)),
            pltpu.SemaphoreType.DMA((2, LAYERS)),
        ],
        compiler_params=pltpu.CompilerParams(collective_id=2, has_side_effects=True),
    )(g, pre_q, margin_q)


def local(inputs, clean_acts, enc_weight, enc_bias, dec_weight, dec_bias, pairing, targets):
    row_count = inputs.shape[0]
    lat_count = enc_weight.shape[2]
    all_rows = pairing.shape[0]
    d_model = inputs.shape[2]
    chunk = d_model // (RING * RING)
    half = row_count // 2
    me = lax.axis_index("latent")
    features, pre_q = layer_pre(inputs[:, 0, :], enc_weight[0], enc_bias)
    dec4 = dec_weight[0].reshape(lat_count, RING, RING, chunk)
    recon_part = jnp.einsum("rf,fabd->abdr", features, dec4, preferred_element_type=jnp.float32)
    bias_part = lax.dynamic_slice_in_dim(dec_bias[0], me * chunk, chunk)
    clean_part = lax.dynamic_slice_in_dim(clean_acts[:, 0, :], me * chunk, chunk, axis=1)
    clean_t = jnp.swapaxes(clean_part.reshape(2, half, chunk), 1, 2)
    recon_error = latent_reduce(recon_part.astype(jnp.bfloat16), bias_part[:, None], clean_t, 3)
    error_a, error_b = latent_gather(recon_error, 4)
    error_all = jnp.concatenate(
        [error_a.reshape(d_model, half), error_b.reshape(d_model, half)], axis=1
    )
    partial_grad_t = jnp.dot(dec_weight[0], error_all, preferred_element_type=jnp.float32)
    quarter = row_count // LAYERS
    row_ids = (
        lax.axis_index("row") * row_count
        + lax.axis_index("layer") * quarter
        + jnp.arange(quarter, dtype=jnp.int32)
    )
    latent_ids = me * lat_count + jnp.arange(lat_count, dtype=jnp.int32)
    every_row = jnp.arange(all_rows, dtype=jnp.int32)
    pair_table_t = (
        (every_row[:, None] == row_ids[None, :]).astype(jnp.float32)
        - (pairing[:, None] == row_ids[None, :]).astype(jnp.float32)
    ).astype(jnp.bfloat16)
    target_hot_t = (latent_ids[:, None] == targets[None, :]).astype(jnp.bfloat16)
    margin_q = jnp.dot(target_hot_t, pair_table_t, preferred_element_type=jnp.float32)
    pre_grad_t = layer_grad(partial_grad_t.astype(jnp.bfloat16), pre_q.T, margin_q)
    enc4 = enc_weight[0].reshape(RING, RING, chunk, lat_count)
    total = latent_reduce_mm(enc4, pre_grad_t, 5)
    return jnp.swapaxes(total.astype(jnp.bfloat16), 1, 2).reshape(row_count, 1, chunk)


def solution(mesh):
    placed = (
        P("row", "layer", None),
        P("row", "layer", None),
        P("layer", None, "latent"),
        P("latent"),
        P("layer", "latent", None),
        P("layer", None),
        P(),
        P(),
    )
    return jax.shard_map(
        local, mesh=mesh, in_specs=placed, out_specs=P("row", "layer", "latent"), check_vma=False
    )
```

```python
import jax
import jax.numpy as jnp
from jax import lax
from jax.experimental import pallas as pl
from jax.experimental.pallas import tpu as pltpu
from jax.sharding import PartitionSpec as P

MARGIN = 16.0
MESH = pl.DeviceIdType.MESH
RING = 4
LAYERS = 4


def _latent_coords():
    me = lax.axis_index("latent")
    return me // RING, me % RING


def _greet(a, b):
    barrier = pltpu.get_barrier_semaphore()
    for k in range(1, RING):
        pl.semaphore_signal(barrier, inc=1, device_id={"latent": a * RING + (b + k) % RING}, device_id_type=MESH)
        pl.semaphore_signal(barrier, inc=1, device_id={"latent": ((a + k) % RING) * RING + b}, device_id_type=MESH)
    pl.semaphore_wait(barrier, 2 * (RING - 1))


def _copy(src, dst, send_sem, recv_sem, peer):
    return pltpu.make_async_remote_copy(
        src_ref=src, dst_ref=dst, send_sem=send_sem, recv_sem=recv_sem,
        device_id={"latent": peer}, device_id_type=MESH,
    )


def _reduce_kernel(x, bias, clean, out, xs, r1a, r1b, s1a, s1b, r2a, r2b, send_sems, recv_sems):
    h = x.shape[-1] // 2
    xa = xs.at[:, :, :, pl.ds(0, h)]
    xb = xs.at[:, :, :, pl.ds(h, h)]
    a, b = _latent_coords()
    _greet(a, b)
    peers_z = [(b + k) % RING for k in range(1, RING)]
    peers_x = [(a + k) % RING for k in range(1, RING)]
    def round_a(j):
        for i in range(RING):
            xs[i, j, :, 0:h] = x[i, j, :, 0:h].astype(xs.dtype)

    def round_b(i):
        for j in range(RING):
            xs[i, j, :, h:2 * h] = x[i, j, :, h:2 * h].astype(xs.dtype)

    first = []
    for tz, tx in zip(peers_z, peers_x):
        round_a(tz)
        c = _copy(xa.at[:, tz], r1a.at[b], send_sems.at[0, tz], recv_sems.at[0, b], a * RING + tz)
        c.start()
        first.append(c)
        round_b(tx)
        c = _copy(xb.at[tx], r1b.at[a], send_sems.at[1, tx], recv_sems.at[1, a], tx * RING + b)
        c.start()
        first.append(c)
    round_a(b)
    round_b(a)
    for t in peers_z:
        _copy(xa.at[:, t], r1a.at[t], send_sems.at[0, t], recv_sems.at[0, t], 0).wait_recv()
    for t in peers_x:
        _copy(xb.at[t], r1b.at[t], send_sems.at[1, t], recv_sems.at[1, t], 0).wait_recv()
    sum_a = xa[:, b].astype(jnp.float32)
    for t in peers_z:
        sum_a = sum_a + r1a[t].astype(jnp.float32)
    sum_b = xb[a].astype(jnp.float32)
    for t in peers_x:
        sum_b = sum_b + r1b[t].astype(jnp.float32)
    s1a[...] = sum_a.astype(s1a.dtype)
    s1b[...] = sum_b.astype(s1b.dtype)
    second = []
    for t in peers_x:
        c = _copy(s1a.at[t], r2a.at[a], send_sems.at[2, t], recv_sems.at[2, a], t * RING + b)
        c.start()
        second.append(c)
    for t in peers_z:
        c = _copy(s1b.at[t], r2b.at[b], send_sems.at[3, t], recv_sems.at[3, b], a * RING + t)
        c.start()
        second.append(c)
    for t in peers_x:
        _copy(s1a.at[t], r2a.at[t], send_sems.at[2, t], recv_sems.at[2, t], 0).wait_recv()
    for t in peers_z:
        _copy(s1b.at[t], r2b.at[t], send_sems.at[3, t], recv_sems.at[3, t], 0).wait_recv()
    own_a = xa[a, b].astype(jnp.float32)
    for t in peers_z:
        own_a = own_a + r1a[t, a].astype(jnp.float32)
    own_b = xb[a, b].astype(jnp.float32)
    for t in peers_x:
        own_b = own_b + r1b[t, b].astype(jnp.float32)
    for t in peers_x:
        own_a = own_a + r2a[t].astype(jnp.float32)
    for t in peers_z:
        own_b = own_b + r2b[t].astype(jnp.float32)
    out[0] = (own_a + bias[...] - clean[0].astype(jnp.float32)).astype(out.dtype)
    out[1] = (own_b + bias[...] - clean[1].astype(jnp.float32)).astype(out.dtype)
    for c in first + second:
        c.wait_send()


def latent_reduce(x, bias, clean, collective_id):
    n, _, h, c = x.shape
    c = c // 2
    dt = jnp.bfloat16
    return pl.pallas_call(
        _reduce_kernel,
        out_shape=jax.ShapeDtypeStruct((2, h, c), jnp.bfloat16),
        in_specs=[pl.BlockSpec(memory_space=pltpu.VMEM)] * 3,
        out_specs=pl.BlockSpec(memory_space=pltpu.VMEM),
        scratch_shapes=[
            pltpu.VMEM((n, n, h, 2 * c), dt),
            pltpu.VMEM((n, n, h, c), dt),
            pltpu.VMEM((n, n, h, c), dt),
            pltpu.VMEM((n, h, c), dt),
            pltpu.VMEM((n, h, c), dt),
            pltpu.VMEM((n, h, c), dt),
            pltpu.VMEM((n, h, c), dt),
            pltpu.SemaphoreType.DMA((4, n)),
            pltpu.SemaphoreType.DMA((4, n)),
        ],
        compiler_params=pltpu.CompilerParams(collective_id=collective_id, has_side_effects=True),
    )(x, bias, clean)


def _reduce_mm_kernel(w, v, out, xa, xb, r1a, r1b, s1a, s1b, r2a, r2b, send_sems, recv_sems):
    a, b = _latent_coords()
    _greet(a, b)
    h = v.shape[1] // 2
    peers_z = [(b + k) % RING for k in range(1, RING)]
    peers_x = [(a + k) % RING for k in range(1, RING)]

    def fill(dst, i, j, half):
        prod = jnp.dot(w[i, j], v[:, half * h:(half + 1) * h], preferred_element_type=jnp.float32)
        dst[i, j] = prod.astype(dst.dtype)

    first = []
    for kz, kx in zip(peers_z, peers_x):
        for i in range(RING):
            fill(xa, i, kz, 0)
        c = _copy(xa.at[:, kz], r1a.at[b], send_sems.at[0, kz], recv_sems.at[0, b], a * RING + kz)
        c.start()
        first.append(c)
        for j in range(RING):
            fill(xb, kx, j, 1)
        c = _copy(xb.at[kx], r1b.at[a], send_sems.at[1, kx], recv_sems.at[1, a], kx * RING + b)
        c.start()
        first.append(c)
    for i in range(RING):
        fill(xa, i, b, 0)
    for j in range(RING):
        fill(xb, a, j, 1)
    for t in peers_z:
        _copy(xa.at[:, t], r1a.at[t], send_sems.at[0, t], recv_sems.at[0, t], 0).wait_recv()
    for t in peers_x:
        _copy(xb.at[t], r1b.at[t], send_sems.at[1, t], recv_sems.at[1, t], 0).wait_recv()
    sum_a = xa[:, b].astype(jnp.float32)
    for t in peers_z:
        sum_a = sum_a + r1a[t].astype(jnp.float32)
    sum_b = xb[a].astype(jnp.float32)
    for t in peers_x:
        sum_b = sum_b + r1b[t].astype(jnp.float32)
    s1a[...] = sum_a.astype(s1a.dtype)
    s1b[...] = sum_b.astype(s1b.dtype)
    second = []
    for t in peers_x:
        c = _copy(s1a.at[t], r2a.at[a], send_sems.at[2, t], recv_sems.at[2, a], t * RING + b)
        c.start()
        second.append(c)
    for t in peers_z:
        c = _copy(s1b.at[t], r2b.at[b], send_sems.at[3, t], recv_sems.at[3, b], a * RING + t)
        c.start()
        second.append(c)
    for t in peers_x:
        _copy(s1a.at[t], r2a.at[t], send_sems.at[2, t], recv_sems.at[2, t], 0).wait_recv()
    for t in peers_z:
        _copy(s1b.at[t], r2b.at[t], send_sems.at[3, t], recv_sems.at[3, t], 0).wait_recv()
    own_a = xa[a, b].astype(jnp.float32)
    own_b = xb[a, b].astype(jnp.float32)
    for k in range(1, RING):
        own_a = own_a + r1a[(b + k) % RING, a].astype(jnp.float32)
        own_b = own_b + r1b[(a + k) % RING, b].astype(jnp.float32)
    for k in range(1, RING):
        own_a = own_a + r2a[(a + k) % RING].astype(jnp.float32)
        own_b = own_b + r2b[(b + k) % RING].astype(jnp.float32)
    out[0] = own_a
    out[1] = own_b
    for c in first + second:
        c.wait_send()


def latent_reduce_mm(w, v, collective_id):
    n, _, d, _ = w.shape
    h = v.shape[1] // 2
    dt = w.dtype
    return pl.pallas_call(
        _reduce_mm_kernel,
        out_shape=jax.ShapeDtypeStruct((2, d, h), jnp.float32),
        in_specs=[pl.BlockSpec(memory_space=pltpu.VMEM)] * 2,
        out_specs=pl.BlockSpec(memory_space=pltpu.VMEM),
        scratch_shapes=[
            pltpu.VMEM((n, n, d, h), dt),
            pltpu.VMEM((n, n, d, h), dt),
            pltpu.VMEM((n, n, d, h), dt),
            pltpu.VMEM((n, n, d, h), dt),
            pltpu.VMEM((n, d, h), dt),
            pltpu.VMEM((n, d, h), dt),
            pltpu.VMEM((n, d, h), dt),
            pltpu.VMEM((n, d, h), dt),
            pltpu.SemaphoreType.DMA((4, n)),
            pltpu.SemaphoreType.DMA((4, n)),
        ],
        compiler_params=pltpu.CompilerParams(collective_id=collective_id, has_side_effects=True),
    )(w, v)


def _gather_kernel(e, oa, ob, g1a, g1b, ga, gb, send_sems, recv_sems):
    a, b = _latent_coords()
    _greet(a, b)
    peers_z = [(b + k) % RING for k in range(1, RING)]
    peers_x = [(a + k) % RING for k in range(1, RING)]
    first = []
    for t in peers_z:
        c = _copy(e.at[0], g1a.at[b], send_sems.at[0, t], recv_sems.at[0, b], a * RING + t)
        c.start()
        first.append(c)
    for t in peers_x:
        c = _copy(e.at[1], g1b.at[a], send_sems.at[1, t], recv_sems.at[1, a], t * RING + b)
        c.start()
        first.append(c)
    g1a[b] = e[0]
    g1b[a] = e[1]
    for t in peers_z:
        _copy(e.at[0], g1a.at[t], send_sems.at[0, t], recv_sems.at[0, t], 0).wait_recv()
    for t in peers_x:
        _copy(e.at[1], g1b.at[t], send_sems.at[1, t], recv_sems.at[1, t], 0).wait_recv()
    second = []
    for t in peers_x:
        c = _copy(g1a, ga.at[a], send_sems.at[2, t], recv_sems.at[2, a], t * RING + b)
        c.start()
        second.append(c)
    for t in peers_z:
        c = _copy(g1b, gb.at[b], send_sems.at[3, t], recv_sems.at[3, b], a * RING + t)
        c.start()
        second.append(c)
    oa[a] = g1a[...]
    for j in range(RING):
        ob[j, b] = g1b[j]
    for t in peers_x:
        _copy(g1a, ga.at[t], send_sems.at[2, t], recv_sems.at[2, t], 0).wait_recv()
        oa[t] = ga[t]
    for t in peers_z:
        _copy(g1b, gb.at[t], send_sems.at[3, t], recv_sems.at[3, t], 0).wait_recv()
        for j in range(RING):
            ob[j, t] = gb[t, j]
    for c in first + second:
        c.wait_send()


def latent_gather(e, collective_id):
    _, h, c = e.shape
    n = RING
    dt = e.dtype
    full = jax.ShapeDtypeStruct((n, n, h, c), dt)
    return pl.pallas_call(
        _gather_kernel,
        out_shape=(full, full),
        in_specs=[pl.BlockSpec(memory_space=pltpu.VMEM)],
        out_specs=(pl.BlockSpec(memory_space=pltpu.VMEM), pl.BlockSpec(memory_space=pltpu.VMEM)),
        scratch_shapes=[
            pltpu.VMEM((n, h, c), dt),
            pltpu.VMEM((n, h, c), dt),
            pltpu.VMEM((n, n, h, c), dt),
            pltpu.VMEM((n, n, h, c), dt),
            pltpu.SemaphoreType.DMA((4, n)),
            pltpu.SemaphoreType.DMA((4, n)),
        ],
        compiler_params=pltpu.CompilerParams(collective_id=collective_id, has_side_effects=True),
    )(e)


def _layer_roles():
    me = lax.axis_index("layer")
    mate = me + 1 - 2 * (me % 2)
    far = (me + 2) % LAYERS
    return me, mate, far, (mate + 2) % LAYERS


def _layer_exchange(quarter, x, out, finish, produce, ra, sb, rb, rc, rd, send_sems, recv_sems):
    me, mate, far, mate_far = _layer_roles()
    barrier = pltpu.get_barrier_semaphore()
    for p in (mate, far):
        pl.semaphore_signal(barrier, inc=1, device_id={"layer": p}, device_id_type=MESH)
    pl.semaphore_wait(barrier, 2)

    def copy(src, dst, k, p):
        return pltpu.make_async_remote_copy(
            src_ref=src, dst_ref=dst, send_sem=send_sems.at[k], recv_sem=recv_sems.at[k],
            device_id={"layer": p}, device_id_type=MESH,
        )

    produce(mate)
    produce(mate_far)
    sent = [copy(quarter(x, mate), ra.at[0], 0, mate), copy(quarter(x, mate_far), ra.at[1], 1, mate)]
    for c in sent:
        c.start()
    produce(far)
    produce(me)
    sent[0].wait_recv()
    sent[1].wait_recv()
    sb[...] = quarter(x, far)[...].astype(jnp.float32) + ra[1].astype(jnp.float32)
    step_b = copy(sb, rb, 2, far)
    step_b.start()
    own = quarter(x, me)[...].astype(jnp.float32) + ra[0].astype(jnp.float32)
    step_b.wait_recv()
    quarter(out, me)[...] = finish(own + rb[...])
    step_c = copy(quarter(out, me), rc, 3, far)
    step_c.start()
    step_c.wait_recv()
    quarter(out, far)[...] = rc[...]
    step_d = [copy(quarter(out, me), rd.at[0], 4, mate), copy(rc, rd.at[1], 5, mate)]
    for c in step_d:
        c.start()
    for c in step_d:
        c.wait_recv()
    quarter(out, mate)[...] = rd[0]
    quarter(out, mate_far)[...] = rd[1]
    for c in sent + [step_b, step_c] + step_d:
        c.wait_send()


def _row_quarter(ref, i):
    q = ref.shape[0] // LAYERS
    return ref.at[pl.ds(pl.multiple_of(i * q, q), q)]


def _lane_quarter(ref, i):
    q = ref.shape[1] // LAYERS
    return ref.at[:, pl.ds(pl.multiple_of(i * q, q), q)]


def _layer_pre_kernel(inp, w, bias, feats, pre_q, x, *scratch):
    def finish(total):
        pre = total + bias[...].reshape(1, -1)
        pre_q[...] = pre
        return jnp.maximum(pre, 0.0).astype(feats.dtype)

    def produce(i):
        _row_quarter(x, i)[...] = jnp.dot(
            _row_quarter(inp, i)[...], w[...], preferred_element_type=jnp.float32
        )

    _layer_exchange(_row_quarter, x, feats, finish, produce, *scratch)


def _layer_scratch(in_q, out_q, in_dtype):
    return [
        pltpu.VMEM((2,) + in_q, in_dtype),
        pltpu.VMEM(in_q, jnp.float32),
        pltpu.VMEM(in_q, jnp.float32),
        pltpu.VMEM(out_q, jnp.bfloat16),
        pltpu.VMEM((2,) + out_q, jnp.bfloat16),
        pltpu.SemaphoreType.DMA((6,)),
        pltpu.SemaphoreType.DMA((6,)),
    ]


def layer_pre(inp, w, bias):
    rows, cols = inp.shape[0], w.shape[1]
    q = rows // LAYERS
    return pl.pallas_call(
        _layer_pre_kernel,
        out_shape=(jax.ShapeDtypeStruct((rows, cols), jnp.bfloat16),
                   jax.ShapeDtypeStruct((q, cols), jnp.float32)),
        in_specs=[pl.BlockSpec(memory_space=pltpu.VMEM)] * 3,
        out_specs=(pl.BlockSpec(memory_space=pltpu.VMEM), pl.BlockSpec(memory_space=pltpu.VMEM)),
        scratch_shapes=[pltpu.VMEM((rows, cols), jnp.float32)]
        + _layer_scratch((q, cols), (q, cols), jnp.float32),
        compiler_params=pltpu.CompilerParams(collective_id=1, has_side_effects=True),
    )(inp, w, bias)


def _layer_peers():
    me = lax.axis_index("layer")
    return me, [(me + k) % LAYERS for k in range(1, LAYERS)]


def _layer_greet(peers):
    barrier = pltpu.get_barrier_semaphore()
    for p in peers:
        pl.semaphore_signal(barrier, inc=1, device_id={"layer": p}, device_id_type=MESH)
    pl.semaphore_wait(barrier, LAYERS - 1)


def _layer_copy(src, dst, send_sems, recv_sems, k, p, slot):
    return pltpu.make_async_remote_copy(
        src_ref=src, dst_ref=dst, send_sem=send_sems.at[k, p], recv_sem=recv_sems.at[k, slot],
        device_id={"layer": p}, device_id_type=MESH,
    )


def _layer_grad_kernel(g, pre_q, margin_q, out, r1, r2, send_sems, recv_sems):
    me, peers = _layer_peers()
    q = g.shape[1] // LAYERS
    lanes = lambda i: pl.ds(pl.multiple_of(i * q, q), q)
    _layer_greet(peers)
    sent = []
    for p in peers:
        c = _layer_copy(g.at[:, lanes(p)], r1.at[me], send_sems, recv_sems, 0, p, me)
        c.start()
        sent.append(c)
    total = g[:, lanes(me)].astype(jnp.float32)
    for p in peers:
        _layer_copy(g.at[:, lanes(p)], r1.at[p], send_sems, recv_sems, 0, p, p).wait_recv()
        total = total + r1[p].astype(jnp.float32)
    grad = jnp.where(pre_q[...] > 0, total - MARGIN * margin_q[...], 0.0)
    out[:, lanes(me)] = grad.astype(out.dtype)
    for p in peers:
        c = _layer_copy(out.at[:, lanes(me)], r2.at[me], send_sems, recv_sems, 1, p, me)
        c.start()
        sent.append(c)
    for p in peers:
        _layer_copy(out.at[:, lanes(p)], r2.at[p], send_sems, recv_sems, 1, p, p).wait_recv()
        out[:, lanes(p)] = r2[p]
    for c in sent:
        c.wait_send()


def layer_grad(g, pre_q, margin_q):
    cols, rows = g.shape
    q = rows // LAYERS
    return pl.pallas_call(
        _layer_grad_kernel,
        out_shape=jax.ShapeDtypeStruct((cols, rows), jnp.bfloat16),
        in_specs=[pl.BlockSpec(memory_space=pltpu.VMEM)] * 3,
        out_specs=pl.BlockSpec(memory_space=pltpu.VMEM),
        scratch_shapes=[
            pltpu.VMEM((LAYERS, cols, q), jnp.bfloat16),
            pltpu.VMEM((LAYERS, cols, q), jnp.bfloat16),
            pltpu.SemaphoreType.DMA((2, LAYERS)),
            pltpu.SemaphoreType.DMA((2, LAYERS)),
        ],
        compiler_params=pltpu.CompilerParams(collective_id=2, has_side_effects=True),
    )(g, pre_q, margin_q)


def local(inputs, clean_acts, enc_weight, enc_bias, dec_weight, dec_bias, pairing, targets):
    row_count = inputs.shape[0]
    lat_count = enc_weight.shape[2]
    all_rows = pairing.shape[0]
    d_model = inputs.shape[2]
    chunk = d_model // (RING * RING)
    half = row_count // 2
    me = lax.axis_index("latent")
    features, pre_q = layer_pre(inputs[:, 0, :], enc_weight[0], enc_bias)
    dec4 = dec_weight[0].reshape(lat_count, RING, RING, chunk)
    recon_part = jnp.einsum("rf,fabd->abdr", features, dec4, preferred_element_type=jnp.float32)
    bias_part = lax.dynamic_slice_in_dim(dec_bias[0], me * chunk, chunk)
    clean_part = lax.dynamic_slice_in_dim(clean_acts[:, 0, :], me * chunk, chunk, axis=1)
    clean_t = jnp.swapaxes(clean_part.reshape(2, half, chunk), 1, 2)
    recon_error = latent_reduce(recon_part, bias_part[:, None], clean_t, 3)
    error_a, error_b = latent_gather(recon_error, 4)
    error_all = jnp.concatenate(
        [error_a.reshape(d_model, half), error_b.reshape(d_model, half)], axis=1
    )
    partial_grad_t = jnp.dot(dec_weight[0], error_all, preferred_element_type=jnp.float32)
    quarter = row_count // LAYERS
    row_ids = (
        lax.axis_index("row") * row_count
        + lax.axis_index("layer") * quarter
        + jnp.arange(quarter, dtype=jnp.int32)
    )
    latent_ids = me * lat_count + jnp.arange(lat_count, dtype=jnp.int32)
    every_row = jnp.arange(all_rows, dtype=jnp.int32)
    pair_table_t = (
        (every_row[:, None] == row_ids[None, :]).astype(jnp.float32)
        - (pairing[:, None] == row_ids[None, :]).astype(jnp.float32)
    ).astype(jnp.bfloat16)
    target_hot_t = (latent_ids[:, None] == targets[None, :]).astype(jnp.bfloat16)
    margin_q = jnp.dot(target_hot_t, pair_table_t, preferred_element_type=jnp.float32)
    pre_grad_t = layer_grad(partial_grad_t.astype(jnp.bfloat16), pre_q.T, margin_q)
    enc4 = enc_weight[0].reshape(RING, RING, chunk, lat_count)
    total = latent_reduce_mm(enc4, pre_grad_t, 5)
    return jnp.swapaxes(total.astype(jnp.bfloat16), 1, 2).reshape(row_count, 1, chunk)


def solution(mesh):
    placed = (
        P("row", "layer", None),
        P("row", "layer", None),
        P("layer", None, "latent"),
        P("latent"),
        P("layer", "latent", None),
        P("layer", None),
        P(),
        P(),
    )
    return jax.shard_map(
        local, mesh=mesh, in_specs=placed, out_specs=P("row", "layer", "latent"), check_vma=False
    )
```

```python
import jax
import jax.numpy as jnp
from jax import lax
from jax.experimental import pallas as pl
from jax.experimental.pallas import tpu as pltpu
from jax.sharding import PartitionSpec as P

MARGIN = 16.0
MESH = pl.DeviceIdType.MESH
RING = 4
LAYERS = 4


def _latent_coords():
    me = lax.axis_index("latent")
    return me // RING, me % RING


def _greet(a, b):
    barrier = pltpu.get_barrier_semaphore()
    for k in range(1, RING):
        pl.semaphore_signal(barrier, inc=1, device_id={"latent": a * RING + (b + k) % RING}, device_id_type=MESH)
        pl.semaphore_signal(barrier, inc=1, device_id={"latent": ((a + k) % RING) * RING + b}, device_id_type=MESH)
    pl.semaphore_wait(barrier, 2 * (RING - 1))


def _copy(src, dst, send_sem, recv_sem, peer):
    return pltpu.make_async_remote_copy(
        src_ref=src, dst_ref=dst, send_sem=send_sem, recv_sem=recv_sem,
        device_id={"latent": peer}, device_id_type=MESH,
    )


def _reduce_kernel(x, bias, clean, out, r1a, r1b, s1a, s1b, r2a, r2b, send_sems, recv_sems):
    h = x.shape[-1] // 2
    xa = x.at[:, :, :, pl.ds(0, h)]
    xb = x.at[:, :, :, pl.ds(h, h)]
    a, b = _latent_coords()
    _greet(a, b)
    peers_z = [(b + k) % RING for k in range(1, RING)]
    peers_x = [(a + k) % RING for k in range(1, RING)]
    first = []
    for t in peers_z:
        c = _copy(xa.at[:, t], r1a.at[b], send_sems.at[0, t], recv_sems.at[0, b], a * RING + t)
        c.start()
        first.append(c)
    for t in peers_x:
        c = _copy(xb.at[t], r1b.at[a], send_sems.at[1, t], recv_sems.at[1, a], t * RING + b)
        c.start()
        first.append(c)
    for t in peers_z:
        _copy(xa.at[:, t], r1a.at[t], send_sems.at[0, t], recv_sems.at[0, t], 0).wait_recv()
    for t in peers_x:
        _copy(xb.at[t], r1b.at[t], send_sems.at[1, t], recv_sems.at[1, t], 0).wait_recv()
    sum_a = xa[:, b].astype(jnp.float32)
    for t in peers_z:
        sum_a = sum_a + r1a[t].astype(jnp.float32)
    sum_b = xb[a].astype(jnp.float32)
    for t in peers_x:
        sum_b = sum_b + r1b[t].astype(jnp.float32)
    s1a[...] = sum_a.astype(s1a.dtype)
    s1b[...] = sum_b.astype(s1b.dtype)
    second = []
    for t in peers_x:
        c = _copy(s1a.at[t], r2a.at[a], send_sems.at[2, t], recv_sems.at[2, a], t * RING + b)
        c.start()
        second.append(c)
    for t in peers_z:
        c = _copy(s1b.at[t], r2b.at[b], send_sems.at[3, t], recv_sems.at[3, b], a * RING + t)
        c.start()
        second.append(c)
    for t in peers_x:
        _copy(s1a.at[t], r2a.at[t], send_sems.at[2, t], recv_sems.at[2, t], 0).wait_recv()
    for t in peers_z:
        _copy(s1b.at[t], r2b.at[t], send_sems.at[3, t], recv_sems.at[3, t], 0).wait_recv()
    own_a = xa[a, b].astype(jnp.float32)
    for t in peers_z:
        own_a = own_a + r1a[t, a].astype(jnp.float32)
    own_b = xb[a, b].astype(jnp.float32)
    for t in peers_x:
        own_b = own_b + r1b[t, b].astype(jnp.float32)
    for t in peers_x:
        own_a = own_a + r2a[t].astype(jnp.float32)
    for t in peers_z:
        own_b = own_b + r2b[t].astype(jnp.float32)
    out[0] = (own_a + bias[...] - clean[0].astype(jnp.float32)).astype(out.dtype)
    out[1] = (own_b + bias[...] - clean[1].astype(jnp.float32)).astype(out.dtype)
    for c in first + second:
        c.wait_send()


def latent_reduce(x, bias, clean, collective_id):
    n, _, h, c = x.shape
    c = c // 2
    dt = x.dtype
    return pl.pallas_call(
        _reduce_kernel,
        out_shape=jax.ShapeDtypeStruct((2, h, c), jnp.bfloat16),
        in_specs=[pl.BlockSpec(memory_space=pltpu.VMEM)] * 3,
        out_specs=pl.BlockSpec(memory_space=pltpu.VMEM),
        scratch_shapes=[
            pltpu.VMEM((n, n, h, c), dt),
            pltpu.VMEM((n, n, h, c), dt),
            pltpu.VMEM((n, h, c), dt),
            pltpu.VMEM((n, h, c), dt),
            pltpu.VMEM((n, h, c), dt),
            pltpu.VMEM((n, h, c), dt),
            pltpu.SemaphoreType.DMA((4, n)),
            pltpu.SemaphoreType.DMA((4, n)),
        ],
        compiler_params=pltpu.CompilerParams(collective_id=collective_id, has_side_effects=True),
    )(x, bias, clean)


def _reduce_mm_kernel(w, v, out, xa, xb, r1a, r1b, s1a, s1b, r2a, r2b, send_sems, recv_sems):
    a, b = _latent_coords()
    _greet(a, b)
    h = v.shape[1] // 2
    peers_z = [(b + k) % RING for k in range(1, RING)]
    peers_x = [(a + k) % RING for k in range(1, RING)]

    def fill(dst, i, j, half):
        prod = jnp.dot(w[i, j], v[:, half * h:(half + 1) * h], preferred_element_type=jnp.float32)
        dst[i, j] = prod.astype(dst.dtype)

    first = []
    for kz, kx in zip(peers_z, peers_x):
        for i in range(RING):
            fill(xa, i, kz, 0)
        c = _copy(xa.at[:, kz], r1a.at[b], send_sems.at[0, kz], recv_sems.at[0, b], a * RING + kz)
        c.start()
        first.append(c)
        for j in range(RING):
            fill(xb, kx, j, 1)
        c = _copy(xb.at[kx], r1b.at[a], send_sems.at[1, kx], recv_sems.at[1, a], kx * RING + b)
        c.start()
        first.append(c)
    for i in range(RING):
        fill(xa, i, b, 0)
    for j in range(RING):
        fill(xb, a, j, 1)
    for t in peers_z:
        _copy(xa.at[:, t], r1a.at[t], send_sems.at[0, t], recv_sems.at[0, t], 0).wait_recv()
    for t in peers_x:
        _copy(xb.at[t], r1b.at[t], send_sems.at[1, t], recv_sems.at[1, t], 0).wait_recv()
    sum_a = xa[:, b].astype(jnp.float32)
    for t in peers_z:
        sum_a = sum_a + r1a[t].astype(jnp.float32)
    sum_b = xb[a].astype(jnp.float32)
    for t in peers_x:
        sum_b = sum_b + r1b[t].astype(jnp.float32)
    s1a[...] = sum_a.astype(s1a.dtype)
    s1b[...] = sum_b.astype(s1b.dtype)
    second = []
    for t in peers_x:
        c = _copy(s1a.at[t], r2a.at[a], send_sems.at[2, t], recv_sems.at[2, a], t * RING + b)
        c.start()
        second.append(c)
    for t in peers_z:
        c = _copy(s1b.at[t], r2b.at[b], send_sems.at[3, t], recv_sems.at[3, b], a * RING + t)
        c.start()
        second.append(c)
    for t in peers_x:
        _copy(s1a.at[t], r2a.at[t], send_sems.at[2, t], recv_sems.at[2, t], 0).wait_recv()
    for t in peers_z:
        _copy(s1b.at[t], r2b.at[t], send_sems.at[3, t], recv_sems.at[3, t], 0).wait_recv()
    own_a = xa[a, b].astype(jnp.float32)
    own_b = xb[a, b].astype(jnp.float32)
    for k in range(1, RING):
        own_a = own_a + r1a[(b + k) % RING, a].astype(jnp.float32)
        own_b = own_b + r1b[(a + k) % RING, b].astype(jnp.float32)
    for k in range(1, RING):
        own_a = own_a + r2a[(a + k) % RING].astype(jnp.float32)
        own_b = own_b + r2b[(b + k) % RING].astype(jnp.float32)
    out[0] = own_a
    out[1] = own_b
    for c in first + second:
        c.wait_send()


def latent_reduce_mm(w, v, collective_id):
    n, _, d, _ = w.shape
    h = v.shape[1] // 2
    dt = w.dtype
    return pl.pallas_call(
        _reduce_mm_kernel,
        out_shape=jax.ShapeDtypeStruct((2, d, h), jnp.float32),
        in_specs=[pl.BlockSpec(memory_space=pltpu.VMEM)] * 2,
        out_specs=pl.BlockSpec(memory_space=pltpu.VMEM),
        scratch_shapes=[
            pltpu.VMEM((n, n, d, h), dt),
            pltpu.VMEM((n, n, d, h), dt),
            pltpu.VMEM((n, n, d, h), dt),
            pltpu.VMEM((n, n, d, h), dt),
            pltpu.VMEM((n, d, h), dt),
            pltpu.VMEM((n, d, h), dt),
            pltpu.VMEM((n, d, h), dt),
            pltpu.VMEM((n, d, h), dt),
            pltpu.SemaphoreType.DMA((4, n)),
            pltpu.SemaphoreType.DMA((4, n)),
        ],
        compiler_params=pltpu.CompilerParams(collective_id=collective_id, has_side_effects=True),
    )(w, v)


def _gather_kernel(e, targets, pairing, oa, ob, margin, g1a, g1b, ga, gb, send_sems, recv_sems):
    a, b = _latent_coords()
    _greet(a, b)
    peers_z = [(b + k) % RING for k in range(1, RING)]
    peers_x = [(a + k) % RING for k in range(1, RING)]
    first = []
    for t in peers_z:
        c = _copy(e.at[0], g1a.at[b], send_sems.at[0, t], recv_sems.at[0, b], a * RING + t)
        c.start()
        first.append(c)
    for t in peers_x:
        c = _copy(e.at[1], g1b.at[a], send_sems.at[1, t], recv_sems.at[1, a], t * RING + b)
        c.start()
        first.append(c)
    g1a[b] = e[0]
    g1b[a] = e[1]
    for t in peers_z:
        _copy(e.at[0], g1a.at[t], send_sems.at[0, t], recv_sems.at[0, t], 0).wait_recv()
    for t in peers_x:
        _copy(e.at[1], g1b.at[t], send_sems.at[1, t], recv_sems.at[1, t], 0).wait_recv()
    second = []
    for t in peers_x:
        c = _copy(g1a, ga.at[a], send_sems.at[2, t], recv_sems.at[2, a], t * RING + b)
        c.start()
        second.append(c)
    for t in peers_z:
        c = _copy(g1b, gb.at[b], send_sems.at[3, t], recv_sems.at[3, b], a * RING + t)
        c.start()
        second.append(c)
    oa[a] = g1a[...]
    f, q = margin.shape
    n_rows = pairing.shape[0]
    lat0 = lax.axis_index("latent") * f
    row0 = lax.axis_index("row") * (LAYERS * q) + lax.axis_index("layer") * q
    lat_ids = lat0 + lax.broadcasted_iota(jnp.int32, (f, n_rows), 0)
    target_hot = (lat_ids == targets[...]).astype(jnp.bfloat16)
    row_ids = row0 + lax.broadcasted_iota(jnp.int32, (n_rows, q), 1)
    every_row = lax.broadcasted_iota(jnp.int32, (n_rows, q), 0)
    pair_table = (
        (every_row == row_ids).astype(jnp.float32) - (pairing[...] == row_ids).astype(jnp.float32)
    ).astype(jnp.bfloat16)
    margin[...] = jnp.dot(target_hot, pair_table, preferred_element_type=jnp.float32)
    for j in range(RING):
        ob[j, b] = g1b[j]
    for t in peers_x:
        _copy(g1a, ga.at[t], send_sems.at[2, t], recv_sems.at[2, t], 0).wait_recv()
        oa[t] = ga[t]
    for t in peers_z:
        _copy(g1b, gb.at[t], send_sems.at[3, t], recv_sems.at[3, t], 0).wait_recv()
        for j in range(RING):
            ob[j, t] = gb[t, j]
    for c in first + second:
        c.wait_send()


def latent_gather(e, targets, pairing, lat_count, collective_id):
    _, h, c = e.shape
    n = RING
    dt = e.dtype
    full = jax.ShapeDtypeStruct((n, n, h, c), dt)
    return pl.pallas_call(
        _gather_kernel,
        out_shape=(full, full, jax.ShapeDtypeStruct((lat_count, 2 * c // LAYERS), jnp.float32)),
        in_specs=[pl.BlockSpec(memory_space=pltpu.VMEM)] * 3,
        out_specs=(pl.BlockSpec(memory_space=pltpu.VMEM),) * 3,
        scratch_shapes=[
            pltpu.VMEM((n, h, c), dt),
            pltpu.VMEM((n, h, c), dt),
            pltpu.VMEM((n, n, h, c), dt),
            pltpu.VMEM((n, n, h, c), dt),
            pltpu.SemaphoreType.DMA((4, n)),
            pltpu.SemaphoreType.DMA((4, n)),
        ],
        compiler_params=pltpu.CompilerParams(collective_id=collective_id, has_side_effects=True),
    )(e, targets, pairing)


def _layer_roles():
    me = lax.axis_index("layer")
    mate = me + 1 - 2 * (me % 2)
    far = (me + 2) % LAYERS
    return me, mate, far, (mate + 2) % LAYERS


def _layer_exchange(quarter, x, out, finish, produce, ra, sb, rb, rc, rd, send_sems, recv_sems):
    me, mate, far, mate_far = _layer_roles()
    barrier = pltpu.get_barrier_semaphore()
    for p in (mate, far):
        pl.semaphore_signal(barrier, inc=1, device_id={"layer": p}, device_id_type=MESH)
    pl.semaphore_wait(barrier, 2)

    def copy(src, dst, k, p):
        return pltpu.make_async_remote_copy(
            src_ref=src, dst_ref=dst, send_sem=send_sems.at[k], recv_sem=recv_sems.at[k],
            device_id={"layer": p}, device_id_type=MESH,
        )

    produce(mate)
    produce(mate_far)
    sent = [copy(quarter(x, mate), ra.at[0], 0, mate), copy(quarter(x, mate_far), ra.at[1], 1, mate)]
    for c in sent:
        c.start()
    produce(far)
    produce(me)
    sent[0].wait_recv()
    sent[1].wait_recv()
    sb[...] = quarter(x, far)[...].astype(jnp.float32) + ra[1].astype(jnp.float32)
    step_b = copy(sb, rb, 2, far)
    step_b.start()
    own = quarter(x, me)[...].astype(jnp.float32) + ra[0].astype(jnp.float32)
    step_b.wait_recv()
    quarter(out, me)[...] = finish(own + rb[...])
    step_c = copy(quarter(out, me), rc, 3, far)
    step_c.start()
    step_c.wait_recv()
    quarter(out, far)[...] = rc[...]
    step_d = [copy(quarter(out, me), rd.at[0], 4, mate), copy(rc, rd.at[1], 5, mate)]
    for c in step_d:
        c.start()
    for c in step_d:
        c.wait_recv()
    quarter(out, mate)[...] = rd[0]
    quarter(out, mate_far)[...] = rd[1]
    for c in sent + [step_b, step_c] + step_d:
        c.wait_send()


def _row_quarter(ref, i):
    q = ref.shape[0] // LAYERS
    return ref.at[pl.ds(pl.multiple_of(i * q, q), q)]


def _lane_quarter(ref, i):
    q = ref.shape[1] // LAYERS
    return ref.at[:, pl.ds(pl.multiple_of(i * q, q), q)]


def _layer_pre_kernel(inp, w, bias, feats, pre_q, x, *scratch):
    def finish(total):
        pre = total + bias[...].reshape(1, -1)
        pre_q[...] = pre
        return jnp.maximum(pre, 0.0).astype(feats.dtype)

    def produce(i):
        _row_quarter(x, i)[...] = jnp.dot(
            _row_quarter(inp, i)[...], w[...], preferred_element_type=jnp.float32
        )

    _layer_exchange(_row_quarter, x, feats, finish, produce, *scratch)


def _layer_scratch(in_q, out_q, in_dtype):
    return [
        pltpu.VMEM((2,) + in_q, in_dtype),
        pltpu.VMEM(in_q, jnp.float32),
        pltpu.VMEM(in_q, jnp.float32),
        pltpu.VMEM(out_q, jnp.bfloat16),
        pltpu.VMEM((2,) + out_q, jnp.bfloat16),
        pltpu.SemaphoreType.DMA((6,)),
        pltpu.SemaphoreType.DMA((6,)),
    ]


def layer_pre(inp, w, bias):
    rows, cols = inp.shape[0], w.shape[1]
    q = rows // LAYERS
    return pl.pallas_call(
        _layer_pre_kernel,
        out_shape=(jax.ShapeDtypeStruct((rows, cols), jnp.bfloat16),
                   jax.ShapeDtypeStruct((q, cols), jnp.float32)),
        in_specs=[pl.BlockSpec(memory_space=pltpu.VMEM)] * 3,
        out_specs=(pl.BlockSpec(memory_space=pltpu.VMEM), pl.BlockSpec(memory_space=pltpu.VMEM)),
        scratch_shapes=[pltpu.VMEM((rows, cols), jnp.float32)]
        + _layer_scratch((q, cols), (q, cols), jnp.float32),
        compiler_params=pltpu.CompilerParams(collective_id=1, has_side_effects=True),
    )(inp, w, bias)


def _layer_peers():
    me = lax.axis_index("layer")
    return me, [(me + k) % LAYERS for k in range(1, LAYERS)]


def _layer_greet(peers):
    barrier = pltpu.get_barrier_semaphore()
    for p in peers:
        pl.semaphore_signal(barrier, inc=1, device_id={"layer": p}, device_id_type=MESH)
    pl.semaphore_wait(barrier, LAYERS - 1)


def _layer_copy(src, dst, send_sems, recv_sems, k, p, slot):
    return pltpu.make_async_remote_copy(
        src_ref=src, dst_ref=dst, send_sem=send_sems.at[k, p], recv_sem=recv_sems.at[k, slot],
        device_id={"layer": p}, device_id_type=MESH,
    )


def _layer_grad_kernel(g, pre_q, margin_q, out, r1, r2, send_sems, recv_sems):
    me, peers = _layer_peers()
    q = g.shape[1] // LAYERS
    lanes = lambda i: pl.ds(pl.multiple_of(i * q, q), q)
    _layer_greet(peers)
    sent = []
    for p in peers:
        c = _layer_copy(g.at[:, lanes(p)], r1.at[me], send_sems, recv_sems, 0, p, me)
        c.start()
        sent.append(c)
    total = g[:, lanes(me)].astype(jnp.float32)
    for p in peers:
        _layer_copy(g.at[:, lanes(p)], r1.at[p], send_sems, recv_sems, 0, p, p).wait_recv()
        total = total + r1[p].astype(jnp.float32)
    grad = jnp.where(pre_q[...] > 0, total - MARGIN * margin_q[...], 0.0)
    out[:, lanes(me)] = grad.astype(out.dtype)
    for p in peers:
        c = _layer_copy(out.at[:, lanes(me)], r2.at[me], send_sems, recv_sems, 1, p, me)
        c.start()
        sent.append(c)
    for p in peers:
        _layer_copy(out.at[:, lanes(p)], r2.at[p], send_sems, recv_sems, 1, p, p).wait_recv()
        out[:, lanes(p)] = r2[p]
    for c in sent:
        c.wait_send()


def layer_grad(g, pre_q, margin_q):
    cols, rows = g.shape
    q = rows // LAYERS
    return pl.pallas_call(
        _layer_grad_kernel,
        out_shape=jax.ShapeDtypeStruct((cols, rows), jnp.bfloat16),
        in_specs=[pl.BlockSpec(memory_space=pltpu.VMEM)] * 3,
        out_specs=pl.BlockSpec(memory_space=pltpu.VMEM),
        scratch_shapes=[
            pltpu.VMEM((LAYERS, cols, q), jnp.bfloat16),
            pltpu.VMEM((LAYERS, cols, q), jnp.bfloat16),
            pltpu.SemaphoreType.DMA((2, LAYERS)),
            pltpu.SemaphoreType.DMA((2, LAYERS)),
        ],
        compiler_params=pltpu.CompilerParams(collective_id=2, has_side_effects=True),
    )(g, pre_q, margin_q)


def local(inputs, clean_acts, enc_weight, enc_bias, dec_weight, dec_bias, pairing, targets):
    row_count = inputs.shape[0]
    lat_count = enc_weight.shape[2]
    all_rows = pairing.shape[0]
    d_model = inputs.shape[2]
    chunk = d_model // (RING * RING)
    half = row_count // 2
    me = lax.axis_index("latent")
    features, pre_q = layer_pre(inputs[:, 0, :], enc_weight[0], enc_bias)
    dec4 = dec_weight[0].reshape(lat_count, RING, RING, chunk)
    recon_part = jnp.einsum("rf,fabd->abdr", features, dec4, preferred_element_type=jnp.float32)
    bias_part = lax.dynamic_slice_in_dim(dec_bias[0], me * chunk, chunk)
    clean_part = lax.dynamic_slice_in_dim(clean_acts[:, 0, :], me * chunk, chunk, axis=1)
    clean_t = jnp.swapaxes(clean_part.reshape(2, half, chunk), 1, 2)
    recon_error = latent_reduce(recon_part.astype(jnp.bfloat16), bias_part[:, None], clean_t, 3)
    error_a, error_b, margin_q = latent_gather(
        recon_error, targets.reshape(1, all_rows), pairing.reshape(all_rows, 1), lat_count, 4
    )
    error_all = jnp.concatenate(
        [error_a.reshape(d_model, half), error_b.reshape(d_model, half)], axis=1
    )
    partial_grad_t = jnp.dot(dec_weight[0], error_all, preferred_element_type=jnp.float32)
    pre_grad_t = layer_grad(partial_grad_t.astype(jnp.bfloat16), pre_q.T, margin_q)
    enc4 = enc_weight[0].reshape(RING, RING, chunk, lat_count)
    total = latent_reduce_mm(enc4, pre_grad_t, 5)
    return jnp.swapaxes(total.astype(jnp.bfloat16), 1, 2).reshape(row_count, 1, chunk)


def solution(mesh):
    placed = (
        P("row", "layer", None),
        P("row", "layer", None),
        P("layer", None, "latent"),
        P("latent"),
        P("layer", "latent", None),
        P("layer", None),
        P(),
        P(),
    )
    return jax.shard_map(
        local, mesh=mesh, in_specs=placed, out_specs=P("row", "layer", "latent"), check_vma=False
    )
```

```python
import jax
import jax.numpy as jnp
from jax import lax
from jax.experimental import pallas as pl
from jax.experimental.pallas import tpu as pltpu
from jax.sharding import PartitionSpec as P

MARGIN = 16.0
MESH = pl.DeviceIdType.MESH
RING = 4
LAYERS = 4


def _latent_coords():
    me = lax.axis_index("latent")
    return me // RING, me % RING


def _greet(a, b):
    barrier = pltpu.get_barrier_semaphore()
    for k in range(1, RING):
        pl.semaphore_signal(barrier, inc=1, device_id={"latent": a * RING + (b + k) % RING}, device_id_type=MESH)
        pl.semaphore_signal(barrier, inc=1, device_id={"latent": ((a + k) % RING) * RING + b}, device_id_type=MESH)
    pl.semaphore_wait(barrier, 2 * (RING - 1))


def _copy(src, dst, send_sem, recv_sem, peer):
    return pltpu.make_async_remote_copy(
        src_ref=src, dst_ref=dst, send_sem=send_sem, recv_sem=recv_sem,
        device_id={"latent": peer}, device_id_type=MESH,
    )


def _reduce_kernel(x, bias, clean, out, r1a, r1b, s1a, s1b, r2a, r2b, send_sems, recv_sems):
    h = x.shape[-1] // 2
    xa = x.at[:, :, :, pl.ds(0, h)]
    xb = x.at[:, :, :, pl.ds(h, h)]
    a, b = _latent_coords()
    _greet(a, b)
    peers_z = [(b + k) % RING for k in range(1, RING)]
    peers_x = [(a + k) % RING for k in range(1, RING)]
    first = []
    for t in peers_z:
        c = _copy(xa.at[:, t], r1a.at[b], send_sems.at[0, t], recv_sems.at[0, b], a * RING + t)
        c.start()
        first.append(c)
    for t in peers_x:
        c = _copy(xb.at[t], r1b.at[a], send_sems.at[1, t], recv_sems.at[1, a], t * RING + b)
        c.start()
        first.append(c)
    for t in peers_z:
        _copy(xa.at[:, t], r1a.at[t], send_sems.at[0, t], recv_sems.at[0, t], 0).wait_recv()
    for t in peers_x:
        _copy(xb.at[t], r1b.at[t], send_sems.at[1, t], recv_sems.at[1, t], 0).wait_recv()
    sum_a = xa[:, b].astype(jnp.float32)
    for t in peers_z:
        sum_a = sum_a + r1a[t].astype(jnp.float32)
    sum_b = xb[a].astype(jnp.float32)
    for t in peers_x:
        sum_b = sum_b + r1b[t].astype(jnp.float32)
    s1a[...] = sum_a.astype(s1a.dtype)
    s1b[...] = sum_b.astype(s1b.dtype)
    second = []
    for t in peers_x:
        c = _copy(s1a.at[t], r2a.at[a], send_sems.at[2, t], recv_sems.at[2, a], t * RING + b)
        c.start()
        second.append(c)
    for t in peers_z:
        c = _copy(s1b.at[t], r2b.at[b], send_sems.at[3, t], recv_sems.at[3, b], a * RING + t)
        c.start()
        second.append(c)
    for t in peers_x:
        _copy(s1a.at[t], r2a.at[t], send_sems.at[2, t], recv_sems.at[2, t], 0).wait_recv()
    for t in peers_z:
        _copy(s1b.at[t], r2b.at[t], send_sems.at[3, t], recv_sems.at[3, t], 0).wait_recv()
    own_a = xa[a, b].astype(jnp.float32)
    for t in peers_z:
        own_a = own_a + r1a[t, a].astype(jnp.float32)
    own_b = xb[a, b].astype(jnp.float32)
    for t in peers_x:
        own_b = own_b + r1b[t, b].astype(jnp.float32)
    for t in peers_x:
        own_a = own_a + r2a[t].astype(jnp.float32)
    for t in peers_z:
        own_b = own_b + r2b[t].astype(jnp.float32)
    out[0] = (own_a + bias[...] - clean[0].astype(jnp.float32)).astype(out.dtype)
    out[1] = (own_b + bias[...] - clean[1].astype(jnp.float32)).astype(out.dtype)
    for c in first + second:
        c.wait_send()


def latent_reduce(x, bias, clean, collective_id):
    n, _, h, c = x.shape
    c = c // 2
    dt = x.dtype
    return pl.pallas_call(
        _reduce_kernel,
        out_shape=jax.ShapeDtypeStruct((2, h, c), jnp.bfloat16),
        in_specs=[pl.BlockSpec(memory_space=pltpu.VMEM)] * 3,
        out_specs=pl.BlockSpec(memory_space=pltpu.VMEM),
        scratch_shapes=[
            pltpu.VMEM((n, n, h, c), dt),
            pltpu.VMEM((n, n, h, c), dt),
            pltpu.VMEM((n, h, c), dt),
            pltpu.VMEM((n, h, c), dt),
            pltpu.VMEM((n, h, c), dt),
            pltpu.VMEM((n, h, c), dt),
            pltpu.SemaphoreType.DMA((4, n)),
            pltpu.SemaphoreType.DMA((4, n)),
        ],
        compiler_params=pltpu.CompilerParams(collective_id=collective_id, has_side_effects=True),
    )(x, bias, clean)


def _reduce_mm_kernel(w, v, out, xa, xb, r1a, r1b, s1a, s1b, r2a, r2b, send_sems, recv_sems):
    a, b = _latent_coords()
    _greet(a, b)
    h = v.shape[1] // 2
    peers_z = [(b + k) % RING for k in range(1, RING)]
    peers_x = [(a + k) % RING for k in range(1, RING)]

    def fill(dst, i, j, half):
        prod = jnp.dot(w[i, j], v[:, half * h:(half + 1) * h], preferred_element_type=jnp.float32)
        dst[i, j] = prod.astype(dst.dtype)

    first = []
    for kz, kx in zip(peers_z, peers_x):
        for i in range(RING):
            fill(xa, i, kz, 0)
        c = _copy(xa.at[:, kz], r1a.at[b], send_sems.at[0, kz], recv_sems.at[0, b], a * RING + kz)
        c.start()
        first.append(c)
        for j in range(RING):
            fill(xb, kx, j, 1)
        c = _copy(xb.at[kx], r1b.at[a], send_sems.at[1, kx], recv_sems.at[1, a], kx * RING + b)
        c.start()
        first.append(c)
    for i in range(RING):
        fill(xa, i, b, 0)
    for j in range(RING):
        fill(xb, a, j, 1)
    for t in peers_z:
        _copy(xa.at[:, t], r1a.at[t], send_sems.at[0, t], recv_sems.at[0, t], 0).wait_recv()
    for t in peers_x:
        _copy(xb.at[t], r1b.at[t], send_sems.at[1, t], recv_sems.at[1, t], 0).wait_recv()
    sum_a = xa[:, b].astype(jnp.float32)
    for t in peers_z:
        sum_a = sum_a + r1a[t].astype(jnp.float32)
    sum_b = xb[a].astype(jnp.float32)
    for t in peers_x:
        sum_b = sum_b + r1b[t].astype(jnp.float32)
    s1a[...] = sum_a.astype(s1a.dtype)
    s1b[...] = sum_b.astype(s1b.dtype)
    second = []
    for t in peers_x:
        c = _copy(s1a.at[t], r2a.at[a], send_sems.at[2, t], recv_sems.at[2, a], t * RING + b)
        c.start()
        second.append(c)
    for t in peers_z:
        c = _copy(s1b.at[t], r2b.at[b], send_sems.at[3, t], recv_sems.at[3, b], a * RING + t)
        c.start()
        second.append(c)
    for t in peers_x:
        _copy(s1a.at[t], r2a.at[t], send_sems.at[2, t], recv_sems.at[2, t], 0).wait_recv()
    for t in peers_z:
        _copy(s1b.at[t], r2b.at[t], send_sems.at[3, t], recv_sems.at[3, t], 0).wait_recv()
    own_a = xa[a, b].astype(jnp.float32)
    own_b = xb[a, b].astype(jnp.float32)
    for k in range(1, RING):
        own_a = own_a + r1a[(b + k) % RING, a].astype(jnp.float32)
        own_b = own_b + r1b[(a + k) % RING, b].astype(jnp.float32)
    for k in range(1, RING):
        own_a = own_a + r2a[(a + k) % RING].astype(jnp.float32)
        own_b = own_b + r2b[(b + k) % RING].astype(jnp.float32)
    out[0] = own_a
    out[1] = own_b
    for c in first + second:
        c.wait_send()


def latent_reduce_mm(w, v, collective_id):
    n, _, d, _ = w.shape
    h = v.shape[1] // 2
    dt = w.dtype
    return pl.pallas_call(
        _reduce_mm_kernel,
        out_shape=jax.ShapeDtypeStruct((2, d, h), jnp.float32),
        in_specs=[pl.BlockSpec(memory_space=pltpu.VMEM)] * 2,
        out_specs=pl.BlockSpec(memory_space=pltpu.VMEM),
        scratch_shapes=[
            pltpu.VMEM((n, n, d, h), dt),
            pltpu.VMEM((n, n, d, h), dt),
            pltpu.VMEM((n, n, d, h), dt),
            pltpu.VMEM((n, n, d, h), dt),
            pltpu.VMEM((n, d, h), dt),
            pltpu.VMEM((n, d, h), dt),
            pltpu.VMEM((n, d, h), dt),
            pltpu.VMEM((n, d, h), dt),
            pltpu.SemaphoreType.DMA((4, n)),
            pltpu.SemaphoreType.DMA((4, n)),
        ],
        compiler_params=pltpu.CompilerParams(collective_id=collective_id, has_side_effects=True),
    )(w, v)


def _gather_kernel(e, targets, pairing, oa, ob, margin, g1a, g1b, ga, gb, send_sems, recv_sems):
    a, b = _latent_coords()
    _greet(a, b)
    peers_z = [(b + k) % RING for k in range(1, RING)]
    peers_x = [(a + k) % RING for k in range(1, RING)]
    first = []
    for t in peers_z:
        c = _copy(e.at[0], g1a.at[b], send_sems.at[0, t], recv_sems.at[0, b], a * RING + t)
        c.start()
        first.append(c)
    for t in peers_x:
        c = _copy(e.at[1], g1b.at[a], send_sems.at[1, t], recv_sems.at[1, a], t * RING + b)
        c.start()
        first.append(c)
    g1a[b] = e[0]
    g1b[a] = e[1]
    for t in peers_z:
        _copy(e.at[0], g1a.at[t], send_sems.at[0, t], recv_sems.at[0, t], 0).wait_recv()
    for t in peers_x:
        _copy(e.at[1], g1b.at[t], send_sems.at[1, t], recv_sems.at[1, t], 0).wait_recv()
    second = []
    for t in peers_x:
        c = _copy(g1a, ga.at[a], send_sems.at[2, t], recv_sems.at[2, a], t * RING + b)
        c.start()
        second.append(c)
    for t in peers_z:
        c = _copy(g1b, gb.at[b], send_sems.at[3, t], recv_sems.at[3, b], a * RING + t)
        c.start()
        second.append(c)
    oa[a] = g1a[...]
    f, q = margin.shape
    n_rows = pairing.shape[1]
    lat0 = lax.axis_index("latent") * f
    row0 = lax.axis_index("row") * (LAYERS * q) + lax.axis_index("layer") * q
    lat_ids = lat0 + lax.broadcasted_iota(jnp.int32, (f, n_rows), 0)
    target_hot = (lat_ids == targets[...]).astype(jnp.bfloat16)
    row_ids = row0 + lax.broadcasted_iota(jnp.int32, (q, n_rows), 0)
    every_row = lax.broadcasted_iota(jnp.int32, (q, n_rows), 1)
    pair_table = (
        (every_row == row_ids).astype(jnp.float32) - (pairing[...] == row_ids).astype(jnp.float32)
    ).astype(jnp.bfloat16)
    margin[...] = lax.dot_general(
        target_hot, pair_table, (((1,), (1,)), ((), ())), preferred_element_type=jnp.float32
    )
    for j in range(RING):
        ob[j, b] = g1b[j]
    for t in peers_x:
        _copy(g1a, ga.at[t], send_sems.at[2, t], recv_sems.at[2, t], 0).wait_recv()
        oa[t] = ga[t]
    for t in peers_z:
        _copy(g1b, gb.at[t], send_sems.at[3, t], recv_sems.at[3, t], 0).wait_recv()
        for j in range(RING):
            ob[j, t] = gb[t, j]
    for c in first + second:
        c.wait_send()


def latent_gather(e, targets, pairing, lat_count, collective_id):
    _, h, c = e.shape
    n = RING
    dt = e.dtype
    full = jax.ShapeDtypeStruct((n, n, h, c), dt)
    return pl.pallas_call(
        _gather_kernel,
        out_shape=(full, full, jax.ShapeDtypeStruct((lat_count, 2 * c // LAYERS), jnp.float32)),
        in_specs=[pl.BlockSpec(memory_space=pltpu.VMEM)] * 3,
        out_specs=(pl.BlockSpec(memory_space=pltpu.VMEM),) * 3,
        scratch_shapes=[
            pltpu.VMEM((n, h, c), dt),
            pltpu.VMEM((n, h, c), dt),
            pltpu.VMEM((n, n, h, c), dt),
            pltpu.VMEM((n, n, h, c), dt),
            pltpu.SemaphoreType.DMA((4, n)),
            pltpu.SemaphoreType.DMA((4, n)),
        ],
        compiler_params=pltpu.CompilerParams(collective_id=collective_id, has_side_effects=True),
    )(e, targets, pairing)


def _layer_roles():
    me = lax.axis_index("layer")
    mate = me + 1 - 2 * (me % 2)
    far = (me + 2) % LAYERS
    return me, mate, far, (mate + 2) % LAYERS


def _layer_exchange(quarter, x, out, finish, produce, ra, sb, rb, rc, rd, send_sems, recv_sems):
    me, mate, far, mate_far = _layer_roles()
    barrier = pltpu.get_barrier_semaphore()
    for p in (mate, far):
        pl.semaphore_signal(barrier, inc=1, device_id={"layer": p}, device_id_type=MESH)
    pl.semaphore_wait(barrier, 2)

    def copy(src, dst, k, p):
        return pltpu.make_async_remote_copy(
            src_ref=src, dst_ref=dst, send_sem=send_sems.at[k], recv_sem=recv_sems.at[k],
            device_id={"layer": p}, device_id_type=MESH,
        )

    produce(mate)
    produce(mate_far)
    sent = [copy(quarter(x, mate), ra.at[0], 0, mate), copy(quarter(x, mate_far), ra.at[1], 1, mate)]
    for c in sent:
        c.start()
    produce(far)
    produce(me)
    sent[0].wait_recv()
    sent[1].wait_recv()
    sb[...] = quarter(x, far)[...].astype(jnp.float32) + ra[1].astype(jnp.float32)
    step_b = copy(sb, rb, 2, far)
    step_b.start()
    own = quarter(x, me)[...].astype(jnp.float32) + ra[0].astype(jnp.float32)
    step_b.wait_recv()
    quarter(out, me)[...] = finish(own + rb[...])
    step_c = copy(quarter(out, me), rc, 3, far)
    step_c.start()
    step_c.wait_recv()
    quarter(out, far)[...] = rc[...]
    step_d = [copy(quarter(out, me), rd.at[0], 4, mate), copy(rc, rd.at[1], 5, mate)]
    for c in step_d:
        c.start()
    for c in step_d:
        c.wait_recv()
    quarter(out, mate)[...] = rd[0]
    quarter(out, mate_far)[...] = rd[1]
    for c in sent + [step_b, step_c] + step_d:
        c.wait_send()


def _row_quarter(ref, i):
    q = ref.shape[0] // LAYERS
    return ref.at[pl.ds(pl.multiple_of(i * q, q), q)]


def _lane_quarter(ref, i):
    q = ref.shape[1] // LAYERS
    return ref.at[:, pl.ds(pl.multiple_of(i * q, q), q)]


def _layer_pre_kernel(inp, w, bias, feats, pre_q, x, *scratch):
    def finish(total):
        pre = total + bias[...].reshape(1, -1)
        pre_q[...] = pre
        return jnp.maximum(pre, 0.0).astype(feats.dtype)

    def produce(i):
        _row_quarter(x, i)[...] = jnp.dot(
            _row_quarter(inp, i)[...], w[...], preferred_element_type=jnp.float32
        )

    _layer_exchange(_row_quarter, x, feats, finish, produce, *scratch)


def _layer_scratch(in_q, out_q, in_dtype):
    return [
        pltpu.VMEM((2,) + in_q, in_dtype),
        pltpu.VMEM(in_q, jnp.float32),
        pltpu.VMEM(in_q, jnp.float32),
        pltpu.VMEM(out_q, jnp.bfloat16),
        pltpu.VMEM((2,) + out_q, jnp.bfloat16),
        pltpu.SemaphoreType.DMA((6,)),
        pltpu.SemaphoreType.DMA((6,)),
    ]


def layer_pre(inp, w, bias):
    rows, cols = inp.shape[0], w.shape[1]
    q = rows // LAYERS
    return pl.pallas_call(
        _layer_pre_kernel,
        out_shape=(jax.ShapeDtypeStruct((rows, cols), jnp.bfloat16),
                   jax.ShapeDtypeStruct((q, cols), jnp.float32)),
        in_specs=[pl.BlockSpec(memory_space=pltpu.VMEM)] * 3,
        out_specs=(pl.BlockSpec(memory_space=pltpu.VMEM), pl.BlockSpec(memory_space=pltpu.VMEM)),
        scratch_shapes=[pltpu.VMEM((rows, cols), jnp.float32)]
        + _layer_scratch((q, cols), (q, cols), jnp.float32),
        compiler_params=pltpu.CompilerParams(collective_id=1, has_side_effects=True),
    )(inp, w, bias)


def _layer_peers():
    me = lax.axis_index("layer")
    return me, [(me + k) % LAYERS for k in range(1, LAYERS)]


def _layer_greet(peers):
    barrier = pltpu.get_barrier_semaphore()
    for p in peers:
        pl.semaphore_signal(barrier, inc=1, device_id={"layer": p}, device_id_type=MESH)
    pl.semaphore_wait(barrier, LAYERS - 1)


def _layer_copy(src, dst, send_sems, recv_sems, k, p, slot):
    return pltpu.make_async_remote_copy(
        src_ref=src, dst_ref=dst, send_sem=send_sems.at[k, p], recv_sem=recv_sems.at[k, slot],
        device_id={"layer": p}, device_id_type=MESH,
    )


def _layer_grad_kernel(g, pre_q, margin_q, out, r1, r2, send_sems, recv_sems):
    me, peers = _layer_peers()
    q = g.shape[1] // LAYERS
    lanes = lambda i: pl.ds(pl.multiple_of(i * q, q), q)
    _layer_greet(peers)
    sent = []
    for p in peers:
        c = _layer_copy(g.at[:, lanes(p)], r1.at[me], send_sems, recv_sems, 0, p, me)
        c.start()
        sent.append(c)
    total = g[:, lanes(me)].astype(jnp.float32)
    for p in peers:
        _layer_copy(g.at[:, lanes(p)], r1.at[p], send_sems, recv_sems, 0, p, p).wait_recv()
        total = total + r1[p].astype(jnp.float32)
    grad = jnp.where(pre_q[...] > 0, total - MARGIN * margin_q[...], 0.0)
    out[:, lanes(me)] = grad.astype(out.dtype)
    for p in peers:
        c = _layer_copy(out.at[:, lanes(me)], r2.at[me], send_sems, recv_sems, 1, p, me)
        c.start()
        sent.append(c)
    for p in peers:
        _layer_copy(out.at[:, lanes(p)], r2.at[p], send_sems, recv_sems, 1, p, p).wait_recv()
        out[:, lanes(p)] = r2[p]
    for c in sent:
        c.wait_send()


def layer_grad(g, pre_q, margin_q):
    cols, rows = g.shape
    q = rows // LAYERS
    return pl.pallas_call(
        _layer_grad_kernel,
        out_shape=jax.ShapeDtypeStruct((cols, rows), jnp.bfloat16),
        in_specs=[pl.BlockSpec(memory_space=pltpu.VMEM)] * 3,
        out_specs=pl.BlockSpec(memory_space=pltpu.VMEM),
        scratch_shapes=[
            pltpu.VMEM((LAYERS, cols, q), jnp.bfloat16),
            pltpu.VMEM((LAYERS, cols, q), jnp.bfloat16),
            pltpu.SemaphoreType.DMA((2, LAYERS)),
            pltpu.SemaphoreType.DMA((2, LAYERS)),
        ],
        compiler_params=pltpu.CompilerParams(collective_id=2, has_side_effects=True),
    )(g, pre_q, margin_q)


def local(inputs, clean_acts, enc_weight, enc_bias, dec_weight, dec_bias, pairing, targets):
    row_count = inputs.shape[0]
    lat_count = enc_weight.shape[2]
    all_rows = pairing.shape[0]
    d_model = inputs.shape[2]
    chunk = d_model // (RING * RING)
    half = row_count // 2
    me = lax.axis_index("latent")
    features, pre_q = layer_pre(inputs[:, 0, :], enc_weight[0], enc_bias)
    dec4 = dec_weight[0].reshape(lat_count, RING, RING, chunk)
    recon_part = jnp.einsum("rf,fabd->abdr", features, dec4, preferred_element_type=jnp.float32)
    bias_part = lax.dynamic_slice_in_dim(dec_bias[0], me * chunk, chunk)
    clean_part = lax.dynamic_slice_in_dim(clean_acts[:, 0, :], me * chunk, chunk, axis=1)
    clean_t = jnp.swapaxes(clean_part.reshape(2, half, chunk), 1, 2)
    recon_error = latent_reduce(recon_part.astype(jnp.bfloat16), bias_part[:, None], clean_t, 3)
    error_a, error_b, margin_q = latent_gather(
        recon_error, targets.reshape(1, all_rows), pairing.reshape(1, all_rows), lat_count, 4
    )
    error_all = jnp.concatenate(
        [error_a.reshape(d_model, half), error_b.reshape(d_model, half)], axis=1
    )
    partial_grad_t = jnp.dot(dec_weight[0], error_all, preferred_element_type=jnp.float32)
    pre_grad_t = layer_grad(partial_grad_t.astype(jnp.bfloat16), pre_q.T, margin_q)
    enc4 = enc_weight[0].reshape(RING, RING, chunk, lat_count)
    total = latent_reduce_mm(enc4, pre_grad_t, 5)
    return jnp.swapaxes(total.astype(jnp.bfloat16), 1, 2).reshape(row_count, 1, chunk)


def solution(mesh):
    placed = (
        P("row", "layer", None),
        P("row", "layer", None),
        P("layer", None, "latent"),
        P("latent"),
        P("layer", "latent", None),
        P("layer", None),
        P(),
        P(),
    )
    return jax.shard_map(
        local, mesh=mesh, in_specs=placed, out_specs=P("row", "layer", "latent"), check_vma=False
    )
```

```python
import jax
import jax.numpy as jnp
from jax import lax
from jax.experimental import pallas as pl
from jax.experimental.pallas import tpu as pltpu
from jax.sharding import PartitionSpec as P

MARGIN = 16.0
MESH = pl.DeviceIdType.MESH
RING = 4
LAYERS = 4


def _latent_coords():
    me = lax.axis_index("latent")
    return me // RING, me % RING


def _greet(a, b):
    barrier = pltpu.get_barrier_semaphore()
    for k in range(1, RING):
        pl.semaphore_signal(barrier, inc=1, device_id={"latent": a * RING + (b + k) % RING}, device_id_type=MESH)
        pl.semaphore_signal(barrier, inc=1, device_id={"latent": ((a + k) % RING) * RING + b}, device_id_type=MESH)
    pl.semaphore_wait(barrier, 2 * (RING - 1))


def _copy(src, dst, send_sem, recv_sem, peer):
    return pltpu.make_async_remote_copy(
        src_ref=src, dst_ref=dst, send_sem=send_sem, recv_sem=recv_sem,
        device_id={"latent": peer}, device_id_type=MESH,
    )


def _reduce_kernel(x, bias, clean, out, r1a, r1b, s1a, s1b, r2a, r2b, send_sems, recv_sems):
    h = x.shape[-1] // 2
    xa = x.at[:, :, :, pl.ds(0, h)]
    xb = x.at[:, :, :, pl.ds(h, h)]
    a, b = _latent_coords()
    _greet(a, b)
    peers_z = [(b + k) % RING for k in range(1, RING)]
    peers_x = [(a + k) % RING for k in range(1, RING)]
    first = []
    for t in peers_z:
        c = _copy(xa.at[:, t], r1a.at[b], send_sems.at[0, t], recv_sems.at[0, b], a * RING + t)
        c.start()
        first.append(c)
    for t in peers_x:
        c = _copy(xb.at[t], r1b.at[a], send_sems.at[1, t], recv_sems.at[1, a], t * RING + b)
        c.start()
        first.append(c)
    for t in peers_z:
        _copy(xa.at[:, t], r1a.at[t], send_sems.at[0, t], recv_sems.at[0, t], 0).wait_recv()
    for t in peers_x:
        _copy(xb.at[t], r1b.at[t], send_sems.at[1, t], recv_sems.at[1, t], 0).wait_recv()
    sum_a = xa[:, b].astype(jnp.float32)
    for t in peers_z:
        sum_a = sum_a + r1a[t].astype(jnp.float32)
    sum_b = xb[a].astype(jnp.float32)
    for t in peers_x:
        sum_b = sum_b + r1b[t].astype(jnp.float32)
    s1a[...] = sum_a.astype(s1a.dtype)
    s1b[...] = sum_b.astype(s1b.dtype)
    second = []
    for t in peers_x:
        c = _copy(s1a.at[t], r2a.at[a], send_sems.at[2, t], recv_sems.at[2, a], t * RING + b)
        c.start()
        second.append(c)
    for t in peers_z:
        c = _copy(s1b.at[t], r2b.at[b], send_sems.at[3, t], recv_sems.at[3, b], a * RING + t)
        c.start()
        second.append(c)
    for t in peers_x:
        _copy(s1a.at[t], r2a.at[t], send_sems.at[2, t], recv_sems.at[2, t], 0).wait_recv()
    for t in peers_z:
        _copy(s1b.at[t], r2b.at[t], send_sems.at[3, t], recv_sems.at[3, t], 0).wait_recv()
    own_a = xa[a, b].astype(jnp.float32)
    for t in peers_z:
        own_a = own_a + r1a[t, a].astype(jnp.float32)
    own_b = xb[a, b].astype(jnp.float32)
    for t in peers_x:
        own_b = own_b + r1b[t, b].astype(jnp.float32)
    for t in peers_x:
        own_a = own_a + r2a[t].astype(jnp.float32)
    for t in peers_z:
        own_b = own_b + r2b[t].astype(jnp.float32)
    out[0] = (own_a + bias[...] - clean[0].astype(jnp.float32)).astype(out.dtype)
    out[1] = (own_b + bias[...] - clean[1].astype(jnp.float32)).astype(out.dtype)
    for c in first + second:
        c.wait_send()


def latent_reduce(x, bias, clean, collective_id):
    n, _, h, c = x.shape
    c = c // 2
    dt = x.dtype
    return pl.pallas_call(
        _reduce_kernel,
        out_shape=jax.ShapeDtypeStruct((2, h, c), jnp.bfloat16),
        in_specs=[pl.BlockSpec(memory_space=pltpu.VMEM)] * 3,
        out_specs=pl.BlockSpec(memory_space=pltpu.VMEM),
        scratch_shapes=[
            pltpu.VMEM((n, n, h, c), dt),
            pltpu.VMEM((n, n, h, c), dt),
            pltpu.VMEM((n, h, c), dt),
            pltpu.VMEM((n, h, c), dt),
            pltpu.VMEM((n, h, c), dt),
            pltpu.VMEM((n, h, c), dt),
            pltpu.SemaphoreType.DMA((4, n)),
            pltpu.SemaphoreType.DMA((4, n)),
        ],
        compiler_params=pltpu.CompilerParams(collective_id=collective_id, has_side_effects=True),
    )(x, bias, clean)


def _reduce_mm_kernel(w, v, out, xa, xb, r1a, r1b, s1a, s1b, r2a, r2b, send_sems, recv_sems):
    a, b = _latent_coords()
    _greet(a, b)
    h = v.shape[1] // 2
    peers_z = [(b + k) % RING for k in range(1, RING)]
    peers_x = [(a + k) % RING for k in range(1, RING)]

    def fill(dst, i, j, half):
        prod = jnp.dot(w[i, j], v[:, half * h:(half + 1) * h], preferred_element_type=jnp.float32)
        dst[i, j] = prod.astype(dst.dtype)

    first = []
    for kz, kx in zip(peers_z, peers_x):
        for i in range(RING):
            fill(xa, i, kz, 0)
        c = _copy(xa.at[:, kz], r1a.at[b], send_sems.at[0, kz], recv_sems.at[0, b], a * RING + kz)
        c.start()
        first.append(c)
        for j in range(RING):
            fill(xb, kx, j, 1)
        c = _copy(xb.at[kx], r1b.at[a], send_sems.at[1, kx], recv_sems.at[1, a], kx * RING + b)
        c.start()
        first.append(c)
    for i in range(RING):
        fill(xa, i, b, 0)
    for j in range(RING):
        fill(xb, a, j, 1)
    for t in peers_z:
        _copy(xa.at[:, t], r1a.at[t], send_sems.at[0, t], recv_sems.at[0, t], 0).wait_recv()
    for t in peers_x:
        _copy(xb.at[t], r1b.at[t], send_sems.at[1, t], recv_sems.at[1, t], 0).wait_recv()
    sum_a = xa[:, b].astype(jnp.float32)
    for t in peers_z:
        sum_a = sum_a + r1a[t].astype(jnp.float32)
    sum_b = xb[a].astype(jnp.float32)
    for t in peers_x:
        sum_b = sum_b + r1b[t].astype(jnp.float32)
    s1a[...] = sum_a.astype(s1a.dtype)
    s1b[...] = sum_b.astype(s1b.dtype)
    second = []
    for t in peers_x:
        c = _copy(s1a.at[t], r2a.at[a], send_sems.at[2, t], recv_sems.at[2, a], t * RING + b)
        c.start()
        second.append(c)
    for t in peers_z:
        c = _copy(s1b.at[t], r2b.at[b], send_sems.at[3, t], recv_sems.at[3, b], a * RING + t)
        c.start()
        second.append(c)
    for t in peers_x:
        _copy(s1a.at[t], r2a.at[t], send_sems.at[2, t], recv_sems.at[2, t], 0).wait_recv()
    for t in peers_z:
        _copy(s1b.at[t], r2b.at[t], send_sems.at[3, t], recv_sems.at[3, t], 0).wait_recv()
    own_a = xa[a, b].astype(jnp.float32)
    own_b = xb[a, b].astype(jnp.float32)
    for k in range(1, RING):
        own_a = own_a + r1a[(b + k) % RING, a].astype(jnp.float32)
        own_b = own_b + r1b[(a + k) % RING, b].astype(jnp.float32)
    for k in range(1, RING):
        own_a = own_a + r2a[(a + k) % RING].astype(jnp.float32)
        own_b = own_b + r2b[(b + k) % RING].astype(jnp.float32)
    out[0] = own_a.astype(out.dtype)
    out[1] = own_b.astype(out.dtype)
    for c in first + second:
        c.wait_send()


def latent_reduce_mm(w, v, collective_id):
    n, _, d, _ = w.shape
    h = v.shape[1] // 2
    dt = w.dtype
    return pl.pallas_call(
        _reduce_mm_kernel,
        out_shape=jax.ShapeDtypeStruct((2, d, h), jnp.bfloat16),
        in_specs=[pl.BlockSpec(memory_space=pltpu.VMEM)] * 2,
        out_specs=pl.BlockSpec(memory_space=pltpu.VMEM),
        scratch_shapes=[
            pltpu.VMEM((n, n, d, h), dt),
            pltpu.VMEM((n, n, d, h), dt),
            pltpu.VMEM((n, n, d, h), dt),
            pltpu.VMEM((n, n, d, h), dt),
            pltpu.VMEM((n, d, h), dt),
            pltpu.VMEM((n, d, h), dt),
            pltpu.VMEM((n, d, h), dt),
            pltpu.VMEM((n, d, h), dt),
            pltpu.SemaphoreType.DMA((4, n)),
            pltpu.SemaphoreType.DMA((4, n)),
        ],
        compiler_params=pltpu.CompilerParams(collective_id=collective_id, has_side_effects=True),
    )(w, v)


def _gather_kernel(e, targets, pairing, oa, ob, margin, g1a, g1b, ga, gb, send_sems, recv_sems):
    a, b = _latent_coords()
    _greet(a, b)
    peers_z = [(b + k) % RING for k in range(1, RING)]
    peers_x = [(a + k) % RING for k in range(1, RING)]
    first = []
    for t in peers_z:
        c = _copy(e.at[0], g1a.at[b], send_sems.at[0, t], recv_sems.at[0, b], a * RING + t)
        c.start()
        first.append(c)
    for t in peers_x:
        c = _copy(e.at[1], g1b.at[a], send_sems.at[1, t], recv_sems.at[1, a], t * RING + b)
        c.start()
        first.append(c)
    g1a[b] = e[0]
    g1b[a] = e[1]
    for t in peers_z:
        _copy(e.at[0], g1a.at[t], send_sems.at[0, t], recv_sems.at[0, t], 0).wait_recv()
    for t in peers_x:
        _copy(e.at[1], g1b.at[t], send_sems.at[1, t], recv_sems.at[1, t], 0).wait_recv()
    second = []
    for t in peers_x:
        c = _copy(g1a, ga.at[a], send_sems.at[2, t], recv_sems.at[2, a], t * RING + b)
        c.start()
        second.append(c)
    for t in peers_z:
        c = _copy(g1b, gb.at[b], send_sems.at[3, t], recv_sems.at[3, b], a * RING + t)
        c.start()
        second.append(c)
    oa[a] = g1a[...]
    f, q = margin.shape
    n_rows = pairing.shape[1]
    lat0 = lax.axis_index("latent") * f
    row0 = lax.axis_index("row") * (LAYERS * q) + lax.axis_index("layer") * q
    lat_ids = lat0 + lax.broadcasted_iota(jnp.int32, (f, n_rows), 0)
    target_hot = (lat_ids == targets[...]).astype(jnp.bfloat16)
    row_ids = row0 + lax.broadcasted_iota(jnp.int32, (q, n_rows), 0)
    every_row = lax.broadcasted_iota(jnp.int32, (q, n_rows), 1)
    pair_table = (
        (every_row == row_ids).astype(jnp.float32) - (pairing[...] == row_ids).astype(jnp.float32)
    ).astype(jnp.bfloat16)
    margin[...] = lax.dot_general(
        target_hot, pair_table, (((1,), (1,)), ((), ())), preferred_element_type=jnp.float32
    )
    for j in range(RING):
        ob[j, b] = g1b[j]
    for t in peers_x:
        _copy(g1a, ga.at[t], send_sems.at[2, t], recv_sems.at[2, t], 0).wait_recv()
        oa[t] = ga[t]
    for t in peers_z:
        _copy(g1b, gb.at[t], send_sems.at[3, t], recv_sems.at[3, t], 0).wait_recv()
        for j in range(RING):
            ob[j, t] = gb[t, j]
    for c in first + second:
        c.wait_send()


def latent_gather(e, targets, pairing, lat_count, collective_id):
    _, h, c = e.shape
    n = RING
    dt = e.dtype
    full = jax.ShapeDtypeStruct((n, n, h, c), dt)
    return pl.pallas_call(
        _gather_kernel,
        out_shape=(full, full, jax.ShapeDtypeStruct((lat_count, 2 * c // LAYERS), jnp.float32)),
        in_specs=[pl.BlockSpec(memory_space=pltpu.VMEM)] * 3,
        out_specs=(pl.BlockSpec(memory_space=pltpu.VMEM),) * 3,
        scratch_shapes=[
            pltpu.VMEM((n, h, c), dt),
            pltpu.VMEM((n, h, c), dt),
            pltpu.VMEM((n, n, h, c), dt),
            pltpu.VMEM((n, n, h, c), dt),
            pltpu.SemaphoreType.DMA((4, n)),
            pltpu.SemaphoreType.DMA((4, n)),
        ],
        compiler_params=pltpu.CompilerParams(collective_id=collective_id, has_side_effects=True),
    )(e, targets, pairing)


def _layer_roles():
    me = lax.axis_index("layer")
    mate = me + 1 - 2 * (me % 2)
    far = (me + 2) % LAYERS
    return me, mate, far, (mate + 2) % LAYERS


def _layer_exchange(quarter, x, out, finish, produce, ra, sb, rb, rc, rd, send_sems, recv_sems):
    me, mate, far, mate_far = _layer_roles()
    barrier = pltpu.get_barrier_semaphore()
    for p in (mate, far):
        pl.semaphore_signal(barrier, inc=1, device_id={"layer": p}, device_id_type=MESH)
    pl.semaphore_wait(barrier, 2)

    def copy(src, dst, k, p):
        return pltpu.make_async_remote_copy(
            src_ref=src, dst_ref=dst, send_sem=send_sems.at[k], recv_sem=recv_sems.at[k],
            device_id={"layer": p}, device_id_type=MESH,
        )

    produce(mate)
    produce(mate_far)
    sent = [copy(quarter(x, mate), ra.at[0], 0, mate), copy(quarter(x, mate_far), ra.at[1], 1, mate)]
    for c in sent:
        c.start()
    produce(far)
    produce(me)
    sent[0].wait_recv()
    sent[1].wait_recv()
    sb[...] = quarter(x, far)[...].astype(jnp.float32) + ra[1].astype(jnp.float32)
    step_b = copy(sb, rb, 2, far)
    step_b.start()
    own = quarter(x, me)[...].astype(jnp.float32) + ra[0].astype(jnp.float32)
    step_b.wait_recv()
    quarter(out, me)[...] = finish(own + rb[...])
    step_c = copy(quarter(out, me), rc, 3, far)
    step_c.start()
    step_c.wait_recv()
    quarter(out, far)[...] = rc[...]
    step_d = [copy(quarter(out, me), rd.at[0], 4, mate), copy(rc, rd.at[1], 5, mate)]
    for c in step_d:
        c.start()
    for c in step_d:
        c.wait_recv()
    quarter(out, mate)[...] = rd[0]
    quarter(out, mate_far)[...] = rd[1]
    for c in sent + [step_b, step_c] + step_d:
        c.wait_send()


def _row_quarter(ref, i):
    q = ref.shape[0] // LAYERS
    return ref.at[pl.ds(pl.multiple_of(i * q, q), q)]


def _lane_quarter(ref, i):
    q = ref.shape[1] // LAYERS
    return ref.at[:, pl.ds(pl.multiple_of(i * q, q), q)]


def _layer_pre_kernel(inp, w, bias, feats, pre_q, x, *scratch):
    def finish(total):
        pre = total + bias[...].reshape(1, -1)
        pre_q[...] = pre
        return jnp.maximum(pre, 0.0).astype(feats.dtype)

    def produce(i):
        _row_quarter(x, i)[...] = jnp.dot(
            _row_quarter(inp, i)[...], w[...], preferred_element_type=jnp.float32
        )

    _layer_exchange(_row_quarter, x, feats, finish, produce, *scratch)


def _layer_scratch(in_q, out_q, in_dtype):
    return [
        pltpu.VMEM((2,) + in_q, in_dtype),
        pltpu.VMEM(in_q, jnp.float32),
        pltpu.VMEM(in_q, jnp.float32),
        pltpu.VMEM(out_q, jnp.bfloat16),
        pltpu.VMEM((2,) + out_q, jnp.bfloat16),
        pltpu.SemaphoreType.DMA((6,)),
        pltpu.SemaphoreType.DMA((6,)),
    ]


def layer_pre(inp, w, bias):
    rows, cols = inp.shape[0], w.shape[1]
    q = rows // LAYERS
    return pl.pallas_call(
        _layer_pre_kernel,
        out_shape=(jax.ShapeDtypeStruct((rows, cols), jnp.bfloat16),
                   jax.ShapeDtypeStruct((q, cols), jnp.float32)),
        in_specs=[pl.BlockSpec(memory_space=pltpu.VMEM)] * 3,
        out_specs=(pl.BlockSpec(memory_space=pltpu.VMEM), pl.BlockSpec(memory_space=pltpu.VMEM)),
        scratch_shapes=[pltpu.VMEM((rows, cols), jnp.float32)]
        + _layer_scratch((q, cols), (q, cols), jnp.float32),
        compiler_params=pltpu.CompilerParams(collective_id=1, has_side_effects=True),
    )(inp, w, bias)


def _layer_peers():
    me = lax.axis_index("layer")
    return me, [(me + k) % LAYERS for k in range(1, LAYERS)]


def _layer_greet(peers):
    barrier = pltpu.get_barrier_semaphore()
    for p in peers:
        pl.semaphore_signal(barrier, inc=1, device_id={"layer": p}, device_id_type=MESH)
    pl.semaphore_wait(barrier, LAYERS - 1)


def _layer_copy(src, dst, send_sems, recv_sems, k, p, slot):
    return pltpu.make_async_remote_copy(
        src_ref=src, dst_ref=dst, send_sem=send_sems.at[k, p], recv_sem=recv_sems.at[k, slot],
        device_id={"layer": p}, device_id_type=MESH,
    )


def _layer_grad_kernel(g, pre_q, margin_q, out, r1, r2, send_sems, recv_sems):
    me, peers = _layer_peers()
    q = g.shape[1] // LAYERS
    lanes = lambda i: pl.ds(pl.multiple_of(i * q, q), q)
    _layer_greet(peers)
    sent = []
    for p in peers:
        c = _layer_copy(g.at[:, lanes(p)], r1.at[me], send_sems, recv_sems, 0, p, me)
        c.start()
        sent.append(c)
    total = g[:, lanes(me)].astype(jnp.float32)
    for p in peers:
        _layer_copy(g.at[:, lanes(p)], r1.at[p], send_sems, recv_sems, 0, p, p).wait_recv()
        total = total + r1[p].astype(jnp.float32)
    grad = jnp.where(pre_q[...] > 0, total - MARGIN * margin_q[...], 0.0)
    out[:, lanes(me)] = grad.astype(out.dtype)
    for p in peers:
        c = _layer_copy(out.at[:, lanes(me)], r2.at[me], send_sems, recv_sems, 1, p, me)
        c.start()
        sent.append(c)
    for p in peers:
        _layer_copy(out.at[:, lanes(p)], r2.at[p], send_sems, recv_sems, 1, p, p).wait_recv()
        out[:, lanes(p)] = r2[p]
    for c in sent:
        c.wait_send()


def layer_grad(g, pre_q, margin_q):
    cols, rows = g.shape
    q = rows // LAYERS
    return pl.pallas_call(
        _layer_grad_kernel,
        out_shape=jax.ShapeDtypeStruct((cols, rows), jnp.bfloat16),
        in_specs=[pl.BlockSpec(memory_space=pltpu.VMEM)] * 3,
        out_specs=pl.BlockSpec(memory_space=pltpu.VMEM),
        scratch_shapes=[
            pltpu.VMEM((LAYERS, cols, q), jnp.bfloat16),
            pltpu.VMEM((LAYERS, cols, q), jnp.bfloat16),
            pltpu.SemaphoreType.DMA((2, LAYERS)),
            pltpu.SemaphoreType.DMA((2, LAYERS)),
        ],
        compiler_params=pltpu.CompilerParams(collective_id=2, has_side_effects=True),
    )(g, pre_q, margin_q)


def local(inputs, clean_acts, enc_weight, enc_bias, dec_weight, dec_bias, pairing, targets):
    row_count = inputs.shape[0]
    lat_count = enc_weight.shape[2]
    all_rows = pairing.shape[0]
    d_model = inputs.shape[2]
    chunk = d_model // (RING * RING)
    half = row_count // 2
    me = lax.axis_index("latent")
    features, pre_q = layer_pre(inputs[:, 0, :], enc_weight[0], enc_bias)
    dec4 = dec_weight[0].reshape(lat_count, RING, RING, chunk)
    recon_part = jnp.einsum("rf,fabd->abdr", features, dec4, preferred_element_type=jnp.float32)
    bias_part = lax.dynamic_slice_in_dim(dec_bias[0], me * chunk, chunk)
    clean_part = lax.dynamic_slice_in_dim(clean_acts[:, 0, :], me * chunk, chunk, axis=1)
    clean_t = jnp.swapaxes(clean_part.reshape(2, half, chunk), 1, 2)
    recon_error = latent_reduce(recon_part.astype(jnp.bfloat16), bias_part[:, None], clean_t, 3)
    error_a, error_b, margin_q = latent_gather(
        recon_error, targets.reshape(1, all_rows), pairing.reshape(1, all_rows), lat_count, 4
    )
    error_all = jnp.concatenate(
        [error_a.reshape(d_model, half), error_b.reshape(d_model, half)], axis=1
    )
    partial_grad_t = jnp.dot(dec_weight[0], error_all, preferred_element_type=jnp.float32)
    pre_grad_t = layer_grad(partial_grad_t.astype(jnp.bfloat16), pre_q.T, margin_q)
    enc4 = enc_weight[0].reshape(RING, RING, chunk, lat_count)
    total = latent_reduce_mm(enc4, pre_grad_t, 5)
    return jnp.swapaxes(total, 1, 2).reshape(row_count, 1, chunk)


def solution(mesh):
    placed = (
        P("row", "layer", None),
        P("row", "layer", None),
        P("layer", None, "latent"),
        P("latent"),
        P("layer", "latent", None),
        P("layer", None),
        P(),
        P(),
    )
    return jax.shard_map(
        local, mesh=mesh, in_specs=placed, out_specs=P("row", "layer", "latent"), check_vma=False
    )
```

```python
import jax
import jax.numpy as jnp
from jax import lax
from jax.experimental import pallas as pl
from jax.experimental.pallas import tpu as pltpu
from jax.sharding import PartitionSpec as P

MARGIN = 16.0
MESH = pl.DeviceIdType.MESH
RING = 4
LAYERS = 4


def _latent_coords():
    me = lax.axis_index("latent")
    return me // RING, me % RING


def _greet(a, b):
    barrier = pltpu.get_barrier_semaphore()
    for k in range(1, RING):
        pl.semaphore_signal(barrier, inc=1, device_id={"latent": a * RING + (b + k) % RING}, device_id_type=MESH)
        pl.semaphore_signal(barrier, inc=1, device_id={"latent": ((a + k) % RING) * RING + b}, device_id_type=MESH)
    pl.semaphore_wait(barrier, 2 * (RING - 1))


def _copy(src, dst, send_sem, recv_sem, peer):
    return pltpu.make_async_remote_copy(
        src_ref=src, dst_ref=dst, send_sem=send_sem, recv_sem=recv_sem,
        device_id={"latent": peer}, device_id_type=MESH,
    )


def _reduce_kernel(x, clean, out, r1a, r1b, s1a, s1b, r2a, r2b, send_sems, recv_sems):
    h = x.shape[-1] // 2
    xa = x.at[:, :, :, pl.ds(0, h)]
    xb = x.at[:, :, :, pl.ds(h, h)]
    a, b = _latent_coords()
    _greet(a, b)
    peers_z = [(b + k) % RING for k in range(1, RING)]
    peers_x = [(a + k) % RING for k in range(1, RING)]
    first = []
    for t in peers_z:
        c = _copy(xa.at[:, t], r1a.at[b], send_sems.at[0, t], recv_sems.at[0, b], a * RING + t)
        c.start()
        first.append(c)
    for t in peers_x:
        c = _copy(xb.at[t], r1b.at[a], send_sems.at[1, t], recv_sems.at[1, a], t * RING + b)
        c.start()
        first.append(c)
    for t in peers_z:
        _copy(xa.at[:, t], r1a.at[t], send_sems.at[0, t], recv_sems.at[0, t], 0).wait_recv()
    for t in peers_x:
        _copy(xb.at[t], r1b.at[t], send_sems.at[1, t], recv_sems.at[1, t], 0).wait_recv()
    sum_a = xa[:, b].astype(jnp.float32)
    for t in peers_z:
        sum_a = sum_a + r1a[t].astype(jnp.float32)
    sum_b = xb[a].astype(jnp.float32)
    for t in peers_x:
        sum_b = sum_b + r1b[t].astype(jnp.float32)
    s1a[...] = sum_a.astype(s1a.dtype)
    s1b[...] = sum_b.astype(s1b.dtype)
    second = []
    for t in peers_x:
        c = _copy(s1a.at[t], r2a.at[a], send_sems.at[2, t], recv_sems.at[2, a], t * RING + b)
        c.start()
        second.append(c)
    for t in peers_z:
        c = _copy(s1b.at[t], r2b.at[b], send_sems.at[3, t], recv_sems.at[3, b], a * RING + t)
        c.start()
        second.append(c)
    for t in peers_x:
        _copy(s1a.at[t], r2a.at[t], send_sems.at[2, t], recv_sems.at[2, t], 0).wait_recv()
    for t in peers_z:
        _copy(s1b.at[t], r2b.at[t], send_sems.at[3, t], recv_sems.at[3, t], 0).wait_recv()
    own_a = xa[a, b].astype(jnp.float32)
    for t in peers_z:
        own_a = own_a + r1a[t, a].astype(jnp.float32)
    own_b = xb[a, b].astype(jnp.float32)
    for t in peers_x:
        own_b = own_b + r1b[t, b].astype(jnp.float32)
    for t in peers_x:
        own_a = own_a + r2a[t].astype(jnp.float32)
    for t in peers_z:
        own_b = own_b + r2b[t].astype(jnp.float32)
    out[0] = (own_a - clean[0]).astype(out.dtype)
    out[1] = (own_b - clean[1]).astype(out.dtype)
    for c in first + second:
        c.wait_send()


def latent_reduce(x, clean, collective_id):
    n, _, h, c = x.shape
    c = c // 2
    dt = x.dtype
    return pl.pallas_call(
        _reduce_kernel,
        out_shape=jax.ShapeDtypeStruct((2, h, c), jnp.bfloat16),
        in_specs=[pl.BlockSpec(memory_space=pltpu.VMEM)] * 2,
        out_specs=pl.BlockSpec(memory_space=pltpu.VMEM),
        scratch_shapes=[
            pltpu.VMEM((n, n, h, c), dt),
            pltpu.VMEM((n, n, h, c), dt),
            pltpu.VMEM((n, h, c), dt),
            pltpu.VMEM((n, h, c), dt),
            pltpu.VMEM((n, h, c), dt),
            pltpu.VMEM((n, h, c), dt),
            pltpu.SemaphoreType.DMA((4, n)),
            pltpu.SemaphoreType.DMA((4, n)),
        ],
        compiler_params=pltpu.CompilerParams(collective_id=collective_id, has_side_effects=True),
    )(x, clean)


def _reduce_mm_kernel(w, v, out, xa, xb, r1a, r1b, s1a, s1b, r2a, r2b, send_sems, recv_sems):
    a, b = _latent_coords()
    _greet(a, b)
    h = v.shape[1] // 2
    peers_z = [(b + k) % RING for k in range(1, RING)]
    peers_x = [(a + k) % RING for k in range(1, RING)]

    def fill(dst, i, j, half):
        prod = jnp.dot(w[i, j], v[:, half * h:(half + 1) * h], preferred_element_type=jnp.float32)
        dst[i, j] = prod.astype(dst.dtype)

    first = []
    for kz, kx in zip(peers_z, peers_x):
        for i in range(RING):
            fill(xa, i, kz, 0)
        c = _copy(xa.at[:, kz], r1a.at[b], send_sems.at[0, kz], recv_sems.at[0, b], a * RING + kz)
        c.start()
        first.append(c)
        for j in range(RING):
            fill(xb, kx, j, 1)
        c = _copy(xb.at[kx], r1b.at[a], send_sems.at[1, kx], recv_sems.at[1, a], kx * RING + b)
        c.start()
        first.append(c)
    for i in range(RING):
        fill(xa, i, b, 0)
    for j in range(RING):
        fill(xb, a, j, 1)
    for t in peers_z:
        _copy(xa.at[:, t], r1a.at[t], send_sems.at[0, t], recv_sems.at[0, t], 0).wait_recv()
    for t in peers_x:
        _copy(xb.at[t], r1b.at[t], send_sems.at[1, t], recv_sems.at[1, t], 0).wait_recv()
    sum_a = xa[:, b].astype(jnp.float32)
    for t in peers_z:
        sum_a = sum_a + r1a[t].astype(jnp.float32)
    sum_b = xb[a].astype(jnp.float32)
    for t in peers_x:
        sum_b = sum_b + r1b[t].astype(jnp.float32)
    s1a[...] = sum_a.astype(s1a.dtype)
    s1b[...] = sum_b.astype(s1b.dtype)
    second = []
    for t in peers_x:
        c = _copy(s1a.at[t], r2a.at[a], send_sems.at[2, t], recv_sems.at[2, a], t * RING + b)
        c.start()
        second.append(c)
    for t in peers_z:
        c = _copy(s1b.at[t], r2b.at[b], send_sems.at[3, t], recv_sems.at[3, b], a * RING + t)
        c.start()
        second.append(c)
    for t in peers_x:
        _copy(s1a.at[t], r2a.at[t], send_sems.at[2, t], recv_sems.at[2, t], 0).wait_recv()
    for t in peers_z:
        _copy(s1b.at[t], r2b.at[t], send_sems.at[3, t], recv_sems.at[3, t], 0).wait_recv()
    own_a = xa[a, b].astype(jnp.float32)
    own_b = xb[a, b].astype(jnp.float32)
    for k in range(1, RING):
        own_a = own_a + r1a[(b + k) % RING, a].astype(jnp.float32)
        own_b = own_b + r1b[(a + k) % RING, b].astype(jnp.float32)
    for k in range(1, RING):
        own_a = own_a + r2a[(a + k) % RING].astype(jnp.float32)
        own_b = own_b + r2b[(b + k) % RING].astype(jnp.float32)
    out[0] = own_a
    out[1] = own_b
    for c in first + second:
        c.wait_send()


def latent_reduce_mm(w, v, collective_id):
    n, _, d, _ = w.shape
    h = v.shape[1] // 2
    dt = w.dtype
    return pl.pallas_call(
        _reduce_mm_kernel,
        out_shape=jax.ShapeDtypeStruct((2, d, h), jnp.float32),
        in_specs=[pl.BlockSpec(memory_space=pltpu.VMEM)] * 2,
        out_specs=pl.BlockSpec(memory_space=pltpu.VMEM),
        scratch_shapes=[
            pltpu.VMEM((n, n, d, h), dt),
            pltpu.VMEM((n, n, d, h), dt),
            pltpu.VMEM((n, n, d, h), dt),
            pltpu.VMEM((n, n, d, h), dt),
            pltpu.VMEM((n, d, h), dt),
            pltpu.VMEM((n, d, h), dt),
            pltpu.VMEM((n, d, h), dt),
            pltpu.VMEM((n, d, h), dt),
            pltpu.SemaphoreType.DMA((4, n)),
            pltpu.SemaphoreType.DMA((4, n)),
        ],
        compiler_params=pltpu.CompilerParams(collective_id=collective_id, has_side_effects=True),
    )(w, v)


def _gather_kernel(e, targets, pairing, oa, ob, margin, g1a, g1b, ga, gb, send_sems, recv_sems):
    a, b = _latent_coords()
    _greet(a, b)
    peers_z = [(b + k) % RING for k in range(1, RING)]
    peers_x = [(a + k) % RING for k in range(1, RING)]
    first = []
    for t in peers_z:
        c = _copy(e.at[0], g1a.at[b], send_sems.at[0, t], recv_sems.at[0, b], a * RING + t)
        c.start()
        first.append(c)
    for t in peers_x:
        c = _copy(e.at[1], g1b.at[a], send_sems.at[1, t], recv_sems.at[1, a], t * RING + b)
        c.start()
        first.append(c)
    g1a[b] = e[0]
    g1b[a] = e[1]
    for t in peers_z:
        _copy(e.at[0], g1a.at[t], send_sems.at[0, t], recv_sems.at[0, t], 0).wait_recv()
    for t in peers_x:
        _copy(e.at[1], g1b.at[t], send_sems.at[1, t], recv_sems.at[1, t], 0).wait_recv()
    second = []
    for t in peers_x:
        c = _copy(g1a, ga.at[a], send_sems.at[2, t], recv_sems.at[2, a], t * RING + b)
        c.start()
        second.append(c)
    for t in peers_z:
        c = _copy(g1b, gb.at[b], send_sems.at[3, t], recv_sems.at[3, b], a * RING + t)
        c.start()
        second.append(c)
    oa[a] = g1a[...]
    f, q = margin.shape
    n_rows = pairing.shape[1]
    lat0 = lax.axis_index("latent") * f
    row0 = lax.axis_index("row") * (LAYERS * q) + lax.axis_index("layer") * q
    lat_ids = lat0 + lax.broadcasted_iota(jnp.int32, (f, n_rows), 0)
    target_hot = (lat_ids == targets[...]).astype(jnp.bfloat16)
    row_ids = row0 + lax.broadcasted_iota(jnp.int32, (q, n_rows), 0)
    every_row = lax.broadcasted_iota(jnp.int32, (q, n_rows), 1)
    pair_table = (
        (every_row == row_ids).astype(jnp.float32) - (pairing[...] == row_ids).astype(jnp.float32)
    ).astype(jnp.bfloat16)
    margin[...] = lax.dot_general(
        target_hot, pair_table, (((1,), (1,)), ((), ())), preferred_element_type=jnp.float32
    )
    for j in range(RING):
        ob[j, b] = g1b[j]
    for t in peers_x:
        _copy(g1a, ga.at[t], send_sems.at[2, t], recv_sems.at[2, t], 0).wait_recv()
        oa[t] = ga[t]
    for t in peers_z:
        _copy(g1b, gb.at[t], send_sems.at[3, t], recv_sems.at[3, t], 0).wait_recv()
        for j in range(RING):
            ob[j, t] = gb[t, j]
    for c in first + second:
        c.wait_send()


def latent_gather(e, targets, pairing, lat_count, collective_id):
    _, h, c = e.shape
    n = RING
    dt = e.dtype
    full = jax.ShapeDtypeStruct((n, n, h, c), dt)
    return pl.pallas_call(
        _gather_kernel,
        out_shape=(full, full, jax.ShapeDtypeStruct((lat_count, 2 * c // LAYERS), jnp.float32)),
        in_specs=[pl.BlockSpec(memory_space=pltpu.VMEM)] * 3,
        out_specs=(pl.BlockSpec(memory_space=pltpu.VMEM),) * 3,
        scratch_shapes=[
            pltpu.VMEM((n, h, c), dt),
            pltpu.VMEM((n, h, c), dt),
            pltpu.VMEM((n, n, h, c), dt),
            pltpu.VMEM((n, n, h, c), dt),
            pltpu.SemaphoreType.DMA((4, n)),
            pltpu.SemaphoreType.DMA((4, n)),
        ],
        compiler_params=pltpu.CompilerParams(collective_id=collective_id, has_side_effects=True),
    )(e, targets, pairing)


def _layer_roles():
    me = lax.axis_index("layer")
    mate = me + 1 - 2 * (me % 2)
    far = (me + 2) % LAYERS
    return me, mate, far, (mate + 2) % LAYERS


def _layer_exchange(quarter, x, out, finish, produce, ra, sb, rb, rc, rd, send_sems, recv_sems):
    me, mate, far, mate_far = _layer_roles()
    barrier = pltpu.get_barrier_semaphore()
    for p in (mate, far):
        pl.semaphore_signal(barrier, inc=1, device_id={"layer": p}, device_id_type=MESH)
    pl.semaphore_wait(barrier, 2)

    def copy(src, dst, k, p):
        return pltpu.make_async_remote_copy(
            src_ref=src, dst_ref=dst, send_sem=send_sems.at[k], recv_sem=recv_sems.at[k],
            device_id={"layer": p}, device_id_type=MESH,
        )

    produce(mate)
    produce(mate_far)
    sent = [copy(quarter(x, mate), ra.at[0], 0, mate), copy(quarter(x, mate_far), ra.at[1], 1, mate)]
    for c in sent:
        c.start()
    produce(far)
    produce(me)
    sent[0].wait_recv()
    sent[1].wait_recv()
    sb[...] = quarter(x, far)[...].astype(jnp.float32) + ra[1].astype(jnp.float32)
    step_b = copy(sb, rb, 2, far)
    step_b.start()
    own = quarter(x, me)[...].astype(jnp.float32) + ra[0].astype(jnp.float32)
    step_b.wait_recv()
    quarter(out, me)[...] = finish(own + rb[...])
    step_c = copy(quarter(out, me), rc, 3, far)
    step_c.start()
    step_c.wait_recv()
    quarter(out, far)[...] = rc[...]
    step_d = [copy(quarter(out, me), rd.at[0], 4, mate), copy(rc, rd.at[1], 5, mate)]
    for c in step_d:
        c.start()
    for c in step_d:
        c.wait_recv()
    quarter(out, mate)[...] = rd[0]
    quarter(out, mate_far)[...] = rd[1]
    for c in sent + [step_b, step_c] + step_d:
        c.wait_send()


def _row_quarter(ref, i):
    q = ref.shape[0] // LAYERS
    return ref.at[pl.ds(pl.multiple_of(i * q, q), q)]


def _lane_quarter(ref, i):
    q = ref.shape[1] // LAYERS
    return ref.at[:, pl.ds(pl.multiple_of(i * q, q), q)]


def _layer_pre_kernel(inp, w, bias, feats, pre_q, x, *scratch):
    def finish(total):
        pre = total + bias[...].reshape(1, -1)
        pre_q[...] = pre
        return jnp.maximum(pre, 0.0).astype(feats.dtype)

    def produce(i):
        _row_quarter(x, i)[...] = jnp.dot(
            _row_quarter(inp, i)[...], w[...], preferred_element_type=jnp.float32
        )

    _layer_exchange(_row_quarter, x, feats, finish, produce, *scratch)


def _layer_scratch(in_q, out_q, in_dtype):
    return [
        pltpu.VMEM((2,) + in_q, in_dtype),
        pltpu.VMEM(in_q, jnp.float32),
        pltpu.VMEM(in_q, jnp.float32),
        pltpu.VMEM(out_q, jnp.bfloat16),
        pltpu.VMEM((2,) + out_q, jnp.bfloat16),
        pltpu.SemaphoreType.DMA((6,)),
        pltpu.SemaphoreType.DMA((6,)),
    ]


def layer_pre(inp, w, bias):
    rows, cols = inp.shape[0], w.shape[1]
    q = rows // LAYERS
    return pl.pallas_call(
        _layer_pre_kernel,
        out_shape=(jax.ShapeDtypeStruct((rows, cols), jnp.bfloat16),
                   jax.ShapeDtypeStruct((q, cols), jnp.float32)),
        in_specs=[pl.BlockSpec(memory_space=pltpu.VMEM)] * 3,
        out_specs=(pl.BlockSpec(memory_space=pltpu.VMEM), pl.BlockSpec(memory_space=pltpu.VMEM)),
        scratch_shapes=[pltpu.VMEM((rows, cols), jnp.float32)]
        + _layer_scratch((q, cols), (q, cols), jnp.float32),
        compiler_params=pltpu.CompilerParams(collective_id=1, has_side_effects=True),
    )(inp, w, bias)


def _layer_peers():
    me = lax.axis_index("layer")
    return me, [(me + k) % LAYERS for k in range(1, LAYERS)]


def _layer_greet(peers):
    barrier = pltpu.get_barrier_semaphore()
    for p in peers:
        pl.semaphore_signal(barrier, inc=1, device_id={"layer": p}, device_id_type=MESH)
    pl.semaphore_wait(barrier, LAYERS - 1)


def _layer_copy(src, dst, send_sems, recv_sems, k, p, slot):
    return pltpu.make_async_remote_copy(
        src_ref=src, dst_ref=dst, send_sem=send_sems.at[k, p], recv_sem=recv_sems.at[k, slot],
        device_id={"layer": p}, device_id_type=MESH,
    )


def _layer_grad_kernel(g, pre_q, margin_q, out, r1, r2, send_sems, recv_sems):
    me, peers = _layer_peers()
    q = g.shape[1] // LAYERS
    lanes = lambda i: pl.ds(pl.multiple_of(i * q, q), q)
    _layer_greet(peers)
    sent = []
    for p in peers:
        c = _layer_copy(g.at[:, lanes(p)], r1.at[me], send_sems, recv_sems, 0, p, me)
        c.start()
        sent.append(c)
    total = g[:, lanes(me)].astype(jnp.float32)
    for p in peers:
        _layer_copy(g.at[:, lanes(p)], r1.at[p], send_sems, recv_sems, 0, p, p).wait_recv()
        total = total + r1[p].astype(jnp.float32)
    grad = jnp.where(pre_q[...] > 0, total - MARGIN * margin_q[...], 0.0)
    out[:, lanes(me)] = grad.astype(out.dtype)
    for p in peers:
        c = _layer_copy(out.at[:, lanes(me)], r2.at[me], send_sems, recv_sems, 1, p, me)
        c.start()
        sent.append(c)
    for p in peers:
        _layer_copy(out.at[:, lanes(p)], r2.at[p], send_sems, recv_sems, 1, p, p).wait_recv()
        out[:, lanes(p)] = r2[p]
    for c in sent:
        c.wait_send()


def layer_grad(g, pre_q, margin_q):
    cols, rows = g.shape
    q = rows // LAYERS
    return pl.pallas_call(
        _layer_grad_kernel,
        out_shape=jax.ShapeDtypeStruct((cols, rows), jnp.bfloat16),
        in_specs=[pl.BlockSpec(memory_space=pltpu.VMEM)] * 3,
        out_specs=pl.BlockSpec(memory_space=pltpu.VMEM),
        scratch_shapes=[
            pltpu.VMEM((LAYERS, cols, q), jnp.bfloat16),
            pltpu.VMEM((LAYERS, cols, q), jnp.bfloat16),
            pltpu.SemaphoreType.DMA((2, LAYERS)),
            pltpu.SemaphoreType.DMA((2, LAYERS)),
        ],
        compiler_params=pltpu.CompilerParams(collective_id=2, has_side_effects=True),
    )(g, pre_q, margin_q)


def local(inputs, clean_acts, enc_weight, enc_bias, dec_weight, dec_bias, pairing, targets):
    row_count = inputs.shape[0]
    lat_count = enc_weight.shape[2]
    all_rows = pairing.shape[0]
    d_model = inputs.shape[2]
    chunk = d_model // (RING * RING)
    half = row_count // 2
    me = lax.axis_index("latent")
    features, pre_q = layer_pre(inputs[:, 0, :], enc_weight[0], enc_bias)
    dec4 = dec_weight[0].reshape(lat_count, RING, RING, chunk)
    recon_part = jnp.einsum("rf,fabd->abdr", features, dec4, preferred_element_type=jnp.float32)
    bias_part = lax.dynamic_slice_in_dim(dec_bias[0], me * chunk, chunk)
    clean_part = lax.dynamic_slice_in_dim(clean_acts[:, 0, :], me * chunk, chunk, axis=1)
    clean_t = jnp.swapaxes(clean_part.reshape(2, half, chunk), 1, 2).astype(jnp.float32)
    recon_error = latent_reduce(recon_part.astype(jnp.bfloat16), clean_t - bias_part[:, None], 3)
    error_a, error_b, margin_q = latent_gather(
        recon_error, targets.reshape(1, all_rows), pairing.reshape(1, all_rows), lat_count, 4
    )
    error_all = jnp.concatenate(
        [error_a.reshape(d_model, half), error_b.reshape(d_model, half)], axis=1
    )
    partial_grad_t = jnp.dot(dec_weight[0], error_all, preferred_element_type=jnp.float32)
    pre_grad_t = layer_grad(partial_grad_t.astype(jnp.bfloat16), pre_q.T, margin_q)
    enc4 = enc_weight[0].reshape(RING, RING, chunk, lat_count)
    total = latent_reduce_mm(enc4, pre_grad_t, 5)
    return jnp.swapaxes(total.astype(jnp.bfloat16), 1, 2).reshape(row_count, 1, chunk)


def solution(mesh):
    placed = (
        P("row", "layer", None),
        P("row", "layer", None),
        P("layer", None, "latent"),
        P("latent"),
        P("layer", "latent", None),
        P("layer", None),
        P(),
        P(),
    )
    return jax.shard_map(
        local, mesh=mesh, in_specs=placed, out_specs=P("row", "layer", "latent"), check_vma=False
    )
```

```python
import jax
import jax.numpy as jnp
from jax import lax
from jax.experimental import pallas as pl
from jax.experimental.pallas import tpu as pltpu
from jax.sharding import PartitionSpec as P

MARGIN = 16.0
MESH = pl.DeviceIdType.MESH
RING = 4
LAYERS = 4


def _latent_coords():
    me = lax.axis_index("latent")
    return me // RING, me % RING


def _greet(a, b):
    barrier = pltpu.get_barrier_semaphore()
    for k in range(1, RING):
        pl.semaphore_signal(barrier, inc=1, device_id={"latent": a * RING + (b + k) % RING}, device_id_type=MESH)
        pl.semaphore_signal(barrier, inc=1, device_id={"latent": ((a + k) % RING) * RING + b}, device_id_type=MESH)
    pl.semaphore_wait(barrier, 2 * (RING - 1))


def _copy(src, dst, send_sem, recv_sem, peer):
    return pltpu.make_async_remote_copy(
        src_ref=src, dst_ref=dst, send_sem=send_sem, recv_sem=recv_sem,
        device_id={"latent": peer}, device_id_type=MESH,
    )


def _reduce_kernel(x, clean, out, r1a, r1b, s1a, s1b, r2a, r2b, send_sems, recv_sems):
    h = x.shape[-1] // 2
    xa = x.at[:, :, :, pl.ds(0, h)]
    xb = x.at[:, :, :, pl.ds(h, h)]
    a, b = _latent_coords()
    _greet(a, b)
    peers_z = [(b + k) % RING for k in range(1, RING)]
    peers_x = [(a + k) % RING for k in range(1, RING)]
    first = []
    for t in peers_z:
        c = _copy(xa.at[:, t], r1a.at[b], send_sems.at[0, t], recv_sems.at[0, b], a * RING + t)
        c.start()
        first.append(c)
    for t in peers_x:
        c = _copy(xb.at[t], r1b.at[a], send_sems.at[1, t], recv_sems.at[1, a], t * RING + b)
        c.start()
        first.append(c)
    for t in peers_z:
        _copy(xa.at[:, t], r1a.at[t], send_sems.at[0, t], recv_sems.at[0, t], 0).wait_recv()
    for t in peers_x:
        _copy(xb.at[t], r1b.at[t], send_sems.at[1, t], recv_sems.at[1, t], 0).wait_recv()
    sum_a = xa[:, b].astype(jnp.float32)
    for t in peers_z:
        sum_a = sum_a + r1a[t].astype(jnp.float32)
    sum_b = xb[a].astype(jnp.float32)
    for t in peers_x:
        sum_b = sum_b + r1b[t].astype(jnp.float32)
    s1a[...] = sum_a.astype(s1a.dtype)
    s1b[...] = sum_b.astype(s1b.dtype)
    second = []
    for t in peers_x:
        c = _copy(s1a.at[t], r2a.at[a], send_sems.at[2, t], recv_sems.at[2, a], t * RING + b)
        c.start()
        second.append(c)
    for t in peers_z:
        c = _copy(s1b.at[t], r2b.at[b], send_sems.at[3, t], recv_sems.at[3, b], a * RING + t)
        c.start()
        second.append(c)
    for t in peers_x:
        _copy(s1a.at[t], r2a.at[t], send_sems.at[2, t], recv_sems.at[2, t], 0).wait_recv()
    for t in peers_z:
        _copy(s1b.at[t], r2b.at[t], send_sems.at[3, t], recv_sems.at[3, t], 0).wait_recv()
    own_a = xa[a, b].astype(jnp.float32)
    for t in peers_z:
        own_a = own_a + r1a[t, a].astype(jnp.float32)
    own_b = xb[a, b].astype(jnp.float32)
    for t in peers_x:
        own_b = own_b + r1b[t, b].astype(jnp.float32)
    for t in peers_x:
        own_a = own_a + r2a[t].astype(jnp.float32)
    for t in peers_z:
        own_b = own_b + r2b[t].astype(jnp.float32)
    out[0] = (own_a - clean[0]).astype(out.dtype)
    out[1] = (own_b - clean[1]).astype(out.dtype)
    for c in first + second:
        c.wait_send()


def latent_reduce(x, clean, collective_id):
    n, _, h, c = x.shape
    c = c // 2
    dt = x.dtype
    return pl.pallas_call(
        _reduce_kernel,
        out_shape=jax.ShapeDtypeStruct((2, h, c), jnp.bfloat16),
        in_specs=[pl.BlockSpec(memory_space=pltpu.VMEM)] * 2,
        out_specs=pl.BlockSpec(memory_space=pltpu.VMEM),
        scratch_shapes=[
            pltpu.VMEM((n, n, h, c), dt),
            pltpu.VMEM((n, n, h, c), dt),
            pltpu.VMEM((n, h, c), dt),
            pltpu.VMEM((n, h, c), dt),
            pltpu.VMEM((n, h, c), dt),
            pltpu.VMEM((n, h, c), dt),
            pltpu.SemaphoreType.DMA((4, n)),
            pltpu.SemaphoreType.DMA((4, n)),
        ],
        compiler_params=pltpu.CompilerParams(collective_id=collective_id, has_side_effects=True),
    )(x, clean)


def _reduce_mm_kernel(w, v, out, xa, xb, r1a, r1b, s1a, s1b, r2a, r2b, send_sems, recv_sems):
    a, b = _latent_coords()
    _greet(a, b)
    h = v.shape[1] // 2
    peers_z = [(b + k) % RING for k in range(1, RING)]
    peers_x = [(a + k) % RING for k in range(1, RING)]

    def fill(dst, i, j, half):
        prod = jnp.dot(w[i, j], v[:, half * h:(half + 1) * h], preferred_element_type=jnp.float32)
        dst[i, j] = prod.astype(dst.dtype)

    first = []
    for kz, kx in zip(peers_z, peers_x):
        for i in range(RING):
            fill(xa, i, kz, 0)
        c = _copy(xa.at[:, kz], r1a.at[b], send_sems.at[0, kz], recv_sems.at[0, b], a * RING + kz)
        c.start()
        first.append(c)
        for j in range(RING):
            fill(xb, kx, j, 1)
        c = _copy(xb.at[kx], r1b.at[a], send_sems.at[1, kx], recv_sems.at[1, a], kx * RING + b)
        c.start()
        first.append(c)
    for i in range(RING):
        fill(xa, i, b, 0)
    for j in range(RING):
        fill(xb, a, j, 1)
    for t in peers_z:
        _copy(xa.at[:, t], r1a.at[t], send_sems.at[0, t], recv_sems.at[0, t], 0).wait_recv()
    for t in peers_x:
        _copy(xb.at[t], r1b.at[t], send_sems.at[1, t], recv_sems.at[1, t], 0).wait_recv()
    sum_a = xa[:, b].astype(jnp.float32)
    for t in peers_z:
        sum_a = sum_a + r1a[t].astype(jnp.float32)
    sum_b = xb[a].astype(jnp.float32)
    for t in peers_x:
        sum_b = sum_b + r1b[t].astype(jnp.float32)
    s1a[...] = sum_a.astype(s1a.dtype)
    s1b[...] = sum_b.astype(s1b.dtype)
    second = []
    for t in peers_x:
        c = _copy(s1a.at[t], r2a.at[a], send_sems.at[2, t], recv_sems.at[2, a], t * RING + b)
        c.start()
        second.append(c)
    for t in peers_z:
        c = _copy(s1b.at[t], r2b.at[b], send_sems.at[3, t], recv_sems.at[3, b], a * RING + t)
        c.start()
        second.append(c)
    for t in peers_x:
        _copy(s1a.at[t], r2a.at[t], send_sems.at[2, t], recv_sems.at[2, t], 0).wait_recv()
    for t in peers_z:
        _copy(s1b.at[t], r2b.at[t], send_sems.at[3, t], recv_sems.at[3, t], 0).wait_recv()
    own_a = xa[a, b].astype(jnp.float32)
    own_b = xb[a, b].astype(jnp.float32)
    for k in range(1, RING):
        own_a = own_a + r1a[(b + k) % RING, a].astype(jnp.float32)
        own_b = own_b + r1b[(a + k) % RING, b].astype(jnp.float32)
    for k in range(1, RING):
        own_a = own_a + r2a[(a + k) % RING].astype(jnp.float32)
        own_b = own_b + r2b[(b + k) % RING].astype(jnp.float32)
    out[0] = own_a
    out[1] = own_b
    for c in first + second:
        c.wait_send()


def latent_reduce_mm(w, v, collective_id):
    n, _, d, _ = w.shape
    h = v.shape[1] // 2
    dt = w.dtype
    return pl.pallas_call(
        _reduce_mm_kernel,
        out_shape=jax.ShapeDtypeStruct((2, d, h), jnp.float32),
        in_specs=[pl.BlockSpec(memory_space=pltpu.VMEM)] * 2,
        out_specs=pl.BlockSpec(memory_space=pltpu.VMEM),
        scratch_shapes=[
            pltpu.VMEM((n, n, d, h), dt),
            pltpu.VMEM((n, n, d, h), dt),
            pltpu.VMEM((n, n, d, h), dt),
            pltpu.VMEM((n, n, d, h), dt),
            pltpu.VMEM((n, d, h), dt),
            pltpu.VMEM((n, d, h), dt),
            pltpu.VMEM((n, d, h), dt),
            pltpu.VMEM((n, d, h), dt),
            pltpu.SemaphoreType.DMA((4, n)),
            pltpu.SemaphoreType.DMA((4, n)),
        ],
        compiler_params=pltpu.CompilerParams(collective_id=collective_id, has_side_effects=True),
    )(w, v)


def _gather_kernel(e, targets, pairing, oa, ob, margin, g1a, g1b, ga, gb, send_sems, recv_sems):
    a, b = _latent_coords()
    _greet(a, b)
    peers_z = [(b + k) % RING for k in range(1, RING)]
    peers_x = [(a + k) % RING for k in range(1, RING)]
    first = []
    for t in peers_z:
        c = _copy(e.at[0], g1a.at[b], send_sems.at[0, t], recv_sems.at[0, b], a * RING + t)
        c.start()
        first.append(c)
    for t in peers_x:
        c = _copy(e.at[1], g1b.at[a], send_sems.at[1, t], recv_sems.at[1, a], t * RING + b)
        c.start()
        first.append(c)
    g1a[b] = e[0]
    g1b[a] = e[1]
    for t in peers_z:
        _copy(e.at[0], g1a.at[t], send_sems.at[0, t], recv_sems.at[0, t], 0).wait_recv()
    for t in peers_x:
        _copy(e.at[1], g1b.at[t], send_sems.at[1, t], recv_sems.at[1, t], 0).wait_recv()
    second = []
    for t in peers_x:
        c = _copy(g1a, ga.at[a], send_sems.at[2, t], recv_sems.at[2, a], t * RING + b)
        c.start()
        second.append(c)
    for t in peers_z:
        c = _copy(g1b, gb.at[b], send_sems.at[3, t], recv_sems.at[3, b], a * RING + t)
        c.start()
        second.append(c)
    oa[a] = g1a[...]
    f, q = margin.shape
    n_rows = pairing.shape[1]
    lat0 = lax.axis_index("latent") * f
    row0 = lax.axis_index("row") * (LAYERS * q) + lax.axis_index("layer") * q
    lat_ids = lat0 + lax.broadcasted_iota(jnp.int32, (f, n_rows), 0)
    target_hot = (lat_ids == targets[...]).astype(jnp.bfloat16)
    row_ids = row0 + lax.broadcasted_iota(jnp.int32, (q, n_rows), 0)
    every_row = lax.broadcasted_iota(jnp.int32, (q, n_rows), 1)
    pair_table = (
        (every_row == row_ids).astype(jnp.float32) - (pairing[...] == row_ids).astype(jnp.float32)
    ).astype(jnp.bfloat16)
    margin[...] = lax.dot_general(
        target_hot, pair_table, (((1,), (1,)), ((), ())), preferred_element_type=jnp.float32
    )
    for j in range(RING):
        ob[j, b] = g1b[j]
    for t in peers_x:
        _copy(g1a, ga.at[t], send_sems.at[2, t], recv_sems.at[2, t], 0).wait_recv()
        oa[t] = ga[t]
    for t in peers_z:
        _copy(g1b, gb.at[t], send_sems.at[3, t], recv_sems.at[3, t], 0).wait_recv()
        for j in range(RING):
            ob[j, t] = gb[t, j]
    for c in first + second:
        c.wait_send()


def latent_gather(e, targets, pairing, lat_count, collective_id):
    _, h, c = e.shape
    n = RING
    dt = e.dtype
    full = jax.ShapeDtypeStruct((n, n, h, c), dt)
    return pl.pallas_call(
        _gather_kernel,
        out_shape=(full, full, jax.ShapeDtypeStruct((lat_count, 2 * c // LAYERS), jnp.float32)),
        in_specs=[pl.BlockSpec(memory_space=pltpu.VMEM)] * 3,
        out_specs=(pl.BlockSpec(memory_space=pltpu.VMEM),) * 3,
        scratch_shapes=[
            pltpu.VMEM((n, h, c), dt),
            pltpu.VMEM((n, h, c), dt),
            pltpu.VMEM((n, n, h, c), dt),
            pltpu.VMEM((n, n, h, c), dt),
            pltpu.SemaphoreType.DMA((4, n)),
            pltpu.SemaphoreType.DMA((4, n)),
        ],
        compiler_params=pltpu.CompilerParams(collective_id=collective_id, has_side_effects=True),
    )(e, targets, pairing)


def _layer_roles():
    me = lax.axis_index("layer")
    mate = me + 1 - 2 * (me % 2)
    far = (me + 2) % LAYERS
    return me, mate, far, (mate + 2) % LAYERS


def _layer_exchange(quarter, x, out, finish, produce, ra, sb, rb, rc, rd, send_sems, recv_sems):
    me, mate, far, mate_far = _layer_roles()
    barrier = pltpu.get_barrier_semaphore()
    for p in (mate, far):
        pl.semaphore_signal(barrier, inc=1, device_id={"layer": p}, device_id_type=MESH)
    pl.semaphore_wait(barrier, 2)

    def copy(src, dst, k, p):
        return pltpu.make_async_remote_copy(
            src_ref=src, dst_ref=dst, send_sem=send_sems.at[k], recv_sem=recv_sems.at[k],
            device_id={"layer": p}, device_id_type=MESH,
        )

    produce(mate)
    produce(mate_far)
    sent = [copy(quarter(x, mate), ra.at[0], 0, mate), copy(quarter(x, mate_far), ra.at[1], 1, mate)]
    for c in sent:
        c.start()
    produce(far)
    produce(me)
    sent[0].wait_recv()
    sent[1].wait_recv()
    sb[...] = quarter(x, far)[...].astype(jnp.float32) + ra[1].astype(jnp.float32)
    step_b = copy(sb, rb, 2, far)
    step_b.start()
    own = quarter(x, me)[...].astype(jnp.float32) + ra[0].astype(jnp.float32)
    step_b.wait_recv()
    quarter(out, me)[...] = finish(own + rb[...])
    step_c = copy(quarter(out, me), rc, 3, far)
    step_c.start()
    step_c.wait_recv()
    quarter(out, far)[...] = rc[...]
    step_d = [copy(quarter(out, me), rd.at[0], 4, mate), copy(rc, rd.at[1], 5, mate)]
    for c in step_d:
        c.start()
    for c in step_d:
        c.wait_recv()
    quarter(out, mate)[...] = rd[0]
    quarter(out, mate_far)[...] = rd[1]
    for c in sent + [step_b, step_c] + step_d:
        c.wait_send()


def _row_quarter(ref, i):
    q = ref.shape[0] // LAYERS
    return ref.at[pl.ds(pl.multiple_of(i * q, q), q)]


def _lane_quarter(ref, i):
    q = ref.shape[1] // LAYERS
    return ref.at[:, pl.ds(pl.multiple_of(i * q, q), q)]


def _layer_pre_kernel(inp, w, bias, feats, pre_q, x, *scratch):
    def finish(total):
        pre = total + bias[...].reshape(1, -1)
        pre_q[...] = pre.T
        return jnp.maximum(pre, 0.0).astype(feats.dtype)

    def produce(i):
        _row_quarter(x, i)[...] = jnp.dot(
            _row_quarter(inp, i)[...], w[...], preferred_element_type=jnp.float32
        )

    _layer_exchange(_row_quarter, x, feats, finish, produce, *scratch)


def _layer_scratch(in_q, out_q, in_dtype):
    return [
        pltpu.VMEM((2,) + in_q, in_dtype),
        pltpu.VMEM(in_q, jnp.float32),
        pltpu.VMEM(in_q, jnp.float32),
        pltpu.VMEM(out_q, jnp.bfloat16),
        pltpu.VMEM((2,) + out_q, jnp.bfloat16),
        pltpu.SemaphoreType.DMA((6,)),
        pltpu.SemaphoreType.DMA((6,)),
    ]


def layer_pre(inp, w, bias):
    rows, cols = inp.shape[0], w.shape[1]
    q = rows // LAYERS
    return pl.pallas_call(
        _layer_pre_kernel,
        out_shape=(jax.ShapeDtypeStruct((rows, cols), jnp.bfloat16),
                   jax.ShapeDtypeStruct((cols, q), jnp.float32)),
        in_specs=[pl.BlockSpec(memory_space=pltpu.VMEM)] * 3,
        out_specs=(pl.BlockSpec(memory_space=pltpu.VMEM), pl.BlockSpec(memory_space=pltpu.VMEM)),
        scratch_shapes=[pltpu.VMEM((rows, cols), jnp.float32)]
        + _layer_scratch((q, cols), (q, cols), jnp.float32),
        compiler_params=pltpu.CompilerParams(collective_id=1, has_side_effects=True),
    )(inp, w, bias)


def _layer_peers():
    me = lax.axis_index("layer")
    return me, [(me + k) % LAYERS for k in range(1, LAYERS)]


def _layer_greet(peers):
    barrier = pltpu.get_barrier_semaphore()
    for p in peers:
        pl.semaphore_signal(barrier, inc=1, device_id={"layer": p}, device_id_type=MESH)
    pl.semaphore_wait(barrier, LAYERS - 1)


def _layer_copy(src, dst, send_sems, recv_sems, k, p, slot):
    return pltpu.make_async_remote_copy(
        src_ref=src, dst_ref=dst, send_sem=send_sems.at[k, p], recv_sem=recv_sems.at[k, slot],
        device_id={"layer": p}, device_id_type=MESH,
    )


def _layer_grad_kernel(g, pre_q, margin_q, out, r1, r2, send_sems, recv_sems):
    me, peers = _layer_peers()
    q = g.shape[1] // LAYERS
    lanes = lambda i: pl.ds(pl.multiple_of(i * q, q), q)
    _layer_greet(peers)
    sent = []
    for p in peers:
        c = _layer_copy(g.at[:, lanes(p)], r1.at[me], send_sems, recv_sems, 0, p, me)
        c.start()
        sent.append(c)
    total = g[:, lanes(me)].astype(jnp.float32)
    for p in peers:
        _layer_copy(g.at[:, lanes(p)], r1.at[p], send_sems, recv_sems, 0, p, p).wait_recv()
        total = total + r1[p].astype(jnp.float32)
    grad = jnp.where(pre_q[...] > 0, total - MARGIN * margin_q[...], 0.0)
    out[:, lanes(me)] = grad.astype(out.dtype)
    for p in peers:
        c = _layer_copy(out.at[:, lanes(me)], r2.at[me], send_sems, recv_sems, 1, p, me)
        c.start()
        sent.append(c)
    for p in peers:
        _layer_copy(out.at[:, lanes(p)], r2.at[p], send_sems, recv_sems, 1, p, p).wait_recv()
        out[:, lanes(p)] = r2[p]
    for c in sent:
        c.wait_send()


def layer_grad(g, pre_q, margin_q):
    cols, rows = g.shape
    q = rows // LAYERS
    return pl.pallas_call(
        _layer_grad_kernel,
        out_shape=jax.ShapeDtypeStruct((cols, rows), jnp.bfloat16),
        in_specs=[pl.BlockSpec(memory_space=pltpu.VMEM)] * 3,
        out_specs=pl.BlockSpec(memory_space=pltpu.VMEM),
        scratch_shapes=[
            pltpu.VMEM((LAYERS, cols, q), jnp.bfloat16),
            pltpu.VMEM((LAYERS, cols, q), jnp.bfloat16),
            pltpu.SemaphoreType.DMA((2, LAYERS)),
            pltpu.SemaphoreType.DMA((2, LAYERS)),
        ],
        compiler_params=pltpu.CompilerParams(collective_id=2, has_side_effects=True),
    )(g, pre_q, margin_q)


def local(inputs, clean_acts, enc_weight, enc_bias, dec_weight, dec_bias, pairing, targets):
    row_count = inputs.shape[0]
    lat_count = enc_weight.shape[2]
    all_rows = pairing.shape[0]
    d_model = inputs.shape[2]
    chunk = d_model // (RING * RING)
    half = row_count // 2
    me = lax.axis_index("latent")
    features, pre_q = layer_pre(inputs[:, 0, :], enc_weight[0], enc_bias)
    dec4 = dec_weight[0].reshape(lat_count, RING, RING, chunk)
    recon_part = jnp.einsum("rf,fabd->abdr", features, dec4, preferred_element_type=jnp.float32)
    bias_part = lax.dynamic_slice_in_dim(dec_bias[0], me * chunk, chunk)
    clean_part = lax.dynamic_slice_in_dim(clean_acts[:, 0, :], me * chunk, chunk, axis=1)
    clean_t = jnp.swapaxes(clean_part.reshape(2, half, chunk), 1, 2).astype(jnp.float32)
    recon_error = latent_reduce(recon_part.astype(jnp.bfloat16), clean_t - bias_part[:, None], 3)
    error_a, error_b, margin_q = latent_gather(
        recon_error, targets.reshape(1, all_rows), pairing.reshape(1, all_rows), lat_count, 4
    )
    error_all = jnp.concatenate(
        [error_a.reshape(d_model, half), error_b.reshape(d_model, half)], axis=1
    )
    partial_grad_t = jnp.dot(dec_weight[0], error_all, preferred_element_type=jnp.float32)
    pre_grad_t = layer_grad(partial_grad_t.astype(jnp.bfloat16), pre_q, margin_q)
    enc4 = enc_weight[0].reshape(RING, RING, chunk, lat_count)
    total = latent_reduce_mm(enc4, pre_grad_t, 5)
    return jnp.swapaxes(total.astype(jnp.bfloat16), 1, 2).reshape(row_count, 1, chunk)


def solution(mesh):
    placed = (
        P("row", "layer", None),
        P("row", "layer", None),
        P("layer", None, "latent"),
        P("latent"),
        P("layer", "latent", None),
        P("layer", None),
        P(),
        P(),
    )
    return jax.shard_map(
        local, mesh=mesh, in_specs=placed, out_specs=P("row", "layer", "latent"), check_vma=False
    )
```
